32 devices in a mesh: head: 8 (over z, x), row: 4 (over y, core).
Axes of the slice: x: 2, y: 2, z: 4, core: 2. Of those that a mesh axis runs over, the one named last changes fastest.
Arguments:
- tokens: bfloat16 [4, 2048, 2048], P('row', 'head'), may hold values from -6 to 6
- w_query: float32 [2048, 2048], P('row', 'head'), may hold values from -0.125 to 0.125
- w_key: float32 [2048, 2048], P('row', 'head'), may hold values from -0.125 to 0.125
- w_value: float32 [2048, 4096], P('row', 'head'), may hold values from -0.125 to 0.125
- w_outgate: float32 [2048, 4096], P('row', 'head'), may hold values from -0.125 to 0.125
- w_alpha: float32 [2048, 16], P('row', 'head'), may hold values from -0.125 to 0.125
- w_beta: float32 [2048, 16], P('row', 'head'), may hold values from -0.125 to 0.125
- conv_query: float32 [4, 2048], P(None, ('head', 'row')), may hold values from -3 to 3
- conv_key: float32 [4, 2048], P(None, ('head', 'row')), may hold values from -3 to 3
- conv_value: float32 [4, 4096], P(None, ('head', 'row')), may hold values from -3 to 3
- a_log: float32 [16], replicated, may hold values from -6 to -1
- dt_bias: float32 [16], replicated, may hold values from -4 to -1
- o_gain: float32 [256], replicated, may hold values from 0.5 to 1.5
- w_out: float32 [4096, 2048], P('head', 'row'), may hold values from -0.125 to 0.125
- gain_in: float32 [2048], replicated, may hold values from 0.5 to 1.5
- gain_ffn: float32 [2048], replicated, may hold values from 0.5 to 1.5
- w_gate: float32 [2048, 5632], P('head', 'row'), may hold values from -0.125 to 0.125
- w_up: float32 [2048, 5632], P('head', 'row'), may hold values from -0.125 to 0.125
- w_down: float32 [5632, 2048], P('row', 'head'), may hold values from -0.109375 to 0.109375
- segments: int32 [4, 2048], P('row'), may hold values from 0 to 2, never falling along the last dimension, each value on 1 to 1024 neighbouring positions
- valid_len: int32 [4], P('row'), may hold values from 1024 to 2048, as said below
- cotangent: bfloat16 [4, 2048, 2048], P('row', 'head'), may hold values from -6 to 6
Outputs:
- output: bfloat16 [4, 2048, 2048], P('row', 'head')
- grad_tokens: float32 [4, 2048, 2048], P('row', 'head')
- grad_w_query: float32 [2048, 2048], P('row', 'head')
- grad_w_key: float32 [2048, 2048], P('row', 'head')
- grad_w_value: float32 [2048, 4096], P('row', 'head')
- grad_w_outgate: float32 [2048, 4096], P('row', 'head')
- grad_w_alpha: float32 [2048, 16], P('row', 'head')
- grad_w_beta: float32 [2048, 16], P('row', 'head')
- grad_conv_query: float32 [4, 2048], P(None, ('head', 'row'))
- grad_conv_key: float32 [4, 2048], P(None, ('head', 'row'))
- grad_conv_value: float32 [4, 4096], P(None, ('head', 'row'))
- grad_a_log: float32 [16], replicated
- grad_dt_bias: float32 [16], replicated
- grad_o_gain: float32 [256], replicated
- grad_w_out: float32 [4096, 2048], P('head', 'row')
- grad_gain_in: float32 [2048], replicated
- grad_gain_ffn: float32 [2048], replicated
- grad_w_gate: float32 [2048, 5632], P('head', 'row')
- grad_w_up: float32 [2048, 5632], P('head', 'row')
- grad_w_down: float32 [5632, 2048], P('row', 'head')
The draws below stay inside these ranges and needn't reach their ends.
Inputs may be any that keep to these rules, and one draw needn't show every extreme that they name: `segments`: within each row group segment numbers run 0, 1, 2 without falling, and the group's longest sequence has exactly 1024 tokens. The first valid_len tokens of a row group are real and the rest are padding; at least one group has no padding.
All inputs are finite; a program needn't handle non-finite values.
Results may differ from the reference program's by a relative error of at most 0.015.
The reference program's roundings to bfloat16 on the way count: a program that leaves them out, or rounds other values in their place, can miss the bound.
Values may be sent and summed in bfloat16 or wider, within the bound.
A program may use at most 320 MiB of HBM per device.

```python
import math
import jax
import jax.numpy as jnp
import numpy as np
from jax import lax

D = 2048
HEADS = 16
DK = 128
DV = 256
FF = 5632
CONV = 4
BLOCK = 64
GROUPS = 4
GROUP_TOK = 2048


def draw_valid_len(key, part):
    lengths = jax.random.randint(key, (GROUPS,), GROUP_TOK // 2, GROUP_TOK + 1)
    full_group = jax.random.randint(jax.random.fold_in(key, 7), (), 0, GROUPS)
    return jnp.where(jnp.arange(GROUPS) == full_group, GROUP_TOK, lengths).astype(jnp.int32)


def levels(key, dims, shards, least, top_value):
    gain = 1.0
    for dim, blocks in shards:
        heights = jax.random.uniform(jax.random.fold_in(jax.random.fold_in(key, 6), dim), (blocks,), jnp.float32, least / len(shards), top_value / len(shards))
        gain = gain * jnp.repeat(jnp.exp(heights), dims[dim] // blocks).reshape((-1,) + (1,) * (len(dims) - 1 - dim))
    return gain


def length_profile(number_of, total, most, lean):
    loads = [(1 << 20) // math.isqrt(rank ** lean) + 1 for rank in range(2, number_of + 1)]
    surplus, counts = total - most - (number_of - 1), [1] * (number_of - 1)
    while surplus > 0:
        candidates = [i for i in range(number_of - 1) if counts[i] < most]
        whole, remaining = sum([loads[i] for i in candidates]), surplus
        for i in candidates:
            more = min(most - counts[i], max(1, remaining * loads[i] // whole), surplus)
            counts[i] = counts[i] + more
            surplus = surplus - more
    return np.array([most] + counts)


def ragged(key, number_of, total, limit, slope):
    if number_of == 2:
        one = jax.random.randint(key, (), max(1, total - limit), min(limit, total - 1) + 1)
        return jnp.stack([one, total - one])
    sizes = jnp.asarray(length_profile(number_of, total, limit, slope), jnp.int32)
    pairs = (number_of - 1) // 2
    source_of, receiver = sizes[1:1 + 2 * pairs:2], sizes[2:2 + 2 * pairs:2]
    slack = jnp.minimum(source_of - 1, limit - receiver)
    moved = jax.random.randint(jax.random.fold_in(key, 1), (pairs,), 0, 1 << 20) % (slack + 1)
    sizes = sizes.at[1:1 + 2 * pairs:2].set(source_of - moved).at[2:2 + 2 * pairs:2].set(receiver + moved)
    return sizes[jax.random.permutation(jax.random.fold_in(key, 2), number_of)]


def noise(key, shape, scale, limit, cuts=(), kind=jnp.bfloat16):
    drawn = scale * jax.random.normal(key, shape, jnp.float32)
    if cuts:
        drawn = drawn * levels(key, shape, cuts, -0.22, 0.18)
    return jnp.clip(drawn, -limit, limit).astype(kind)


def setup_inputs(seed: int = 0) -> dict:
    seeds = jax.random.split(jax.random.key(seed), 23)
    tokens = noise(seeds[0], (GROUPS, GROUP_TOK, D), 1.0, 6.0, ((0, 4), (1, 8)))
    w_query = noise(seeds[1], (D, HEADS * DK), D ** -0.5, 0.125, ((0, 4), (1, 8)), jnp.float32)
    w_key = noise(seeds[2], (D, HEADS * DK), D ** -0.5, 0.125, ((0, 4), (1, 8)), jnp.float32)
    w_value = noise(seeds[3], (D, HEADS * DV), D ** -0.5, 0.125, ((0, 4), (1, 8)), jnp.float32)
    w_outgate = noise(seeds[4], (D, HEADS * DV), D ** -0.5, 0.125, ((0, 4), (1, 8)), jnp.float32)
    w_alpha = noise(seeds[5], (D, HEADS), D ** -0.5, 0.125, ((0, 4), (1, 8)), jnp.float32)
    w_beta = noise(seeds[6], (D, HEADS), D ** -0.5, 0.125, ((0, 4), (1, 8)), jnp.float32)
    conv_query = noise(seeds[7], (CONV, HEADS * DK), CONV ** -0.5, 3.0, ((1, 32),), jnp.float32)
    conv_key = noise(seeds[8], (CONV, HEADS * DK), CONV ** -0.5, 3.0, ((1, 32),), jnp.float32)
    conv_value = noise(seeds[9], (CONV, HEADS * DV), CONV ** -0.5, 3.0, ((1, 32),), jnp.float32)
    a_log = jnp.clip(jax.random.uniform(seeds[10], (HEADS,), jnp.float32, -6.0, -1.0), -6.0, -1.0)
    dt_bias = jnp.clip(jax.random.uniform(seeds[11], (HEADS,), jnp.float32, -4.0, -1.0), -4.0, -1.0)
    o_gain = jnp.clip(1.0 + 0.1 * jax.random.normal(seeds[12], (DV,), jnp.float32), 0.5, 1.5)
    w_out = noise(seeds[13], (HEADS * DV, D), (HEADS * DV // 2) ** -0.5, 0.125, ((0, 8), (1, 4)), jnp.float32)
    gain_in = jnp.clip(1.0 + 0.1 * jax.random.normal(seeds[14], (D,), jnp.float32), 0.5, 1.5)
    gain_ffn = jnp.clip(1.0 + 0.1 * jax.random.normal(seeds[15], (D,), jnp.float32), 0.5, 1.5)
    w_gate = noise(seeds[16], (D, FF), D ** -0.5, 0.125, ((0, 8), (1, 4)), jnp.float32)
    w_up = noise(seeds[17], (D, FF), D ** -0.5, 0.125, ((0, 8), (1, 4)), jnp.float32)
    w_down = noise(seeds[18], (FF, D), (FF // 2) ** -0.5, 0.109375, ((0, 4), (1, 8)), jnp.float32)
    segments = jax.vmap(lambda own: jnp.searchsorted(jnp.cumsum(ragged(own, 3, GROUP_TOK, GROUP_TOK // 2, 0)), jnp.arange(GROUP_TOK), side="right"))(jax.random.split(seeds[19], GROUPS)).reshape((GROUPS, GROUP_TOK)).astype(jnp.int32)
    valid_len = draw_valid_len(jax.random.fold_in(seeds[22], 71), 0)
    cotangent = noise(seeds[21], (GROUPS, GROUP_TOK, D), 1.0, 6.0, ((0, 4), (1, 8)))
    return {"tokens": tokens, "w_query": w_query, "w_key": w_key, "w_value": w_value, "w_outgate": w_outgate, "w_alpha": w_alpha, "w_beta": w_beta, "conv_query": conv_query, "conv_key": conv_key, "conv_value": conv_value, "a_log": a_log, "dt_bias": dt_bias, "o_gain": o_gain, "w_out": w_out, "gain_in": gain_in, "gain_ffn": gain_ffn, "w_gate": w_gate, "w_up": w_up, "w_down": w_down, "segments": segments, "valid_len": valid_len, "cotangent": cotangent}


precise = lax.Precision.HIGHEST
epsilon = 1e-06
o_floor = 0.001

@jax.custom_vjp
def low(v):
    return lax.optimization_barrier(v.astype(jnp.bfloat16)).astype(jnp.float32)

@jax.custom_vjp
def low_back(v):
    return v

def low_keep(v):
    return (low(v), None)

def low_pass(kept, grad):
    return (grad,)

def back_keep(v):
    return (v, None)

def back_low(kept, grad):
    return (low(grad),)
low.defvjp(low_keep, low_pass)
low_back.defvjp(back_keep, back_low)

def rms_norm(vector, gain_vec, floor_add=epsilon):
    return vector * lax.rsqrt(lax.optimization_barrier(jnp.mean(vector * vector, axis=-1, keepdims=True)) + floor_add) * gain_vec

def unit_norm(vector):
    return vector * lax.rsqrt(lax.optimization_barrier(jnp.sum(vector * vector, axis=-1, keepdims=True)) + epsilon)

def short_conv(signal, kernel, seg_ids):
    tap_count = kernel.shape[0]
    length = signal.shape[0]
    summed = signal * kernel[tap_count - 1]
    for offset in range(1, tap_count):
        shifted = jnp.concatenate([jnp.zeros((offset, signal.shape[1]), signal.dtype), signal[:length - offset]], axis=0)
        seg_shift = jnp.concatenate([jnp.full((offset,), -1, jnp.int32), seg_ids[:length - offset].astype(jnp.int32)])
        keep_mask = (seg_shift == seg_ids.astype(jnp.int32)).astype(signal.dtype)
        summed = summed + shifted * kernel[tap_count - 1 - offset] * keep_mask[:, None]
    return summed

def span_step(carried_in, pieces):
    state_mat, last_seg = carried_in
    queries, keys_n, values, decays, beta_rate, seg_ids = pieces
    block_len = queries.shape[0]
    cumulative = jnp.cumsum(decays)
    places = jnp.arange(block_len)
    lower_tri = places[:, None] >= places[None, :]
    inside = jnp.logical_and(seg_ids[:, None] == seg_ids[None, :], lower_tri)
    log_gap = jnp.where(inside, cumulative[:, None] - cumulative[None, :], 0.0)
    within = jnp.exp(log_gap) * inside.astype(jnp.float32)
    strict = within * (places[:, None] > places[None, :]).astype(jnp.float32)
    carried = jnp.exp(cumulative) * (seg_ids == last_seg).astype(jnp.float32)
    key_gram = jnp.dot(keys_n, keys_n.T, precision=precise)
    system = jnp.eye(block_len, dtype=jnp.float32) + beta_rate[:, None] * strict * key_gram
    right_side = beta_rate[:, None] * (values - carried[:, None] * jnp.dot(keys_n, state_mat.T, precision=precise))
    update = jax.scipy.linalg.solve_triangular(system, right_side, lower=True, unit_diagonal=True)
    scores = jnp.dot(queries, keys_n.T, precision=precise) * within
    output = carried[:, None] * jnp.dot(queries, state_mat.T, precision=precise) + jnp.dot(scores, update, precision=precise)
    tail_row = within[block_len - 1]
    new_state = carried[block_len - 1] * state_mat + jnp.dot(update.T, tail_row[:, None] * keys_n, precision=precise)
    return ((new_state, seg_ids[block_len - 1]), output)

def delta_rule(queries, keys_n, values, decays, beta_rate, seg_ids):
    length = queries.shape[0]
    count_blocks = length // BLOCK

    def blocks(array):
        return array.reshape((count_blocks, BLOCK) + array.shape[1:])
    initial = (jnp.zeros((values.shape[1], keys_n.shape[1]), jnp.float32), jnp.int32(-1))
    final_carry, outputs = lax.scan(jax.checkpoint(span_step), initial, (blocks(queries), blocks(keys_n), blocks(values), blocks(decays), blocks(beta_rate), blocks(seg_ids.astype(jnp.int32))))
    return outputs.reshape(length, values.shape[1])

def head_mixer(proj_query, proj_key, proj_value, proj_gate, proj_alpha, proj_beta, kernel_query, kernel_key, kernel_value, a_here, dt_here, o_gain, seg_ids, live_mask):
    queries = unit_norm(jax.nn.silu(short_conv(proj_query, kernel_query, seg_ids))) * (1.0 / math.sqrt(proj_query.shape[1]))
    keys_n = unit_norm(jax.nn.silu(short_conv(proj_key, kernel_key, seg_ids)))
    values = jax.nn.silu(short_conv(proj_value, kernel_value, seg_ids))
    decays = -jnp.exp(a_here) * jax.nn.softplus(proj_alpha + dt_here)
    beta_rate = jax.nn.sigmoid(proj_beta)
    recurrent = delta_rule(queries, keys_n, values, decays, beta_rate, seg_ids)
    return rms_norm(recurrent, o_gain, o_floor) * jax.nn.silu(proj_gate) * live_mask[:, None]

def forward(tokens, w_query, w_key, w_value, w_outgate, w_alpha, w_beta, conv_query, conv_key, conv_value, a_log, dt_bias, o_gain, w_out, gain_in, gain_ffn, w_gate, w_up, w_down, segments, live_mask):
    groups = tokens.shape[0]
    length = tokens.shape[1]
    normed_in = low(rms_norm(tokens, gain_in))

    def project(weight):
        return low_back(jnp.einsum('gtd,dc->gtc', normed_in, low(weight), precision=precise))

    def by_head(array, width):
        return jnp.moveaxis(array.reshape(groups, length, HEADS, width), 2, 1)

    def kernel_heads(kernel, width):
        return jnp.moveaxis(low(kernel).reshape(kernel.shape[0], HEADS, width), 1, 0)
    per_head = jax.vmap(head_mixer, in_axes=(0,) * 11 + (None, None, None))
    per_group = jax.vmap(per_head, in_axes=(0,) * 6 + (None,) * 6 + (0, 0))
    mixed_heads = per_group(by_head(project(w_query), DK), by_head(project(w_key), DK), by_head(project(w_value), DV), by_head(project(w_outgate), DV), jnp.moveaxis(project(w_alpha), 2, 1), jnp.moveaxis(project(w_beta), 2, 1), kernel_heads(conv_query, DK), kernel_heads(conv_key, DK), kernel_heads(conv_value, DV), a_log, dt_bias, o_gain, segments, live_mask)
    mixed_out = low(jnp.moveaxis(mixed_heads, 1, 2).reshape(groups, length, HEADS * DV))
    middle = tokens + low_back(jnp.einsum('gtc,cd->gtd', mixed_out, low(w_out), precision=precise))
    normed_ffn = low(rms_norm(middle, gain_ffn))
    gate_pre = low_back(jnp.einsum('gtd,df->gtf', normed_ffn, low(w_gate), precision=precise))
    up_pre = low_back(jnp.einsum('gtd,df->gtf', normed_ffn, low(w_up), precision=precise))
    hidden = low(jax.nn.silu(gate_pre) * up_pre)
    return middle + low_back(jnp.einsum('gtf,fd->gtd', hidden, low(w_down), precision=precise))

def reference(tokens, w_query, w_key, w_value, w_outgate, w_alpha, w_beta, conv_query, conv_key, conv_value, a_log, dt_bias, o_gain, w_out, gain_in, gain_ffn, w_gate, w_up, w_down, segments, valid_len, cotangent):
    live_mask = (jnp.arange(GROUP_TOK)[None, :] < valid_len[:, None]).astype(jnp.float32)
    floats = (tokens.astype(jnp.float32), w_query, w_key, w_value, w_outgate, w_alpha, w_beta, conv_query, conv_key, conv_value, a_log, dt_bias, o_gain, w_out, gain_in, gain_ffn, w_gate, w_up, w_down)

    def closed(*values_in):
        return forward(*values_in, segments, live_mask)
    result, pullback = jax.vjp(closed, *floats)
    gradients = pullback(cotangent.astype(jnp.float32))
    return (result.astype(jnp.bfloat16), gradients[0], gradients[1], gradients[2], gradients[3], gradients[4], gradients[5], gradients[6], gradients[7], gradients[8], gradients[9], gradients[10], gradients[11], gradients[12], gradients[13], gradients[14], gradients[15], gradients[16], gradients[17], gradients[18])
```

```python
from functools import partial
import math

import jax
import jax.numpy as jnp
from jax import lax
from jax.sharding import PartitionSpec as P
from jax.experimental import pallas as pl
from jax.experimental.pallas import tpu as pltpu

BLOCK = 64


precise = lax.Precision.HIGHEST
epsilon = 1e-06
o_floor = 0.001


def rms_norm(vector, gain_vec, floor_add=epsilon):
    return (
        vector * lax.rsqrt(jnp.mean(vector * vector, axis=-1, keepdims=True) + floor_add) * gain_vec
    )


def unit_norm(vector):
    return vector * lax.rsqrt(jnp.sum(vector * vector, axis=-1, keepdims=True) + epsilon)


def swiglu(gate_pre, up_pre):
    return jax.nn.silu(gate_pre) * up_pre


def short_conv(signal, kernel, seg_ids):
    tap_count = kernel.shape[0]
    length = signal.shape[0]
    summed = signal * kernel[tap_count - 1]
    for offset in range(1, tap_count):
        shifted = jnp.concatenate(
            [jnp.zeros((offset, signal.shape[1]), signal.dtype), signal[: length - offset]], axis=0
        )
        seg_shift = jnp.concatenate(
            [jnp.full((offset,), -1, jnp.int32), seg_ids[: length - offset]]
        )
        keep_mask = (seg_shift == seg_ids).astype(signal.dtype)
        summed = summed + shifted * kernel[tap_count - 1 - offset] * keep_mask[:, None]
    return summed


def _recur_fwd_kernel(nb, u0_ref, w_ref, kt_ref, c_ref, s_out, u_out, s_scr):
    @pl.when(pl.program_id(1) == 0)
    def _():
        s_scr[...] = jnp.zeros_like(s_scr)

    def step(j, carry):
        state = s_scr[...]
        s_out[0, j] = state
        update = u0_ref[0, j] - lax.dot_general(
            w_ref[0, j], state, (((1,), (1,)), ((), ())),
            precision=precise, preferred_element_type=jnp.float32,
        )
        u_out[0, j] = update
        s_scr[...] = c_ref[0, j] * state + lax.dot_general(
            update, kt_ref[0, j], (((0,), (0,)), ((), ())),
            precision=precise, preferred_element_type=jnp.float32,
        )
        return carry

    lax.fori_loop(0, nb, step, 0)


def _recur_bwd_kernel(
    nb, s_ref, u_ref, w_ref, kt_ref, c_ref, ds_ref, du_ref,
    du0_out, dw_out, dkt_out, dc_out, g_scr,
):
    @pl.when(pl.program_id(1) == 0)
    def _():
        g_scr[...] = jnp.zeros_like(g_scr)

    def step(i, carry):
        j = nb - 1 - i
        grad_state = g_scr[...]
        state = s_ref[0, j]
        grad_update = du_ref[0, j] + lax.dot_general(
            kt_ref[0, j], grad_state, (((1,), (1,)), ((), ())),
            precision=precise, preferred_element_type=jnp.float32,
        )
        dkt_out[0, j] = jnp.dot(
            u_ref[0, j], grad_state, precision=precise, preferred_element_type=jnp.float32
        )
        dc_out[0, j] = jnp.sum(grad_state * state, axis=0, keepdims=True)
        du0_out[0, j] = grad_update
        dw_out[0, j] = -jnp.dot(
            grad_update, state, precision=precise, preferred_element_type=jnp.float32
        )
        g_scr[...] = (
            c_ref[0, j] * grad_state
            - lax.dot_general(
                grad_update, w_ref[0, j], (((0,), (0,)), ((), ())),
                precision=precise, preferred_element_type=jnp.float32,
            )
            + ds_ref[0, j]
        )
        return carry

    lax.fori_loop(0, nb, step, 0)


def _chunk_spec(nb, tail, reverse, count):
    if reverse:
        return pl.BlockSpec((1, nb) + tail, lambda h, b: (h, count - 1 - b, 0, 0))
    return pl.BlockSpec((1, nb) + tail, lambda h, b: (h, b, 0, 0))


def _recur_forward(u0, w, kt, c):
    heads, count, chunk, dv = u0.shape
    dk = w.shape[-1]
    nb = min(8, count)
    blocks = count // nb
    flops = 4 * heads * count * chunk * dk * dv * 6
    moved = 4 * heads * count * (2 * chunk * dv + 2 * chunk * dk + dv * dk)
    return pl.pallas_call(
        partial(_recur_fwd_kernel, nb),
        grid=(heads, blocks),
        in_specs=[
            _chunk_spec(nb, (chunk, dv), False, blocks),
            _chunk_spec(nb, (chunk, dk), False, blocks),
            _chunk_spec(nb, (chunk, dk), False, blocks),
            _chunk_spec(nb, (1, dk), False, blocks),
        ],
        out_specs=[
            _chunk_spec(nb, (dv, dk), False, blocks),
            _chunk_spec(nb, (chunk, dv), False, blocks),
        ],
        out_shape=[
            jax.ShapeDtypeStruct((heads, count, dv, dk), jnp.float32),
            jax.ShapeDtypeStruct((heads, count, chunk, dv), jnp.float32),
        ],
        scratch_shapes=[pltpu.VMEM((dv, dk), jnp.float32)],
        compiler_params=pltpu.CompilerParams(dimension_semantics=("arbitrary", "arbitrary")),
        cost_estimate=pl.CostEstimate(flops=flops, transcendentals=0, bytes_accessed=moved),
        name="delta_state_forward",
    )(u0, w, kt, c)


def _recur_backward(states, updates, w, kt, c, d_states, d_updates):
    heads, count, chunk, dv = updates.shape
    dk = w.shape[-1]
    nb = min(8, count)
    blocks = count // nb
    flops = 8 * heads * count * chunk * dk * dv * 6
    moved = 4 * heads * count * (4 * chunk * dv + 4 * chunk * dk + 2 * dv * dk)
    return pl.pallas_call(
        partial(_recur_bwd_kernel, nb),
        grid=(heads, blocks),
        in_specs=[
            _chunk_spec(nb, (dv, dk), True, blocks),
            _chunk_spec(nb, (chunk, dv), True, blocks),
            _chunk_spec(nb, (chunk, dk), True, blocks),
            _chunk_spec(nb, (chunk, dk), True, blocks),
            _chunk_spec(nb, (1, dk), True, blocks),
            _chunk_spec(nb, (dv, dk), True, blocks),
            _chunk_spec(nb, (chunk, dv), True, blocks),
        ],
        out_specs=[
            _chunk_spec(nb, (chunk, dv), True, blocks),
            _chunk_spec(nb, (chunk, dk), True, blocks),
            _chunk_spec(nb, (chunk, dk), True, blocks),
            _chunk_spec(nb, (1, dk), True, blocks),
        ],
        out_shape=[
            jax.ShapeDtypeStruct((heads, count, chunk, dv), jnp.float32),
            jax.ShapeDtypeStruct((heads, count, chunk, dk), jnp.float32),
            jax.ShapeDtypeStruct((heads, count, chunk, dk), jnp.float32),
            jax.ShapeDtypeStruct((heads, count, 1, dk), jnp.float32),
        ],
        scratch_shapes=[pltpu.VMEM((dv, dk), jnp.float32)],
        compiler_params=pltpu.CompilerParams(dimension_semantics=("arbitrary", "arbitrary")),
        cost_estimate=pl.CostEstimate(flops=flops, transcendentals=0, bytes_accessed=moved),
        name="delta_state_backward",
    )(states, updates, w, kt, c, d_states, d_updates)


@jax.custom_vjp
def state_recurrence(u0, w, kt, c):
    return _recur_forward(u0, w, kt, c)


def _recurrence_fwd(u0, w, kt, c):
    states, updates = _recur_forward(u0, w, kt, c)
    return (states, updates), (states, updates, w, kt, c)


def _recurrence_bwd(saved, grads):
    states, updates, w, kt, c = saved
    d_states, d_updates = grads
    du0, dw, dkt, dc_lanes = _recur_backward(states, updates, w, kt, c, d_states, d_updates)
    return du0, dw, dkt, dc_lanes


state_recurrence.defvjp(_recurrence_fwd, _recurrence_bwd)


def chunk_prepare(queries, keys_n, values, decays, beta_rate, seg_ids):
    length, dk = keys_n.shape
    count = length // BLOCK
    q = queries.reshape(count, BLOCK, dk)
    k = keys_n.reshape(count, BLOCK, dk)
    v = values.reshape(count, BLOCK, values.shape[1])
    beta = beta_rate.reshape(count, BLOCK)
    seg = seg_ids.reshape(count, BLOCK)
    cumulative = jnp.cumsum(decays.reshape(count, BLOCK), axis=1)
    places = jnp.arange(BLOCK)
    lower_tri = places[:, None] >= places[None, :]
    inside = jnp.logical_and(seg[:, :, None] == seg[:, None, :], lower_tri)
    log_gap = jnp.where(inside, cumulative[:, :, None] - cumulative[:, None, :], 0.0)
    within = jnp.exp(log_gap) * inside.astype(jnp.float32)
    strict = within * (places[:, None] > places[None, :]).astype(jnp.float32)
    last_seg = jnp.concatenate([jnp.full((1,), -1, seg.dtype), seg[:-1, BLOCK - 1]])
    carried = jnp.exp(cumulative) * (seg == last_seg[:, None]).astype(jnp.float32)
    key_gram = jnp.einsum("nid,njd->nij", k, k, precision=precise)
    system = jnp.eye(BLOCK, dtype=jnp.float32) + beta[:, :, None] * strict * key_gram
    right_side = jnp.concatenate([beta[:, :, None] * v, (beta * carried)[:, :, None] * k], axis=2)
    solved = lax.linalg.triangular_solve(
        system, right_side, left_side=True, lower=True, unit_diagonal=True
    )
    dv = v.shape[2]
    kt = within[:, BLOCK - 1, :, None] * k
    scores = jnp.einsum("nid,njd->nij", q, k, precision=precise) * within
    return solved[:, :, :dv], solved[:, :, dv:], kt, carried[:, BLOCK - 1], carried, scores


def chunk_finish(queries, carried, scores, states, updates):
    count = states.shape[0]
    q = queries.reshape(count, BLOCK, queries.shape[1])
    output = carried[:, :, None] * jnp.einsum(
        "nid,nvd->niv", q, states, precision=precise
    ) + jnp.einsum("nij,njv->niv", scores, updates, precision=precise)
    return output.reshape(count * BLOCK, states.shape[1])


def delta_rule(queries, keys_n, values, decays, beta_rate, seg_ids):
    u0, w, kt, tail, carried, scores = jax.vmap(chunk_prepare, in_axes=(0, 0, 0, 0, 0, None))(
        queries, keys_n, values, decays, beta_rate, seg_ids
    )
    c = jnp.broadcast_to(tail[:, :, None, None], tail.shape + (1, w.shape[-1]))
    states, updates = state_recurrence(u0, w, kt, c)
    return jax.vmap(chunk_finish)(queries, carried, scores, states, updates)


def head_inputs(proj_query, proj_key, proj_value, proj_alpha, proj_beta,
                kernel_query, kernel_key, kernel_value, a_here, dt_here, seg_ids):
    queries = unit_norm(jax.nn.silu(short_conv(proj_query, kernel_query, seg_ids))) * (
        1.0 / math.sqrt(proj_query.shape[1])
    )
    keys_n = unit_norm(jax.nn.silu(short_conv(proj_key, kernel_key, seg_ids)))
    values = jax.nn.silu(short_conv(proj_value, kernel_value, seg_ids))
    decays = -jnp.exp(a_here) * jax.nn.softplus(proj_alpha + dt_here)
    beta_rate = jax.nn.sigmoid(proj_beta)
    return queries, keys_n, values, decays, beta_rate


def head_output(recurrent, proj_gate, o_gain, live_mask):
    return rms_norm(recurrent, o_gain, o_floor) * jax.nn.silu(proj_gate) * live_mask[:, None]


def local_mixer(
    proj_query,
    proj_key,
    proj_value,
    proj_gate,
    proj_alpha,
    proj_beta,
    kernel_query,
    kernel_key,
    kernel_value,
    a_here,
    dt_here,
    o_gain,
    seg_ids=None,
    live_mask=None,
):
    row_count = proj_query.shape[0]
    heads_here = proj_alpha.shape[1]

    def by_head(array):
        return jnp.moveaxis(array.reshape(row_count, heads_here, -1), 1, 0)

    def kernel_heads(kernel):
        return jnp.moveaxis(kernel.reshape(kernel.shape[0], heads_here, -1), 1, 0)

    queries, keys_n, values, decays, beta_rate = jax.vmap(
        head_inputs, in_axes=(0,) * 10 + (None,)
    )(
        by_head(proj_query),
        by_head(proj_key),
        by_head(proj_value),
        proj_alpha.T,
        proj_beta.T,
        kernel_heads(kernel_query),
        kernel_heads(kernel_key),
        kernel_heads(kernel_value),
        a_here,
        dt_here,
        seg_ids,
    )
    recurrent = delta_rule(queries, keys_n, values, decays, beta_rate, seg_ids)
    mixed_heads = jax.vmap(head_output, in_axes=(0, 0, None, None))(
        recurrent, by_head(proj_gate), o_gain, live_mask
    )
    return jnp.moveaxis(mixed_heads, 0, 1).reshape(row_count, -1)


def contract_rows(left, right):
    return lax.dot_general(
        left, right, (((0,), (0,)), ((), ())), preferred_element_type=jnp.float32
    )


def contract_cols(left, right):
    return lax.dot_general(
        left, right, (((1,), (1,)), ((), ())), preferred_element_type=jnp.float32
    )


def on_device(
    tokens,
    w_query,
    w_key,
    w_value,
    w_outgate,
    w_alpha,
    w_beta,
    conv_query,
    conv_key,
    conv_value,
    a_log,
    dt_bias,
    o_gain,
    w_out,
    gain_in,
    gain_ffn,
    w_gate,
    w_up,
    w_down,
    segments,
    valid_len,
    cotangent,
):
    residual = tokens[0].astype(jnp.float32)
    heads_here = w_alpha.shape[1]
    head_first = lax.axis_index("head") * heads_here
    norm_one, pull_one = jax.vjp(rms_norm, residual, gain_in)
    normed_one = norm_one.astype(jnp.bfloat16)
    row_count = lax.psum(1, "row")
    w_local = jnp.concatenate(
        [w_query, w_key, w_value, w_outgate, w_alpha, w_beta], axis=1
    ).astype(jnp.bfloat16)
    edges = [0]
    for member in (w_query, w_key, w_value, w_outgate, w_alpha, w_beta):
        edges.append(edges[-1] + member.shape[1])
    w_inward = lax.all_gather(w_local, "row", axis=0, tiled=True)
    conv_local = jnp.concatenate([conv_query, conv_key, conv_value], axis=1).astype(jnp.bfloat16)
    conv_edges = [0, conv_query.shape[1], conv_query.shape[1] + conv_key.shape[1], conv_local.shape[1]]
    conv_all = lax.all_gather(conv_local, "row", axis=1, tiled=True).reshape(
        conv_local.shape[0], row_count, conv_local.shape[1]
    )
    conv_parts = [
        conv_all[:, :, conv_edges[i] : conv_edges[i + 1]].reshape(conv_local.shape[0], -1)
        for i in range(3)
    ]
    out_matrix = lax.all_gather(w_out.astype(jnp.bfloat16), "row", axis=1, tiled=True)
    ff_width = w_gate.shape[1]
    ffn_local = jnp.concatenate([w_gate, w_up, w_down.T], axis=1).astype(jnp.bfloat16)
    ffn_all = lax.all_gather(ffn_local, "head", axis=0, tiled=True)
    grad_out = cotangent[0]
    grad_out_rows = lax.all_gather(grad_out, "row", axis=0, tiled=True)
    all_rows = lax.all_gather(normed_one, "head", axis=0, tiled=True)
    projected = jnp.dot(all_rows, w_inward, preferred_element_type=jnp.float32)
    proj_parts = [projected[:, edges[spot] : edges[spot + 1]] for spot in range(6)]
    seg_ids = segments[0]
    live_mask = (jnp.arange(seg_ids.shape[0]) < valid_len[0]).astype(jnp.float32)
    a_here = lax.dynamic_slice_in_dim(a_log, head_first, heads_here)
    dt_here = lax.dynamic_slice_in_dim(dt_bias, head_first, heads_here)
    mixer_fn = partial(local_mixer, seg_ids=seg_ids, live_mask=live_mask)
    mixed, pull_core = jax.vjp(
        mixer_fn,
        proj_parts[0],
        proj_parts[1],
        proj_parts[2],
        proj_parts[3],
        proj_parts[4],
        proj_parts[5],
        conv_parts[0].astype(jnp.float32),
        conv_parts[1].astype(jnp.float32),
        conv_parts[2].astype(jnp.float32),
        a_here,
        dt_here,
        o_gain,
    )
    mixed, ffn_all, grad_out_rows = lax.optimization_barrier((mixed, ffn_all, grad_out_rows))
    w_gate_all = ffn_all[:, :ff_width]
    w_up_all = ffn_all[:, ff_width : 2 * ff_width]
    w_down_t = ffn_all[:, 2 * ff_width :]
    mixed_half = mixed.astype(jnp.bfloat16)
    mixer_output = lax.psum_scatter(
        jnp.dot(mixed_half, out_matrix, preferred_element_type=jnp.float32).astype(jnp.bfloat16),
        "head",
        scatter_dimension=0,
        tiled=True,
    ).astype(jnp.float32)
    middle = residual + mixer_output
    norm_two, pull_two = jax.vjp(rms_norm, middle, gain_ffn)
    normed_two = norm_two.astype(jnp.bfloat16)
    ffn_inputs = lax.all_gather(normed_two, "row", axis=0, tiled=True)
    gate_pre = jnp.dot(ffn_inputs, w_gate_all, preferred_element_type=jnp.float32)
    up_pre = jnp.dot(ffn_inputs, w_up_all, preferred_element_type=jnp.float32)
    hidden_val, pull_act = jax.vjp(swiglu, gate_pre, up_pre)
    hidden_half = hidden_val.astype(jnp.bfloat16)
    ffn_partial = contract_cols(hidden_half, w_down_t).astype(jnp.bfloat16)
    grad_hidden = jnp.dot(grad_out_rows, w_down_t, preferred_element_type=jnp.float32)
    grad_down_t = contract_rows(grad_out_rows, hidden_half)
    grad_gate_f, grad_up_f = pull_act(grad_hidden)
    grad_gate = grad_gate_f.astype(jnp.bfloat16)
    grad_upper = grad_up_f.astype(jnp.bfloat16)
    grad_wgate = contract_rows(ffn_inputs, grad_gate)
    grad_wup = contract_rows(ffn_inputs, grad_upper)
    grad_norm_two = lax.psum_scatter(
        (contract_cols(grad_gate, w_gate_all) + contract_cols(grad_upper, w_up_all)).astype(
            jnp.bfloat16
        ),
        "row",
        scatter_dimension=0,
        tiled=True,
    ).astype(jnp.float32)
    grad_mid_part, grad_gain_ffn = pull_two(grad_norm_two)
    grad_middle = grad_out.astype(jnp.float32) + grad_mid_part
    ffn_grad_cat = jnp.concatenate([grad_wgate, grad_wup, grad_down_t], axis=1).astype(
        jnp.bfloat16
    )
    grad_mid_half = grad_middle.astype(jnp.bfloat16)
    grad_mid_rows = lax.all_gather(grad_mid_half, "head", axis=0, tiled=True)
    grad_mid_rows, ffn_partial, ffn_grad_cat = lax.optimization_barrier(
        (grad_mid_rows, ffn_partial, ffn_grad_cat)
    )
    ffn_output = lax.psum_scatter(ffn_partial, "row", scatter_dimension=0, tiled=True)
    ffn_grad_all = lax.psum_scatter(ffn_grad_cat, "head", scatter_dimension=0, tiled=True)
    grad_mixed = contract_cols(grad_mid_rows, out_matrix)
    grad_wout = contract_rows(mixed_half, grad_mid_rows)
    wout_grad = lax.psum_scatter(
        grad_wout.astype(jnp.bfloat16), "row", scatter_dimension=1, tiled=True
    )
    core_grads = pull_core(grad_mixed)
    core_grads, ffn_output, ffn_grad_all, wout_grad = lax.optimization_barrier(
        (core_grads, ffn_output, ffn_grad_all, wout_grad)
    )
    final_out = (middle + ffn_output.astype(jnp.float32)).astype(jnp.bfloat16)
    ffn_grad_all = ffn_grad_all.astype(jnp.float32)
    ffn_grads = (
        ffn_grad_all[:, :ff_width],
        ffn_grad_all[:, ff_width : 2 * ff_width],
        ffn_grad_all[:, 2 * ff_width :].T,
    )
    grad_proj = jnp.concatenate(
        [core_grads[0], core_grads[1], core_grads[2], core_grads[3], core_grads[4], core_grads[5]],
        axis=1,
    ).astype(jnp.bfloat16)
    grad_inward = contract_rows(all_rows, grad_proj).astype(jnp.bfloat16)
    grad_norm_one = lax.psum_scatter(
        contract_cols(grad_proj, w_inward).astype(jnp.bfloat16),
        "head",
        scatter_dimension=0,
        tiled=True,
    )
    grad_norm_one, grad_inward = lax.optimization_barrier((grad_norm_one, grad_inward))
    grad_norm_one = grad_norm_one.astype(jnp.float32)
    grad_in_part, grad_gain_in = pull_one(grad_norm_one)
    grad_input = grad_middle + grad_in_part
    inward_all = lax.psum_scatter(
        grad_inward, "row", scatter_dimension=0, tiled=True
    ).astype(jnp.float32)
    conv_grad_local = jnp.concatenate(
        [
            core_grads[6 + i].reshape(conv_local.shape[0], row_count, -1)
            for i in range(3)
        ],
        axis=2,
    ).reshape(conv_local.shape[0], -1)
    conv_grad = lax.psum_scatter(
        conv_grad_local.astype(jnp.bfloat16), "row", scatter_dimension=1, tiled=True
    ).astype(jnp.float32)
    mixer_grads = tuple(inward_all[:, edges[spot] : edges[spot + 1]] for spot in range(6)) + tuple(
        conv_grad[:, conv_edges[i] : conv_edges[i + 1]] for i in range(3)
    ) + (wout_grad.astype(jnp.float32),)
    head_total = a_log.shape[0]
    grad_a_full = lax.dynamic_update_slice_in_dim(
        jnp.zeros((head_total,), jnp.float32), core_grads[9], head_first, 0
    )
    grad_dt_full = lax.dynamic_update_slice_in_dim(
        jnp.zeros((head_total,), jnp.float32), core_grads[10], head_first, 0
    )
    small_sums = lax.psum(
        (grad_gain_in, grad_gain_ffn, core_grads[11], grad_a_full, grad_dt_full), ("head", "row")
    )
    return (
        final_out[None],
        grad_input[None],
        mixer_grads[0],
        mixer_grads[1],
        mixer_grads[2],
        mixer_grads[3],
        mixer_grads[4],
        mixer_grads[5],
        mixer_grads[6],
        mixer_grads[7],
        mixer_grads[8],
        small_sums[3],
        small_sums[4],
        small_sums[2],
        mixer_grads[9],
        small_sums[0],
        small_sums[1],
        ffn_grads[0],
        ffn_grads[1],
        ffn_grads[2],
    )


def solution(mesh):
    return jax.shard_map(
        on_device,
        mesh=mesh,
        in_specs=(
            P("row", "head", None),
            P("row", "head"),
            P("row", "head"),
            P("row", "head"),
            P("row", "head"),
            P("row", "head"),
            P("row", "head"),
            P(None, ("head", "row")),
            P(None, ("head", "row")),
            P(None, ("head", "row")),
            P(),
            P(),
            P(),
            P("head", "row"),
            P(),
            P(),
            P("head", "row"),
            P("head", "row"),
            P("row", "head"),
            P("row", None),
            P("row"),
            P("row", "head", None),
        ),
        out_specs=(
            P("row", "head", None),
            P("row", "head", None),
            P("row", "head"),
            P("row", "head"),
            P("row", "head"),
            P("row", "head"),
            P("row", "head"),
            P("row", "head"),
            P(None, ("head", "row")),
            P(None, ("head", "row")),
            P(None, ("head", "row")),
            P(),
            P(),
            P(),
            P("head", "row"),
            P(),
            P(),
            P("head", "row"),
            P("head", "row"),
            P("row", "head"),
        ),
        check_vma=False,
    )
```

```python
from functools import partial
import math

import jax
import jax.numpy as jnp
from jax import lax
from jax.sharding import PartitionSpec as P
from jax.experimental import pallas as pl
from jax.experimental.pallas import tpu as pltpu

BLOCK = 64


precise = lax.Precision.HIGHEST
epsilon = 1e-06
o_floor = 0.001


def rms_norm(vector, gain_vec, floor_add=epsilon):
    return (
        vector * lax.rsqrt(jnp.mean(vector * vector, axis=-1, keepdims=True) + floor_add) * gain_vec
    )


def unit_norm(vector):
    return vector * lax.rsqrt(jnp.sum(vector * vector, axis=-1, keepdims=True) + epsilon)


def swiglu(gate_pre, up_pre):
    return jax.nn.silu(gate_pre) * up_pre


def short_conv(signal, kernel, seg_ids):
    tap_count = kernel.shape[0]
    length = signal.shape[0]
    summed = signal * kernel[tap_count - 1]
    for offset in range(1, tap_count):
        shifted = jnp.concatenate(
            [jnp.zeros((offset, signal.shape[1]), signal.dtype), signal[: length - offset]], axis=0
        )
        seg_shift = jnp.concatenate(
            [jnp.full((offset,), -1, jnp.int32), seg_ids[: length - offset]]
        )
        keep_mask = (seg_shift == seg_ids).astype(signal.dtype)
        summed = summed + shifted * kernel[tap_count - 1 - offset] * keep_mask[:, None]
    return summed


def _recur_fwd_kernel(nb, u0_ref, w_ref, kt_ref, c_ref, s_out, u_out, s_scr):
    @pl.when(pl.program_id(1) == 0)
    def _():
        s_scr[...] = jnp.zeros_like(s_scr)

    def step(j, carry):
        state = s_scr[...]
        s_out[0, j] = state
        update = u0_ref[0, j] - lax.dot_general(
            w_ref[0, j], state, (((1,), (1,)), ((), ())),
            precision=precise, preferred_element_type=jnp.float32,
        )
        u_out[0, j] = update
        s_scr[...] = c_ref[0, j] * state + lax.dot_general(
            update, kt_ref[0, j], (((0,), (0,)), ((), ())),
            precision=precise, preferred_element_type=jnp.float32,
        )
        return carry

    lax.fori_loop(0, nb, step, 0)


def _recur_bwd_kernel(
    nb, s_ref, u_ref, w_ref, kt_ref, c_ref, ds_ref, du_ref,
    du0_out, dw_out, dkt_out, dc_out, g_scr,
):
    @pl.when(pl.program_id(1) == 0)
    def _():
        g_scr[...] = jnp.zeros_like(g_scr)

    def step(i, carry):
        j = nb - 1 - i
        grad_state = g_scr[...]
        state = s_ref[0, j]
        grad_update = du_ref[0, j] + lax.dot_general(
            kt_ref[0, j], grad_state, (((1,), (1,)), ((), ())),
            precision=precise, preferred_element_type=jnp.float32,
        )
        dkt_out[0, j] = jnp.dot(
            u_ref[0, j], grad_state, precision=precise, preferred_element_type=jnp.float32
        )
        dc_out[0, j] = jnp.sum(grad_state * state, axis=0, keepdims=True)
        du0_out[0, j] = grad_update
        dw_out[0, j] = -jnp.dot(
            grad_update, state, precision=precise, preferred_element_type=jnp.float32
        )
        g_scr[...] = (
            c_ref[0, j] * grad_state
            - lax.dot_general(
                grad_update, w_ref[0, j], (((0,), (0,)), ((), ())),
                precision=precise, preferred_element_type=jnp.float32,
            )
            + ds_ref[0, j]
        )
        return carry

    lax.fori_loop(0, nb, step, 0)


def _chunk_spec(nb, tail, reverse, count):
    if reverse:
        return pl.BlockSpec((1, nb) + tail, lambda h, b: (h, count - 1 - b, 0, 0))
    return pl.BlockSpec((1, nb) + tail, lambda h, b: (h, b, 0, 0))


def _recur_forward(u0, w, kt, c):
    heads, count, chunk, dv = u0.shape
    dk = w.shape[-1]
    nb = min(8, count)
    blocks = count // nb
    flops = 4 * heads * count * chunk * dk * dv * 6
    moved = 4 * heads * count * (2 * chunk * dv + 2 * chunk * dk + dv * dk)
    return pl.pallas_call(
        partial(_recur_fwd_kernel, nb),
        grid=(heads, blocks),
        in_specs=[
            _chunk_spec(nb, (chunk, dv), False, blocks),
            _chunk_spec(nb, (chunk, dk), False, blocks),
            _chunk_spec(nb, (chunk, dk), False, blocks),
            _chunk_spec(nb, (1, dk), False, blocks),
        ],
        out_specs=[
            _chunk_spec(nb, (dv, dk), False, blocks),
            _chunk_spec(nb, (chunk, dv), False, blocks),
        ],
        out_shape=[
            jax.ShapeDtypeStruct((heads, count, dv, dk), jnp.float32),
            jax.ShapeDtypeStruct((heads, count, chunk, dv), jnp.float32),
        ],
        scratch_shapes=[pltpu.VMEM((dv, dk), jnp.float32)],
        compiler_params=pltpu.CompilerParams(dimension_semantics=("arbitrary", "arbitrary")),
        cost_estimate=pl.CostEstimate(flops=flops, transcendentals=0, bytes_accessed=moved),
        name="delta_state_forward",
    )(u0, w, kt, c)


def _recur_backward(states, updates, w, kt, c, d_states, d_updates):
    heads, count, chunk, dv = updates.shape
    dk = w.shape[-1]
    nb = min(8, count)
    blocks = count // nb
    flops = 8 * heads * count * chunk * dk * dv * 6
    moved = 4 * heads * count * (4 * chunk * dv + 4 * chunk * dk + 2 * dv * dk)
    return pl.pallas_call(
        partial(_recur_bwd_kernel, nb),
        grid=(heads, blocks),
        in_specs=[
            _chunk_spec(nb, (dv, dk), True, blocks),
            _chunk_spec(nb, (chunk, dv), True, blocks),
            _chunk_spec(nb, (chunk, dk), True, blocks),
            _chunk_spec(nb, (chunk, dk), True, blocks),
            _chunk_spec(nb, (1, dk), True, blocks),
            _chunk_spec(nb, (dv, dk), True, blocks),
            _chunk_spec(nb, (chunk, dv), True, blocks),
        ],
        out_specs=[
            _chunk_spec(nb, (chunk, dv), True, blocks),
            _chunk_spec(nb, (chunk, dk), True, blocks),
            _chunk_spec(nb, (chunk, dk), True, blocks),
            _chunk_spec(nb, (1, dk), True, blocks),
        ],
        out_shape=[
            jax.ShapeDtypeStruct((heads, count, chunk, dv), jnp.float32),
            jax.ShapeDtypeStruct((heads, count, chunk, dk), jnp.float32),
            jax.ShapeDtypeStruct((heads, count, chunk, dk), jnp.float32),
            jax.ShapeDtypeStruct((heads, count, 1, dk), jnp.float32),
        ],
        scratch_shapes=[pltpu.VMEM((dv, dk), jnp.float32)],
        compiler_params=pltpu.CompilerParams(dimension_semantics=("arbitrary", "arbitrary")),
        cost_estimate=pl.CostEstimate(flops=flops, transcendentals=0, bytes_accessed=moved),
        name="delta_state_backward",
    )(states, updates, w, kt, c, d_states, d_updates)


@jax.custom_vjp
def state_recurrence(u0, w, kt, c):
    return _recur_forward(u0, w, kt, c)


def _recurrence_fwd(u0, w, kt, c):
    states, updates = _recur_forward(u0, w, kt, c)
    return (states, updates), (states, updates, w, kt, c)


def _recurrence_bwd(saved, grads):
    states, updates, w, kt, c = saved
    d_states, d_updates = grads
    du0, dw, dkt, dc_lanes = _recur_backward(states, updates, w, kt, c, d_states, d_updates)
    return du0, dw, dkt, dc_lanes


state_recurrence.defvjp(_recurrence_fwd, _recurrence_bwd)


def chunk_prepare(queries, keys_n, values, decays, beta_rate, seg_ids):
    length, dk = keys_n.shape
    count = length // BLOCK
    q = queries.reshape(count, BLOCK, dk)
    k = keys_n.reshape(count, BLOCK, dk)
    v = values.reshape(count, BLOCK, values.shape[1])
    beta = beta_rate.reshape(count, BLOCK)
    seg = seg_ids.reshape(count, BLOCK)
    cumulative = jnp.cumsum(decays.reshape(count, BLOCK), axis=1)
    places = jnp.arange(BLOCK)
    lower_tri = places[:, None] >= places[None, :]
    inside = jnp.logical_and(seg[:, :, None] == seg[:, None, :], lower_tri)
    log_gap = jnp.where(inside, cumulative[:, :, None] - cumulative[:, None, :], 0.0)
    within = jnp.exp(log_gap) * inside.astype(jnp.float32)
    strict = within * (places[:, None] > places[None, :]).astype(jnp.float32)
    last_seg = jnp.concatenate([jnp.full((1,), -1, seg.dtype), seg[:-1, BLOCK - 1]])
    carried = jnp.exp(cumulative) * (seg == last_seg[:, None]).astype(jnp.float32)
    key_gram = jnp.einsum("nid,njd->nij", k, k, precision=precise)
    system = jnp.eye(BLOCK, dtype=jnp.float32) + beta[:, :, None] * strict * key_gram
    right_side = jnp.concatenate([beta[:, :, None] * v, (beta * carried)[:, :, None] * k], axis=2)
    solved = lax.linalg.triangular_solve(
        system, right_side, left_side=True, lower=True, unit_diagonal=True
    )
    dv = v.shape[2]
    kt = within[:, BLOCK - 1, :, None] * k
    scores = jnp.einsum("nid,njd->nij", q, k, precision=precise) * within
    return solved[:, :, :dv], solved[:, :, dv:], kt, carried[:, BLOCK - 1], carried, scores


def chunk_finish(queries, carried, scores, states, updates):
    count = states.shape[0]
    q = queries.reshape(count, BLOCK, queries.shape[1])
    output = carried[:, :, None] * jnp.einsum(
        "nid,nvd->niv", q, states, precision=precise
    ) + jnp.einsum("nij,njv->niv", scores, updates, precision=precise)
    return output.reshape(count * BLOCK, states.shape[1])


def delta_rule(queries, keys_n, values, decays, beta_rate, seg_ids):
    u0, w, kt, tail, carried, scores = jax.vmap(chunk_prepare, in_axes=(0, 0, 0, 0, 0, None))(
        queries, keys_n, values, decays, beta_rate, seg_ids
    )
    c = jnp.broadcast_to(tail[:, :, None, None], tail.shape + (1, w.shape[-1]))
    states, updates = state_recurrence(u0, w, kt, c)
    return jax.vmap(chunk_finish)(queries, carried, scores, states, updates)


def head_inputs(proj_query, proj_key, proj_value, proj_alpha, proj_beta,
                kernel_query, kernel_key, kernel_value, a_here, dt_here, seg_ids):
    queries = unit_norm(jax.nn.silu(short_conv(proj_query, kernel_query, seg_ids))) * (
        1.0 / math.sqrt(proj_query.shape[1])
    )
    keys_n = unit_norm(jax.nn.silu(short_conv(proj_key, kernel_key, seg_ids)))
    values = jax.nn.silu(short_conv(proj_value, kernel_value, seg_ids))
    decays = -jnp.exp(a_here) * jax.nn.softplus(proj_alpha + dt_here)
    beta_rate = jax.nn.sigmoid(proj_beta)
    return queries, keys_n, values, decays, beta_rate


def head_output(recurrent, proj_gate, o_gain, live_mask):
    return rms_norm(recurrent, o_gain, o_floor) * jax.nn.silu(proj_gate) * live_mask[:, None]


def local_mixer(
    proj_query,
    proj_key,
    proj_value,
    proj_gate,
    proj_alpha,
    proj_beta,
    kernel_query,
    kernel_key,
    kernel_value,
    a_here,
    dt_here,
    o_gain,
    seg_ids=None,
    live_mask=None,
):
    row_count = proj_query.shape[0]
    heads_here = proj_alpha.shape[1]

    def by_head(array):
        return jnp.moveaxis(array.reshape(row_count, heads_here, -1), 1, 0)

    def kernel_heads(kernel):
        return jnp.moveaxis(kernel.reshape(kernel.shape[0], heads_here, -1), 1, 0)

    queries, keys_n, values, decays, beta_rate = jax.vmap(
        head_inputs, in_axes=(0,) * 10 + (None,)
    )(
        by_head(proj_query),
        by_head(proj_key),
        by_head(proj_value),
        proj_alpha.T,
        proj_beta.T,
        kernel_heads(kernel_query),
        kernel_heads(kernel_key),
        kernel_heads(kernel_value),
        a_here,
        dt_here,
        seg_ids,
    )
    recurrent = delta_rule(queries, keys_n, values, decays, beta_rate, seg_ids)
    mixed_heads = jax.vmap(head_output, in_axes=(0, 0, None, None))(
        recurrent, by_head(proj_gate), o_gain, live_mask
    )
    return jnp.moveaxis(mixed_heads, 0, 1).reshape(row_count, -1)


MESH_ID = pl.DeviceIdType.MESH


def _ring_position(h, major, minor):
    a = h // minor
    b = h % minor
    return b * major + a + (b % 2) * (major - 1 - 2 * a)


def _ring_member(q, major, minor):
    count = major * minor
    q = (q + count) % count
    b = q // major
    r = q % major
    return (r + (b % 2) * (major - 1 - 2 * r)) * minor + b


def _ring_sides(major, minor):
    p = _ring_position(lax.axis_index("head"), major, minor)
    return p, _ring_member(p + 1, major, minor), _ring_member(p - 1, major, minor)


def _greet(nxt, prv, row):
    barrier = pltpu.get_barrier_semaphore()
    pl.semaphore_signal(barrier, 1, device_id=(prv, row), device_id_type=MESH_ID)
    pl.semaphore_signal(barrier, 1, device_id=(nxt, row), device_id_type=MESH_ID)
    pl.semaphore_wait(barrier, 2)


def _ring_gather_kernel(major, minor, x_ref, out_ref, send_sem, recv_sem):
    count = major * minor
    blk = x_ref.shape[0]
    half = blk // 2
    row = lax.axis_index("row")
    p, nxt, prv = _ring_sides(major, minor)
    out_ref[pl.ds(pl.multiple_of(lax.axis_index("head") * blk, blk), blk), :] = x_ref[...]
    _greet(nxt, prv, row)

    def piece(pos, off):
        return out_ref.at[pl.ds(pl.multiple_of(_ring_member(pos, major, minor) * blk + off, half), half)]

    def outgoing(d, s):
        pos = p - s if d == 0 else p + s
        target = nxt if d == 0 else prv
        ref = piece(pos, d * half)
        return pltpu.make_async_remote_copy(
            ref, ref, send_sem.at[d, s], recv_sem.at[d, s], device_id=(target, row),
            device_id_type=MESH_ID,
        )

    def incoming(d, s):
        pos = p - 1 - s if d == 0 else p + 1 + s
        source = prv if d == 0 else nxt
        ref = piece(pos, d * half)
        return pltpu.make_async_remote_copy(
            ref, ref, send_sem.at[d, s], recv_sem.at[d, s], device_id=(source, row),
            device_id_type=MESH_ID,
        )

    for s in range(count - 1):
        for d in (0, 1):
            if s > 0:
                incoming(d, s - 1).wait_recv()
            outgoing(d, s).start()
    for d in (0, 1):
        incoming(d, count - 2).wait_recv()
    for s in range(count - 1):
        for d in (0, 1):
            outgoing(d, s).wait_send()


def _ring_scatter_kernel(major, minor, y_ref, out_ref, buf, send_sem, recv_sem):
    count = major * minor
    blk = out_ref.shape[0]
    half = blk // 2
    row = lax.axis_index("row")
    p, nxt, prv = _ring_sides(major, minor)
    _greet(nxt, prv, row)

    def piece(pos, off):
        return y_ref.at[pl.ds(pl.multiple_of(_ring_member(pos, major, minor) * blk + off, half), half)]

    def outgoing(d, s):
        pos = p - s - 1 if d == 0 else p + s + 1
        target = nxt if d == 0 else prv
        source = piece(pos, d * half) if s == 0 else buf.at[d, s - 1]
        return pltpu.make_async_remote_copy(
            source, buf.at[d, s], send_sem.at[d, s], recv_sem.at[d, s],
            device_id=(target, row), device_id_type=MESH_ID,
        )

    def incoming(d, s):
        source = prv if d == 0 else nxt
        return pltpu.make_async_remote_copy(
            buf.at[d, s], buf.at[d, s], send_sem.at[d, s], recv_sem.at[d, s],
            device_id=(source, row), device_id_type=MESH_ID,
        )

    for s in range(count - 1):
        for d in (0, 1):
            if s > 0:
                incoming(d, s - 1).wait_recv()
                pos = p - s - 1 if d == 0 else p + s + 1
                buf[d, s - 1] = (
                    buf[d, s - 1].astype(jnp.float32)
                    + piece(pos, d * half)[...].astype(jnp.float32)
                ).astype(buf.dtype)
            outgoing(d, s).start()
    for d in (0, 1):
        incoming(d, count - 2).wait_recv()
        out_ref[pl.ds(d * half, half), :] = piece(p, d * half)[...].astype(
            jnp.float32
        ) + buf[d, count - 2].astype(jnp.float32)
    for s in range(count - 1):
        for d in (0, 1):
            outgoing(d, s).wait_send()


def ring_gather(x, ring, collective):
    major, minor = ring
    count = major * minor
    blk, width = x.shape
    return pl.pallas_call(
        partial(_ring_gather_kernel, major, minor),
        out_shape=jax.ShapeDtypeStruct((count * blk, width), x.dtype),
        in_specs=[pl.BlockSpec(memory_space=pltpu.VMEM)],
        out_specs=pl.BlockSpec(memory_space=pltpu.VMEM),
        scratch_shapes=[
            pltpu.SemaphoreType.DMA((2, count - 1)),
            pltpu.SemaphoreType.DMA((2, count - 1)),
        ],
        compiler_params=pltpu.CompilerParams(collective_id=collective, has_side_effects=True),
        name="ring_gather_head",
    )(x)


def ring_scatter(y, ring, collective):
    major, minor = ring
    count = major * minor
    rows, width = y.shape
    blk = rows // count
    return pl.pallas_call(
        partial(_ring_scatter_kernel, major, minor),
        out_shape=jax.ShapeDtypeStruct((blk, width), jnp.float32),
        in_specs=[pl.BlockSpec(memory_space=pltpu.VMEM)],
        out_specs=pl.BlockSpec(memory_space=pltpu.VMEM),
        scratch_shapes=[
            pltpu.VMEM((2, count - 1, blk // 2, width), y.dtype),
            pltpu.SemaphoreType.DMA((2, count - 1)),
            pltpu.SemaphoreType.DMA((2, count - 1)),
        ],
        compiler_params=pltpu.CompilerParams(collective_id=collective, has_side_effects=True),
        name="ring_scatter_head",
    )(y)


def head_ring(mesh):
    count = mesh.shape["head"]
    try:
        spots = [tuple(device.coords) for device in mesh.devices[:, 0]]
    except (AttributeError, TypeError):
        return (count, 1)
    moving = [axis for axis in range(len(spots[0])) if spots[0][axis] != spots[1][axis]]
    if len(moving) != 1:
        return (count, 1)
    minor = len({spot[moving[0]] for spot in spots})
    if count % minor or minor % 2:
        return (count, 1)
    return (count // minor, minor)


def contract_rows(left, right):
    return lax.dot_general(
        left, right, (((0,), (0,)), ((), ())), preferred_element_type=jnp.float32
    )


def contract_cols(left, right):
    return lax.dot_general(
        left, right, (((1,), (1,)), ((), ())), preferred_element_type=jnp.float32
    )


def on_device(
    ring,
    tokens,
    w_query,
    w_key,
    w_value,
    w_outgate,
    w_alpha,
    w_beta,
    conv_query,
    conv_key,
    conv_value,
    a_log,
    dt_bias,
    o_gain,
    w_out,
    gain_in,
    gain_ffn,
    w_gate,
    w_up,
    w_down,
    segments,
    valid_len,
    cotangent,
):
    residual = tokens[0].astype(jnp.float32)
    heads_here = w_alpha.shape[1]
    head_first = lax.axis_index("head") * heads_here
    norm_one, pull_one = jax.vjp(rms_norm, residual, gain_in)
    normed_one = norm_one.astype(jnp.bfloat16)
    row_count = lax.psum(1, "row")
    w_local = jnp.concatenate(
        [w_query, w_key, w_value, w_outgate, w_alpha, w_beta], axis=1
    ).astype(jnp.bfloat16)
    edges = [0]
    for member in (w_query, w_key, w_value, w_outgate, w_alpha, w_beta):
        edges.append(edges[-1] + member.shape[1])
    w_inward = lax.all_gather(w_local, "row", axis=0, tiled=True)
    conv_local = jnp.concatenate([conv_query, conv_key, conv_value], axis=1).astype(jnp.bfloat16)
    conv_edges = [0, conv_query.shape[1], conv_query.shape[1] + conv_key.shape[1], conv_local.shape[1]]
    conv_all = lax.all_gather(conv_local, "row", axis=1, tiled=True).reshape(
        conv_local.shape[0], row_count, conv_local.shape[1]
    )
    conv_parts = [
        conv_all[:, :, conv_edges[i] : conv_edges[i + 1]].reshape(conv_local.shape[0], -1)
        for i in range(3)
    ]
    out_matrix = lax.all_gather(w_out.astype(jnp.bfloat16), "row", axis=1, tiled=True)
    ff_width = w_gate.shape[1]
    ffn_local = jnp.concatenate([w_gate, w_up, w_down.T], axis=1).astype(jnp.bfloat16)
    ffn_all = lax.all_gather(ffn_local, "head", axis=0, tiled=True)
    grad_out = cotangent[0]
    grad_out_rows = lax.all_gather(grad_out, "row", axis=0, tiled=True)
    all_rows = ring_gather(normed_one, ring, 0)
    projected = jnp.dot(all_rows, w_inward, preferred_element_type=jnp.float32)
    proj_parts = [projected[:, edges[spot] : edges[spot + 1]] for spot in range(6)]
    seg_ids = segments[0]
    live_mask = (jnp.arange(seg_ids.shape[0]) < valid_len[0]).astype(jnp.float32)
    a_here = lax.dynamic_slice_in_dim(a_log, head_first, heads_here)
    dt_here = lax.dynamic_slice_in_dim(dt_bias, head_first, heads_here)
    mixer_fn = partial(local_mixer, seg_ids=seg_ids, live_mask=live_mask)
    mixed, pull_core = jax.vjp(
        mixer_fn,
        proj_parts[0],
        proj_parts[1],
        proj_parts[2],
        proj_parts[3],
        proj_parts[4],
        proj_parts[5],
        conv_parts[0].astype(jnp.float32),
        conv_parts[1].astype(jnp.float32),
        conv_parts[2].astype(jnp.float32),
        a_here,
        dt_here,
        o_gain,
    )
    mixed, ffn_all, grad_out_rows = lax.optimization_barrier((mixed, ffn_all, grad_out_rows))
    w_gate_all = ffn_all[:, :ff_width]
    w_up_all = ffn_all[:, ff_width : 2 * ff_width]
    w_down_t = ffn_all[:, 2 * ff_width :]
    mixed_half = mixed.astype(jnp.bfloat16)
    mixer_output = ring_scatter(
        jnp.dot(mixed_half, out_matrix, preferred_element_type=jnp.float32).astype(jnp.bfloat16),
        ring,
        1,
    )
    middle = residual + mixer_output
    norm_two, pull_two = jax.vjp(rms_norm, middle, gain_ffn)
    normed_two = norm_two.astype(jnp.bfloat16)
    ffn_inputs = lax.all_gather(normed_two, "row", axis=0, tiled=True)
    gate_pre = jnp.dot(ffn_inputs, w_gate_all, preferred_element_type=jnp.float32)
    up_pre = jnp.dot(ffn_inputs, w_up_all, preferred_element_type=jnp.float32)
    hidden_val, pull_act = jax.vjp(swiglu, gate_pre, up_pre)
    hidden_half = hidden_val.astype(jnp.bfloat16)
    ffn_partial = contract_cols(hidden_half, w_down_t).astype(jnp.bfloat16)
    grad_hidden = jnp.dot(grad_out_rows, w_down_t, preferred_element_type=jnp.float32)
    grad_down_t = contract_rows(grad_out_rows, hidden_half)
    grad_gate_f, grad_up_f = pull_act(grad_hidden)
    grad_gate = grad_gate_f.astype(jnp.bfloat16)
    grad_upper = grad_up_f.astype(jnp.bfloat16)
    grad_wgate = contract_rows(ffn_inputs, grad_gate)
    grad_wup = contract_rows(ffn_inputs, grad_upper)
    grad_norm_two = lax.psum_scatter(
        (contract_cols(grad_gate, w_gate_all) + contract_cols(grad_upper, w_up_all)).astype(
            jnp.bfloat16
        ),
        "row",
        scatter_dimension=0,
        tiled=True,
    ).astype(jnp.float32)
    grad_mid_part, grad_gain_ffn = pull_two(grad_norm_two)
    grad_middle = grad_out.astype(jnp.float32) + grad_mid_part
    ffn_grad_cat = jnp.concatenate([grad_wgate, grad_wup, grad_down_t], axis=1).astype(
        jnp.bfloat16
    )
    grad_mid_half = grad_middle.astype(jnp.bfloat16)
    grad_mid_rows = ring_gather(grad_mid_half, ring, 2)
    grad_mid_rows, ffn_partial, ffn_grad_cat = lax.optimization_barrier(
        (grad_mid_rows, ffn_partial, ffn_grad_cat)
    )
    ffn_output = lax.psum_scatter(ffn_partial, "row", scatter_dimension=0, tiled=True)
    ffn_grad_all = lax.psum_scatter(ffn_grad_cat, "head", scatter_dimension=0, tiled=True)
    grad_mixed = contract_cols(grad_mid_rows, out_matrix)
    grad_wout = contract_rows(mixed_half, grad_mid_rows)
    wout_grad = lax.psum_scatter(
        grad_wout.astype(jnp.bfloat16), "row", scatter_dimension=1, tiled=True
    )
    core_grads = pull_core(grad_mixed)
    core_grads, ffn_output, ffn_grad_all, wout_grad = lax.optimization_barrier(
        (core_grads, ffn_output, ffn_grad_all, wout_grad)
    )
    final_out = (middle + ffn_output.astype(jnp.float32)).astype(jnp.bfloat16)
    ffn_grad_all = ffn_grad_all.astype(jnp.float32)
    ffn_grads = (
        ffn_grad_all[:, :ff_width],
        ffn_grad_all[:, ff_width : 2 * ff_width],
        ffn_grad_all[:, 2 * ff_width :].T,
    )
    grad_proj = jnp.concatenate(
        [core_grads[0], core_grads[1], core_grads[2], core_grads[3], core_grads[4], core_grads[5]],
        axis=1,
    ).astype(jnp.bfloat16)
    grad_inward = contract_rows(all_rows, grad_proj).astype(jnp.bfloat16)
    grad_norm_one = ring_scatter(contract_cols(grad_proj, w_inward).astype(jnp.bfloat16), ring, 3)
    grad_in_part, grad_gain_in = pull_one(grad_norm_one)
    grad_input = grad_middle + grad_in_part
    inward_all = lax.psum_scatter(
        grad_inward, "row", scatter_dimension=0, tiled=True
    ).astype(jnp.float32)
    conv_grad_local = jnp.concatenate(
        [
            core_grads[6 + i].reshape(conv_local.shape[0], row_count, -1)
            for i in range(3)
        ],
        axis=2,
    ).reshape(conv_local.shape[0], -1)
    conv_grad = lax.psum_scatter(
        conv_grad_local.astype(jnp.bfloat16), "row", scatter_dimension=1, tiled=True
    ).astype(jnp.float32)
    mixer_grads = tuple(inward_all[:, edges[spot] : edges[spot + 1]] for spot in range(6)) + tuple(
        conv_grad[:, conv_edges[i] : conv_edges[i + 1]] for i in range(3)
    ) + (wout_grad.astype(jnp.float32),)
    head_total = a_log.shape[0]
    grad_a_full = lax.dynamic_update_slice_in_dim(
        jnp.zeros((head_total,), jnp.float32), core_grads[9], head_first, 0
    )
    grad_dt_full = lax.dynamic_update_slice_in_dim(
        jnp.zeros((head_total,), jnp.float32), core_grads[10], head_first, 0
    )
    small_sums = lax.psum(
        (grad_gain_in, grad_gain_ffn, core_grads[11], grad_a_full, grad_dt_full), ("head", "row")
    )
    return (
        final_out[None],
        grad_input[None],
        mixer_grads[0],
        mixer_grads[1],
        mixer_grads[2],
        mixer_grads[3],
        mixer_grads[4],
        mixer_grads[5],
        mixer_grads[6],
        mixer_grads[7],
        mixer_grads[8],
        small_sums[3],
        small_sums[4],
        small_sums[2],
        mixer_grads[9],
        small_sums[0],
        small_sums[1],
        ffn_grads[0],
        ffn_grads[1],
        ffn_grads[2],
    )


def solution(mesh):
    return jax.shard_map(
        partial(on_device, head_ring(mesh)),
        mesh=mesh,
        in_specs=(
            P("row", "head", None),
            P("row", "head"),
            P("row", "head"),
            P("row", "head"),
            P("row", "head"),
            P("row", "head"),
            P("row", "head"),
            P(None, ("head", "row")),
            P(None, ("head", "row")),
            P(None, ("head", "row")),
            P(),
            P(),
            P(),
            P("head", "row"),
            P(),
            P(),
            P("head", "row"),
            P("head", "row"),
            P("row", "head"),
            P("row", None),
            P("row"),
            P("row", "head", None),
        ),
        out_specs=(
            P("row", "head", None),
            P("row", "head", None),
            P("row", "head"),
            P("row", "head"),
            P("row", "head"),
            P("row", "head"),
            P("row", "head"),
            P("row", "head"),
            P(None, ("head", "row")),
            P(None, ("head", "row")),
            P(None, ("head", "row")),
            P(),
            P(),
            P(),
            P("head", "row"),
            P(),
            P(),
            P("head", "row"),
            P("head", "row"),
            P("row", "head"),
        ),
        check_vma=False,
    )
```

```python
from functools import partial
import math

import jax
import jax.numpy as jnp
from jax import lax
from jax.sharding import PartitionSpec as P
from jax.experimental import pallas as pl
from jax.experimental.pallas import tpu as pltpu

BLOCK = 64


precise = lax.Precision.HIGHEST
epsilon = 1e-06
o_floor = 0.001


def rms_norm(vector, gain_vec, floor_add=epsilon):
    return (
        vector * lax.rsqrt(jnp.mean(vector * vector, axis=-1, keepdims=True) + floor_add) * gain_vec
    )


def unit_norm(vector):
    return vector * lax.rsqrt(jnp.sum(vector * vector, axis=-1, keepdims=True) + epsilon)


def swiglu(gate_pre, up_pre):
    return jax.nn.silu(gate_pre) * up_pre


def short_conv(signal, kernel, seg_ids):
    tap_count = kernel.shape[0]
    length = signal.shape[0]
    summed = signal * kernel[tap_count - 1]
    for offset in range(1, tap_count):
        shifted = jnp.concatenate(
            [jnp.zeros((offset, signal.shape[1]), signal.dtype), signal[: length - offset]], axis=0
        )
        seg_shift = jnp.concatenate(
            [jnp.full((offset,), -1, jnp.int32), seg_ids[: length - offset]]
        )
        keep_mask = (seg_shift == seg_ids).astype(signal.dtype)
        summed = summed + shifted * kernel[tap_count - 1 - offset] * keep_mask[:, None]
    return summed


def _recur_fwd_kernel(nb, u0_ref, w_ref, kt_ref, c_ref, s_out, u_out, s_scr):
    @pl.when(pl.program_id(1) == 0)
    def _():
        s_scr[...] = jnp.zeros_like(s_scr)

    def step(j, carry):
        state = s_scr[...]
        s_out[0, j] = state
        update = u0_ref[0, j] - lax.dot_general(
            w_ref[0, j], state, (((1,), (1,)), ((), ())),
            precision=precise, preferred_element_type=jnp.float32,
        )
        u_out[0, j] = update
        s_scr[...] = c_ref[0, j] * state + lax.dot_general(
            update, kt_ref[0, j], (((0,), (0,)), ((), ())),
            precision=precise, preferred_element_type=jnp.float32,
        )
        return carry

    lax.fori_loop(0, nb, step, 0)


def _recur_bwd_kernel(
    nb, s_ref, u_ref, w_ref, kt_ref, c_ref, ds_ref, du_ref,
    du0_out, dw_out, dkt_out, dc_out, g_scr,
):
    @pl.when(pl.program_id(1) == 0)
    def _():
        g_scr[...] = jnp.zeros_like(g_scr)

    def step(i, carry):
        j = nb - 1 - i
        grad_state = g_scr[...]
        state = s_ref[0, j]
        grad_update = du_ref[0, j] + lax.dot_general(
            kt_ref[0, j], grad_state, (((1,), (1,)), ((), ())),
            precision=precise, preferred_element_type=jnp.float32,
        )
        dkt_out[0, j] = jnp.dot(
            u_ref[0, j], grad_state, precision=precise, preferred_element_type=jnp.float32
        )
        dc_out[0, j] = jnp.sum(grad_state * state, axis=0, keepdims=True)
        du0_out[0, j] = grad_update
        dw_out[0, j] = -jnp.dot(
            grad_update, state, precision=precise, preferred_element_type=jnp.float32
        )
        g_scr[...] = (
            c_ref[0, j] * grad_state
            - lax.dot_general(
                grad_update, w_ref[0, j], (((0,), (0,)), ((), ())),
                precision=precise, preferred_element_type=jnp.float32,
            )
            + ds_ref[0, j]
        )
        return carry

    lax.fori_loop(0, nb, step, 0)


def _chunk_spec(nb, tail, reverse, count):
    if reverse:
        return pl.BlockSpec((1, nb) + tail, lambda h, b: (h, count - 1 - b, 0, 0))
    return pl.BlockSpec((1, nb) + tail, lambda h, b: (h, b, 0, 0))


def _recur_forward(u0, w, kt, c):
    heads, count, chunk, dv = u0.shape
    dk = w.shape[-1]
    nb = min(8, count)
    blocks = count // nb
    flops = 4 * heads * count * chunk * dk * dv * 6
    moved = 4 * heads * count * (2 * chunk * dv + 2 * chunk * dk + dv * dk)
    return pl.pallas_call(
        partial(_recur_fwd_kernel, nb),
        grid=(heads, blocks),
        in_specs=[
            _chunk_spec(nb, (chunk, dv), False, blocks),
            _chunk_spec(nb, (chunk, dk), False, blocks),
            _chunk_spec(nb, (chunk, dk), False, blocks),
            _chunk_spec(nb, (1, dk), False, blocks),
        ],
        out_specs=[
            _chunk_spec(nb, (dv, dk), False, blocks),
            _chunk_spec(nb, (chunk, dv), False, blocks),
        ],
        out_shape=[
            jax.ShapeDtypeStruct((heads, count, dv, dk), jnp.float32),
            jax.ShapeDtypeStruct((heads, count, chunk, dv), jnp.float32),
        ],
        scratch_shapes=[pltpu.VMEM((dv, dk), jnp.float32)],
        compiler_params=pltpu.CompilerParams(dimension_semantics=("arbitrary", "arbitrary")),
        cost_estimate=pl.CostEstimate(flops=flops, transcendentals=0, bytes_accessed=moved),
        name="delta_state_forward",
    )(u0, w, kt, c)


def _recur_backward(states, updates, w, kt, c, d_states, d_updates):
    heads, count, chunk, dv = updates.shape
    dk = w.shape[-1]
    nb = min(8, count)
    blocks = count // nb
    flops = 8 * heads * count * chunk * dk * dv * 6
    moved = 4 * heads * count * (4 * chunk * dv + 4 * chunk * dk + 2 * dv * dk)
    return pl.pallas_call(
        partial(_recur_bwd_kernel, nb),
        grid=(heads, blocks),
        in_specs=[
            _chunk_spec(nb, (dv, dk), True, blocks),
            _chunk_spec(nb, (chunk, dv), True, blocks),
            _chunk_spec(nb, (chunk, dk), True, blocks),
            _chunk_spec(nb, (chunk, dk), True, blocks),
            _chunk_spec(nb, (1, dk), True, blocks),
            _chunk_spec(nb, (dv, dk), True, blocks),
            _chunk_spec(nb, (chunk, dv), True, blocks),
        ],
        out_specs=[
            _chunk_spec(nb, (chunk, dv), True, blocks),
            _chunk_spec(nb, (chunk, dk), True, blocks),
            _chunk_spec(nb, (chunk, dk), True, blocks),
            _chunk_spec(nb, (1, dk), True, blocks),
        ],
        out_shape=[
            jax.ShapeDtypeStruct((heads, count, chunk, dv), jnp.float32),
            jax.ShapeDtypeStruct((heads, count, chunk, dk), jnp.float32),
            jax.ShapeDtypeStruct((heads, count, chunk, dk), jnp.float32),
            jax.ShapeDtypeStruct((heads, count, 1, dk), jnp.float32),
        ],
        scratch_shapes=[pltpu.VMEM((dv, dk), jnp.float32)],
        compiler_params=pltpu.CompilerParams(dimension_semantics=("arbitrary", "arbitrary")),
        cost_estimate=pl.CostEstimate(flops=flops, transcendentals=0, bytes_accessed=moved),
        name="delta_state_backward",
    )(states, updates, w, kt, c, d_states, d_updates)


@jax.custom_vjp
def state_recurrence(u0, w, kt, c):
    return _recur_forward(u0, w, kt, c)


def _recurrence_fwd(u0, w, kt, c):
    states, updates = _recur_forward(u0, w, kt, c)
    return (states, updates), (states, updates, w, kt, c)


def _recurrence_bwd(saved, grads):
    states, updates, w, kt, c = saved
    d_states, d_updates = grads
    du0, dw, dkt, dc_lanes = _recur_backward(states, updates, w, kt, c, d_states, d_updates)
    return du0, dw, dkt, dc_lanes


state_recurrence.defvjp(_recurrence_fwd, _recurrence_bwd)


def chunk_prepare(queries, keys_n, values, decays, beta_rate, seg_ids):
    length, dk = keys_n.shape
    count = length // BLOCK
    q = queries.reshape(count, BLOCK, dk)
    k = keys_n.reshape(count, BLOCK, dk)
    v = values.reshape(count, BLOCK, values.shape[1])
    beta = beta_rate.reshape(count, BLOCK)
    seg = seg_ids.reshape(count, BLOCK)
    cumulative = jnp.cumsum(decays.reshape(count, BLOCK), axis=1)
    places = jnp.arange(BLOCK)
    lower_tri = places[:, None] >= places[None, :]
    inside = jnp.logical_and(seg[:, :, None] == seg[:, None, :], lower_tri)
    log_gap = jnp.where(inside, cumulative[:, :, None] - cumulative[:, None, :], 0.0)
    within = jnp.exp(log_gap) * inside.astype(jnp.float32)
    strict = within * (places[:, None] > places[None, :]).astype(jnp.float32)
    last_seg = jnp.concatenate([jnp.full((1,), -1, seg.dtype), seg[:-1, BLOCK - 1]])
    carried = jnp.exp(cumulative) * (seg == last_seg[:, None]).astype(jnp.float32)
    key_gram = jnp.einsum("nid,njd->nij", k, k, precision=precise)
    system = jnp.eye(BLOCK, dtype=jnp.float32) + beta[:, :, None] * strict * key_gram
    right_side = jnp.concatenate([beta[:, :, None] * v, (beta * carried)[:, :, None] * k], axis=2)
    solved = lax.linalg.triangular_solve(
        system, right_side, left_side=True, lower=True, unit_diagonal=True
    )
    dv = v.shape[2]
    kt = within[:, BLOCK - 1, :, None] * k
    scores = jnp.einsum("nid,njd->nij", q, k, precision=precise) * within
    return solved[:, :, :dv], solved[:, :, dv:], kt, carried[:, BLOCK - 1], carried, scores


def chunk_finish(queries, carried, scores, states, updates):
    count = states.shape[0]
    q = queries.reshape(count, BLOCK, queries.shape[1])
    output = carried[:, :, None] * jnp.einsum(
        "nid,nvd->niv", q, states, precision=precise
    ) + jnp.einsum("nij,njv->niv", scores, updates, precision=precise)
    return output.reshape(count * BLOCK, states.shape[1])


def delta_rule(queries, keys_n, values, decays, beta_rate, seg_ids):
    u0, w, kt, tail, carried, scores = jax.vmap(chunk_prepare, in_axes=(0, 0, 0, 0, 0, None))(
        queries, keys_n, values, decays, beta_rate, seg_ids
    )
    c = jnp.broadcast_to(tail[:, :, None, None], tail.shape + (1, w.shape[-1]))
    states, updates = state_recurrence(u0, w, kt, c)
    return jax.vmap(chunk_finish)(queries, carried, scores, states, updates)


def head_inputs(proj_query, proj_key, proj_value, proj_alpha, proj_beta,
                kernel_query, kernel_key, kernel_value, a_here, dt_here, seg_ids):
    queries = unit_norm(jax.nn.silu(short_conv(proj_query, kernel_query, seg_ids))) * (
        1.0 / math.sqrt(proj_query.shape[1])
    )
    keys_n = unit_norm(jax.nn.silu(short_conv(proj_key, kernel_key, seg_ids)))
    values = jax.nn.silu(short_conv(proj_value, kernel_value, seg_ids))
    decays = -jnp.exp(a_here) * jax.nn.softplus(proj_alpha + dt_here)
    beta_rate = jax.nn.sigmoid(proj_beta)
    return queries, keys_n, values, decays, beta_rate


def head_output(recurrent, proj_gate, o_gain, live_mask):
    return rms_norm(recurrent, o_gain, o_floor) * jax.nn.silu(proj_gate) * live_mask[:, None]


def local_mixer(
    proj_query,
    proj_key,
    proj_value,
    proj_gate,
    proj_alpha,
    proj_beta,
    kernel_query,
    kernel_key,
    kernel_value,
    a_here,
    dt_here,
    o_gain,
    seg_ids=None,
    live_mask=None,
):
    row_count = proj_query.shape[0]
    heads_here = proj_alpha.shape[1]

    def by_head(array):
        return jnp.moveaxis(array.reshape(row_count, heads_here, -1), 1, 0)

    def kernel_heads(kernel):
        return jnp.moveaxis(kernel.reshape(kernel.shape[0], heads_here, -1), 1, 0)

    queries, keys_n, values, decays, beta_rate = jax.vmap(
        head_inputs, in_axes=(0,) * 10 + (None,)
    )(
        by_head(proj_query),
        by_head(proj_key),
        by_head(proj_value),
        proj_alpha.T,
        proj_beta.T,
        kernel_heads(kernel_query),
        kernel_heads(kernel_key),
        kernel_heads(kernel_value),
        a_here,
        dt_here,
        seg_ids,
    )
    recurrent = delta_rule(queries, keys_n, values, decays, beta_rate, seg_ids)
    mixed_heads = jax.vmap(head_output, in_axes=(0, 0, None, None))(
        recurrent, by_head(proj_gate), o_gain, live_mask
    )
    return jnp.moveaxis(mixed_heads, 0, 1).reshape(row_count, -1)


MESH_ID = pl.DeviceIdType.MESH


def _ring_position(h, major, minor):
    a = h // minor
    b = h % minor
    return b * major + a + (b % 2) * (major - 1 - 2 * a)


def _ring_member(q, major, minor):
    count = major * minor
    q = (q + count) % count
    b = q // major
    r = q % major
    return (r + (b % 2) * (major - 1 - 2 * r)) * minor + b


def _ring_sides(major, minor):
    p = _ring_position(lax.axis_index("head"), major, minor)
    return p, _ring_member(p + 1, major, minor), _ring_member(p - 1, major, minor)


def _greet(nxt, prv, row):
    barrier = pltpu.get_barrier_semaphore()
    pl.semaphore_signal(barrier, 1, device_id=(prv, row), device_id_type=MESH_ID)
    pl.semaphore_signal(barrier, 1, device_id=(nxt, row), device_id_type=MESH_ID)
    pl.semaphore_wait(barrier, 2)


def _ring_gather_kernel(major, minor, x_ref, out_ref, send_sem, recv_sem):
    count = major * minor
    blk = x_ref.shape[0]
    half = blk // 2
    row = lax.axis_index("row")
    p, nxt, prv = _ring_sides(major, minor)
    out_ref[pl.ds(pl.multiple_of(lax.axis_index("head") * blk, blk), blk), :] = x_ref[...]
    _greet(nxt, prv, row)

    def piece(pos, off):
        return out_ref.at[pl.ds(pl.multiple_of(_ring_member(pos, major, minor) * blk + off, half), half)]

    def outgoing(d, s):
        pos = p - s if d == 0 else p + s
        target = nxt if d == 0 else prv
        ref = piece(pos, d * half)
        return pltpu.make_async_remote_copy(
            ref, ref, send_sem.at[d, s], recv_sem.at[d, s], device_id=(target, row),
            device_id_type=MESH_ID,
        )

    def incoming(d, s):
        pos = p - 1 - s if d == 0 else p + 1 + s
        source = prv if d == 0 else nxt
        ref = piece(pos, d * half)
        return pltpu.make_async_remote_copy(
            ref, ref, send_sem.at[d, s], recv_sem.at[d, s], device_id=(source, row),
            device_id_type=MESH_ID,
        )

    for s in range(count - 1):
        for d in (0, 1):
            if s > 0:
                incoming(d, s - 1).wait_recv()
            outgoing(d, s).start()
    for d in (0, 1):
        incoming(d, count - 2).wait_recv()
    for s in range(count - 1):
        for d in (0, 1):
            outgoing(d, s).wait_send()


def _ring_scatter_kernel(major, minor, y_ref, out_ref, buf, send_sem, recv_sem):
    count = major * minor
    blk = out_ref.shape[0]
    half = blk // 2
    row = lax.axis_index("row")
    p, nxt, prv = _ring_sides(major, minor)
    _greet(nxt, prv, row)

    def piece(pos, off):
        return y_ref.at[pl.ds(pl.multiple_of(_ring_member(pos, major, minor) * blk + off, half), half)]

    def outgoing(d, s):
        pos = p - s - 1 if d == 0 else p + s + 1
        target = nxt if d == 0 else prv
        source = piece(pos, d * half) if s == 0 else buf.at[d, s - 1]
        return pltpu.make_async_remote_copy(
            source, buf.at[d, s], send_sem.at[d, s], recv_sem.at[d, s],
            device_id=(target, row), device_id_type=MESH_ID,
        )

    def incoming(d, s):
        source = prv if d == 0 else nxt
        return pltpu.make_async_remote_copy(
            buf.at[d, s], buf.at[d, s], send_sem.at[d, s], recv_sem.at[d, s],
            device_id=(source, row), device_id_type=MESH_ID,
        )

    for s in range(count - 1):
        for d in (0, 1):
            if s > 0:
                incoming(d, s - 1).wait_recv()
                pos = p - s - 1 if d == 0 else p + s + 1
                buf[d, s - 1] = (
                    buf[d, s - 1].astype(jnp.float32)
                    + piece(pos, d * half)[...].astype(jnp.float32)
                ).astype(buf.dtype)
            outgoing(d, s).start()
    for d in (0, 1):
        incoming(d, count - 2).wait_recv()
        out_ref[pl.ds(d * half, half), :] = piece(p, d * half)[...].astype(
            jnp.float32
        ) + buf[d, count - 2].astype(jnp.float32)
    for s in range(count - 1):
        for d in (0, 1):
            outgoing(d, s).wait_send()


def ring_gather(x, ring, collective):
    major, minor = ring
    count = major * minor
    blk, width = x.shape
    return pl.pallas_call(
        partial(_ring_gather_kernel, major, minor),
        out_shape=jax.ShapeDtypeStruct((count * blk, width), x.dtype),
        in_specs=[pl.BlockSpec(memory_space=pltpu.VMEM)],
        out_specs=pl.BlockSpec(memory_space=pltpu.VMEM),
        scratch_shapes=[
            pltpu.SemaphoreType.DMA((2, count - 1)),
            pltpu.SemaphoreType.DMA((2, count - 1)),
        ],
        compiler_params=pltpu.CompilerParams(collective_id=collective, has_side_effects=True),
        name="ring_gather_head",
    )(x)


def ring_scatter(y, ring, collective):
    major, minor = ring
    count = major * minor
    rows, width = y.shape
    blk = rows // count
    return pl.pallas_call(
        partial(_ring_scatter_kernel, major, minor),
        out_shape=jax.ShapeDtypeStruct((blk, width), jnp.float32),
        in_specs=[pl.BlockSpec(memory_space=pltpu.VMEM)],
        out_specs=pl.BlockSpec(memory_space=pltpu.VMEM),
        scratch_shapes=[
            pltpu.VMEM((2, count - 1, blk // 2, width), y.dtype),
            pltpu.SemaphoreType.DMA((2, count - 1)),
            pltpu.SemaphoreType.DMA((2, count - 1)),
        ],
        compiler_params=pltpu.CompilerParams(collective_id=collective, has_side_effects=True),
        name="ring_scatter_head",
    )(y)


def head_ring(mesh):
    count = mesh.shape["head"]
    try:
        spots = [tuple(device.coords) for device in mesh.devices[:, 0]]
    except (AttributeError, TypeError):
        return (count, 1)
    moving = [axis for axis in range(len(spots[0])) if spots[0][axis] != spots[1][axis]]
    if len(moving) != 1:
        return (count, 1)
    minor = len({spot[moving[0]] for spot in spots})
    if count % minor or minor % 2:
        return (count, 1)
    return (count // minor, minor)


def contract_rows(left, right):
    return lax.dot_general(
        left, right, (((0,), (0,)), ((), ())), preferred_element_type=jnp.float32
    )


def contract_cols(left, right):
    return lax.dot_general(
        left, right, (((1,), (1,)), ((), ())), preferred_element_type=jnp.float32
    )


def on_device(
    ring,
    tokens,
    w_query,
    w_key,
    w_value,
    w_outgate,
    w_alpha,
    w_beta,
    conv_query,
    conv_key,
    conv_value,
    a_log,
    dt_bias,
    o_gain,
    w_out,
    gain_in,
    gain_ffn,
    w_gate,
    w_up,
    w_down,
    segments,
    valid_len,
    cotangent,
):
    residual = tokens[0].astype(jnp.float32)
    heads_here = w_alpha.shape[1]
    head_first = lax.axis_index("head") * heads_here
    norm_one, pull_one = jax.vjp(rms_norm, residual, gain_in)
    normed_one = norm_one.astype(jnp.bfloat16)
    row_count = lax.psum(1, "row")
    w_local = jnp.concatenate(
        [w_query, w_key, w_value, w_outgate, w_alpha, w_beta], axis=1
    ).astype(jnp.bfloat16)
    edges = [0]
    for member in (w_query, w_key, w_value, w_outgate, w_alpha, w_beta):
        edges.append(edges[-1] + member.shape[1])
    w_inward = lax.all_gather(w_local, "row", axis=0, tiled=True)
    conv_local = jnp.concatenate([conv_query, conv_key, conv_value], axis=1).astype(jnp.bfloat16)
    conv_edges = [0, conv_query.shape[1], conv_query.shape[1] + conv_key.shape[1], conv_local.shape[1]]
    conv_all = lax.all_gather(conv_local, "row", axis=1, tiled=True).reshape(
        conv_local.shape[0], row_count, conv_local.shape[1]
    )
    conv_parts = [
        conv_all[:, :, conv_edges[i] : conv_edges[i + 1]].reshape(conv_local.shape[0], -1)
        for i in range(3)
    ]
    out_matrix = lax.all_gather(w_out.astype(jnp.bfloat16), "row", axis=1, tiled=True)
    ff_width = w_gate.shape[1]
    ffn_local = jnp.concatenate([w_gate, w_up, w_down.T], axis=1).astype(jnp.bfloat16)
    grad_out = cotangent[0]
    grad_out_rows = lax.all_gather(grad_out, "row", axis=0, tiled=True)
    all_rows = ring_gather(normed_one, ring, 0)
    all_rows, out_matrix, ffn_local = lax.optimization_barrier((all_rows, out_matrix, ffn_local))
    ffn_all = lax.all_gather(ffn_local, "head", axis=0, tiled=True)
    projected = jnp.dot(all_rows, w_inward, preferred_element_type=jnp.float32)
    proj_parts = [projected[:, edges[spot] : edges[spot + 1]] for spot in range(6)]
    seg_ids = segments[0]
    live_mask = (jnp.arange(seg_ids.shape[0]) < valid_len[0]).astype(jnp.float32)
    a_here = lax.dynamic_slice_in_dim(a_log, head_first, heads_here)
    dt_here = lax.dynamic_slice_in_dim(dt_bias, head_first, heads_here)
    mixer_fn = partial(local_mixer, seg_ids=seg_ids, live_mask=live_mask)
    mixed, pull_core = jax.vjp(
        mixer_fn,
        proj_parts[0],
        proj_parts[1],
        proj_parts[2],
        proj_parts[3],
        proj_parts[4],
        proj_parts[5],
        conv_parts[0].astype(jnp.float32),
        conv_parts[1].astype(jnp.float32),
        conv_parts[2].astype(jnp.float32),
        a_here,
        dt_here,
        o_gain,
    )
    mixed, ffn_all, grad_out_rows = lax.optimization_barrier((mixed, ffn_all, grad_out_rows))
    w_gate_all = ffn_all[:, :ff_width]
    w_up_all = ffn_all[:, ff_width : 2 * ff_width]
    w_down_t = ffn_all[:, 2 * ff_width :]
    mixed_half = mixed.astype(jnp.bfloat16)
    mixer_output = ring_scatter(
        jnp.dot(mixed_half, out_matrix, preferred_element_type=jnp.float32).astype(jnp.bfloat16),
        ring,
        1,
    )
    middle = residual + mixer_output
    norm_two, pull_two = jax.vjp(rms_norm, middle, gain_ffn)
    normed_two = norm_two.astype(jnp.bfloat16)
    ffn_inputs = lax.all_gather(normed_two, "row", axis=0, tiled=True)
    gate_pre = jnp.dot(ffn_inputs, w_gate_all, preferred_element_type=jnp.float32)
    up_pre = jnp.dot(ffn_inputs, w_up_all, preferred_element_type=jnp.float32)
    hidden_val, pull_act = jax.vjp(swiglu, gate_pre, up_pre)
    hidden_half = hidden_val.astype(jnp.bfloat16)
    ffn_partial = contract_cols(hidden_half, w_down_t).astype(jnp.bfloat16)
    grad_hidden = jnp.dot(grad_out_rows, w_down_t, preferred_element_type=jnp.float32)
    grad_down_t = contract_rows(grad_out_rows, hidden_half)
    grad_gate_f, grad_up_f = pull_act(grad_hidden)
    grad_gate = grad_gate_f.astype(jnp.bfloat16)
    grad_upper = grad_up_f.astype(jnp.bfloat16)
    grad_wgate = contract_rows(ffn_inputs, grad_gate)
    grad_wup = contract_rows(ffn_inputs, grad_upper)
    grad_norm_two = lax.psum_scatter(
        (contract_cols(grad_gate, w_gate_all) + contract_cols(grad_upper, w_up_all)).astype(
            jnp.bfloat16
        ),
        "row",
        scatter_dimension=0,
        tiled=True,
    ).astype(jnp.float32)
    grad_mid_part, grad_gain_ffn = pull_two(grad_norm_two)
    grad_middle = grad_out.astype(jnp.float32) + grad_mid_part
    ffn_grad_cat = jnp.concatenate([grad_wgate, grad_wup, grad_down_t], axis=1).astype(
        jnp.bfloat16
    )
    grad_mid_half = grad_middle.astype(jnp.bfloat16)
    grad_mid_rows = ring_gather(grad_mid_half, ring, 2)
    ffn_grad_all = lax.psum_scatter(ffn_grad_cat, "head", scatter_dimension=0, tiled=True)
    ffn_output = lax.psum_scatter(ffn_partial, "row", scatter_dimension=0, tiled=True)
    grad_mixed = contract_cols(grad_mid_rows, out_matrix)
    grad_wout = contract_rows(mixed_half, grad_mid_rows).astype(jnp.bfloat16)
    wout_grad = lax.psum_scatter(grad_wout, "row", scatter_dimension=1, tiled=True)
    core_grads = pull_core(grad_mixed)
    core_grads, ffn_output, ffn_grad_all = lax.optimization_barrier(
        (core_grads, ffn_output, ffn_grad_all)
    )
    final_out = (middle + ffn_output.astype(jnp.float32)).astype(jnp.bfloat16)
    ffn_grad_all = ffn_grad_all.astype(jnp.float32)
    ffn_grads = (
        ffn_grad_all[:, :ff_width],
        ffn_grad_all[:, ff_width : 2 * ff_width],
        ffn_grad_all[:, 2 * ff_width :].T,
    )
    grad_proj = jnp.concatenate(
        [core_grads[0], core_grads[1], core_grads[2], core_grads[3], core_grads[4], core_grads[5]],
        axis=1,
    ).astype(jnp.bfloat16)
    grad_inward = contract_rows(all_rows, grad_proj).astype(jnp.bfloat16)
    grad_norm_one = ring_scatter(contract_cols(grad_proj, w_inward).astype(jnp.bfloat16), ring, 3)
    grad_norm_one, wout_grad = lax.optimization_barrier((grad_norm_one, wout_grad))
    grad_in_part, grad_gain_in = pull_one(grad_norm_one)
    grad_input = grad_middle + grad_in_part
    inward_all = lax.psum_scatter(
        grad_inward, "row", scatter_dimension=0, tiled=True
    ).astype(jnp.float32)
    conv_grad_local = jnp.concatenate(
        [
            core_grads[6 + i].reshape(conv_local.shape[0], row_count, -1)
            for i in range(3)
        ],
        axis=2,
    ).reshape(conv_local.shape[0], -1)
    conv_grad = lax.psum_scatter(
        conv_grad_local.astype(jnp.bfloat16), "row", scatter_dimension=1, tiled=True
    ).astype(jnp.float32)
    mixer_grads = tuple(inward_all[:, edges[spot] : edges[spot + 1]] for spot in range(6)) + tuple(
        conv_grad[:, conv_edges[i] : conv_edges[i + 1]] for i in range(3)
    ) + (wout_grad.astype(jnp.float32),)
    head_total = a_log.shape[0]
    grad_a_full = lax.dynamic_update_slice_in_dim(
        jnp.zeros((head_total,), jnp.float32), core_grads[9], head_first, 0
    )
    grad_dt_full = lax.dynamic_update_slice_in_dim(
        jnp.zeros((head_total,), jnp.float32), core_grads[10], head_first, 0
    )
    small_sums = lax.psum(
        (grad_gain_in, grad_gain_ffn, core_grads[11], grad_a_full, grad_dt_full), ("head", "row")
    )
    return (
        final_out[None],
        grad_input[None],
        mixer_grads[0],
        mixer_grads[1],
        mixer_grads[2],
        mixer_grads[3],
        mixer_grads[4],
        mixer_grads[5],
        mixer_grads[6],
        mixer_grads[7],
        mixer_grads[8],
        small_sums[3],
        small_sums[4],
        small_sums[2],
        mixer_grads[9],
        small_sums[0],
        small_sums[1],
        ffn_grads[0],
        ffn_grads[1],
        ffn_grads[2],
    )


def solution(mesh):
    return jax.shard_map(
        partial(on_device, head_ring(mesh)),
        mesh=mesh,
        in_specs=(
            P("row", "head", None),
            P("row", "head"),
            P("row", "head"),
            P("row", "head"),
            P("row", "head"),
            P("row", "head"),
            P("row", "head"),
            P(None, ("head", "row")),
            P(None, ("head", "row")),
            P(None, ("head", "row")),
            P(),
            P(),
            P(),
            P("head", "row"),
            P(),
            P(),
            P("head", "row"),
            P("head", "row"),
            P("row", "head"),
            P("row", None),
            P("row"),
            P("row", "head", None),
        ),
        out_specs=(
            P("row", "head", None),
            P("row", "head", None),
            P("row", "head"),
            P("row", "head"),
            P("row", "head"),
            P("row", "head"),
            P("row", "head"),
            P("row", "head"),
            P(None, ("head", "row")),
            P(None, ("head", "row")),
            P(None, ("head", "row")),
            P(),
            P(),
            P(),
            P("head", "row"),
            P(),
            P(),
            P("head", "row"),
            P("head", "row"),
            P("row", "head"),
        ),
        check_vma=False,
    )
```

```python
from functools import partial
import math

import jax
import jax.numpy as jnp
from jax import lax
from jax.sharding import PartitionSpec as P
from jax.experimental import pallas as pl
from jax.experimental.pallas import tpu as pltpu

BLOCK = 64


precise = lax.Precision.HIGHEST
epsilon = 1e-06
o_floor = 0.001


def rms_norm(vector, gain_vec, floor_add=epsilon):
    return (
        vector * lax.rsqrt(jnp.mean(vector * vector, axis=-1, keepdims=True) + floor_add) * gain_vec
    )


def unit_norm(vector):
    return vector * lax.rsqrt(jnp.sum(vector * vector, axis=-1, keepdims=True) + epsilon)


def swiglu(gate_pre, up_pre):
    return jax.nn.silu(gate_pre) * up_pre


def short_conv(signal, kernel, seg_ids):
    tap_count = kernel.shape[0]
    length = signal.shape[0]
    summed = signal * kernel[tap_count - 1]
    for offset in range(1, tap_count):
        shifted = jnp.concatenate(
            [jnp.zeros((offset, signal.shape[1]), signal.dtype), signal[: length - offset]], axis=0
        )
        seg_shift = jnp.concatenate(
            [jnp.full((offset,), -1, jnp.int32), seg_ids[: length - offset]]
        )
        keep_mask = (seg_shift == seg_ids).astype(signal.dtype)
        summed = summed + shifted * kernel[tap_count - 1 - offset] * keep_mask[:, None]
    return summed


def _recur_fwd_kernel(nb, u0_ref, w_ref, kt_ref, c_ref, s_out, u_out, s_scr):
    @pl.when(pl.program_id(1) == 0)
    def _():
        s_scr[...] = jnp.zeros_like(s_scr)

    def step(j, carry):
        state = s_scr[...]
        s_out[0, j] = state
        update = u0_ref[0, j] - lax.dot_general(
            w_ref[0, j], state, (((1,), (1,)), ((), ())),
            precision=precise, preferred_element_type=jnp.float32,
        )
        u_out[0, j] = update
        s_scr[...] = c_ref[0, j] * state + lax.dot_general(
            update, kt_ref[0, j], (((0,), (0,)), ((), ())),
            precision=precise, preferred_element_type=jnp.float32,
        )
        return carry

    lax.fori_loop(0, nb, step, 0)


def _recur_bwd_kernel(
    nb, s_ref, u_ref, w_ref, kt_ref, c_ref, ds_ref, du_ref,
    du0_out, dw_out, dkt_out, dc_out, g_scr,
):
    @pl.when(pl.program_id(1) == 0)
    def _():
        g_scr[...] = jnp.zeros_like(g_scr)

    def step(i, carry):
        j = nb - 1 - i
        grad_state = g_scr[...]
        state = s_ref[0, j]
        grad_update = du_ref[0, j] + lax.dot_general(
            kt_ref[0, j], grad_state, (((1,), (1,)), ((), ())),
            precision=precise, preferred_element_type=jnp.float32,
        )
        dkt_out[0, j] = jnp.dot(
            u_ref[0, j], grad_state, precision=precise, preferred_element_type=jnp.float32
        )
        dc_out[0, j] = jnp.sum(grad_state * state, axis=0, keepdims=True)
        du0_out[0, j] = grad_update
        dw_out[0, j] = -jnp.dot(
            grad_update, state, precision=precise, preferred_element_type=jnp.float32
        )
        g_scr[...] = (
            c_ref[0, j] * grad_state
            - lax.dot_general(
                grad_update, w_ref[0, j], (((0,), (0,)), ((), ())),
                precision=precise, preferred_element_type=jnp.float32,
            )
            + ds_ref[0, j]
        )
        return carry

    lax.fori_loop(0, nb, step, 0)


def _chunk_spec(nb, tail, reverse, count):
    if reverse:
        return pl.BlockSpec((1, nb) + tail, lambda h, b: (h, count - 1 - b, 0, 0))
    return pl.BlockSpec((1, nb) + tail, lambda h, b: (h, b, 0, 0))


def _recur_forward(u0, w, kt, c):
    heads, count, chunk, dv = u0.shape
    dk = w.shape[-1]
    nb = min(8, count)
    blocks = count // nb
    flops = 4 * heads * count * chunk * dk * dv * 6
    moved = 4 * heads * count * (2 * chunk * dv + 2 * chunk * dk + dv * dk)
    return pl.pallas_call(
        partial(_recur_fwd_kernel, nb),
        grid=(heads, blocks),
        in_specs=[
            _chunk_spec(nb, (chunk, dv), False, blocks),
            _chunk_spec(nb, (chunk, dk), False, blocks),
            _chunk_spec(nb, (chunk, dk), False, blocks),
            _chunk_spec(nb, (1, dk), False, blocks),
        ],
        out_specs=[
            _chunk_spec(nb, (dv, dk), False, blocks),
            _chunk_spec(nb, (chunk, dv), False, blocks),
        ],
        out_shape=[
            jax.ShapeDtypeStruct((heads, count, dv, dk), jnp.float32),
            jax.ShapeDtypeStruct((heads, count, chunk, dv), jnp.float32),
        ],
        scratch_shapes=[pltpu.VMEM((dv, dk), jnp.float32)],
        compiler_params=pltpu.CompilerParams(dimension_semantics=("arbitrary", "arbitrary")),
        cost_estimate=pl.CostEstimate(flops=flops, transcendentals=0, bytes_accessed=moved),
        name="delta_state_forward",
    )(u0, w, kt, c)


def _recur_backward(states, updates, w, kt, c, d_states, d_updates):
    heads, count, chunk, dv = updates.shape
    dk = w.shape[-1]
    nb = min(8, count)
    blocks = count // nb
    flops = 8 * heads * count * chunk * dk * dv * 6
    moved = 4 * heads * count * (4 * chunk * dv + 4 * chunk * dk + 2 * dv * dk)
    return pl.pallas_call(
        partial(_recur_bwd_kernel, nb),
        grid=(heads, blocks),
        in_specs=[
            _chunk_spec(nb, (dv, dk), True, blocks),
            _chunk_spec(nb, (chunk, dv), True, blocks),
            _chunk_spec(nb, (chunk, dk), True, blocks),
            _chunk_spec(nb, (chunk, dk), True, blocks),
            _chunk_spec(nb, (1, dk), True, blocks),
            _chunk_spec(nb, (dv, dk), True, blocks),
            _chunk_spec(nb, (chunk, dv), True, blocks),
        ],
        out_specs=[
            _chunk_spec(nb, (chunk, dv), True, blocks),
            _chunk_spec(nb, (chunk, dk), True, blocks),
            _chunk_spec(nb, (chunk, dk), True, blocks),
            _chunk_spec(nb, (1, dk), True, blocks),
        ],
        out_shape=[
            jax.ShapeDtypeStruct((heads, count, chunk, dv), jnp.float32),
            jax.ShapeDtypeStruct((heads, count, chunk, dk), jnp.float32),
            jax.ShapeDtypeStruct((heads, count, chunk, dk), jnp.float32),
            jax.ShapeDtypeStruct((heads, count, 1, dk), jnp.float32),
        ],
        scratch_shapes=[pltpu.VMEM((dv, dk), jnp.float32)],
        compiler_params=pltpu.CompilerParams(dimension_semantics=("arbitrary", "arbitrary")),
        cost_estimate=pl.CostEstimate(flops=flops, transcendentals=0, bytes_accessed=moved),
        name="delta_state_backward",
    )(states, updates, w, kt, c, d_states, d_updates)


@jax.custom_vjp
def state_recurrence(u0, w, kt, c):
    return _recur_forward(u0, w, kt, c)


def _recurrence_fwd(u0, w, kt, c):
    states, updates = _recur_forward(u0, w, kt, c)
    return (states, updates), (states, updates, w, kt, c)


def _recurrence_bwd(saved, grads):
    states, updates, w, kt, c = saved
    d_states, d_updates = grads
    du0, dw, dkt, dc_lanes = _recur_backward(states, updates, w, kt, c, d_states, d_updates)
    return du0, dw, dkt, dc_lanes


state_recurrence.defvjp(_recurrence_fwd, _recurrence_bwd)


def chunk_prepare(queries, keys_n, values, decays, beta_rate, seg_ids):
    length, dk = keys_n.shape
    count = length // BLOCK
    q = queries.reshape(count, BLOCK, dk)
    k = keys_n.reshape(count, BLOCK, dk)
    v = values.reshape(count, BLOCK, values.shape[1])
    beta = beta_rate.reshape(count, BLOCK)
    seg = seg_ids.reshape(count, BLOCK)
    cumulative = jnp.cumsum(decays.reshape(count, BLOCK), axis=1)
    places = jnp.arange(BLOCK)
    lower_tri = places[:, None] >= places[None, :]
    inside = jnp.logical_and(seg[:, :, None] == seg[:, None, :], lower_tri)
    log_gap = jnp.where(inside, cumulative[:, :, None] - cumulative[:, None, :], 0.0)
    within = jnp.exp(log_gap) * inside.astype(jnp.float32)
    strict = within * (places[:, None] > places[None, :]).astype(jnp.float32)
    last_seg = jnp.concatenate([jnp.full((1,), -1, seg.dtype), seg[:-1, BLOCK - 1]])
    carried = jnp.exp(cumulative) * (seg == last_seg[:, None]).astype(jnp.float32)
    key_gram = jnp.einsum("nid,njd->nij", k, k, precision=precise)
    system = jnp.eye(BLOCK, dtype=jnp.float32) + beta[:, :, None] * strict * key_gram
    right_side = jnp.concatenate([beta[:, :, None] * v, (beta * carried)[:, :, None] * k], axis=2)
    solved = lax.linalg.triangular_solve(
        system, right_side, left_side=True, lower=True, unit_diagonal=True
    )
    dv = v.shape[2]
    kt = within[:, BLOCK - 1, :, None] * k
    scores = jnp.einsum("nid,njd->nij", q, k, precision=precise) * within
    return solved[:, :, :dv], solved[:, :, dv:], kt, carried[:, BLOCK - 1], carried, scores


def chunk_finish(queries, carried, scores, states, updates):
    count = states.shape[0]
    q = queries.reshape(count, BLOCK, queries.shape[1])
    output = carried[:, :, None] * jnp.einsum(
        "nid,nvd->niv", q, states, precision=precise
    ) + jnp.einsum("nij,njv->niv", scores, updates, precision=precise)
    return output.reshape(count * BLOCK, states.shape[1])


def delta_rule(queries, keys_n, values, decays, beta_rate, seg_ids):
    u0, w, kt, tail, carried, scores = jax.vmap(chunk_prepare, in_axes=(0, 0, 0, 0, 0, None))(
        queries, keys_n, values, decays, beta_rate, seg_ids
    )
    c = jnp.broadcast_to(tail[:, :, None, None], tail.shape + (1, w.shape[-1]))
    states, updates = state_recurrence(u0, w, kt, c)
    return jax.vmap(chunk_finish)(queries, carried, scores, states, updates)


def head_inputs(proj_query, proj_key, proj_value, proj_alpha, proj_beta,
                kernel_query, kernel_key, kernel_value, a_here, dt_here, seg_ids):
    queries = unit_norm(jax.nn.silu(short_conv(proj_query, kernel_query, seg_ids))) * (
        1.0 / math.sqrt(proj_query.shape[1])
    )
    keys_n = unit_norm(jax.nn.silu(short_conv(proj_key, kernel_key, seg_ids)))
    values = jax.nn.silu(short_conv(proj_value, kernel_value, seg_ids))
    decays = -jnp.exp(a_here) * jax.nn.softplus(proj_alpha + dt_here)
    beta_rate = jax.nn.sigmoid(proj_beta)
    return queries, keys_n, values, decays, beta_rate


def head_output(recurrent, proj_gate, o_gain, live_mask):
    return rms_norm(recurrent, o_gain, o_floor) * jax.nn.silu(proj_gate) * live_mask[:, None]


def local_mixer(
    proj_query,
    proj_key,
    proj_value,
    proj_gate,
    proj_alpha,
    proj_beta,
    kernel_query,
    kernel_key,
    kernel_value,
    a_here,
    dt_here,
    o_gain,
    seg_ids=None,
    live_mask=None,
):
    row_count = proj_query.shape[0]
    heads_here = proj_alpha.shape[1]

    def by_head(array):
        return jnp.moveaxis(array.reshape(row_count, heads_here, -1), 1, 0)

    def kernel_heads(kernel):
        return jnp.moveaxis(kernel.reshape(kernel.shape[0], heads_here, -1), 1, 0)

    queries, keys_n, values, decays, beta_rate = jax.vmap(
        head_inputs, in_axes=(0,) * 10 + (None,)
    )(
        by_head(proj_query),
        by_head(proj_key),
        by_head(proj_value),
        proj_alpha.T,
        proj_beta.T,
        kernel_heads(kernel_query),
        kernel_heads(kernel_key),
        kernel_heads(kernel_value),
        a_here,
        dt_here,
        seg_ids,
    )
    recurrent = delta_rule(queries, keys_n, values, decays, beta_rate, seg_ids)
    mixed_heads = jax.vmap(head_output, in_axes=(0, 0, None, None))(
        recurrent, by_head(proj_gate), o_gain, live_mask
    )
    return jnp.moveaxis(mixed_heads, 0, 1).reshape(row_count, -1)


MESH_ID = pl.DeviceIdType.MESH


def _ring_position(h, major, minor):
    a = h // minor
    b = h % minor
    return b * major + a + (b % 2) * (major - 1 - 2 * a)


def _ring_member(q, major, minor):
    count = major * minor
    q = (q + count) % count
    b = q // major
    r = q % major
    return (r + (b % 2) * (major - 1 - 2 * r)) * minor + b


def _ring_sides(major, minor):
    p = _ring_position(lax.axis_index("head"), major, minor)
    return p, _ring_member(p + 1, major, minor), _ring_member(p - 1, major, minor)


def _greet(nxt, prv, row):
    barrier = pltpu.get_barrier_semaphore()
    pl.semaphore_signal(barrier, 1, device_id=(prv, row), device_id_type=MESH_ID)
    pl.semaphore_signal(barrier, 1, device_id=(nxt, row), device_id_type=MESH_ID)
    pl.semaphore_wait(barrier, 2)


def _ring_gather_kernel(major, minor, x_ref, out_ref, send_sem, recv_sem):
    count = major * minor
    blk = x_ref.shape[0]
    half = blk // 2
    row = lax.axis_index("row")
    p, nxt, prv = _ring_sides(major, minor)
    out_ref[pl.ds(pl.multiple_of(lax.axis_index("head") * blk, blk), blk), :] = x_ref[...]
    _greet(nxt, prv, row)

    def piece(pos, off):
        return out_ref.at[pl.ds(pl.multiple_of(_ring_member(pos, major, minor) * blk + off, half), half)]

    def outgoing(d, s):
        pos = p - s if d == 0 else p + s
        target = nxt if d == 0 else prv
        ref = piece(pos, d * half)
        return pltpu.make_async_remote_copy(
            ref, ref, send_sem.at[d, s], recv_sem.at[d, s], device_id=(target, row),
            device_id_type=MESH_ID,
        )

    def incoming(d, s):
        pos = p - 1 - s if d == 0 else p + 1 + s
        source = prv if d == 0 else nxt
        ref = piece(pos, d * half)
        return pltpu.make_async_remote_copy(
            ref, ref, send_sem.at[d, s], recv_sem.at[d, s], device_id=(source, row),
            device_id_type=MESH_ID,
        )

    for s in range(count - 1):
        for d in (0, 1):
            if s > 0:
                incoming(d, s - 1).wait_recv()
            outgoing(d, s).start()
    for d in (0, 1):
        incoming(d, count - 2).wait_recv()
    for s in range(count - 1):
        for d in (0, 1):
            outgoing(d, s).wait_send()


def _ring_scatter_kernel(major, minor, y_ref, out_ref, buf, send_sem, recv_sem):
    count = major * minor
    blk = out_ref.shape[0]
    half = blk // 2
    row = lax.axis_index("row")
    p, nxt, prv = _ring_sides(major, minor)
    _greet(nxt, prv, row)

    def piece(pos, off):
        return y_ref.at[pl.ds(pl.multiple_of(_ring_member(pos, major, minor) * blk + off, half), half)]

    def outgoing(d, s):
        pos = p - s - 1 if d == 0 else p + s + 1
        target = nxt if d == 0 else prv
        source = piece(pos, d * half) if s == 0 else buf.at[d, s - 1]
        return pltpu.make_async_remote_copy(
            source, buf.at[d, s], send_sem.at[d, s], recv_sem.at[d, s],
            device_id=(target, row), device_id_type=MESH_ID,
        )

    def incoming(d, s):
        source = prv if d == 0 else nxt
        return pltpu.make_async_remote_copy(
            buf.at[d, s], buf.at[d, s], send_sem.at[d, s], recv_sem.at[d, s],
            device_id=(source, row), device_id_type=MESH_ID,
        )

    for s in range(count - 1):
        for d in (0, 1):
            if s > 0:
                incoming(d, s - 1).wait_recv()
                pos = p - s - 1 if d == 0 else p + s + 1
                buf[d, s - 1] = (
                    buf[d, s - 1].astype(jnp.float32)
                    + piece(pos, d * half)[...].astype(jnp.float32)
                ).astype(buf.dtype)
            outgoing(d, s).start()
    for d in (0, 1):
        incoming(d, count - 2).wait_recv()
        out_ref[pl.ds(d * half, half), :] = piece(p, d * half)[...].astype(
            jnp.float32
        ) + buf[d, count - 2].astype(jnp.float32)
    for s in range(count - 1):
        for d in (0, 1):
            outgoing(d, s).wait_send()


def ring_gather(x, ring, collective):
    major, minor = ring
    count = major * minor
    blk, width = x.shape
    return pl.pallas_call(
        partial(_ring_gather_kernel, major, minor),
        out_shape=jax.ShapeDtypeStruct((count * blk, width), x.dtype),
        in_specs=[pl.BlockSpec(memory_space=pltpu.VMEM)],
        out_specs=pl.BlockSpec(memory_space=pltpu.VMEM),
        scratch_shapes=[
            pltpu.SemaphoreType.DMA((2, count - 1)),
            pltpu.SemaphoreType.DMA((2, count - 1)),
        ],
        compiler_params=pltpu.CompilerParams(collective_id=collective, has_side_effects=True),
        name="ring_gather_head",
    )(x)


def ring_scatter(y, ring, collective):
    major, minor = ring
    count = major * minor
    rows, width = y.shape
    blk = rows // count
    return pl.pallas_call(
        partial(_ring_scatter_kernel, major, minor),
        out_shape=jax.ShapeDtypeStruct((blk, width), jnp.float32),
        in_specs=[pl.BlockSpec(memory_space=pltpu.VMEM)],
        out_specs=pl.BlockSpec(memory_space=pltpu.VMEM),
        scratch_shapes=[
            pltpu.VMEM((2, count - 1, blk // 2, width), y.dtype),
            pltpu.SemaphoreType.DMA((2, count - 1)),
            pltpu.SemaphoreType.DMA((2, count - 1)),
        ],
        compiler_params=pltpu.CompilerParams(collective_id=collective, has_side_effects=True),
        name="ring_scatter_head",
    )(y)


def head_ring(mesh):
    count = mesh.shape["head"]
    try:
        spots = [tuple(device.coords) for device in mesh.devices[:, 0]]
    except (AttributeError, TypeError):
        return (count, 1)
    moving = [axis for axis in range(len(spots[0])) if spots[0][axis] != spots[1][axis]]
    if len(moving) != 1:
        return (count, 1)
    minor = len({spot[moving[0]] for spot in spots})
    if count % minor or minor % 2:
        return (count, 1)
    return (count // minor, minor)


def contract_rows(left, right):
    return lax.dot_general(
        left, right, (((0,), (0,)), ((), ())), preferred_element_type=jnp.float32
    )


def contract_cols(left, right):
    return lax.dot_general(
        left, right, (((1,), (1,)), ((), ())), preferred_element_type=jnp.float32
    )


def on_device(
    ring,
    tokens,
    w_query,
    w_key,
    w_value,
    w_outgate,
    w_alpha,
    w_beta,
    conv_query,
    conv_key,
    conv_value,
    a_log,
    dt_bias,
    o_gain,
    w_out,
    gain_in,
    gain_ffn,
    w_gate,
    w_up,
    w_down,
    segments,
    valid_len,
    cotangent,
):
    residual = tokens[0].astype(jnp.float32)
    heads_here = w_alpha.shape[1]
    head_first = lax.axis_index("head") * heads_here
    norm_one, pull_one = jax.vjp(rms_norm, residual, gain_in)
    normed_one = norm_one.astype(jnp.bfloat16)
    row_count = lax.psum(1, "row")
    w_local = jnp.concatenate(
        [w_query, w_key, w_value, w_outgate, w_alpha, w_beta], axis=1
    ).astype(jnp.bfloat16)
    edges = [0]
    for member in (w_query, w_key, w_value, w_outgate, w_alpha, w_beta):
        edges.append(edges[-1] + member.shape[1])
    w_inward = lax.all_gather(w_local, "row", axis=0, tiled=True)
    conv_local = jnp.concatenate([conv_query, conv_key, conv_value], axis=1).astype(jnp.bfloat16)
    conv_edges = [0, conv_query.shape[1], conv_query.shape[1] + conv_key.shape[1], conv_local.shape[1]]
    conv_all = lax.all_gather(conv_local, "row", axis=1, tiled=True).reshape(
        conv_local.shape[0], row_count, conv_local.shape[1]
    )
    conv_parts = [
        conv_all[:, :, conv_edges[i] : conv_edges[i + 1]].reshape(conv_local.shape[0], -1)
        for i in range(3)
    ]
    out_matrix = lax.all_gather(w_out.astype(jnp.bfloat16), "row", axis=1, tiled=True)
    ff_width = w_gate.shape[1]
    ffn_local = jnp.concatenate([w_gate, w_up, w_down.T], axis=1).astype(jnp.bfloat16)
    grad_out = cotangent[0]
    grad_out_rows = lax.all_gather(grad_out, "row", axis=0, tiled=True)
    all_rows = ring_gather(normed_one, ring, 0)
    all_rows, out_matrix, ffn_local = lax.optimization_barrier((all_rows, out_matrix, ffn_local))
    ffn_all = lax.all_gather(ffn_local, "head", axis=0, tiled=True)
    projected = jnp.dot(all_rows, w_inward, preferred_element_type=jnp.float32)
    proj_parts = [projected[:, edges[spot] : edges[spot + 1]] for spot in range(6)]
    seg_ids = segments[0]
    live_mask = (jnp.arange(seg_ids.shape[0]) < valid_len[0]).astype(jnp.float32)
    a_here = lax.dynamic_slice_in_dim(a_log, head_first, heads_here)
    dt_here = lax.dynamic_slice_in_dim(dt_bias, head_first, heads_here)
    mixer_fn = partial(local_mixer, seg_ids=seg_ids, live_mask=live_mask)
    mixed, pull_core = jax.vjp(
        mixer_fn,
        proj_parts[0],
        proj_parts[1],
        proj_parts[2],
        proj_parts[3],
        proj_parts[4],
        proj_parts[5],
        conv_parts[0].astype(jnp.float32),
        conv_parts[1].astype(jnp.float32),
        conv_parts[2].astype(jnp.float32),
        a_here,
        dt_here,
        o_gain,
    )
    mixed, ffn_all, grad_out_rows = lax.optimization_barrier((mixed, ffn_all, grad_out_rows))
    w_gate_all = ffn_all[:, :ff_width]
    w_up_all = ffn_all[:, ff_width : 2 * ff_width]
    w_down_t = ffn_all[:, 2 * ff_width :]
    mixed_half = mixed.astype(jnp.bfloat16)
    mixer_output = ring_scatter(
        jnp.dot(mixed_half, out_matrix, preferred_element_type=jnp.float32).astype(jnp.bfloat16),
        ring,
        1,
    )
    middle = residual + mixer_output
    norm_two, pull_two = jax.vjp(rms_norm, middle, gain_ffn)
    normed_two = norm_two.astype(jnp.bfloat16)
    ffn_inputs = lax.all_gather(normed_two, "row", axis=0, tiled=True)
    gate_pre = jnp.dot(ffn_inputs, w_gate_all, preferred_element_type=jnp.float32)
    up_pre = jnp.dot(ffn_inputs, w_up_all, preferred_element_type=jnp.float32)
    hidden_val, pull_act = jax.vjp(swiglu, gate_pre, up_pre)
    hidden_half = hidden_val.astype(jnp.bfloat16)
    ffn_partial = contract_cols(hidden_half, w_down_t).astype(jnp.bfloat16)
    grad_hidden = jnp.dot(grad_out_rows, w_down_t, preferred_element_type=jnp.float32)
    grad_down_t = contract_rows(grad_out_rows, hidden_half)
    grad_gate_f, grad_up_f = pull_act(grad_hidden)
    grad_gate = grad_gate_f.astype(jnp.bfloat16)
    grad_upper = grad_up_f.astype(jnp.bfloat16)
    grad_wgate = contract_rows(ffn_inputs, grad_gate)
    grad_wup = contract_rows(ffn_inputs, grad_upper)
    grad_norm_two = lax.psum_scatter(
        (contract_cols(grad_gate, w_gate_all) + contract_cols(grad_upper, w_up_all)).astype(
            jnp.bfloat16
        ),
        "row",
        scatter_dimension=0,
        tiled=True,
    ).astype(jnp.float32)
    grad_mid_part, grad_gain_ffn = pull_two(grad_norm_two)
    grad_middle = grad_out.astype(jnp.float32) + grad_mid_part
    ffn_grad_cat = jnp.concatenate([grad_wgate, grad_wup, grad_down_t], axis=1).astype(
        jnp.bfloat16
    )
    grad_mid_half = grad_middle.astype(jnp.bfloat16)
    grad_mid_rows = ring_gather(grad_mid_half, ring, 2)
    ffn_output = lax.psum_scatter(ffn_partial, "row", scatter_dimension=0, tiled=True)
    grad_mid_rows, ffn_grad_cat = lax.optimization_barrier((grad_mid_rows, ffn_grad_cat))
    ffn_grad_all = lax.psum_scatter(ffn_grad_cat, "head", scatter_dimension=0, tiled=True)
    grad_mixed = contract_cols(grad_mid_rows, out_matrix)
    grad_wout = contract_rows(mixed_half, grad_mid_rows).astype(jnp.bfloat16)
    wout_grad = lax.psum_scatter(grad_wout, "row", scatter_dimension=1, tiled=True)
    core_grads = pull_core(grad_mixed)
    core_grads, ffn_output, ffn_grad_all = lax.optimization_barrier(
        (core_grads, ffn_output, ffn_grad_all)
    )
    final_out = (middle + ffn_output.astype(jnp.float32)).astype(jnp.bfloat16)
    ffn_grad_all = ffn_grad_all.astype(jnp.float32)
    ffn_grads = (
        ffn_grad_all[:, :ff_width],
        ffn_grad_all[:, ff_width : 2 * ff_width],
        ffn_grad_all[:, 2 * ff_width :].T,
    )
    grad_proj = jnp.concatenate(
        [core_grads[0], core_grads[1], core_grads[2], core_grads[3], core_grads[4], core_grads[5]],
        axis=1,
    ).astype(jnp.bfloat16)
    grad_inward = contract_rows(all_rows, grad_proj).astype(jnp.bfloat16)
    grad_norm_one = ring_scatter(contract_cols(grad_proj, w_inward).astype(jnp.bfloat16), ring, 3)
    grad_norm_one, wout_grad = lax.optimization_barrier((grad_norm_one, wout_grad))
    grad_in_part, grad_gain_in = pull_one(grad_norm_one)
    grad_input = grad_middle + grad_in_part
    inward_all = lax.psum_scatter(
        grad_inward, "row", scatter_dimension=0, tiled=True
    ).astype(jnp.float32)
    conv_grad_local = jnp.concatenate(
        [
            core_grads[6 + i].reshape(conv_local.shape[0], row_count, -1)
            for i in range(3)
        ],
        axis=2,
    ).reshape(conv_local.shape[0], -1)
    conv_grad = lax.psum_scatter(
        conv_grad_local.astype(jnp.bfloat16), "row", scatter_dimension=1, tiled=True
    ).astype(jnp.float32)
    mixer_grads = tuple(inward_all[:, edges[spot] : edges[spot + 1]] for spot in range(6)) + tuple(
        conv_grad[:, conv_edges[i] : conv_edges[i + 1]] for i in range(3)
    ) + (wout_grad.astype(jnp.float32),)
    head_total = a_log.shape[0]
    grad_a_full = lax.dynamic_update_slice_in_dim(
        jnp.zeros((head_total,), jnp.float32), core_grads[9], head_first, 0
    )
    grad_dt_full = lax.dynamic_update_slice_in_dim(
        jnp.zeros((head_total,), jnp.float32), core_grads[10], head_first, 0
    )
    small_sums = lax.psum(
        (grad_gain_in, grad_gain_ffn, core_grads[11], grad_a_full, grad_dt_full), ("head", "row")
    )
    return (
        final_out[None],
        grad_input[None],
        mixer_grads[0],
        mixer_grads[1],
        mixer_grads[2],
        mixer_grads[3],
        mixer_grads[4],
        mixer_grads[5],
        mixer_grads[6],
        mixer_grads[7],
        mixer_grads[8],
        small_sums[3],
        small_sums[4],
        small_sums[2],
        mixer_grads[9],
        small_sums[0],
        small_sums[1],
        ffn_grads[0],
        ffn_grads[1],
        ffn_grads[2],
    )


def solution(mesh):
    return jax.shard_map(
        partial(on_device, head_ring(mesh)),
        mesh=mesh,
        in_specs=(
            P("row", "head", None),
            P("row", "head"),
            P("row", "head"),
            P("row", "head"),
            P("row", "head"),
            P("row", "head"),
            P("row", "head"),
            P(None, ("head", "row")),
            P(None, ("head", "row")),
            P(None, ("head", "row")),
            P(),
            P(),
            P(),
            P("head", "row"),
            P(),
            P(),
            P("head", "row"),
            P("head", "row"),
            P("row", "head"),
            P("row", None),
            P("row"),
            P("row", "head", None),
        ),
        out_specs=(
            P("row", "head", None),
            P("row", "head", None),
            P("row", "head"),
            P("row", "head"),
            P("row", "head"),
            P("row", "head"),
            P("row", "head"),
            P("row", "head"),
            P(None, ("head", "row")),
            P(None, ("head", "row")),
            P(None, ("head", "row")),
            P(),
            P(),
            P(),
            P("head", "row"),
            P(),
            P(),
            P("head", "row"),
            P("head", "row"),
            P("row", "head"),
        ),
        check_vma=False,
    )
```

```python
from functools import partial
import math

import jax
import jax.numpy as jnp
from jax import lax
from jax.sharding import PartitionSpec as P
from jax.experimental import pallas as pl
from jax.experimental.pallas import tpu as pltpu

BLOCK = 64


precise = lax.Precision.HIGHEST
epsilon = 1e-06
o_floor = 0.001


def rms_norm(vector, gain_vec, floor_add=epsilon):
    return (
        vector * lax.rsqrt(jnp.mean(vector * vector, axis=-1, keepdims=True) + floor_add) * gain_vec
    )


def unit_norm(vector):
    return vector * lax.rsqrt(jnp.sum(vector * vector, axis=-1, keepdims=True) + epsilon)


def swiglu(gate_pre, up_pre):
    return jax.nn.silu(gate_pre) * up_pre


def short_conv(signal, kernel, seg_ids):
    tap_count = kernel.shape[0]
    length = signal.shape[0]
    summed = signal * kernel[tap_count - 1]
    for offset in range(1, tap_count):
        shifted = jnp.concatenate(
            [jnp.zeros((offset, signal.shape[1]), signal.dtype), signal[: length - offset]], axis=0
        )
        seg_shift = jnp.concatenate(
            [jnp.full((offset,), -1, jnp.int32), seg_ids[: length - offset]]
        )
        keep_mask = (seg_shift == seg_ids).astype(signal.dtype)
        summed = summed + shifted * kernel[tap_count - 1 - offset] * keep_mask[:, None]
    return summed


def _recur_fwd_kernel(nb, u0_ref, w_ref, kt_ref, c_ref, s_out, u_out, s_scr):
    @pl.when(pl.program_id(1) == 0)
    def _():
        s_scr[...] = jnp.zeros_like(s_scr)

    def step(j, carry):
        state = s_scr[...]
        s_out[0, j] = state
        update = u0_ref[0, j] - lax.dot_general(
            w_ref[0, j], state, (((1,), (1,)), ((), ())),
            precision=precise, preferred_element_type=jnp.float32,
        )
        u_out[0, j] = update
        s_scr[...] = c_ref[0, j] * state + lax.dot_general(
            update, kt_ref[0, j], (((0,), (0,)), ((), ())),
            precision=precise, preferred_element_type=jnp.float32,
        )
        return carry

    lax.fori_loop(0, nb, step, 0)


def _recur_bwd_kernel(
    nb, s_ref, u_ref, w_ref, kt_ref, c_ref, ds_ref, du_ref,
    du0_out, dw_out, dkt_out, dc_out, g_scr,
):
    @pl.when(pl.program_id(1) == 0)
    def _():
        g_scr[...] = jnp.zeros_like(g_scr)

    def step(i, carry):
        j = nb - 1 - i
        grad_state = g_scr[...]
        state = s_ref[0, j]
        grad_update = du_ref[0, j] + lax.dot_general(
            kt_ref[0, j], grad_state, (((1,), (1,)), ((), ())),
            precision=precise, preferred_element_type=jnp.float32,
        )
        dkt_out[0, j] = jnp.dot(
            u_ref[0, j], grad_state, precision=precise, preferred_element_type=jnp.float32
        )
        dc_out[0, j] = jnp.sum(grad_state * state, axis=0, keepdims=True)
        du0_out[0, j] = grad_update
        dw_out[0, j] = -jnp.dot(
            grad_update, state, precision=precise, preferred_element_type=jnp.float32
        )
        g_scr[...] = (
            c_ref[0, j] * grad_state
            - lax.dot_general(
                grad_update, w_ref[0, j], (((0,), (0,)), ((), ())),
                precision=precise, preferred_element_type=jnp.float32,
            )
            + ds_ref[0, j]
        )
        return carry

    lax.fori_loop(0, nb, step, 0)


def _chunk_spec(nb, tail, reverse, count):
    if reverse:
        return pl.BlockSpec((1, nb) + tail, lambda h, b: (h, count - 1 - b, 0, 0))
    return pl.BlockSpec((1, nb) + tail, lambda h, b: (h, b, 0, 0))


def _recur_forward(u0, w, kt, c):
    heads, count, chunk, dv = u0.shape
    dk = w.shape[-1]
    nb = min(8, count)
    blocks = count // nb
    flops = 4 * heads * count * chunk * dk * dv * 6
    moved = 4 * heads * count * (2 * chunk * dv + 2 * chunk * dk + dv * dk)
    return pl.pallas_call(
        partial(_recur_fwd_kernel, nb),
        grid=(heads, blocks),
        in_specs=[
            _chunk_spec(nb, (chunk, dv), False, blocks),
            _chunk_spec(nb, (chunk, dk), False, blocks),
            _chunk_spec(nb, (chunk, dk), False, blocks),
            _chunk_spec(nb, (1, dk), False, blocks),
        ],
        out_specs=[
            _chunk_spec(nb, (dv, dk), False, blocks),
            _chunk_spec(nb, (chunk, dv), False, blocks),
        ],
        out_shape=[
            jax.ShapeDtypeStruct((heads, count, dv, dk), jnp.float32),
            jax.ShapeDtypeStruct((heads, count, chunk, dv), jnp.float32),
        ],
        scratch_shapes=[pltpu.VMEM((dv, dk), jnp.float32)],
        compiler_params=pltpu.CompilerParams(dimension_semantics=("arbitrary", "arbitrary")),
        cost_estimate=pl.CostEstimate(flops=flops, transcendentals=0, bytes_accessed=moved),
        name="delta_state_forward",
    )(u0, w, kt, c)


def _recur_backward(states, updates, w, kt, c, d_states, d_updates):
    heads, count, chunk, dv = updates.shape
    dk = w.shape[-1]
    nb = min(8, count)
    blocks = count // nb
    flops = 8 * heads * count * chunk * dk * dv * 6
    moved = 4 * heads * count * (4 * chunk * dv + 4 * chunk * dk + 2 * dv * dk)
    return pl.pallas_call(
        partial(_recur_bwd_kernel, nb),
        grid=(heads, blocks),
        in_specs=[
            _chunk_spec(nb, (dv, dk), True, blocks),
            _chunk_spec(nb, (chunk, dv), True, blocks),
            _chunk_spec(nb, (chunk, dk), True, blocks),
            _chunk_spec(nb, (chunk, dk), True, blocks),
            _chunk_spec(nb, (1, dk), True, blocks),
            _chunk_spec(nb, (dv, dk), True, blocks),
            _chunk_spec(nb, (chunk, dv), True, blocks),
        ],
        out_specs=[
            _chunk_spec(nb, (chunk, dv), True, blocks),
            _chunk_spec(nb, (chunk, dk), True, blocks),
            _chunk_spec(nb, (chunk, dk), True, blocks),
            _chunk_spec(nb, (1, dk), True, blocks),
        ],
        out_shape=[
            jax.ShapeDtypeStruct((heads, count, chunk, dv), jnp.float32),
            jax.ShapeDtypeStruct((heads, count, chunk, dk), jnp.float32),
            jax.ShapeDtypeStruct((heads, count, chunk, dk), jnp.float32),
            jax.ShapeDtypeStruct((heads, count, 1, dk), jnp.float32),
        ],
        scratch_shapes=[pltpu.VMEM((dv, dk), jnp.float32)],
        compiler_params=pltpu.CompilerParams(dimension_semantics=("arbitrary", "arbitrary")),
        cost_estimate=pl.CostEstimate(flops=flops, transcendentals=0, bytes_accessed=moved),
        name="delta_state_backward",
    )(states, updates, w, kt, c, d_states, d_updates)


@jax.custom_vjp
def state_recurrence(u0, w, kt, c):
    return _recur_forward(u0, w, kt, c)


def _recurrence_fwd(u0, w, kt, c):
    states, updates = _recur_forward(u0, w, kt, c)
    return (states, updates), (states, updates, w, kt, c)


def _recurrence_bwd(saved, grads):
    states, updates, w, kt, c = saved
    d_states, d_updates = grads
    du0, dw, dkt, dc_lanes = _recur_backward(states, updates, w, kt, c, d_states, d_updates)
    return du0, dw, dkt, dc_lanes


state_recurrence.defvjp(_recurrence_fwd, _recurrence_bwd)


def chunk_prepare(queries, keys_n, values, decays, beta_rate, seg_ids):
    length, dk = keys_n.shape
    count = length // BLOCK
    q = queries.reshape(count, BLOCK, dk)
    k = keys_n.reshape(count, BLOCK, dk)
    v = values.reshape(count, BLOCK, values.shape[1])
    beta = beta_rate.reshape(count, BLOCK)
    seg = seg_ids.reshape(count, BLOCK)
    cumulative = jnp.cumsum(decays.reshape(count, BLOCK), axis=1)
    places = jnp.arange(BLOCK)
    lower_tri = places[:, None] >= places[None, :]
    inside = jnp.logical_and(seg[:, :, None] == seg[:, None, :], lower_tri)
    log_gap = jnp.where(inside, cumulative[:, :, None] - cumulative[:, None, :], 0.0)
    within = jnp.exp(log_gap) * inside.astype(jnp.float32)
    strict = within * (places[:, None] > places[None, :]).astype(jnp.float32)
    last_seg = jnp.concatenate([jnp.full((1,), -1, seg.dtype), seg[:-1, BLOCK - 1]])
    carried = jnp.exp(cumulative) * (seg == last_seg[:, None]).astype(jnp.float32)
    key_gram = jnp.einsum("nid,njd->nij", k, k, precision=precise)
    system = jnp.eye(BLOCK, dtype=jnp.float32) + beta[:, :, None] * strict * key_gram
    right_side = jnp.concatenate([beta[:, :, None] * v, (beta * carried)[:, :, None] * k], axis=2)
    solved = lax.linalg.triangular_solve(
        system, right_side, left_side=True, lower=True, unit_diagonal=True
    )
    dv = v.shape[2]
    kt = within[:, BLOCK - 1, :, None] * k
    scores = jnp.einsum("nid,njd->nij", q, k, precision=precise) * within
    return solved[:, :, :dv], solved[:, :, dv:], kt, carried[:, BLOCK - 1], carried, scores


def chunk_finish(queries, carried, scores, states, updates):
    count = states.shape[0]
    q = queries.reshape(count, BLOCK, queries.shape[1])
    output = carried[:, :, None] * jnp.einsum(
        "nid,nvd->niv", q, states, precision=precise
    ) + jnp.einsum("nij,njv->niv", scores, updates, precision=precise)
    return output.reshape(count * BLOCK, states.shape[1])


def delta_rule(queries, keys_n, values, decays, beta_rate, seg_ids):
    u0, w, kt, tail, carried, scores = jax.vmap(chunk_prepare, in_axes=(0, 0, 0, 0, 0, None))(
        queries, keys_n, values, decays, beta_rate, seg_ids
    )
    c = jnp.broadcast_to(tail[:, :, None, None], tail.shape + (1, w.shape[-1]))
    states, updates = state_recurrence(u0, w, kt, c)
    return jax.vmap(chunk_finish)(queries, carried, scores, states, updates)


def head_inputs(proj_query, proj_key, proj_value, proj_alpha, proj_beta,
                kernel_query, kernel_key, kernel_value, a_here, dt_here, seg_ids):
    queries = unit_norm(jax.nn.silu(short_conv(proj_query, kernel_query, seg_ids))) * (
        1.0 / math.sqrt(proj_query.shape[1])
    )
    keys_n = unit_norm(jax.nn.silu(short_conv(proj_key, kernel_key, seg_ids)))
    values = jax.nn.silu(short_conv(proj_value, kernel_value, seg_ids))
    decays = -jnp.exp(a_here) * jax.nn.softplus(proj_alpha + dt_here)
    beta_rate = jax.nn.sigmoid(proj_beta)
    return queries, keys_n, values, decays, beta_rate


def head_output(recurrent, proj_gate, o_gain, live_mask):
    return rms_norm(recurrent, o_gain, o_floor) * jax.nn.silu(proj_gate) * live_mask[:, None]


def local_mixer(
    proj_query,
    proj_key,
    proj_value,
    proj_gate,
    proj_alpha,
    proj_beta,
    kernel_query,
    kernel_key,
    kernel_value,
    a_here,
    dt_here,
    o_gain,
    seg_ids=None,
    live_mask=None,
):
    row_count = proj_query.shape[0]
    heads_here = proj_alpha.shape[1]

    def by_head(array):
        return jnp.moveaxis(array.reshape(row_count, heads_here, -1), 1, 0)

    def kernel_heads(kernel):
        return jnp.moveaxis(kernel.reshape(kernel.shape[0], heads_here, -1), 1, 0)

    queries, keys_n, values, decays, beta_rate = jax.vmap(
        head_inputs, in_axes=(0,) * 10 + (None,)
    )(
        by_head(proj_query),
        by_head(proj_key),
        by_head(proj_value),
        proj_alpha.T,
        proj_beta.T,
        kernel_heads(kernel_query),
        kernel_heads(kernel_key),
        kernel_heads(kernel_value),
        a_here,
        dt_here,
        seg_ids,
    )
    recurrent = delta_rule(queries, keys_n, values, decays, beta_rate, seg_ids)
    mixed_heads = jax.vmap(head_output, in_axes=(0, 0, None, None))(
        recurrent, by_head(proj_gate), o_gain, live_mask
    )
    return jnp.moveaxis(mixed_heads, 0, 1).reshape(row_count, -1)


MESH_ID = pl.DeviceIdType.MESH


def _ring_position(h, major, minor):
    a = h // minor
    b = h % minor
    return b * major + a + (b % 2) * (major - 1 - 2 * a)


def _ring_member(q, major, minor):
    count = major * minor
    q = (q + count) % count
    b = q // major
    r = q % major
    return (r + (b % 2) * (major - 1 - 2 * r)) * minor + b


def _ring_sides(axis, major, minor):
    p = _ring_position(lax.axis_index(axis), major, minor)
    return p, _ring_member(p + 1, major, minor), _ring_member(p - 1, major, minor)


def _peer(axis, target):
    if axis == "head":
        return (target, lax.axis_index("row"))
    return (lax.axis_index("head"), target)


def _greet(axis, nxt, prv):
    barrier = pltpu.get_barrier_semaphore()
    pl.semaphore_signal(barrier, 1, device_id=_peer(axis, prv), device_id_type=MESH_ID)
    pl.semaphore_signal(barrier, 1, device_id=_peer(axis, nxt), device_id_type=MESH_ID)
    pl.semaphore_wait(barrier, 2)


def _ring_gather_kernel(axis, major, minor, x_ref, out_ref, send_sem, recv_sem):
    count = major * minor
    blk = x_ref.shape[0]
    half = blk // 2
    p, nxt, prv = _ring_sides(axis, major, minor)
    out_ref[pl.ds(pl.multiple_of(lax.axis_index(axis) * blk, blk), blk), :] = x_ref[...]
    _greet(axis, nxt, prv)

    def piece(pos, off):
        return out_ref.at[pl.ds(pl.multiple_of(_ring_member(pos, major, minor) * blk + off, half), half)]

    def outgoing(d, s):
        pos = p - s if d == 0 else p + s
        target = nxt if d == 0 else prv
        ref = piece(pos, d * half)
        return pltpu.make_async_remote_copy(
            ref, ref, send_sem.at[d, s], recv_sem.at[d, s], device_id=_peer(axis, target),
            device_id_type=MESH_ID,
        )

    def incoming(d, s):
        pos = p - 1 - s if d == 0 else p + 1 + s
        source = prv if d == 0 else nxt
        ref = piece(pos, d * half)
        return pltpu.make_async_remote_copy(
            ref, ref, send_sem.at[d, s], recv_sem.at[d, s], device_id=_peer(axis, source),
            device_id_type=MESH_ID,
        )

    for s in range(count - 1):
        for d in (0, 1):
            if s > 0:
                incoming(d, s - 1).wait_recv()
            outgoing(d, s).start()
    for d in (0, 1):
        incoming(d, count - 2).wait_recv()
    for s in range(count - 1):
        for d in (0, 1):
            outgoing(d, s).wait_send()


def _ring_scatter_kernel(axis, major, minor, y_ref, out_ref, buf, send_sem, recv_sem):
    count = major * minor
    blk = out_ref.shape[0]
    half = blk // 2
    p, nxt, prv = _ring_sides(axis, major, minor)
    _greet(axis, nxt, prv)

    def piece(pos, off):
        return y_ref.at[pl.ds(pl.multiple_of(_ring_member(pos, major, minor) * blk + off, half), half)]

    def outgoing(d, s):
        pos = p - s - 1 if d == 0 else p + s + 1
        target = nxt if d == 0 else prv
        source = piece(pos, d * half) if s == 0 else buf.at[d, s - 1]
        return pltpu.make_async_remote_copy(
            source, buf.at[d, s], send_sem.at[d, s], recv_sem.at[d, s],
            device_id=_peer(axis, target), device_id_type=MESH_ID,
        )

    def incoming(d, s):
        source = prv if d == 0 else nxt
        return pltpu.make_async_remote_copy(
            buf.at[d, s], buf.at[d, s], send_sem.at[d, s], recv_sem.at[d, s],
            device_id=_peer(axis, source), device_id_type=MESH_ID,
        )

    for s in range(count - 1):
        for d in (0, 1):
            if s > 0:
                incoming(d, s - 1).wait_recv()
                pos = p - s - 1 if d == 0 else p + s + 1
                buf[d, s - 1] = (
                    buf[d, s - 1].astype(jnp.float32)
                    + piece(pos, d * half)[...].astype(jnp.float32)
                ).astype(buf.dtype)
            outgoing(d, s).start()
    for d in (0, 1):
        incoming(d, count - 2).wait_recv()
        out_ref[pl.ds(d * half, half), :] = piece(p, d * half)[...].astype(
            jnp.float32
        ) + buf[d, count - 2].astype(jnp.float32)
    for s in range(count - 1):
        for d in (0, 1):
            outgoing(d, s).wait_send()


def ring_gather(x, ring, collective):
    axis, major, minor = ring
    count = major * minor
    blk, width = x.shape
    return pl.pallas_call(
        partial(_ring_gather_kernel, axis, major, minor),
        out_shape=jax.ShapeDtypeStruct((count * blk, width), x.dtype),
        in_specs=[pl.BlockSpec(memory_space=pltpu.VMEM)],
        out_specs=pl.BlockSpec(memory_space=pltpu.VMEM),
        scratch_shapes=[
            pltpu.SemaphoreType.DMA((2, count - 1)),
            pltpu.SemaphoreType.DMA((2, count - 1)),
        ],
        compiler_params=pltpu.CompilerParams(collective_id=collective, has_side_effects=True),
        name="ring_gather_" + axis,
    )(x)


def ring_scatter(y, ring, collective):
    axis, major, minor = ring
    count = major * minor
    rows, width = y.shape
    blk = rows // count
    return pl.pallas_call(
        partial(_ring_scatter_kernel, axis, major, minor),
        out_shape=jax.ShapeDtypeStruct((blk, width), jnp.float32),
        in_specs=[pl.BlockSpec(memory_space=pltpu.VMEM)],
        out_specs=pl.BlockSpec(memory_space=pltpu.VMEM),
        scratch_shapes=[
            pltpu.VMEM((2, count - 1, blk // 2, width), y.dtype),
            pltpu.SemaphoreType.DMA((2, count - 1)),
            pltpu.SemaphoreType.DMA((2, count - 1)),
        ],
        compiler_params=pltpu.CompilerParams(collective_id=collective, has_side_effects=True),
        name="ring_scatter_" + axis,
    )(y)


def axis_ring(mesh, axis):
    count = mesh.shape[axis]
    members = mesh.devices[:, 0] if axis == "head" else mesh.devices[0, :]
    try:
        spots = [tuple(device.coords) + (device.core_on_chip,) for device in members]
    except (AttributeError, TypeError):
        return (axis, count, 1)
    moving = [spot for spot in range(len(spots[0])) if spots[0][spot] != spots[1][spot]]
    if len(moving) != 1:
        return (axis, count, 1)
    minor = len({spot[moving[0]] for spot in spots})
    if count % minor or minor % 2:
        return (axis, count, 1)
    return (axis, count // minor, minor)


def contract_rows(left, right):
    return lax.dot_general(
        left, right, (((0,), (0,)), ((), ())), preferred_element_type=jnp.float32
    )


def contract_cols(left, right):
    return lax.dot_general(
        left, right, (((1,), (1,)), ((), ())), preferred_element_type=jnp.float32
    )


def on_device(
    ring,
    row_ring,
    tokens,
    w_query,
    w_key,
    w_value,
    w_outgate,
    w_alpha,
    w_beta,
    conv_query,
    conv_key,
    conv_value,
    a_log,
    dt_bias,
    o_gain,
    w_out,
    gain_in,
    gain_ffn,
    w_gate,
    w_up,
    w_down,
    segments,
    valid_len,
    cotangent,
):
    residual = tokens[0].astype(jnp.float32)
    heads_here = w_alpha.shape[1]
    head_first = lax.axis_index("head") * heads_here
    norm_one, pull_one = jax.vjp(rms_norm, residual, gain_in)
    normed_one = norm_one.astype(jnp.bfloat16)
    row_count = lax.psum(1, "row")
    w_local = jnp.concatenate(
        [w_query, w_key, w_value, w_outgate, w_alpha, w_beta], axis=1
    ).astype(jnp.bfloat16)
    edges = [0]
    for member in (w_query, w_key, w_value, w_outgate, w_alpha, w_beta):
        edges.append(edges[-1] + member.shape[1])
    w_inward = lax.all_gather(w_local, "row", axis=0, tiled=True)
    conv_local = jnp.concatenate([conv_query, conv_key, conv_value], axis=1).astype(jnp.bfloat16)
    conv_edges = [0, conv_query.shape[1], conv_query.shape[1] + conv_key.shape[1], conv_local.shape[1]]
    conv_all = lax.all_gather(conv_local, "row", axis=1, tiled=True).reshape(
        conv_local.shape[0], row_count, conv_local.shape[1]
    )
    conv_parts = [
        conv_all[:, :, conv_edges[i] : conv_edges[i + 1]].reshape(conv_local.shape[0], -1)
        for i in range(3)
    ]
    out_matrix = lax.all_gather(w_out.astype(jnp.bfloat16), "row", axis=1, tiled=True)
    ff_width = w_gate.shape[1]
    ffn_local = jnp.concatenate([w_gate, w_up, w_down.T], axis=1).astype(jnp.bfloat16)
    grad_out = cotangent[0]
    grad_out_rows = lax.all_gather(grad_out, "row", axis=0, tiled=True)
    all_rows = ring_gather(normed_one, ring, 0)
    all_rows, out_matrix, ffn_local = lax.optimization_barrier((all_rows, out_matrix, ffn_local))
    ffn_all = lax.all_gather(ffn_local, "head", axis=0, tiled=True)
    projected = jnp.dot(all_rows, w_inward, preferred_element_type=jnp.float32)
    proj_parts = [projected[:, edges[spot] : edges[spot + 1]] for spot in range(6)]
    seg_ids = segments[0]
    live_mask = (jnp.arange(seg_ids.shape[0]) < valid_len[0]).astype(jnp.float32)
    a_here = lax.dynamic_slice_in_dim(a_log, head_first, heads_here)
    dt_here = lax.dynamic_slice_in_dim(dt_bias, head_first, heads_here)
    mixer_fn = partial(local_mixer, seg_ids=seg_ids, live_mask=live_mask)
    mixed, pull_core = jax.vjp(
        mixer_fn,
        proj_parts[0],
        proj_parts[1],
        proj_parts[2],
        proj_parts[3],
        proj_parts[4],
        proj_parts[5],
        conv_parts[0].astype(jnp.float32),
        conv_parts[1].astype(jnp.float32),
        conv_parts[2].astype(jnp.float32),
        a_here,
        dt_here,
        o_gain,
    )
    mixed, ffn_all, grad_out_rows = lax.optimization_barrier((mixed, ffn_all, grad_out_rows))
    w_gate_all = ffn_all[:, :ff_width]
    w_up_all = ffn_all[:, ff_width : 2 * ff_width]
    w_down_t = ffn_all[:, 2 * ff_width :]
    mixed_half = mixed.astype(jnp.bfloat16)
    mixer_output = ring_scatter(
        jnp.dot(mixed_half, out_matrix, preferred_element_type=jnp.float32).astype(jnp.bfloat16),
        ring,
        1,
    )
    middle = residual + mixer_output
    norm_two, pull_two = jax.vjp(rms_norm, middle, gain_ffn)
    normed_two = norm_two.astype(jnp.bfloat16)
    ffn_inputs = ring_gather(normed_two, row_ring, 4)
    gate_pre = jnp.dot(ffn_inputs, w_gate_all, preferred_element_type=jnp.float32)
    up_pre = jnp.dot(ffn_inputs, w_up_all, preferred_element_type=jnp.float32)
    hidden_val, pull_act = jax.vjp(swiglu, gate_pre, up_pre)
    hidden_half = hidden_val.astype(jnp.bfloat16)
    ffn_partial = contract_cols(hidden_half, w_down_t).astype(jnp.bfloat16)
    grad_hidden = jnp.dot(grad_out_rows, w_down_t, preferred_element_type=jnp.float32)
    grad_down_t = contract_rows(grad_out_rows, hidden_half)
    grad_gate_f, grad_up_f = pull_act(grad_hidden)
    grad_gate = grad_gate_f.astype(jnp.bfloat16)
    grad_upper = grad_up_f.astype(jnp.bfloat16)
    grad_wgate = contract_rows(ffn_inputs, grad_gate)
    grad_wup = contract_rows(ffn_inputs, grad_upper)
    grad_norm_two = ring_scatter(
        (contract_cols(grad_gate, w_gate_all) + contract_cols(grad_upper, w_up_all)).astype(
            jnp.bfloat16
        ),
        row_ring,
        5,
    )
    grad_mid_part, grad_gain_ffn = pull_two(grad_norm_two)
    grad_middle = grad_out.astype(jnp.float32) + grad_mid_part
    ffn_grad_cat = jnp.concatenate([grad_wgate, grad_wup, grad_down_t], axis=1).astype(
        jnp.bfloat16
    )
    grad_mid_half = grad_middle.astype(jnp.bfloat16)
    grad_mid_rows = ring_gather(grad_mid_half, ring, 2)
    ffn_output = lax.psum_scatter(ffn_partial, "row", scatter_dimension=0, tiled=True)
    grad_mid_rows, ffn_grad_cat = lax.optimization_barrier((grad_mid_rows, ffn_grad_cat))
    ffn_grad_all = lax.psum_scatter(ffn_grad_cat, "head", scatter_dimension=0, tiled=True)
    grad_mixed = contract_cols(grad_mid_rows, out_matrix)
    grad_wout = contract_rows(mixed_half, grad_mid_rows).astype(jnp.bfloat16)
    wout_grad = lax.psum_scatter(grad_wout, "row", scatter_dimension=1, tiled=True)
    core_grads = pull_core(grad_mixed)
    core_grads, ffn_output, ffn_grad_all = lax.optimization_barrier(
        (core_grads, ffn_output, ffn_grad_all)
    )
    final_out = (middle + ffn_output.astype(jnp.float32)).astype(jnp.bfloat16)
    ffn_grad_all = ffn_grad_all.astype(jnp.float32)
    ffn_grads = (
        ffn_grad_all[:, :ff_width],
        ffn_grad_all[:, ff_width : 2 * ff_width],
        ffn_grad_all[:, 2 * ff_width :].T,
    )
    grad_proj = jnp.concatenate(
        [core_grads[0], core_grads[1], core_grads[2], core_grads[3], core_grads[4], core_grads[5]],
        axis=1,
    ).astype(jnp.bfloat16)
    grad_inward = contract_rows(all_rows, grad_proj).astype(jnp.bfloat16)
    grad_norm_one = ring_scatter(contract_cols(grad_proj, w_inward).astype(jnp.bfloat16), ring, 3)
    grad_norm_one, wout_grad = lax.optimization_barrier((grad_norm_one, wout_grad))
    grad_in_part, grad_gain_in = pull_one(grad_norm_one)
    grad_input = grad_middle + grad_in_part
    inward_all = lax.psum_scatter(
        grad_inward, "row", scatter_dimension=0, tiled=True
    ).astype(jnp.float32)
    conv_grad_local = jnp.concatenate(
        [
            core_grads[6 + i].reshape(conv_local.shape[0], row_count, -1)
            for i in range(3)
        ],
        axis=2,
    ).reshape(conv_local.shape[0], -1)
    conv_grad = lax.psum_scatter(
        conv_grad_local.astype(jnp.bfloat16), "row", scatter_dimension=1, tiled=True
    ).astype(jnp.float32)
    mixer_grads = tuple(inward_all[:, edges[spot] : edges[spot + 1]] for spot in range(6)) + tuple(
        conv_grad[:, conv_edges[i] : conv_edges[i + 1]] for i in range(3)
    ) + (wout_grad.astype(jnp.float32),)
    head_total = a_log.shape[0]
    grad_a_full = lax.dynamic_update_slice_in_dim(
        jnp.zeros((head_total,), jnp.float32), core_grads[9], head_first, 0
    )
    grad_dt_full = lax.dynamic_update_slice_in_dim(
        jnp.zeros((head_total,), jnp.float32), core_grads[10], head_first, 0
    )
    small_sums = lax.psum(
        (grad_gain_in, grad_gain_ffn, core_grads[11], grad_a_full, grad_dt_full), ("head", "row")
    )
    return (
        final_out[None],
        grad_input[None],
        mixer_grads[0],
        mixer_grads[1],
        mixer_grads[2],
        mixer_grads[3],
        mixer_grads[4],
        mixer_grads[5],
        mixer_grads[6],
        mixer_grads[7],
        mixer_grads[8],
        small_sums[3],
        small_sums[4],
        small_sums[2],
        mixer_grads[9],
        small_sums[0],
        small_sums[1],
        ffn_grads[0],
        ffn_grads[1],
        ffn_grads[2],
    )


def solution(mesh):
    return jax.shard_map(
        partial(on_device, axis_ring(mesh, "head"), axis_ring(mesh, "row")),
        mesh=mesh,
        in_specs=(
            P("row", "head", None),
            P("row", "head"),
            P("row", "head"),
            P("row", "head"),
            P("row", "head"),
            P("row", "head"),
            P("row", "head"),
            P(None, ("head", "row")),
            P(None, ("head", "row")),
            P(None, ("head", "row")),
            P(),
            P(),
            P(),
            P("head", "row"),
            P(),
            P(),
            P("head", "row"),
            P("head", "row"),
            P("row", "head"),
            P("row", None),
            P("row"),
            P("row", "head", None),
        ),
        out_specs=(
            P("row", "head", None),
            P("row", "head", None),
            P("row", "head"),
            P("row", "head"),
            P("row", "head"),
            P("row", "head"),
            P("row", "head"),
            P("row", "head"),
            P(None, ("head", "row")),
            P(None, ("head", "row")),
            P(None, ("head", "row")),
            P(),
            P(),
            P(),
            P("head", "row"),
            P(),
            P(),
            P("head", "row"),
            P("head", "row"),
            P("row", "head"),
        ),
        check_vma=False,
    )
```

```python
from functools import partial
import math

import jax
import jax.numpy as jnp
from jax import lax
from jax.sharding import PartitionSpec as P
from jax.experimental import pallas as pl
from jax.experimental.pallas import tpu as pltpu

BLOCK = 64


precise = lax.Precision.HIGHEST
epsilon = 1e-06
o_floor = 0.001


def rms_norm(vector, gain_vec, floor_add=epsilon):
    return (
        vector * lax.rsqrt(jnp.mean(vector * vector, axis=-1, keepdims=True) + floor_add) * gain_vec
    )


def unit_norm(vector):
    return vector * lax.rsqrt(jnp.sum(vector * vector, axis=-1, keepdims=True) + epsilon)


def swiglu(gate_pre, up_pre):
    return jax.nn.silu(gate_pre) * up_pre


def short_conv(signal, kernel, seg_ids):
    tap_count = kernel.shape[0]
    length = signal.shape[0]
    summed = signal * kernel[tap_count - 1]
    for offset in range(1, tap_count):
        shifted = jnp.concatenate(
            [jnp.zeros((offset, signal.shape[1]), signal.dtype), signal[: length - offset]], axis=0
        )
        seg_shift = jnp.concatenate(
            [jnp.full((offset,), -1, jnp.int32), seg_ids[: length - offset]]
        )
        keep_mask = (seg_shift == seg_ids).astype(signal.dtype)
        summed = summed + shifted * kernel[tap_count - 1 - offset] * keep_mask[:, None]
    return summed


def _recur_fwd_kernel(nb, u0_ref, w_ref, kt_ref, c_ref, s_out, u_out, s_scr):
    @pl.when(pl.program_id(1) == 0)
    def _():
        s_scr[...] = jnp.zeros_like(s_scr)

    def step(j, carry):
        state = s_scr[...]
        s_out[0, j] = state
        update = u0_ref[0, j] - lax.dot_general(
            w_ref[0, j], state, (((1,), (1,)), ((), ())),
            precision=precise, preferred_element_type=jnp.float32,
        )
        u_out[0, j] = update
        s_scr[...] = c_ref[0, j] * state + lax.dot_general(
            update, kt_ref[0, j], (((0,), (0,)), ((), ())),
            precision=precise, preferred_element_type=jnp.float32,
        )
        return carry

    lax.fori_loop(0, nb, step, 0)


def _recur_bwd_kernel(
    nb, s_ref, u_ref, w_ref, kt_ref, c_ref, ds_ref, du_ref,
    du0_out, dw_out, dkt_out, dc_out, g_scr,
):
    @pl.when(pl.program_id(1) == 0)
    def _():
        g_scr[...] = jnp.zeros_like(g_scr)

    def step(i, carry):
        j = nb - 1 - i
        grad_state = g_scr[...]
        state = s_ref[0, j]
        grad_update = du_ref[0, j] + lax.dot_general(
            kt_ref[0, j], grad_state, (((1,), (1,)), ((), ())),
            precision=precise, preferred_element_type=jnp.float32,
        )
        dkt_out[0, j] = jnp.dot(
            u_ref[0, j], grad_state, precision=precise, preferred_element_type=jnp.float32
        )
        dc_out[0, j] = jnp.sum(grad_state * state, axis=0, keepdims=True)
        du0_out[0, j] = grad_update
        dw_out[0, j] = -jnp.dot(
            grad_update, state, precision=precise, preferred_element_type=jnp.float32
        )
        g_scr[...] = (
            c_ref[0, j] * grad_state
            - lax.dot_general(
                grad_update, w_ref[0, j], (((0,), (0,)), ((), ())),
                precision=precise, preferred_element_type=jnp.float32,
            )
            + ds_ref[0, j]
        )
        return carry

    lax.fori_loop(0, nb, step, 0)


def _chunk_spec(nb, tail, reverse, count):
    if reverse:
        return pl.BlockSpec((1, nb) + tail, lambda h, b: (h, count - 1 - b, 0, 0))
    return pl.BlockSpec((1, nb) + tail, lambda h, b: (h, b, 0, 0))


def _recur_forward(u0, w, kt, c):
    heads, count, chunk, dv = u0.shape
    dk = w.shape[-1]
    nb = min(8, count)
    blocks = count // nb
    flops = 4 * heads * count * chunk * dk * dv * 6
    moved = 4 * heads * count * (2 * chunk * dv + 2 * chunk * dk + dv * dk)
    return pl.pallas_call(
        partial(_recur_fwd_kernel, nb),
        grid=(heads, blocks),
        in_specs=[
            _chunk_spec(nb, (chunk, dv), False, blocks),
            _chunk_spec(nb, (chunk, dk), False, blocks),
            _chunk_spec(nb, (chunk, dk), False, blocks),
            _chunk_spec(nb, (1, dk), False, blocks),
        ],
        out_specs=[
            _chunk_spec(nb, (dv, dk), False, blocks),
            _chunk_spec(nb, (chunk, dv), False, blocks),
        ],
        out_shape=[
            jax.ShapeDtypeStruct((heads, count, dv, dk), jnp.float32),
            jax.ShapeDtypeStruct((heads, count, chunk, dv), jnp.float32),
        ],
        scratch_shapes=[pltpu.VMEM((dv, dk), jnp.float32)],
        compiler_params=pltpu.CompilerParams(dimension_semantics=("arbitrary", "arbitrary")),
        cost_estimate=pl.CostEstimate(flops=flops, transcendentals=0, bytes_accessed=moved),
        name="delta_state_forward",
    )(u0, w, kt, c)


def _recur_backward(states, updates, w, kt, c, d_states, d_updates):
    heads, count, chunk, dv = updates.shape
    dk = w.shape[-1]
    nb = min(8, count)
    blocks = count // nb
    flops = 8 * heads * count * chunk * dk * dv * 6
    moved = 4 * heads * count * (4 * chunk * dv + 4 * chunk * dk + 2 * dv * dk)
    return pl.pallas_call(
        partial(_recur_bwd_kernel, nb),
        grid=(heads, blocks),
        in_specs=[
            _chunk_spec(nb, (dv, dk), True, blocks),
            _chunk_spec(nb, (chunk, dv), True, blocks),
            _chunk_spec(nb, (chunk, dk), True, blocks),
            _chunk_spec(nb, (chunk, dk), True, blocks),
            _chunk_spec(nb, (1, dk), True, blocks),
            _chunk_spec(nb, (dv, dk), True, blocks),
            _chunk_spec(nb, (chunk, dv), True, blocks),
        ],
        out_specs=[
            _chunk_spec(nb, (chunk, dv), True, blocks),
            _chunk_spec(nb, (chunk, dk), True, blocks),
            _chunk_spec(nb, (chunk, dk), True, blocks),
            _chunk_spec(nb, (1, dk), True, blocks),
        ],
        out_shape=[
            jax.ShapeDtypeStruct((heads, count, chunk, dv), jnp.float32),
            jax.ShapeDtypeStruct((heads, count, chunk, dk), jnp.float32),
            jax.ShapeDtypeStruct((heads, count, chunk, dk), jnp.float32),
            jax.ShapeDtypeStruct((heads, count, 1, dk), jnp.float32),
        ],
        scratch_shapes=[pltpu.VMEM((dv, dk), jnp.float32)],
        compiler_params=pltpu.CompilerParams(dimension_semantics=("arbitrary", "arbitrary")),
        cost_estimate=pl.CostEstimate(flops=flops, transcendentals=0, bytes_accessed=moved),
        name="delta_state_backward",
    )(states, updates, w, kt, c, d_states, d_updates)


@jax.custom_vjp
def state_recurrence(u0, w, kt, c):
    return _recur_forward(u0, w, kt, c)


def _recurrence_fwd(u0, w, kt, c):
    states, updates = _recur_forward(u0, w, kt, c)
    return (states, updates), (states, updates, w, kt, c)


def _recurrence_bwd(saved, grads):
    states, updates, w, kt, c = saved
    d_states, d_updates = grads
    du0, dw, dkt, dc_lanes = _recur_backward(states, updates, w, kt, c, d_states, d_updates)
    return du0, dw, dkt, dc_lanes


state_recurrence.defvjp(_recurrence_fwd, _recurrence_bwd)


def chunk_prepare(queries, keys_n, values, decays, beta_rate, seg_ids):
    length, dk = keys_n.shape
    count = length // BLOCK
    q = queries.reshape(count, BLOCK, dk)
    k = keys_n.reshape(count, BLOCK, dk)
    v = values.reshape(count, BLOCK, values.shape[1])
    beta = beta_rate.reshape(count, BLOCK)
    seg = seg_ids.reshape(count, BLOCK)
    cumulative = jnp.cumsum(decays.reshape(count, BLOCK), axis=1)
    places = jnp.arange(BLOCK)
    lower_tri = places[:, None] >= places[None, :]
    inside = jnp.logical_and(seg[:, :, None] == seg[:, None, :], lower_tri)
    log_gap = jnp.where(inside, cumulative[:, :, None] - cumulative[:, None, :], 0.0)
    within = jnp.exp(log_gap) * inside.astype(jnp.float32)
    strict = within * (places[:, None] > places[None, :]).astype(jnp.float32)
    last_seg = jnp.concatenate([jnp.full((1,), -1, seg.dtype), seg[:-1, BLOCK - 1]])
    carried = jnp.exp(cumulative) * (seg == last_seg[:, None]).astype(jnp.float32)
    key_gram = jnp.einsum("nid,njd->nij", k, k, precision=precise)
    system = jnp.eye(BLOCK, dtype=jnp.float32) + beta[:, :, None] * strict * key_gram
    right_side = jnp.concatenate([beta[:, :, None] * v, (beta * carried)[:, :, None] * k], axis=2)
    solved = lax.linalg.triangular_solve(
        system, right_side, left_side=True, lower=True, unit_diagonal=True
    )
    dv = v.shape[2]
    kt = within[:, BLOCK - 1, :, None] * k
    scores = jnp.einsum("nid,njd->nij", q, k, precision=precise) * within
    return solved[:, :, :dv], solved[:, :, dv:], kt, carried[:, BLOCK - 1], carried, scores


def chunk_finish(queries, carried, scores, states, updates):
    count = states.shape[0]
    q = queries.reshape(count, BLOCK, queries.shape[1])
    output = carried[:, :, None] * jnp.einsum(
        "nid,nvd->niv", q, states, precision=precise
    ) + jnp.einsum("nij,njv->niv", scores, updates, precision=precise)
    return output.reshape(count * BLOCK, states.shape[1])


def delta_rule(queries, keys_n, values, decays, beta_rate, seg_ids):
    u0, w, kt, tail, carried, scores = jax.vmap(chunk_prepare, in_axes=(0, 0, 0, 0, 0, None))(
        queries, keys_n, values, decays, beta_rate, seg_ids
    )
    c = jnp.broadcast_to(tail[:, :, None, None], tail.shape + (1, w.shape[-1]))
    states, updates = state_recurrence(u0, w, kt, c)
    return jax.vmap(chunk_finish)(queries, carried, scores, states, updates)


def head_inputs(proj_query, proj_key, proj_value, proj_alpha, proj_beta,
                kernel_query, kernel_key, kernel_value, a_here, dt_here, seg_ids):
    queries = unit_norm(jax.nn.silu(short_conv(proj_query, kernel_query, seg_ids))) * (
        1.0 / math.sqrt(proj_query.shape[1])
    )
    keys_n = unit_norm(jax.nn.silu(short_conv(proj_key, kernel_key, seg_ids)))
    values = jax.nn.silu(short_conv(proj_value, kernel_value, seg_ids))
    decays = -jnp.exp(a_here) * jax.nn.softplus(proj_alpha + dt_here)
    beta_rate = jax.nn.sigmoid(proj_beta)
    return queries, keys_n, values, decays, beta_rate


def head_output(recurrent, proj_gate, o_gain, live_mask):
    return rms_norm(recurrent, o_gain, o_floor) * jax.nn.silu(proj_gate) * live_mask[:, None]


def local_mixer(
    proj_query,
    proj_key,
    proj_value,
    proj_gate,
    proj_alpha,
    proj_beta,
    kernel_query,
    kernel_key,
    kernel_value,
    a_here,
    dt_here,
    o_gain,
    seg_ids=None,
    live_mask=None,
):
    row_count = proj_query.shape[0]
    heads_here = proj_alpha.shape[1]

    def by_head(array):
        return jnp.moveaxis(array.reshape(row_count, heads_here, -1), 1, 0)

    def kernel_heads(kernel):
        return jnp.moveaxis(kernel.reshape(kernel.shape[0], heads_here, -1), 1, 0)

    queries, keys_n, values, decays, beta_rate = jax.vmap(
        head_inputs, in_axes=(0,) * 10 + (None,)
    )(
        by_head(proj_query),
        by_head(proj_key),
        by_head(proj_value),
        proj_alpha.T,
        proj_beta.T,
        kernel_heads(kernel_query),
        kernel_heads(kernel_key),
        kernel_heads(kernel_value),
        a_here,
        dt_here,
        seg_ids,
    )
    recurrent = delta_rule(queries, keys_n, values, decays, beta_rate, seg_ids)
    mixed_heads = jax.vmap(head_output, in_axes=(0, 0, None, None))(
        recurrent, by_head(proj_gate), o_gain, live_mask
    )
    return jnp.moveaxis(mixed_heads, 0, 1).reshape(row_count, -1)


MESH_ID = pl.DeviceIdType.MESH


def _ring_position(h, major, minor):
    a = h // minor
    b = h % minor
    return b * major + a + (b % 2) * (major - 1 - 2 * a)


def _ring_member(q, major, minor):
    count = major * minor
    q = (q + count) % count
    b = q // major
    r = q % major
    return (r + (b % 2) * (major - 1 - 2 * r)) * minor + b


def _ring_sides(major, minor):
    p = _ring_position(lax.axis_index("head"), major, minor)
    return p, _ring_member(p + 1, major, minor), _ring_member(p - 1, major, minor)


def _greet(nxt, prv, row):
    barrier = pltpu.get_barrier_semaphore()
    pl.semaphore_signal(barrier, 1, device_id=(prv, row), device_id_type=MESH_ID)
    pl.semaphore_signal(barrier, 1, device_id=(nxt, row), device_id_type=MESH_ID)
    pl.semaphore_wait(barrier, 2)


def _ring_gather_kernel(major, minor, x_ref, out_ref, send_sem, recv_sem):
    count = major * minor
    blk = x_ref.shape[0]
    half = blk // 2
    row = lax.axis_index("row")
    p, nxt, prv = _ring_sides(major, minor)
    out_ref[pl.ds(pl.multiple_of(lax.axis_index("head") * blk, blk), blk), :] = x_ref[...]
    _greet(nxt, prv, row)

    def piece(pos, off):
        return out_ref.at[pl.ds(pl.multiple_of(_ring_member(pos, major, minor) * blk + off, half), half)]

    def outgoing(d, s):
        pos = p - s if d == 0 else p + s
        target = nxt if d == 0 else prv
        ref = piece(pos, d * half)
        return pltpu.make_async_remote_copy(
            ref, ref, send_sem.at[d, s], recv_sem.at[d, s], device_id=(target, row),
            device_id_type=MESH_ID,
        )

    def incoming(d, s):
        pos = p - 1 - s if d == 0 else p + 1 + s
        source = prv if d == 0 else nxt
        ref = piece(pos, d * half)
        return pltpu.make_async_remote_copy(
            ref, ref, send_sem.at[d, s], recv_sem.at[d, s], device_id=(source, row),
            device_id_type=MESH_ID,
        )

    for s in range(count - 1):
        for d in (0, 1):
            if s > 0:
                incoming(d, s - 1).wait_recv()
            outgoing(d, s).start()
    for d in (0, 1):
        incoming(d, count - 2).wait_recv()
    for s in range(count - 1):
        for d in (0, 1):
            outgoing(d, s).wait_send()


def _ring_scatter_kernel(major, minor, y_ref, out_ref, buf, send_sem, recv_sem):
    count = major * minor
    blk = out_ref.shape[0]
    half = blk // 2
    row = lax.axis_index("row")
    p, nxt, prv = _ring_sides(major, minor)
    _greet(nxt, prv, row)

    def piece(pos, off):
        return y_ref.at[pl.ds(pl.multiple_of(_ring_member(pos, major, minor) * blk + off, half), half)]

    def outgoing(d, s):
        pos = p - s - 1 if d == 0 else p + s + 1
        target = nxt if d == 0 else prv
        source = piece(pos, d * half) if s == 0 else buf.at[d, s - 1]
        return pltpu.make_async_remote_copy(
            source, buf.at[d, s], send_sem.at[d, s], recv_sem.at[d, s],
            device_id=(target, row), device_id_type=MESH_ID,
        )

    def incoming(d, s):
        source = prv if d == 0 else nxt
        return pltpu.make_async_remote_copy(
            buf.at[d, s], buf.at[d, s], send_sem.at[d, s], recv_sem.at[d, s],
            device_id=(source, row), device_id_type=MESH_ID,
        )

    for s in range(count - 1):
        for d in (0, 1):
            if s > 0:
                incoming(d, s - 1).wait_recv()
                pos = p - s - 1 if d == 0 else p + s + 1
                buf[d, s - 1] = (
                    buf[d, s - 1].astype(jnp.float32)
                    + piece(pos, d * half)[...].astype(jnp.float32)
                ).astype(buf.dtype)
            outgoing(d, s).start()
    for d in (0, 1):
        incoming(d, count - 2).wait_recv()
        out_ref[pl.ds(d * half, half), :] = piece(p, d * half)[...].astype(
            jnp.float32
        ) + buf[d, count - 2].astype(jnp.float32)
    for s in range(count - 1):
        for d in (0, 1):
            outgoing(d, s).wait_send()


def ring_gather(x, ring, collective):
    major, minor = ring
    count = major * minor
    blk, width = x.shape
    return pl.pallas_call(
        partial(_ring_gather_kernel, major, minor),
        out_shape=jax.ShapeDtypeStruct((count * blk, width), x.dtype),
        in_specs=[pl.BlockSpec(memory_space=pltpu.VMEM)],
        out_specs=pl.BlockSpec(memory_space=pltpu.VMEM),
        scratch_shapes=[
            pltpu.SemaphoreType.DMA((2, count - 1)),
            pltpu.SemaphoreType.DMA((2, count - 1)),
        ],
        compiler_params=pltpu.CompilerParams(collective_id=collective, has_side_effects=True),
        name="ring_gather_head",
    )(x)


def ring_scatter(y, ring, collective):
    major, minor = ring
    count = major * minor
    rows, width = y.shape
    blk = rows // count
    return pl.pallas_call(
        partial(_ring_scatter_kernel, major, minor),
        out_shape=jax.ShapeDtypeStruct((blk, width), jnp.float32),
        in_specs=[pl.BlockSpec(memory_space=pltpu.VMEM)],
        out_specs=pl.BlockSpec(memory_space=pltpu.VMEM),
        scratch_shapes=[
            pltpu.VMEM((2, count - 1, blk // 2, width), y.dtype),
            pltpu.SemaphoreType.DMA((2, count - 1)),
            pltpu.SemaphoreType.DMA((2, count - 1)),
        ],
        compiler_params=pltpu.CompilerParams(collective_id=collective, has_side_effects=True),
        name="ring_scatter_head",
    )(y)


def head_ring(mesh):
    count = mesh.shape["head"]
    try:
        spots = [tuple(device.coords) for device in mesh.devices[:, 0]]
    except (AttributeError, TypeError):
        return (count, 1)
    moving = [axis for axis in range(len(spots[0])) if spots[0][axis] != spots[1][axis]]
    if len(moving) != 1:
        return (count, 1)
    minor = len({spot[moving[0]] for spot in spots})
    if count % minor or minor % 2:
        return (count, 1)
    return (count // minor, minor)


def contract_rows(left, right):
    return lax.dot_general(
        left, right, (((0,), (0,)), ((), ())), preferred_element_type=jnp.float32
    )


def contract_cols(left, right):
    return lax.dot_general(
        left, right, (((1,), (1,)), ((), ())), preferred_element_type=jnp.float32
    )


def on_device(
    ring,
    tokens,
    w_query,
    w_key,
    w_value,
    w_outgate,
    w_alpha,
    w_beta,
    conv_query,
    conv_key,
    conv_value,
    a_log,
    dt_bias,
    o_gain,
    w_out,
    gain_in,
    gain_ffn,
    w_gate,
    w_up,
    w_down,
    segments,
    valid_len,
    cotangent,
):
    residual = tokens[0].astype(jnp.float32)
    heads_here = w_alpha.shape[1]
    head_first = lax.axis_index("head") * heads_here
    norm_one, pull_one = jax.vjp(rms_norm, residual, gain_in)
    normed_one = norm_one.astype(jnp.bfloat16)
    row_count = lax.psum(1, "row")
    w_local = jnp.concatenate(
        [w_query, w_key, w_value, w_outgate, w_alpha, w_beta], axis=1
    ).astype(jnp.bfloat16)
    edges = [0]
    for member in (w_query, w_key, w_value, w_outgate, w_alpha, w_beta):
        edges.append(edges[-1] + member.shape[1])
    w_inward = lax.all_gather(w_local, "row", axis=0, tiled=True)
    conv_local = jnp.concatenate([conv_query, conv_key, conv_value], axis=1).astype(jnp.bfloat16)
    conv_edges = [0, conv_query.shape[1], conv_query.shape[1] + conv_key.shape[1], conv_local.shape[1]]
    conv_all = lax.all_gather(conv_local, "row", axis=1, tiled=True).reshape(
        conv_local.shape[0], row_count, conv_local.shape[1]
    )
    conv_parts = [
        conv_all[:, :, conv_edges[i] : conv_edges[i + 1]].reshape(conv_local.shape[0], -1)
        for i in range(3)
    ]
    out_matrix = lax.all_gather(w_out.astype(jnp.bfloat16), "row", axis=1, tiled=True)
    ff_width = w_gate.shape[1]
    ffn_local = jnp.concatenate([w_gate, w_up, w_down.T], axis=1).astype(jnp.bfloat16)
    grad_out = cotangent[0]
    grad_out_rows = lax.all_gather(grad_out, "row", axis=0, tiled=True)
    all_rows = ring_gather(normed_one, ring, 0)
    all_rows, out_matrix, ffn_local = lax.optimization_barrier((all_rows, out_matrix, ffn_local))
    ffn_all = lax.all_gather(ffn_local, "head", axis=0, tiled=True)
    projected = jnp.dot(all_rows, w_inward, preferred_element_type=jnp.float32)
    proj_parts = [projected[:, edges[spot] : edges[spot + 1]] for spot in range(6)]
    seg_ids = segments[0]
    live_mask = (jnp.arange(seg_ids.shape[0]) < valid_len[0]).astype(jnp.float32)
    a_here = lax.dynamic_slice_in_dim(a_log, head_first, heads_here)
    dt_here = lax.dynamic_slice_in_dim(dt_bias, head_first, heads_here)
    mixer_fn = partial(local_mixer, seg_ids=seg_ids, live_mask=live_mask)
    mixed, pull_core = jax.vjp(
        mixer_fn,
        proj_parts[0],
        proj_parts[1],
        proj_parts[2],
        proj_parts[3],
        proj_parts[4],
        proj_parts[5],
        conv_parts[0].astype(jnp.float32),
        conv_parts[1].astype(jnp.float32),
        conv_parts[2].astype(jnp.float32),
        a_here,
        dt_here,
        o_gain,
    )
    mixed, ffn_all, grad_out_rows = lax.optimization_barrier((mixed, ffn_all, grad_out_rows))
    w_gate_all = ffn_all[:, :ff_width]
    w_up_all = ffn_all[:, ff_width : 2 * ff_width]
    w_down_t = ffn_all[:, 2 * ff_width :]
    mixed_half = mixed.astype(jnp.bfloat16)
    mixer_output = ring_scatter(
        jnp.dot(mixed_half, out_matrix, preferred_element_type=jnp.float32).astype(jnp.bfloat16),
        ring,
        1,
    )
    middle = residual + mixer_output
    norm_two, pull_two = jax.vjp(rms_norm, middle, gain_ffn)
    normed_two = norm_two.astype(jnp.bfloat16)
    ffn_inputs = lax.all_gather(normed_two, "row", axis=0, tiled=True)
    gate_pre = jnp.dot(ffn_inputs, w_gate_all, preferred_element_type=jnp.float32)
    up_pre = jnp.dot(ffn_inputs, w_up_all, preferred_element_type=jnp.float32)
    hidden_val, pull_act = jax.vjp(swiglu, gate_pre, up_pre)
    hidden_half = hidden_val.astype(jnp.bfloat16)
    ffn_partial = contract_cols(hidden_half, w_down_t).astype(jnp.bfloat16)
    grad_hidden = jnp.dot(grad_out_rows, w_down_t, preferred_element_type=jnp.float32)
    grad_down_t = contract_rows(grad_out_rows, hidden_half)
    grad_gate_f, grad_up_f = pull_act(grad_hidden)
    grad_gate = grad_gate_f.astype(jnp.bfloat16)
    grad_upper = grad_up_f.astype(jnp.bfloat16)
    grad_wgate = contract_rows(ffn_inputs, grad_gate)
    grad_wup = contract_rows(ffn_inputs, grad_upper)
    grad_norm_two = lax.psum_scatter(
        (contract_cols(grad_gate, w_gate_all) + contract_cols(grad_upper, w_up_all)).astype(
            jnp.bfloat16
        ),
        "row",
        scatter_dimension=0,
        tiled=True,
    ).astype(jnp.float32)
    grad_mid_part, grad_gain_ffn = pull_two(grad_norm_two)
    grad_middle = grad_out.astype(jnp.float32) + grad_mid_part
    ffn_grad_cat = jnp.concatenate([grad_wgate, grad_wup, grad_down_t], axis=1).astype(
        jnp.bfloat16
    )
    grad_mid_half = grad_middle.astype(jnp.bfloat16)
    grad_mid_rows = ring_gather(grad_mid_half, ring, 2)
    ffn_output = lax.psum_scatter(ffn_partial, "row", scatter_dimension=0, tiled=True)
    grad_mid_rows, ffn_grad_cat = lax.optimization_barrier((grad_mid_rows, ffn_grad_cat))
    ffn_grad_all = lax.psum_scatter(ffn_grad_cat, "head", scatter_dimension=0, tiled=True)
    grad_mixed = contract_cols(grad_mid_rows, out_matrix)
    grad_wout = contract_rows(mixed_half, grad_mid_rows).astype(jnp.bfloat16)
    wout_grad = lax.psum_scatter(grad_wout, "row", scatter_dimension=1, tiled=True)
    core_grads = pull_core(grad_mixed)
    core_grads, ffn_output, ffn_grad_all = lax.optimization_barrier(
        (core_grads, ffn_output, ffn_grad_all)
    )
    final_out = (middle + ffn_output.astype(jnp.float32)).astype(jnp.bfloat16)
    ffn_grad_all = ffn_grad_all.astype(jnp.float32)
    ffn_grads = (
        ffn_grad_all[:, :ff_width],
        ffn_grad_all[:, ff_width : 2 * ff_width],
        ffn_grad_all[:, 2 * ff_width :].T,
    )
    grad_proj = jnp.concatenate(
        [core_grads[0], core_grads[1], core_grads[2], core_grads[3], core_grads[4], core_grads[5]],
        axis=1,
    ).astype(jnp.bfloat16)
    grad_inward = contract_rows(all_rows, grad_proj).astype(jnp.bfloat16)
    norm_one_partial = contract_cols(grad_proj, w_inward).astype(jnp.bfloat16)
    grad_gain_in = jnp.sum(
        norm_one_partial.astype(jnp.float32) * all_rows.astype(jnp.float32), axis=0
    ) / gain_in
    grad_norm_one = ring_scatter(norm_one_partial, ring, 3)
    grad_norm_one, wout_grad = lax.optimization_barrier((grad_norm_one, wout_grad))
    grad_in_part = pull_one(grad_norm_one)[0]
    grad_input = grad_middle + grad_in_part
    inward_all = lax.psum_scatter(
        grad_inward, "row", scatter_dimension=0, tiled=True
    ).astype(jnp.float32)
    conv_grad_local = jnp.concatenate(
        [
            core_grads[6 + i].reshape(conv_local.shape[0], row_count, -1)
            for i in range(3)
        ],
        axis=2,
    ).reshape(conv_local.shape[0], -1)
    conv_grad = lax.psum_scatter(
        conv_grad_local.astype(jnp.bfloat16), "row", scatter_dimension=1, tiled=True
    ).astype(jnp.float32)
    mixer_grads = tuple(inward_all[:, edges[spot] : edges[spot + 1]] for spot in range(6)) + tuple(
        conv_grad[:, conv_edges[i] : conv_edges[i + 1]] for i in range(3)
    ) + (wout_grad.astype(jnp.float32),)
    head_total = a_log.shape[0]
    grad_a_full = lax.dynamic_update_slice_in_dim(
        jnp.zeros((head_total,), jnp.float32), core_grads[9], head_first, 0
    )
    grad_dt_full = lax.dynamic_update_slice_in_dim(
        jnp.zeros((head_total,), jnp.float32), core_grads[10], head_first, 0
    )
    small_parts = (grad_gain_in, grad_gain_ffn, core_grads[11], grad_a_full, grad_dt_full)
    small_all = lax.psum(jnp.pad(jnp.concatenate(small_parts), (0, 16384 - 4384)), ("head", "row"))
    small_edges = [0]
    for part in small_parts:
        small_edges.append(small_edges[-1] + part.shape[0])
    small_sums = [small_all[small_edges[i] : small_edges[i + 1]] for i in range(5)]
    return (
        final_out[None],
        grad_input[None],
        mixer_grads[0],
        mixer_grads[1],
        mixer_grads[2],
        mixer_grads[3],
        mixer_grads[4],
        mixer_grads[5],
        mixer_grads[6],
        mixer_grads[7],
        mixer_grads[8],
        small_sums[3],
        small_sums[4],
        small_sums[2],
        mixer_grads[9],
        small_sums[0],
        small_sums[1],
        ffn_grads[0],
        ffn_grads[1],
        ffn_grads[2],
    )


def solution(mesh):
    return jax.shard_map(
        partial(on_device, head_ring(mesh)),
        mesh=mesh,
        in_specs=(
            P("row", "head", None),
            P("row", "head"),
            P("row", "head"),
            P("row", "head"),
            P("row", "head"),
            P("row", "head"),
            P("row", "head"),
            P(None, ("head", "row")),
            P(None, ("head", "row")),
            P(None, ("head", "row")),
            P(),
            P(),
            P(),
            P("head", "row"),
            P(),
            P(),
            P("head", "row"),
            P("head", "row"),
            P("row", "head"),
            P("row", None),
            P("row"),
            P("row", "head", None),
        ),
        out_specs=(
            P("row", "head", None),
            P("row", "head", None),
            P("row", "head"),
            P("row", "head"),
            P("row", "head"),
            P("row", "head"),
            P("row", "head"),
            P("row", "head"),
            P(None, ("head", "row")),
            P(None, ("head", "row")),
            P(None, ("head", "row")),
            P(),
            P(),
            P(),
            P("head", "row"),
            P(),
            P(),
            P("head", "row"),
            P("head", "row"),
            P("row", "head"),
        ),
        check_vma=False,
    )
```

```python
from functools import partial
import math

import jax
import jax.numpy as jnp
from jax import lax
from jax.sharding import PartitionSpec as P
from jax.experimental import pallas as pl
from jax.experimental.pallas import tpu as pltpu

BLOCK = 64


precise = lax.Precision.HIGHEST
epsilon = 1e-06
o_floor = 0.001


def rms_norm(vector, gain_vec, floor_add=epsilon):
    return (
        vector * lax.rsqrt(jnp.mean(vector * vector, axis=-1, keepdims=True) + floor_add) * gain_vec
    )


def unit_norm(vector):
    return vector * lax.rsqrt(jnp.sum(vector * vector, axis=-1, keepdims=True) + epsilon)


def swiglu(gate_pre, up_pre):
    return jax.nn.silu(gate_pre) * up_pre


def short_conv(signal, kernel, seg_ids):
    tap_count = kernel.shape[0]
    length = signal.shape[0]
    summed = signal * kernel[tap_count - 1]
    for offset in range(1, tap_count):
        shifted = jnp.concatenate(
            [jnp.zeros((offset, signal.shape[1]), signal.dtype), signal[: length - offset]], axis=0
        )
        seg_shift = jnp.concatenate(
            [jnp.full((offset,), -1, jnp.int32), seg_ids[: length - offset]]
        )
        keep_mask = (seg_shift == seg_ids).astype(signal.dtype)
        summed = summed + shifted * kernel[tap_count - 1 - offset] * keep_mask[:, None]
    return summed


def _recur_fwd_kernel(nb, u0_ref, w_ref, kt_ref, c_ref, s_out, u_out, s_scr):
    @pl.when(pl.program_id(1) == 0)
    def _():
        s_scr[...] = jnp.zeros_like(s_scr)

    def step(j, carry):
        state = s_scr[...]
        s_out[0, j] = state
        update = u0_ref[0, j] - lax.dot_general(
            w_ref[0, j], state, (((1,), (1,)), ((), ())),
            precision=precise, preferred_element_type=jnp.float32,
        )
        u_out[0, j] = update
        s_scr[...] = c_ref[0, j] * state + lax.dot_general(
            update, kt_ref[0, j], (((0,), (0,)), ((), ())),
            precision=precise, preferred_element_type=jnp.float32,
        )
        return carry

    lax.fori_loop(0, nb, step, 0)


def _recur_bwd_kernel(
    nb, s_ref, u_ref, w_ref, kt_ref, c_ref, ds_ref, du_ref,
    du0_out, dw_out, dkt_out, dc_out, g_scr,
):
    @pl.when(pl.program_id(1) == 0)
    def _():
        g_scr[...] = jnp.zeros_like(g_scr)

    def step(i, carry):
        j = nb - 1 - i
        grad_state = g_scr[...]
        state = s_ref[0, j]
        grad_update = du_ref[0, j] + lax.dot_general(
            kt_ref[0, j], grad_state, (((1,), (1,)), ((), ())),
            precision=precise, preferred_element_type=jnp.float32,
        )
        dkt_out[0, j] = jnp.dot(
            u_ref[0, j], grad_state, precision=precise, preferred_element_type=jnp.float32
        )
        dc_out[0, j] = jnp.sum(grad_state * state, axis=0, keepdims=True)
        du0_out[0, j] = grad_update
        dw_out[0, j] = -jnp.dot(
            grad_update, state, precision=precise, preferred_element_type=jnp.float32
        )
        g_scr[...] = (
            c_ref[0, j] * grad_state
            - lax.dot_general(
                grad_update, w_ref[0, j], (((0,), (0,)), ((), ())),
                precision=precise, preferred_element_type=jnp.float32,
            )
            + ds_ref[0, j]
        )
        return carry

    lax.fori_loop(0, nb, step, 0)


def _chunk_spec(nb, tail, reverse, count):
    if reverse:
        return pl.BlockSpec((1, nb) + tail, lambda h, b: (h, count - 1 - b, 0, 0))
    return pl.BlockSpec((1, nb) + tail, lambda h, b: (h, b, 0, 0))


def _recur_forward(u0, w, kt, c):
    heads, count, chunk, dv = u0.shape
    dk = w.shape[-1]
    nb = min(8, count)
    blocks = count // nb
    flops = 4 * heads * count * chunk * dk * dv * 6
    moved = 4 * heads * count * (2 * chunk * dv + 2 * chunk * dk + dv * dk)
    return pl.pallas_call(
        partial(_recur_fwd_kernel, nb),
        grid=(heads, blocks),
        in_specs=[
            _chunk_spec(nb, (chunk, dv), False, blocks),
            _chunk_spec(nb, (chunk, dk), False, blocks),
            _chunk_spec(nb, (chunk, dk), False, blocks),
            _chunk_spec(nb, (1, dk), False, blocks),
        ],
        out_specs=[
            _chunk_spec(nb, (dv, dk), False, blocks),
            _chunk_spec(nb, (chunk, dv), False, blocks),
        ],
        out_shape=[
            jax.ShapeDtypeStruct((heads, count, dv, dk), jnp.float32),
            jax.ShapeDtypeStruct((heads, count, chunk, dv), jnp.float32),
        ],
        scratch_shapes=[pltpu.VMEM((dv, dk), jnp.float32)],
        compiler_params=pltpu.CompilerParams(dimension_semantics=("arbitrary", "arbitrary")),
        cost_estimate=pl.CostEstimate(flops=flops, transcendentals=0, bytes_accessed=moved),
        name="delta_state_forward",
    )(u0, w, kt, c)


def _recur_backward(states, updates, w, kt, c, d_states, d_updates):
    heads, count, chunk, dv = updates.shape
    dk = w.shape[-1]
    nb = min(8, count)
    blocks = count // nb
    flops = 8 * heads * count * chunk * dk * dv * 6
    moved = 4 * heads * count * (4 * chunk * dv + 4 * chunk * dk + 2 * dv * dk)
    return pl.pallas_call(
        partial(_recur_bwd_kernel, nb),
        grid=(heads, blocks),
        in_specs=[
            _chunk_spec(nb, (dv, dk), True, blocks),
            _chunk_spec(nb, (chunk, dv), True, blocks),
            _chunk_spec(nb, (chunk, dk), True, blocks),
            _chunk_spec(nb, (chunk, dk), True, blocks),
            _chunk_spec(nb, (1, dk), True, blocks),
            _chunk_spec(nb, (dv, dk), True, blocks),
            _chunk_spec(nb, (chunk, dv), True, blocks),
        ],
        out_specs=[
            _chunk_spec(nb, (chunk, dv), True, blocks),
            _chunk_spec(nb, (chunk, dk), True, blocks),
            _chunk_spec(nb, (chunk, dk), True, blocks),
            _chunk_spec(nb, (1, dk), True, blocks),
        ],
        out_shape=[
            jax.ShapeDtypeStruct((heads, count, chunk, dv), jnp.float32),
            jax.ShapeDtypeStruct((heads, count, chunk, dk), jnp.float32),
            jax.ShapeDtypeStruct((heads, count, chunk, dk), jnp.float32),
            jax.ShapeDtypeStruct((heads, count, 1, dk), jnp.float32),
        ],
        scratch_shapes=[pltpu.VMEM((dv, dk), jnp.float32)],
        compiler_params=pltpu.CompilerParams(dimension_semantics=("arbitrary", "arbitrary")),
        cost_estimate=pl.CostEstimate(flops=flops, transcendentals=0, bytes_accessed=moved),
        name="delta_state_backward",
    )(states, updates, w, kt, c, d_states, d_updates)


@jax.custom_vjp
def state_recurrence(u0, w, kt, c):
    return _recur_forward(u0, w, kt, c)


def _recurrence_fwd(u0, w, kt, c):
    states, updates = _recur_forward(u0, w, kt, c)
    return (states, updates), (states, updates, w, kt, c)


def _recurrence_bwd(saved, grads):
    states, updates, w, kt, c = saved
    d_states, d_updates = grads
    du0, dw, dkt, dc_lanes = _recur_backward(states, updates, w, kt, c, d_states, d_updates)
    return du0, dw, dkt, dc_lanes


state_recurrence.defvjp(_recurrence_fwd, _recurrence_bwd)


def chunk_prepare(queries, keys_n, values, decays, beta_rate, seg_ids):
    length, dk = keys_n.shape
    count = length // BLOCK
    q = queries.reshape(count, BLOCK, dk)
    k = keys_n.reshape(count, BLOCK, dk)
    v = values.reshape(count, BLOCK, values.shape[1])
    beta = beta_rate.reshape(count, BLOCK)
    seg = seg_ids.reshape(count, BLOCK)
    cumulative = jnp.cumsum(decays.reshape(count, BLOCK), axis=1)
    places = jnp.arange(BLOCK)
    lower_tri = places[:, None] >= places[None, :]
    inside = jnp.logical_and(seg[:, :, None] == seg[:, None, :], lower_tri)
    log_gap = jnp.where(inside, cumulative[:, :, None] - cumulative[:, None, :], 0.0)
    within = jnp.exp(log_gap) * inside.astype(jnp.float32)
    strict = within * (places[:, None] > places[None, :]).astype(jnp.float32)
    last_seg = jnp.concatenate([jnp.full((1,), -1, seg.dtype), seg[:-1, BLOCK - 1]])
    carried = jnp.exp(cumulative) * (seg == last_seg[:, None]).astype(jnp.float32)
    key_gram = jnp.einsum("nid,njd->nij", k, k, precision=precise)
    system = jnp.eye(BLOCK, dtype=jnp.float32) + beta[:, :, None] * strict * key_gram
    right_side = jnp.concatenate([beta[:, :, None] * v, (beta * carried)[:, :, None] * k], axis=2)
    solved = lax.linalg.triangular_solve(
        system, right_side, left_side=True, lower=True, unit_diagonal=True
    )
    dv = v.shape[2]
    kt = within[:, BLOCK - 1, :, None] * k
    scores = jnp.einsum("nid,njd->nij", q, k, precision=precise) * within
    return solved[:, :, :dv], solved[:, :, dv:], kt, carried[:, BLOCK - 1], carried, scores


def chunk_finish(queries, carried, scores, states, updates):
    count = states.shape[0]
    q = queries.reshape(count, BLOCK, queries.shape[1])
    output = carried[:, :, None] * jnp.einsum(
        "nid,nvd->niv", q, states, precision=precise
    ) + jnp.einsum("nij,njv->niv", scores, updates, precision=precise)
    return output.reshape(count * BLOCK, states.shape[1])


def delta_rule(queries, keys_n, values, decays, beta_rate, seg_ids):
    u0, w, kt, tail, carried, scores = jax.vmap(chunk_prepare, in_axes=(0, 0, 0, 0, 0, None))(
        queries, keys_n, values, decays, beta_rate, seg_ids
    )
    c = jnp.broadcast_to(tail[:, :, None, None], tail.shape + (1, w.shape[-1]))
    states, updates = state_recurrence(u0, w, kt, c)
    return jax.vmap(chunk_finish)(queries, carried, scores, states, updates)


def head_inputs(proj_query, proj_key, proj_value, proj_alpha, proj_beta,
                kernel_query, kernel_key, kernel_value, a_here, dt_here, seg_ids):
    queries = unit_norm(jax.nn.silu(short_conv(proj_query, kernel_query, seg_ids))) * (
        1.0 / math.sqrt(proj_query.shape[1])
    )
    keys_n = unit_norm(jax.nn.silu(short_conv(proj_key, kernel_key, seg_ids)))
    values = jax.nn.silu(short_conv(proj_value, kernel_value, seg_ids))
    decays = -jnp.exp(a_here) * jax.nn.softplus(proj_alpha + dt_here)
    beta_rate = jax.nn.sigmoid(proj_beta)
    return queries, keys_n, values, decays, beta_rate


def head_output(recurrent, proj_gate, o_gain, live_mask):
    return rms_norm(recurrent, o_gain, o_floor) * jax.nn.silu(proj_gate) * live_mask[:, None]


def local_mixer(
    proj_query,
    proj_key,
    proj_value,
    proj_gate,
    proj_alpha,
    proj_beta,
    kernel_query,
    kernel_key,
    kernel_value,
    a_here,
    dt_here,
    o_gain,
    seg_ids=None,
    live_mask=None,
):
    row_count = proj_query.shape[0]
    heads_here = proj_alpha.shape[1]

    def by_head(array):
        return jnp.moveaxis(array.reshape(row_count, heads_here, -1), 1, 0)

    def kernel_heads(kernel):
        return jnp.moveaxis(kernel.reshape(kernel.shape[0], heads_here, -1), 1, 0)

    queries, keys_n, values, decays, beta_rate = jax.vmap(
        head_inputs, in_axes=(0,) * 10 + (None,)
    )(
        by_head(proj_query),
        by_head(proj_key),
        by_head(proj_value),
        proj_alpha.T,
        proj_beta.T,
        kernel_heads(kernel_query),
        kernel_heads(kernel_key),
        kernel_heads(kernel_value),
        a_here,
        dt_here,
        seg_ids,
    )
    recurrent = delta_rule(queries, keys_n, values, decays, beta_rate, seg_ids)
    mixed_heads = jax.vmap(head_output, in_axes=(0, 0, None, None))(
        recurrent, by_head(proj_gate), o_gain, live_mask
    )
    return jnp.moveaxis(mixed_heads, 0, 1).reshape(row_count, -1)


MESH_ID = pl.DeviceIdType.MESH


def _ring_position(h, major, minor):
    a = h // minor
    b = h % minor
    return b * major + a + (b % 2) * (major - 1 - 2 * a)


def _ring_member(q, major, minor):
    count = major * minor
    q = (q + count) % count
    b = q // major
    r = q % major
    return (r + (b % 2) * (major - 1 - 2 * r)) * minor + b


def _ring_sides(major, minor):
    p = _ring_position(lax.axis_index("head"), major, minor)
    return p, _ring_member(p + 1, major, minor), _ring_member(p - 1, major, minor)


def _greet(nxt, prv, row):
    barrier = pltpu.get_barrier_semaphore()
    pl.semaphore_signal(barrier, 1, device_id=(prv, row), device_id_type=MESH_ID)
    pl.semaphore_signal(barrier, 1, device_id=(nxt, row), device_id_type=MESH_ID)
    pl.semaphore_wait(barrier, 2)


def _ring_gather_kernel(major, minor, x_ref, out_ref, send_sem, recv_sem):
    count = major * minor
    blk = x_ref.shape[0]
    half = blk // 2
    row = lax.axis_index("row")
    p, nxt, prv = _ring_sides(major, minor)
    out_ref[pl.ds(pl.multiple_of(lax.axis_index("head") * blk, blk), blk), :] = x_ref[...]
    _greet(nxt, prv, row)

    def piece(pos, off):
        return out_ref.at[pl.ds(pl.multiple_of(_ring_member(pos, major, minor) * blk + off, half), half)]

    def outgoing(d, s):
        pos = p - s if d == 0 else p + s
        target = nxt if d == 0 else prv
        ref = piece(pos, d * half)
        return pltpu.make_async_remote_copy(
            ref, ref, send_sem.at[d, s], recv_sem.at[d, s], device_id=(target, row),
            device_id_type=MESH_ID,
        )

    def incoming(d, s):
        pos = p - 1 - s if d == 0 else p + 1 + s
        source = prv if d == 0 else nxt
        ref = piece(pos, d * half)
        return pltpu.make_async_remote_copy(
            ref, ref, send_sem.at[d, s], recv_sem.at[d, s], device_id=(source, row),
            device_id_type=MESH_ID,
        )

    for s in range(count - 1):
        for d in (0, 1):
            if s > 0:
                incoming(d, s - 1).wait_recv()
            outgoing(d, s).start()
    for d in (0, 1):
        incoming(d, count - 2).wait_recv()
    for s in range(count - 1):
        for d in (0, 1):
            outgoing(d, s).wait_send()


def _ring_scatter_kernel(major, minor, y_ref, out_ref, buf, send_sem, recv_sem):
    count = major * minor
    blk = out_ref.shape[0]
    half = blk // 2
    row = lax.axis_index("row")
    p, nxt, prv = _ring_sides(major, minor)
    _greet(nxt, prv, row)

    def piece(pos, off):
        return y_ref.at[pl.ds(pl.multiple_of(_ring_member(pos, major, minor) * blk + off, half), half)]

    def outgoing(d, s):
        pos = p - s - 1 if d == 0 else p + s + 1
        target = nxt if d == 0 else prv
        source = piece(pos, d * half) if s == 0 else buf.at[d, s - 1]
        return pltpu.make_async_remote_copy(
            source, buf.at[d, s], send_sem.at[d, s], recv_sem.at[d, s],
            device_id=(target, row), device_id_type=MESH_ID,
        )

    def incoming(d, s):
        source = prv if d == 0 else nxt
        return pltpu.make_async_remote_copy(
            buf.at[d, s], buf.at[d, s], send_sem.at[d, s], recv_sem.at[d, s],
            device_id=(source, row), device_id_type=MESH_ID,
        )

    for s in range(count - 1):
        for d in (0, 1):
            if s > 0:
                incoming(d, s - 1).wait_recv()
                pos = p - s - 1 if d == 0 else p + s + 1
                buf[d, s - 1] = (
                    buf[d, s - 1].astype(jnp.float32)
                    + piece(pos, d * half)[...].astype(jnp.float32)
                ).astype(buf.dtype)
            outgoing(d, s).start()
    for d in (0, 1):
        incoming(d, count - 2).wait_recv()
        out_ref[pl.ds(d * half, half), :] = piece(p, d * half)[...].astype(
            jnp.float32
        ) + buf[d, count - 2].astype(jnp.float32)
    for s in range(count - 1):
        for d in (0, 1):
            outgoing(d, s).wait_send()


def ring_gather(x, ring, collective):
    major, minor = ring
    count = major * minor
    blk, width = x.shape
    return pl.pallas_call(
        partial(_ring_gather_kernel, major, minor),
        out_shape=jax.ShapeDtypeStruct((count * blk, width), x.dtype),
        in_specs=[pl.BlockSpec(memory_space=pltpu.VMEM)],
        out_specs=pl.BlockSpec(memory_space=pltpu.VMEM),
        scratch_shapes=[
            pltpu.SemaphoreType.DMA((2, count - 1)),
            pltpu.SemaphoreType.DMA((2, count - 1)),
        ],
        compiler_params=pltpu.CompilerParams(collective_id=collective, has_side_effects=True),
        name="ring_gather_head",
    )(x)


def ring_scatter(y, ring, collective):
    major, minor = ring
    count = major * minor
    rows, width = y.shape
    blk = rows // count
    return pl.pallas_call(
        partial(_ring_scatter_kernel, major, minor),
        out_shape=jax.ShapeDtypeStruct((blk, width), jnp.float32),
        in_specs=[pl.BlockSpec(memory_space=pltpu.VMEM)],
        out_specs=pl.BlockSpec(memory_space=pltpu.VMEM),
        scratch_shapes=[
            pltpu.VMEM((2, count - 1, blk // 2, width), y.dtype),
            pltpu.SemaphoreType.DMA((2, count - 1)),
            pltpu.SemaphoreType.DMA((2, count - 1)),
        ],
        compiler_params=pltpu.CompilerParams(collective_id=collective, has_side_effects=True),
        name="ring_scatter_head",
    )(y)


def head_ring(mesh):
    count = mesh.shape["head"]
    try:
        spots = [tuple(device.coords) for device in mesh.devices[:, 0]]
    except (AttributeError, TypeError):
        return (count, 1)
    moving = [axis for axis in range(len(spots[0])) if spots[0][axis] != spots[1][axis]]
    if len(moving) != 1:
        return (count, 1)
    minor = len({spot[moving[0]] for spot in spots})
    if count % minor or minor % 2:
        return (count, 1)
    return (count // minor, minor)


def contract_rows(left, right):
    return lax.dot_general(
        left, right, (((0,), (0,)), ((), ())), preferred_element_type=jnp.float32
    )


def contract_cols(left, right):
    return lax.dot_general(
        left, right, (((1,), (1,)), ((), ())), preferred_element_type=jnp.float32
    )


def on_device(
    ring,
    tokens,
    w_query,
    w_key,
    w_value,
    w_outgate,
    w_alpha,
    w_beta,
    conv_query,
    conv_key,
    conv_value,
    a_log,
    dt_bias,
    o_gain,
    w_out,
    gain_in,
    gain_ffn,
    w_gate,
    w_up,
    w_down,
    segments,
    valid_len,
    cotangent,
):
    residual = tokens[0].astype(jnp.float32)
    heads_here = w_alpha.shape[1]
    head_first = lax.axis_index("head") * heads_here
    norm_one, pull_one = jax.vjp(rms_norm, residual, gain_in)
    normed_one = norm_one.astype(jnp.bfloat16)
    row_count = lax.psum(1, "row")
    w_local = jnp.concatenate(
        [w_query, w_key, w_value, w_outgate, w_alpha, w_beta], axis=1
    ).astype(jnp.bfloat16)
    edges = [0]
    for member in (w_query, w_key, w_value, w_outgate, w_alpha, w_beta):
        edges.append(edges[-1] + member.shape[1])
    w_inward = lax.all_gather(w_local, "row", axis=0, tiled=True)
    conv_local = jnp.concatenate([conv_query, conv_key, conv_value], axis=1).astype(jnp.bfloat16)
    conv_edges = [0, conv_query.shape[1], conv_query.shape[1] + conv_key.shape[1], conv_local.shape[1]]
    conv_all = lax.all_gather(conv_local, "row", axis=1, tiled=True).reshape(
        conv_local.shape[0], row_count, conv_local.shape[1]
    )
    conv_parts = [
        conv_all[:, :, conv_edges[i] : conv_edges[i + 1]].reshape(conv_local.shape[0], -1)
        for i in range(3)
    ]
    out_matrix = lax.all_gather(w_out.astype(jnp.bfloat16), "row", axis=1, tiled=True)
    ff_width = w_gate.shape[1]
    ffn_local = jnp.concatenate([w_gate, w_up, w_down.T], axis=1).astype(jnp.bfloat16)
    grad_out = cotangent[0]
    grad_out_rows = lax.all_gather(grad_out, "row", axis=0, tiled=True)
    all_rows = ring_gather(normed_one, ring, 0)
    all_rows, out_matrix, ffn_local = lax.optimization_barrier((all_rows, out_matrix, ffn_local))
    ffn_all = lax.all_gather(ffn_local, "head", axis=0, tiled=True)
    projected = jnp.dot(all_rows, w_inward, preferred_element_type=jnp.float32)
    proj_parts = [projected[:, edges[spot] : edges[spot + 1]] for spot in range(6)]
    seg_ids = segments[0]
    live_mask = (jnp.arange(seg_ids.shape[0]) < valid_len[0]).astype(jnp.float32)
    a_here = lax.dynamic_slice_in_dim(a_log, head_first, heads_here)
    dt_here = lax.dynamic_slice_in_dim(dt_bias, head_first, heads_here)
    mixer_fn = partial(local_mixer, seg_ids=seg_ids, live_mask=live_mask)
    mixed, pull_core = jax.vjp(
        mixer_fn,
        proj_parts[0],
        proj_parts[1],
        proj_parts[2],
        proj_parts[3],
        proj_parts[4],
        proj_parts[5],
        conv_parts[0].astype(jnp.float32),
        conv_parts[1].astype(jnp.float32),
        conv_parts[2].astype(jnp.float32),
        a_here,
        dt_here,
        o_gain,
    )
    mixed, ffn_all, grad_out_rows = lax.optimization_barrier((mixed, ffn_all, grad_out_rows))
    w_gate_all = ffn_all[:, :ff_width]
    w_up_all = ffn_all[:, ff_width : 2 * ff_width]
    w_down_t = ffn_all[:, 2 * ff_width :]
    mixed_half = mixed.astype(jnp.bfloat16)
    mixer_output = ring_scatter(
        jnp.dot(mixed_half, out_matrix, preferred_element_type=jnp.float32).astype(jnp.bfloat16),
        ring,
        1,
    )
    middle = residual + mixer_output
    norm_two, pull_two = jax.vjp(rms_norm, middle, gain_ffn)
    normed_two = norm_two.astype(jnp.bfloat16)
    ffn_inputs = lax.all_gather(normed_two, "row", axis=0, tiled=True)
    gate_pre = jnp.dot(ffn_inputs, w_gate_all, preferred_element_type=jnp.float32)
    up_pre = jnp.dot(ffn_inputs, w_up_all, preferred_element_type=jnp.float32)
    hidden_val, pull_act = jax.vjp(swiglu, gate_pre, up_pre)
    hidden_half = hidden_val.astype(jnp.bfloat16)
    ffn_partial = contract_cols(hidden_half, w_down_t).astype(jnp.bfloat16)
    grad_hidden = jnp.dot(grad_out_rows, w_down_t, preferred_element_type=jnp.float32)
    grad_down_t = contract_rows(grad_out_rows, hidden_half)
    grad_gate_f, grad_up_f = pull_act(grad_hidden)
    grad_gate = grad_gate_f.astype(jnp.bfloat16)
    grad_upper = grad_up_f.astype(jnp.bfloat16)
    grad_wgate = contract_rows(ffn_inputs, grad_gate)
    grad_wup = contract_rows(ffn_inputs, grad_upper)
    grad_norm_two = lax.psum_scatter(
        (contract_cols(grad_gate, w_gate_all) + contract_cols(grad_upper, w_up_all)).astype(
            jnp.bfloat16
        ),
        "row",
        scatter_dimension=0,
        tiled=True,
    ).astype(jnp.float32)
    grad_mid_part, grad_gain_ffn = pull_two(grad_norm_two)
    grad_middle = grad_out.astype(jnp.float32) + grad_mid_part
    ffn_grad_cat = jnp.concatenate([grad_wgate, grad_wup, grad_down_t], axis=1).astype(
        jnp.bfloat16
    )
    grad_mid_half = grad_middle.astype(jnp.bfloat16)
    grad_mid_rows = ring_gather(grad_mid_half, ring, 2)
    ffn_output = lax.psum_scatter(ffn_partial, "row", scatter_dimension=0, tiled=True)
    grad_mid_rows, ffn_grad_cat = lax.optimization_barrier((grad_mid_rows, ffn_grad_cat))
    ffn_grad_all = lax.psum_scatter(ffn_grad_cat, "head", scatter_dimension=0, tiled=True)
    grad_mixed = contract_cols(grad_mid_rows, out_matrix)
    grad_wout = contract_rows(mixed_half, grad_mid_rows).astype(jnp.bfloat16)
    wout_grad = lax.psum_scatter(grad_wout, "row", scatter_dimension=1, tiled=True)
    core_grads = pull_core(grad_mixed)
    core_grads, ffn_output, ffn_grad_all = lax.optimization_barrier(
        (core_grads, ffn_output, ffn_grad_all)
    )
    final_out = (middle + ffn_output.astype(jnp.float32)).astype(jnp.bfloat16)
    ffn_grad_all = ffn_grad_all.astype(jnp.float32)
    ffn_grads = (
        ffn_grad_all[:, :ff_width],
        ffn_grad_all[:, ff_width : 2 * ff_width],
        ffn_grad_all[:, 2 * ff_width :].T,
    )
    grad_proj = jnp.concatenate(
        [core_grads[0], core_grads[1], core_grads[2], core_grads[3], core_grads[4], core_grads[5]],
        axis=1,
    ).astype(jnp.bfloat16)
    grad_inward = contract_rows(all_rows, grad_proj).astype(jnp.bfloat16)
    norm_one_partial = contract_cols(grad_proj, w_inward).astype(jnp.bfloat16)
    grad_gain_in = jnp.sum(
        norm_one_partial.astype(jnp.float32) * all_rows.astype(jnp.float32), axis=0
    ) / gain_in
    grad_norm_one = ring_scatter(norm_one_partial, ring, 3)
    grad_norm_one, wout_grad = lax.optimization_barrier((grad_norm_one, wout_grad))
    grad_in_part = pull_one(grad_norm_one)[0]
    grad_input = grad_middle + grad_in_part
    inward_all = lax.psum_scatter(
        grad_inward, "row", scatter_dimension=0, tiled=True
    ).astype(jnp.float32)
    conv_grad_local = jnp.concatenate(
        [
            core_grads[6 + i].reshape(conv_local.shape[0], row_count, -1)
            for i in range(3)
        ],
        axis=2,
    ).reshape(conv_local.shape[0], -1)
    conv_grad = lax.psum_scatter(
        conv_grad_local.astype(jnp.bfloat16), "row", scatter_dimension=1, tiled=True
    ).astype(jnp.float32)
    mixer_grads = tuple(inward_all[:, edges[spot] : edges[spot + 1]] for spot in range(6)) + tuple(
        conv_grad[:, conv_edges[i] : conv_edges[i + 1]] for i in range(3)
    ) + (wout_grad.astype(jnp.float32),)
    head_total = a_log.shape[0]
    grad_a_full = lax.dynamic_update_slice_in_dim(
        jnp.zeros((head_total,), jnp.float32), core_grads[9], head_first, 0
    )
    grad_dt_full = lax.dynamic_update_slice_in_dim(
        jnp.zeros((head_total,), jnp.float32), core_grads[10], head_first, 0
    )
    small_parts = (grad_gain_in, grad_gain_ffn, core_grads[11], grad_a_full, grad_dt_full)
    small_all = lax.psum(lax.psum(jnp.concatenate(small_parts), "row"), "head")
    small_edges = [0]
    for part in small_parts:
        small_edges.append(small_edges[-1] + part.shape[0])
    small_sums = [small_all[small_edges[i] : small_edges[i + 1]] for i in range(5)]
    return (
        final_out[None],
        grad_input[None],
        mixer_grads[0],
        mixer_grads[1],
        mixer_grads[2],
        mixer_grads[3],
        mixer_grads[4],
        mixer_grads[5],
        mixer_grads[6],
        mixer_grads[7],
        mixer_grads[8],
        small_sums[3],
        small_sums[4],
        small_sums[2],
        mixer_grads[9],
        small_sums[0],
        small_sums[1],
        ffn_grads[0],
        ffn_grads[1],
        ffn_grads[2],
    )


def solution(mesh):
    return jax.shard_map(
        partial(on_device, head_ring(mesh)),
        mesh=mesh,
        in_specs=(
            P("row", "head", None),
            P("row", "head"),
            P("row", "head"),
            P("row", "head"),
            P("row", "head"),
            P("row", "head"),
            P("row", "head"),
            P(None, ("head", "row")),
            P(None, ("head", "row")),
            P(None, ("head", "row")),
            P(),
            P(),
            P(),
            P("head", "row"),
            P(),
            P(),
            P("head", "row"),
            P("head", "row"),
            P("row", "head"),
            P("row", None),
            P("row"),
            P("row", "head", None),
        ),
        out_specs=(
            P("row", "head", None),
            P("row", "head", None),
            P("row", "head"),
            P("row", "head"),
            P("row", "head"),
            P("row", "head"),
            P("row", "head"),
            P("row", "head"),
            P(None, ("head", "row")),
            P(None, ("head", "row")),
            P(None, ("head", "row")),
            P(),
            P(),
            P(),
            P("head", "row"),
            P(),
            P(),
            P("head", "row"),
            P("head", "row"),
            P("row", "head"),
        ),
        check_vma=False,
    )
```

```python
from functools import partial
import math

import jax
import jax.numpy as jnp
from jax import lax
from jax.sharding import PartitionSpec as P
from jax.experimental import pallas as pl
from jax.experimental.pallas import tpu as pltpu

BLOCK = 64


precise = lax.Precision.HIGHEST
epsilon = 1e-06
o_floor = 0.001


def rms_norm(vector, gain_vec, floor_add=epsilon):
    return (
        vector * lax.rsqrt(jnp.mean(vector * vector, axis=-1, keepdims=True) + floor_add) * gain_vec
    )


def unit_norm(vector):
    return vector * lax.rsqrt(jnp.sum(vector * vector, axis=-1, keepdims=True) + epsilon)


def swiglu(gate_pre, up_pre):
    return jax.nn.silu(gate_pre) * up_pre


def short_conv(signal, kernel, seg_ids):
    tap_count = kernel.shape[0]
    length = signal.shape[0]
    summed = signal * kernel[tap_count - 1]
    for offset in range(1, tap_count):
        shifted = jnp.concatenate(
            [jnp.zeros((offset, signal.shape[1]), signal.dtype), signal[: length - offset]], axis=0
        )
        seg_shift = jnp.concatenate(
            [jnp.full((offset,), -1, jnp.int32), seg_ids[: length - offset]]
        )
        keep_mask = (seg_shift == seg_ids).astype(signal.dtype)
        summed = summed + shifted * kernel[tap_count - 1 - offset] * keep_mask[:, None]
    return summed


def _recur_fwd_kernel(nb, u0_ref, w_ref, kt_ref, c_ref, s_out, u_out, s_scr):
    @pl.when(pl.program_id(1) == 0)
    def _():
        s_scr[...] = jnp.zeros_like(s_scr)

    def step(j, carry):
        state = s_scr[...]
        s_out[0, j] = state
        update = u0_ref[0, j] - lax.dot_general(
            w_ref[0, j], state, (((1,), (1,)), ((), ())),
            precision=precise, preferred_element_type=jnp.float32,
        )
        u_out[0, j] = update
        s_scr[...] = c_ref[0, j] * state + lax.dot_general(
            update, kt_ref[0, j], (((0,), (0,)), ((), ())),
            precision=precise, preferred_element_type=jnp.float32,
        )
        return carry

    lax.fori_loop(0, nb, step, 0)


def _recur_bwd_kernel(
    nb, s_ref, u_ref, w_ref, kt_ref, c_ref, ds_ref, du_ref,
    du0_out, dw_out, dkt_out, dc_out, g_scr,
):
    @pl.when(pl.program_id(1) == 0)
    def _():
        g_scr[...] = jnp.zeros_like(g_scr)

    def step(i, carry):
        j = nb - 1 - i
        grad_state = g_scr[...]
        state = s_ref[0, j]
        grad_update = du_ref[0, j] + lax.dot_general(
            kt_ref[0, j], grad_state, (((1,), (1,)), ((), ())),
            precision=precise, preferred_element_type=jnp.float32,
        )
        dkt_out[0, j] = jnp.dot(
            u_ref[0, j], grad_state, precision=precise, preferred_element_type=jnp.float32
        )
        dc_out[0, j] = jnp.sum(grad_state * state, axis=0, keepdims=True)
        du0_out[0, j] = grad_update
        dw_out[0, j] = -jnp.dot(
            grad_update, state, precision=precise, preferred_element_type=jnp.float32
        )
        g_scr[...] = (
            c_ref[0, j] * grad_state
            - lax.dot_general(
                grad_update, w_ref[0, j], (((0,), (0,)), ((), ())),
                precision=precise, preferred_element_type=jnp.float32,
            )
            + ds_ref[0, j]
        )
        return carry

    lax.fori_loop(0, nb, step, 0)


def _chunk_spec(nb, tail, reverse, count):
    if reverse:
        return pl.BlockSpec((1, nb) + tail, lambda h, b: (h, count - 1 - b, 0, 0))
    return pl.BlockSpec((1, nb) + tail, lambda h, b: (h, b, 0, 0))


def _recur_forward(u0, w, kt, c):
    heads, count, chunk, dv = u0.shape
    dk = w.shape[-1]
    nb = min(8, count)
    blocks = count // nb
    flops = 4 * heads * count * chunk * dk * dv * 6
    moved = 4 * heads * count * (2 * chunk * dv + 2 * chunk * dk + dv * dk)
    return pl.pallas_call(
        partial(_recur_fwd_kernel, nb),
        grid=(heads, blocks),
        in_specs=[
            _chunk_spec(nb, (chunk, dv), False, blocks),
            _chunk_spec(nb, (chunk, dk), False, blocks),
            _chunk_spec(nb, (chunk, dk), False, blocks),
            _chunk_spec(nb, (1, dk), False, blocks),
        ],
        out_specs=[
            _chunk_spec(nb, (dv, dk), False, blocks),
            _chunk_spec(nb, (chunk, dv), False, blocks),
        ],
        out_shape=[
            jax.ShapeDtypeStruct((heads, count, dv, dk), jnp.float32),
            jax.ShapeDtypeStruct((heads, count, chunk, dv), jnp.float32),
        ],
        scratch_shapes=[pltpu.VMEM((dv, dk), jnp.float32)],
        compiler_params=pltpu.CompilerParams(dimension_semantics=("arbitrary", "arbitrary")),
        cost_estimate=pl.CostEstimate(flops=flops, transcendentals=0, bytes_accessed=moved),
        name="delta_state_forward",
    )(u0, w, kt, c)


def _recur_backward(states, updates, w, kt, c, d_states, d_updates):
    heads, count, chunk, dv = updates.shape
    dk = w.shape[-1]
    nb = min(8, count)
    blocks = count // nb
    flops = 8 * heads * count * chunk * dk * dv * 6
    moved = 4 * heads * count * (4 * chunk * dv + 4 * chunk * dk + 2 * dv * dk)
    return pl.pallas_call(
        partial(_recur_bwd_kernel, nb),
        grid=(heads, blocks),
        in_specs=[
            _chunk_spec(nb, (dv, dk), True, blocks),
            _chunk_spec(nb, (chunk, dv), True, blocks),
            _chunk_spec(nb, (chunk, dk), True, blocks),
            _chunk_spec(nb, (chunk, dk), True, blocks),
            _chunk_spec(nb, (1, dk), True, blocks),
            _chunk_spec(nb, (dv, dk), True, blocks),
            _chunk_spec(nb, (chunk, dv), True, blocks),
        ],
        out_specs=[
            _chunk_spec(nb, (chunk, dv), True, blocks),
            _chunk_spec(nb, (chunk, dk), True, blocks),
            _chunk_spec(nb, (chunk, dk), True, blocks),
            _chunk_spec(nb, (1, dk), True, blocks),
        ],
        out_shape=[
            jax.ShapeDtypeStruct((heads, count, chunk, dv), jnp.float32),
            jax.ShapeDtypeStruct((heads, count, chunk, dk), jnp.float32),
            jax.ShapeDtypeStruct((heads, count, chunk, dk), jnp.float32),
            jax.ShapeDtypeStruct((heads, count, 1, dk), jnp.float32),
        ],
        scratch_shapes=[pltpu.VMEM((dv, dk), jnp.float32)],
        compiler_params=pltpu.CompilerParams(dimension_semantics=("arbitrary", "arbitrary")),
        cost_estimate=pl.CostEstimate(flops=flops, transcendentals=0, bytes_accessed=moved),
        name="delta_state_backward",
    )(states, updates, w, kt, c, d_states, d_updates)


@jax.custom_vjp
def state_recurrence(u0, w, kt, c):
    return _recur_forward(u0, w, kt, c)


def _recurrence_fwd(u0, w, kt, c):
    states, updates = _recur_forward(u0, w, kt, c)
    return (states, updates), (states, updates, w, kt, c)


def _recurrence_bwd(saved, grads):
    states, updates, w, kt, c = saved
    d_states, d_updates = grads
    du0, dw, dkt, dc_lanes = _recur_backward(states, updates, w, kt, c, d_states, d_updates)
    return du0, dw, dkt, dc_lanes


state_recurrence.defvjp(_recurrence_fwd, _recurrence_bwd)


def _unit_lower_inverse_small(system):
    size = system.shape[-1]
    strict = system - jnp.eye(size, dtype=system.dtype)
    power = -strict
    inverse = jnp.eye(size, dtype=system.dtype) + power
    done = 2
    while done < size:
        power = jnp.matmul(power, power, precision=precise)
        inverse = inverse + jnp.matmul(power, inverse, precision=precise)
        done *= 2
    return inverse


def _unit_lower_inverse_forward(system):
    size = system.shape[-1]
    base = min(8, size)
    lead = system.shape[:-2]
    count = size // base
    blocks = system.reshape(lead + (count, base, count, base))
    diag = jnp.stack([blocks[..., i, :, i, :] for i in range(count)], axis=-3)
    inverse = _unit_lower_inverse_small(diag)
    width = base
    while width < size:
        pairs = inverse.shape[-3] // 2
        upper = inverse[..., 0::2, :, :]
        lower = inverse[..., 1::2, :, :]
        below = jnp.stack(
            [
                system[..., (2 * i + 1) * width : (2 * i + 2) * width, 2 * i * width : (2 * i + 1) * width]
                for i in range(pairs)
            ],
            axis=-3,
        )
        corner = -jnp.matmul(
            lower, jnp.matmul(below, upper, precision=precise), precision=precise
        )
        zeros = jnp.zeros_like(upper)
        top = jnp.concatenate([upper, zeros], axis=-1)
        bottom = jnp.concatenate([corner, lower], axis=-1)
        inverse = jnp.concatenate([top, bottom], axis=-2)
        width *= 2
    return inverse[..., 0, :, :]


@jax.custom_vjp
def unit_lower_inverse(system):
    return _unit_lower_inverse_forward(system)


def _inverse_fwd(system):
    inverse = _unit_lower_inverse_forward(system)
    return inverse, inverse


def _inverse_bwd(inverse, grad):
    size = inverse.shape[-1]
    flipped = jnp.swapaxes(inverse, -1, -2)
    full = -jnp.matmul(jnp.matmul(flipped, grad, precision=precise), flipped, precision=precise)
    places = jnp.arange(size)
    return (full * (places[:, None] > places[None, :]).astype(full.dtype),)


unit_lower_inverse.defvjp(_inverse_fwd, _inverse_bwd)


def chunk_prepare(queries, keys_n, values, decays, beta_rate, seg_ids):
    length, dk = keys_n.shape
    count = length // BLOCK
    q = queries.reshape(count, BLOCK, dk)
    k = keys_n.reshape(count, BLOCK, dk)
    v = values.reshape(count, BLOCK, values.shape[1])
    beta = beta_rate.reshape(count, BLOCK)
    seg = seg_ids.reshape(count, BLOCK)
    cumulative = jnp.cumsum(decays.reshape(count, BLOCK), axis=1)
    places = jnp.arange(BLOCK)
    lower_tri = places[:, None] >= places[None, :]
    inside = jnp.logical_and(seg[:, :, None] == seg[:, None, :], lower_tri)
    log_gap = jnp.where(inside, cumulative[:, :, None] - cumulative[:, None, :], 0.0)
    within = jnp.exp(log_gap) * inside.astype(jnp.float32)
    strict = within * (places[:, None] > places[None, :]).astype(jnp.float32)
    last_seg = jnp.concatenate([jnp.full((1,), -1, seg.dtype), seg[:-1, BLOCK - 1]])
    carried = jnp.exp(cumulative) * (seg == last_seg[:, None]).astype(jnp.float32)
    key_gram = jnp.einsum("nid,njd->nij", k, k, precision=precise)
    system = jnp.eye(BLOCK, dtype=jnp.float32) + beta[:, :, None] * strict * key_gram
    right_side = jnp.concatenate([beta[:, :, None] * v, (beta * carried)[:, :, None] * k], axis=2)
    solved = jnp.matmul(unit_lower_inverse(system), right_side, precision=precise)
    dv = v.shape[2]
    kt = within[:, BLOCK - 1, :, None] * k
    scores = jnp.einsum("nid,njd->nij", q, k, precision=precise) * within
    return solved[:, :, :dv], solved[:, :, dv:], kt, carried[:, BLOCK - 1], carried, scores


def chunk_finish(queries, carried, scores, states, updates):
    count = states.shape[0]
    q = queries.reshape(count, BLOCK, queries.shape[1])
    output = carried[:, :, None] * jnp.einsum(
        "nid,nvd->niv", q, states, precision=precise
    ) + jnp.einsum("nij,njv->niv", scores, updates, precision=precise)
    return output.reshape(count * BLOCK, states.shape[1])


def delta_rule(queries, keys_n, values, decays, beta_rate, seg_ids):
    u0, w, kt, tail, carried, scores = jax.vmap(chunk_prepare, in_axes=(0, 0, 0, 0, 0, None))(
        queries, keys_n, values, decays, beta_rate, seg_ids
    )
    c = jnp.broadcast_to(tail[:, :, None, None], tail.shape + (1, w.shape[-1]))
    states, updates = state_recurrence(u0, w, kt, c)
    return jax.vmap(chunk_finish)(queries, carried, scores, states, updates)


def head_inputs(proj_query, proj_key, proj_value, proj_alpha, proj_beta,
                kernel_query, kernel_key, kernel_value, a_here, dt_here, seg_ids):
    queries = unit_norm(jax.nn.silu(short_conv(proj_query, kernel_query, seg_ids))) * (
        1.0 / math.sqrt(proj_query.shape[1])
    )
    keys_n = unit_norm(jax.nn.silu(short_conv(proj_key, kernel_key, seg_ids)))
    values = jax.nn.silu(short_conv(proj_value, kernel_value, seg_ids))
    decays = -jnp.exp(a_here) * jax.nn.softplus(proj_alpha + dt_here)
    beta_rate = jax.nn.sigmoid(proj_beta)
    return queries, keys_n, values, decays, beta_rate


def head_output(recurrent, proj_gate, o_gain, live_mask):
    return rms_norm(recurrent, o_gain, o_floor) * jax.nn.silu(proj_gate) * live_mask[:, None]


def local_mixer(
    proj_query,
    proj_key,
    proj_value,
    proj_gate,
    proj_alpha,
    proj_beta,
    kernel_query,
    kernel_key,
    kernel_value,
    a_here,
    dt_here,
    o_gain,
    seg_ids=None,
    live_mask=None,
):
    row_count = proj_query.shape[0]
    heads_here = proj_alpha.shape[1]

    def by_head(array):
        return jnp.moveaxis(array.reshape(row_count, heads_here, -1), 1, 0)

    def kernel_heads(kernel):
        return jnp.moveaxis(kernel.reshape(kernel.shape[0], heads_here, -1), 1, 0)

    queries, keys_n, values, decays, beta_rate = jax.vmap(
        head_inputs, in_axes=(0,) * 10 + (None,)
    )(
        by_head(proj_query),
        by_head(proj_key),
        by_head(proj_value),
        proj_alpha.T,
        proj_beta.T,
        kernel_heads(kernel_query),
        kernel_heads(kernel_key),
        kernel_heads(kernel_value),
        a_here,
        dt_here,
        seg_ids,
    )
    recurrent = delta_rule(queries, keys_n, values, decays, beta_rate, seg_ids)
    mixed_heads = jax.vmap(head_output, in_axes=(0, 0, None, None))(
        recurrent, by_head(proj_gate), o_gain, live_mask
    )
    return jnp.moveaxis(mixed_heads, 0, 1).reshape(row_count, -1)


MESH_ID = pl.DeviceIdType.MESH


def _ring_position(h, major, minor):
    a = h // minor
    b = h % minor
    return b * major + a + (b % 2) * (major - 1 - 2 * a)


def _ring_member(q, major, minor):
    count = major * minor
    q = (q + count) % count
    b = q // major
    r = q % major
    return (r + (b % 2) * (major - 1 - 2 * r)) * minor + b


def _ring_sides(major, minor):
    p = _ring_position(lax.axis_index("head"), major, minor)
    return p, _ring_member(p + 1, major, minor), _ring_member(p - 1, major, minor)


def _greet(nxt, prv, row):
    barrier = pltpu.get_barrier_semaphore()
    pl.semaphore_signal(barrier, 1, device_id=(prv, row), device_id_type=MESH_ID)
    pl.semaphore_signal(barrier, 1, device_id=(nxt, row), device_id_type=MESH_ID)
    pl.semaphore_wait(barrier, 2)


def _ring_gather_kernel(major, minor, x_ref, out_ref, send_sem, recv_sem):
    count = major * minor
    blk = x_ref.shape[0]
    half = blk // 2
    row = lax.axis_index("row")
    p, nxt, prv = _ring_sides(major, minor)
    out_ref[pl.ds(pl.multiple_of(lax.axis_index("head") * blk, blk), blk), :] = x_ref[...]
    _greet(nxt, prv, row)

    def piece(pos, off):
        return out_ref.at[pl.ds(pl.multiple_of(_ring_member(pos, major, minor) * blk + off, half), half)]

    def outgoing(d, s):
        pos = p - s if d == 0 else p + s
        target = nxt if d == 0 else prv
        ref = piece(pos, d * half)
        return pltpu.make_async_remote_copy(
            ref, ref, send_sem.at[d, s], recv_sem.at[d, s], device_id=(target, row),
            device_id_type=MESH_ID,
        )

    def incoming(d, s):
        pos = p - 1 - s if d == 0 else p + 1 + s
        source = prv if d == 0 else nxt
        ref = piece(pos, d * half)
        return pltpu.make_async_remote_copy(
            ref, ref, send_sem.at[d, s], recv_sem.at[d, s], device_id=(source, row),
            device_id_type=MESH_ID,
        )

    for s in range(count - 1):
        for d in (0, 1):
            if s > 0:
                incoming(d, s - 1).wait_recv()
            outgoing(d, s).start()
    for d in (0, 1):
        incoming(d, count - 2).wait_recv()
    for s in range(count - 1):
        for d in (0, 1):
            outgoing(d, s).wait_send()


def _ring_scatter_kernel(major, minor, y_ref, out_ref, buf, send_sem, recv_sem):
    count = major * minor
    blk = out_ref.shape[0]
    half = blk // 2
    row = lax.axis_index("row")
    p, nxt, prv = _ring_sides(major, minor)
    _greet(nxt, prv, row)

    def piece(pos, off):
        return y_ref.at[pl.ds(pl.multiple_of(_ring_member(pos, major, minor) * blk + off, half), half)]

    def outgoing(d, s):
        pos = p - s - 1 if d == 0 else p + s + 1
        target = nxt if d == 0 else prv
        source = piece(pos, d * half) if s == 0 else buf.at[d, s - 1]
        return pltpu.make_async_remote_copy(
            source, buf.at[d, s], send_sem.at[d, s], recv_sem.at[d, s],
            device_id=(target, row), device_id_type=MESH_ID,
        )

    def incoming(d, s):
        source = prv if d == 0 else nxt
        return pltpu.make_async_remote_copy(
            buf.at[d, s], buf.at[d, s], send_sem.at[d, s], recv_sem.at[d, s],
            device_id=(source, row), device_id_type=MESH_ID,
        )

    for s in range(count - 1):
        for d in (0, 1):
            if s > 0:
                incoming(d, s - 1).wait_recv()
                pos = p - s - 1 if d == 0 else p + s + 1
                buf[d, s - 1] = (
                    buf[d, s - 1].astype(jnp.float32)
                    + piece(pos, d * half)[...].astype(jnp.float32)
                ).astype(buf.dtype)
            outgoing(d, s).start()
    for d in (0, 1):
        incoming(d, count - 2).wait_recv()
        out_ref[pl.ds(d * half, half), :] = piece(p, d * half)[...].astype(
            jnp.float32
        ) + buf[d, count - 2].astype(jnp.float32)
    for s in range(count - 1):
        for d in (0, 1):
            outgoing(d, s).wait_send()


def ring_gather(x, ring, collective):
    major, minor = ring
    count = major * minor
    blk, width = x.shape
    return pl.pallas_call(
        partial(_ring_gather_kernel, major, minor),
        out_shape=jax.ShapeDtypeStruct((count * blk, width), x.dtype),
        in_specs=[pl.BlockSpec(memory_space=pltpu.VMEM)],
        out_specs=pl.BlockSpec(memory_space=pltpu.VMEM),
        scratch_shapes=[
            pltpu.SemaphoreType.DMA((2, count - 1)),
            pltpu.SemaphoreType.DMA((2, count - 1)),
        ],
        compiler_params=pltpu.CompilerParams(collective_id=collective, has_side_effects=True),
        name="ring_gather_head",
    )(x)


def ring_scatter(y, ring, collective):
    major, minor = ring
    count = major * minor
    rows, width = y.shape
    blk = rows // count
    return pl.pallas_call(
        partial(_ring_scatter_kernel, major, minor),
        out_shape=jax.ShapeDtypeStruct((blk, width), jnp.float32),
        in_specs=[pl.BlockSpec(memory_space=pltpu.VMEM)],
        out_specs=pl.BlockSpec(memory_space=pltpu.VMEM),
        scratch_shapes=[
            pltpu.VMEM((2, count - 1, blk // 2, width), y.dtype),
            pltpu.SemaphoreType.DMA((2, count - 1)),
            pltpu.SemaphoreType.DMA((2, count - 1)),
        ],
        compiler_params=pltpu.CompilerParams(collective_id=collective, has_side_effects=True),
        name="ring_scatter_head",
    )(y)


def head_ring(mesh):
    count = mesh.shape["head"]
    try:
        spots = [tuple(device.coords) for device in mesh.devices[:, 0]]
    except (AttributeError, TypeError):
        return (count, 1)
    moving = [axis for axis in range(len(spots[0])) if spots[0][axis] != spots[1][axis]]
    if len(moving) != 1:
        return (count, 1)
    minor = len({spot[moving[0]] for spot in spots})
    if count % minor or minor % 2:
        return (count, 1)
    return (count // minor, minor)


def contract_rows(left, right):
    return lax.dot_general(
        left, right, (((0,), (0,)), ((), ())), preferred_element_type=jnp.float32
    )


def contract_cols(left, right):
    return lax.dot_general(
        left, right, (((1,), (1,)), ((), ())), preferred_element_type=jnp.float32
    )


def on_device(
    ring,
    tokens,
    w_query,
    w_key,
    w_value,
    w_outgate,
    w_alpha,
    w_beta,
    conv_query,
    conv_key,
    conv_value,
    a_log,
    dt_bias,
    o_gain,
    w_out,
    gain_in,
    gain_ffn,
    w_gate,
    w_up,
    w_down,
    segments,
    valid_len,
    cotangent,
):
    residual = tokens[0].astype(jnp.float32)
    heads_here = w_alpha.shape[1]
    head_first = lax.axis_index("head") * heads_here
    norm_one, pull_one = jax.vjp(rms_norm, residual, gain_in)
    normed_one = norm_one.astype(jnp.bfloat16)
    row_count = lax.psum(1, "row")
    w_local = jnp.concatenate(
        [w_query, w_key, w_value, w_outgate, w_alpha, w_beta], axis=1
    ).astype(jnp.bfloat16)
    edges = [0]
    for member in (w_query, w_key, w_value, w_outgate, w_alpha, w_beta):
        edges.append(edges[-1] + member.shape[1])
    w_inward = lax.all_gather(w_local, "row", axis=0, tiled=True)
    conv_local = jnp.concatenate([conv_query, conv_key, conv_value], axis=1).astype(jnp.bfloat16)
    conv_edges = [0, conv_query.shape[1], conv_query.shape[1] + conv_key.shape[1], conv_local.shape[1]]
    conv_all = lax.all_gather(conv_local, "row", axis=1, tiled=True).reshape(
        conv_local.shape[0], row_count, conv_local.shape[1]
    )
    conv_parts = [
        conv_all[:, :, conv_edges[i] : conv_edges[i + 1]].reshape(conv_local.shape[0], -1)
        for i in range(3)
    ]
    out_matrix = lax.all_gather(w_out.astype(jnp.bfloat16), "row", axis=1, tiled=True)
    ff_width = w_gate.shape[1]
    ffn_local = jnp.concatenate([w_gate, w_up, w_down.T], axis=1).astype(jnp.bfloat16)
    grad_out = cotangent[0]
    grad_out_rows = lax.all_gather(grad_out, "row", axis=0, tiled=True)
    all_rows = ring_gather(normed_one, ring, 0)
    all_rows, out_matrix, ffn_local = lax.optimization_barrier((all_rows, out_matrix, ffn_local))
    ffn_all = lax.all_gather(ffn_local, "head", axis=0, tiled=True)
    projected = jnp.dot(all_rows, w_inward, preferred_element_type=jnp.float32)
    proj_parts = [projected[:, edges[spot] : edges[spot + 1]] for spot in range(6)]
    seg_ids = segments[0]
    live_mask = (jnp.arange(seg_ids.shape[0]) < valid_len[0]).astype(jnp.float32)
    a_here = lax.dynamic_slice_in_dim(a_log, head_first, heads_here)
    dt_here = lax.dynamic_slice_in_dim(dt_bias, head_first, heads_here)
    mixer_fn = partial(local_mixer, seg_ids=seg_ids, live_mask=live_mask)
    mixed, pull_core = jax.vjp(
        mixer_fn,
        proj_parts[0],
        proj_parts[1],
        proj_parts[2],
        proj_parts[3],
        proj_parts[4],
        proj_parts[5],
        conv_parts[0].astype(jnp.float32),
        conv_parts[1].astype(jnp.float32),
        conv_parts[2].astype(jnp.float32),
        a_here,
        dt_here,
        o_gain,
    )
    mixed, ffn_all, grad_out_rows = lax.optimization_barrier((mixed, ffn_all, grad_out_rows))
    w_gate_all = ffn_all[:, :ff_width]
    w_up_all = ffn_all[:, ff_width : 2 * ff_width]
    w_down_t = ffn_all[:, 2 * ff_width :]
    mixed_half = mixed.astype(jnp.bfloat16)
    mixer_output = ring_scatter(
        jnp.dot(mixed_half, out_matrix, preferred_element_type=jnp.float32).astype(jnp.bfloat16),
        ring,
        1,
    )
    middle = residual + mixer_output
    norm_two, pull_two = jax.vjp(rms_norm, middle, gain_ffn)
    normed_two = norm_two.astype(jnp.bfloat16)
    ffn_inputs = lax.all_gather(normed_two, "row", axis=0, tiled=True)
    gate_pre = jnp.dot(ffn_inputs, w_gate_all, preferred_element_type=jnp.float32)
    up_pre = jnp.dot(ffn_inputs, w_up_all, preferred_element_type=jnp.float32)
    hidden_val, pull_act = jax.vjp(swiglu, gate_pre, up_pre)
    hidden_half = hidden_val.astype(jnp.bfloat16)
    ffn_partial = contract_cols(hidden_half, w_down_t).astype(jnp.bfloat16)
    grad_hidden = jnp.dot(grad_out_rows, w_down_t, preferred_element_type=jnp.float32)
    grad_down_t = contract_rows(grad_out_rows, hidden_half)
    grad_gate_f, grad_up_f = pull_act(grad_hidden)
    grad_gate = grad_gate_f.astype(jnp.bfloat16)
    grad_upper = grad_up_f.astype(jnp.bfloat16)
    grad_wgate = contract_rows(ffn_inputs, grad_gate)
    grad_wup = contract_rows(ffn_inputs, grad_upper)
    grad_norm_two = lax.psum_scatter(
        (contract_cols(grad_gate, w_gate_all) + contract_cols(grad_upper, w_up_all)).astype(
            jnp.bfloat16
        ),
        "row",
        scatter_dimension=0,
        tiled=True,
    ).astype(jnp.float32)
    grad_mid_part, grad_gain_ffn = pull_two(grad_norm_two)
    grad_middle = grad_out.astype(jnp.float32) + grad_mid_part
    ffn_grad_cat = jnp.concatenate([grad_wgate, grad_wup, grad_down_t], axis=1).astype(
        jnp.bfloat16
    )
    grad_mid_half = grad_middle.astype(jnp.bfloat16)
    grad_mid_rows = ring_gather(grad_mid_half, ring, 2)
    ffn_output = lax.psum_scatter(ffn_partial, "row", scatter_dimension=0, tiled=True)
    grad_mid_rows, ffn_grad_cat = lax.optimization_barrier((grad_mid_rows, ffn_grad_cat))
    ffn_grad_all = lax.psum_scatter(ffn_grad_cat, "head", scatter_dimension=0, tiled=True)
    grad_mixed = contract_cols(grad_mid_rows, out_matrix)
    grad_wout = contract_rows(mixed_half, grad_mid_rows).astype(jnp.bfloat16)
    wout_grad = lax.psum_scatter(grad_wout, "row", scatter_dimension=1, tiled=True)
    core_grads = pull_core(grad_mixed)
    core_grads, ffn_output, ffn_grad_all = lax.optimization_barrier(
        (core_grads, ffn_output, ffn_grad_all)
    )
    final_out = (middle + ffn_output.astype(jnp.float32)).astype(jnp.bfloat16)
    ffn_grad_all = ffn_grad_all.astype(jnp.float32)
    ffn_grads = (
        ffn_grad_all[:, :ff_width],
        ffn_grad_all[:, ff_width : 2 * ff_width],
        ffn_grad_all[:, 2 * ff_width :].T,
    )
    grad_proj = jnp.concatenate(
        [core_grads[0], core_grads[1], core_grads[2], core_grads[3], core_grads[4], core_grads[5]],
        axis=1,
    ).astype(jnp.bfloat16)
    grad_inward = contract_rows(all_rows, grad_proj).astype(jnp.bfloat16)
    grad_norm_one = ring_scatter(contract_cols(grad_proj, w_inward).astype(jnp.bfloat16), ring, 3)
    grad_norm_one, wout_grad = lax.optimization_barrier((grad_norm_one, wout_grad))
    grad_in_part, grad_gain_in = pull_one(grad_norm_one)
    grad_input = grad_middle + grad_in_part
    inward_all = lax.psum_scatter(
        grad_inward, "row", scatter_dimension=0, tiled=True
    ).astype(jnp.float32)
    conv_grad_local = jnp.concatenate(
        [
            core_grads[6 + i].reshape(conv_local.shape[0], row_count, -1)
            for i in range(3)
        ],
        axis=2,
    ).reshape(conv_local.shape[0], -1)
    conv_grad = lax.psum_scatter(
        conv_grad_local.astype(jnp.bfloat16), "row", scatter_dimension=1, tiled=True
    ).astype(jnp.float32)
    mixer_grads = tuple(inward_all[:, edges[spot] : edges[spot + 1]] for spot in range(6)) + tuple(
        conv_grad[:, conv_edges[i] : conv_edges[i + 1]] for i in range(3)
    ) + (wout_grad.astype(jnp.float32),)
    head_total = a_log.shape[0]
    grad_a_full = lax.dynamic_update_slice_in_dim(
        jnp.zeros((head_total,), jnp.float32), core_grads[9], head_first, 0
    )
    grad_dt_full = lax.dynamic_update_slice_in_dim(
        jnp.zeros((head_total,), jnp.float32), core_grads[10], head_first, 0
    )
    small_sums = lax.psum(
        (grad_gain_in, grad_gain_ffn, core_grads[11], grad_a_full, grad_dt_full), ("head", "row")
    )
    return (
        final_out[None],
        grad_input[None],
        mixer_grads[0],
        mixer_grads[1],
        mixer_grads[2],
        mixer_grads[3],
        mixer_grads[4],
        mixer_grads[5],
        mixer_grads[6],
        mixer_grads[7],
        mixer_grads[8],
        small_sums[3],
        small_sums[4],
        small_sums[2],
        mixer_grads[9],
        small_sums[0],
        small_sums[1],
        ffn_grads[0],
        ffn_grads[1],
        ffn_grads[2],
    )


def solution(mesh):
    return jax.shard_map(
        partial(on_device, head_ring(mesh)),
        mesh=mesh,
        in_specs=(
            P("row", "head", None),
            P("row", "head"),
            P("row", "head"),
            P("row", "head"),
            P("row", "head"),
            P("row", "head"),
            P("row", "head"),
            P(None, ("head", "row")),
            P(None, ("head", "row")),
            P(None, ("head", "row")),
            P(),
            P(),
            P(),
            P("head", "row"),
            P(),
            P(),
            P("head", "row"),
            P("head", "row"),
            P("row", "head"),
            P("row", None),
            P("row"),
            P("row", "head", None),
        ),
        out_specs=(
            P("row", "head", None),
            P("row", "head", None),
            P("row", "head"),
            P("row", "head"),
            P("row", "head"),
            P("row", "head"),
            P("row", "head"),
            P("row", "head"),
            P(None, ("head", "row")),
            P(None, ("head", "row")),
            P(None, ("head", "row")),
            P(),
            P(),
            P(),
            P("head", "row"),
            P(),
            P(),
            P("head", "row"),
            P("head", "row"),
            P("row", "head"),
        ),
        check_vma=False,
    )
```

```python
from functools import partial
import math

import jax
import jax.numpy as jnp
from jax import lax
from jax.sharding import PartitionSpec as P
from jax.experimental import pallas as pl
from jax.experimental.pallas import tpu as pltpu

BLOCK = 64


precise = lax.Precision.HIGHEST
epsilon = 1e-06
o_floor = 0.001


def rms_norm(vector, gain_vec, floor_add=epsilon):
    return (
        vector * lax.rsqrt(jnp.mean(vector * vector, axis=-1, keepdims=True) + floor_add) * gain_vec
    )


def unit_norm(vector):
    return vector * lax.rsqrt(jnp.sum(vector * vector, axis=-1, keepdims=True) + epsilon)


def swiglu(gate_pre, up_pre):
    return jax.nn.silu(gate_pre) * up_pre


def short_conv(signal, kernel, seg_ids):
    tap_count = kernel.shape[0]
    length = signal.shape[0]
    summed = signal * kernel[tap_count - 1]
    for offset in range(1, tap_count):
        shifted = jnp.concatenate(
            [jnp.zeros((offset, signal.shape[1]), signal.dtype), signal[: length - offset]], axis=0
        )
        seg_shift = jnp.concatenate(
            [jnp.full((offset,), -1, jnp.int32), seg_ids[: length - offset]]
        )
        keep_mask = (seg_shift == seg_ids).astype(signal.dtype)
        summed = summed + shifted * kernel[tap_count - 1 - offset] * keep_mask[:, None]
    return summed


def _recur_fwd_kernel(nb, u0_ref, w_ref, kt_ref, c_ref, s_out, u_out, s_scr):
    @pl.when(pl.program_id(1) == 0)
    def _():
        s_scr[...] = jnp.zeros_like(s_scr)

    def step(j, carry):
        state = s_scr[...]
        s_out[0, j] = state
        update = u0_ref[0, j] - lax.dot_general(
            w_ref[0, j], state, (((1,), (1,)), ((), ())),
            precision=precise, preferred_element_type=jnp.float32,
        )
        u_out[0, j] = update
        s_scr[...] = c_ref[0, j] * state + lax.dot_general(
            update, kt_ref[0, j], (((0,), (0,)), ((), ())),
            precision=precise, preferred_element_type=jnp.float32,
        )
        return carry

    lax.fori_loop(0, nb, step, 0)


def _recur_bwd_kernel(
    nb, s_ref, u_ref, w_ref, kt_ref, c_ref, ds_ref, du_ref,
    du0_out, dw_out, dkt_out, dc_out, g_scr,
):
    @pl.when(pl.program_id(1) == 0)
    def _():
        g_scr[...] = jnp.zeros_like(g_scr)

    def step(i, carry):
        j = nb - 1 - i
        grad_state = g_scr[...]
        state = s_ref[0, j]
        grad_update = du_ref[0, j] + lax.dot_general(
            kt_ref[0, j], grad_state, (((1,), (1,)), ((), ())),
            precision=precise, preferred_element_type=jnp.float32,
        )
        dkt_out[0, j] = jnp.dot(
            u_ref[0, j], grad_state, precision=precise, preferred_element_type=jnp.float32
        )
        dc_out[0, j] = jnp.sum(grad_state * state, axis=0, keepdims=True)
        du0_out[0, j] = grad_update
        dw_out[0, j] = -jnp.dot(
            grad_update, state, precision=precise, preferred_element_type=jnp.float32
        )
        g_scr[...] = (
            c_ref[0, j] * grad_state
            - lax.dot_general(
                grad_update, w_ref[0, j], (((0,), (0,)), ((), ())),
                precision=precise, preferred_element_type=jnp.float32,
            )
            + ds_ref[0, j]
        )
        return carry

    lax.fori_loop(0, nb, step, 0)


def _chunk_spec(nb, tail, reverse, count):
    if reverse:
        return pl.BlockSpec((1, nb) + tail, lambda h, b: (h, count - 1 - b, 0, 0))
    return pl.BlockSpec((1, nb) + tail, lambda h, b: (h, b, 0, 0))


def _recur_forward(u0, w, kt, c):
    heads, count, chunk, dv = u0.shape
    dk = w.shape[-1]
    nb = min(8, count)
    blocks = count // nb
    flops = 4 * heads * count * chunk * dk * dv * 6
    moved = 4 * heads * count * (2 * chunk * dv + 2 * chunk * dk + dv * dk)
    return pl.pallas_call(
        partial(_recur_fwd_kernel, nb),
        grid=(heads, blocks),
        in_specs=[
            _chunk_spec(nb, (chunk, dv), False, blocks),
            _chunk_spec(nb, (chunk, dk), False, blocks),
            _chunk_spec(nb, (chunk, dk), False, blocks),
            _chunk_spec(nb, (1, dk), False, blocks),
        ],
        out_specs=[
            _chunk_spec(nb, (dv, dk), False, blocks),
            _chunk_spec(nb, (chunk, dv), False, blocks),
        ],
        out_shape=[
            jax.ShapeDtypeStruct((heads, count, dv, dk), jnp.float32),
            jax.ShapeDtypeStruct((heads, count, chunk, dv), jnp.float32),
        ],
        scratch_shapes=[pltpu.VMEM((dv, dk), jnp.float32)],
        compiler_params=pltpu.CompilerParams(dimension_semantics=("arbitrary", "arbitrary")),
        cost_estimate=pl.CostEstimate(flops=flops, transcendentals=0, bytes_accessed=moved),
        name="delta_state_forward",
    )(u0, w, kt, c)


def _recur_backward(states, updates, w, kt, c, d_states, d_updates):
    heads, count, chunk, dv = updates.shape
    dk = w.shape[-1]
    nb = min(8, count)
    blocks = count // nb
    flops = 8 * heads * count * chunk * dk * dv * 6
    moved = 4 * heads * count * (4 * chunk * dv + 4 * chunk * dk + 2 * dv * dk)
    return pl.pallas_call(
        partial(_recur_bwd_kernel, nb),
        grid=(heads, blocks),
        in_specs=[
            _chunk_spec(nb, (dv, dk), True, blocks),
            _chunk_spec(nb, (chunk, dv), True, blocks),
            _chunk_spec(nb, (chunk, dk), True, blocks),
            _chunk_spec(nb, (chunk, dk), True, blocks),
            _chunk_spec(nb, (1, dk), True, blocks),
            _chunk_spec(nb, (dv, dk), True, blocks),
            _chunk_spec(nb, (chunk, dv), True, blocks),
        ],
        out_specs=[
            _chunk_spec(nb, (chunk, dv), True, blocks),
            _chunk_spec(nb, (chunk, dk), True, blocks),
            _chunk_spec(nb, (chunk, dk), True, blocks),
            _chunk_spec(nb, (1, dk), True, blocks),
        ],
        out_shape=[
            jax.ShapeDtypeStruct((heads, count, chunk, dv), jnp.float32),
            jax.ShapeDtypeStruct((heads, count, chunk, dk), jnp.float32),
            jax.ShapeDtypeStruct((heads, count, chunk, dk), jnp.float32),
            jax.ShapeDtypeStruct((heads, count, 1, dk), jnp.float32),
        ],
        scratch_shapes=[pltpu.VMEM((dv, dk), jnp.float32)],
        compiler_params=pltpu.CompilerParams(dimension_semantics=("arbitrary", "arbitrary")),
        cost_estimate=pl.CostEstimate(flops=flops, transcendentals=0, bytes_accessed=moved),
        name="delta_state_backward",
    )(states, updates, w, kt, c, d_states, d_updates)


@jax.custom_vjp
def state_recurrence(u0, w, kt, c):
    return _recur_forward(u0, w, kt, c)


def _recurrence_fwd(u0, w, kt, c):
    states, updates = _recur_forward(u0, w, kt, c)
    return (states, updates), (states, updates, w, kt, c)


def _recurrence_bwd(saved, grads):
    states, updates, w, kt, c = saved
    d_states, d_updates = grads
    du0, dw, dkt, dc_lanes = _recur_backward(states, updates, w, kt, c, d_states, d_updates)
    return du0, dw, dkt, dc_lanes


state_recurrence.defvjp(_recurrence_fwd, _recurrence_bwd)


def _unit_lower_inverse_small(system):
    size = system.shape[-1]
    strict = system - jnp.eye(size, dtype=system.dtype)
    power = -strict
    inverse = jnp.eye(size, dtype=system.dtype) + power
    done = 2
    while done < size:
        power = jnp.matmul(power, power, precision=precise)
        inverse = inverse + jnp.matmul(power, inverse, precision=precise)
        done *= 2
    return inverse


def _unit_lower_inverse_forward(system):
    size = system.shape[-1]
    base = min(8, size)
    lead = system.shape[:-2]
    count = size // base
    blocks = system.reshape(lead + (count, base, count, base))
    diag = jnp.stack([blocks[..., i, :, i, :] for i in range(count)], axis=-3)
    inverse = _unit_lower_inverse_small(diag)
    width = base
    while width < size:
        pairs = inverse.shape[-3] // 2
        upper = inverse[..., 0::2, :, :]
        lower = inverse[..., 1::2, :, :]
        below = jnp.stack(
            [
                system[..., (2 * i + 1) * width : (2 * i + 2) * width, 2 * i * width : (2 * i + 1) * width]
                for i in range(pairs)
            ],
            axis=-3,
        )
        corner = -jnp.matmul(
            lower, jnp.matmul(below, upper, precision=precise), precision=precise
        )
        zeros = jnp.zeros_like(upper)
        top = jnp.concatenate([upper, zeros], axis=-1)
        bottom = jnp.concatenate([corner, lower], axis=-1)
        inverse = jnp.concatenate([top, bottom], axis=-2)
        width *= 2
    return inverse[..., 0, :, :]


@jax.custom_vjp
def unit_lower_inverse(system):
    return _unit_lower_inverse_forward(system)


def _inverse_fwd(system):
    inverse = _unit_lower_inverse_forward(system)
    return inverse, inverse


def _inverse_bwd(inverse, grad):
    size = inverse.shape[-1]
    flipped = jnp.swapaxes(inverse, -1, -2)
    full = -jnp.matmul(jnp.matmul(flipped, grad, precision=precise), flipped, precision=precise)
    places = jnp.arange(size)
    return (full * (places[:, None] > places[None, :]).astype(full.dtype),)


unit_lower_inverse.defvjp(_inverse_fwd, _inverse_bwd)


def chunk_prepare(queries, keys_n, values, decays, beta_rate, seg_ids):
    length, dk = keys_n.shape
    count = length // BLOCK
    q = queries.reshape(count, BLOCK, dk)
    k = keys_n.reshape(count, BLOCK, dk)
    v = values.reshape(count, BLOCK, values.shape[1])
    beta = beta_rate.reshape(count, BLOCK)
    seg = seg_ids.reshape(count, BLOCK)
    cumulative = jnp.cumsum(decays.reshape(count, BLOCK), axis=1)
    places = jnp.arange(BLOCK)
    lower_tri = places[:, None] >= places[None, :]
    inside = jnp.logical_and(seg[:, :, None] == seg[:, None, :], lower_tri)
    log_gap = jnp.where(inside, cumulative[:, :, None] - cumulative[:, None, :], 0.0)
    within = jnp.exp(log_gap) * inside.astype(jnp.float32)
    strict = within * (places[:, None] > places[None, :]).astype(jnp.float32)
    last_seg = jnp.concatenate([jnp.full((1,), -1, seg.dtype), seg[:-1, BLOCK - 1]])
    carried = jnp.exp(cumulative) * (seg == last_seg[:, None]).astype(jnp.float32)
    key_gram = jnp.einsum("nid,njd->nij", k, k, precision=precise)
    system = jnp.eye(BLOCK, dtype=jnp.float32) + beta[:, :, None] * strict * key_gram
    right_side = jnp.concatenate([beta[:, :, None] * v, (beta * carried)[:, :, None] * k], axis=2)
    solved = jnp.matmul(unit_lower_inverse(system), right_side, precision=precise)
    dv = v.shape[2]
    kt = within[:, BLOCK - 1, :, None] * k
    scores = jnp.einsum("nid,njd->nij", q, k, precision=precise) * within
    return solved[:, :, :dv], solved[:, :, dv:], kt, carried[:, BLOCK - 1], carried, scores


def chunk_finish(queries, carried, scores, states, updates):
    count = states.shape[0]
    q = queries.reshape(count, BLOCK, queries.shape[1])
    output = carried[:, :, None] * jnp.einsum(
        "nid,nvd->niv", q, states, precision=precise
    ) + jnp.einsum("nij,njv->niv", scores, updates, precision=precise)
    return output.reshape(count * BLOCK, states.shape[1])


def delta_rule(queries, keys_n, values, decays, beta_rate, seg_ids):
    u0, w, kt, tail, carried, scores = jax.vmap(chunk_prepare, in_axes=(0, 0, 0, 0, 0, None))(
        queries, keys_n, values, decays, beta_rate, seg_ids
    )
    c = jnp.broadcast_to(tail[:, :, None, None], tail.shape + (1, w.shape[-1]))
    states, updates = state_recurrence(u0, w, kt, c)
    return jax.vmap(chunk_finish)(queries, carried, scores, states, updates)


def head_inputs(proj_query, proj_key, proj_value, proj_alpha, proj_beta,
                kernel_query, kernel_key, kernel_value, a_here, dt_here, seg_ids):
    queries = unit_norm(jax.nn.silu(short_conv(proj_query, kernel_query, seg_ids))) * (
        1.0 / math.sqrt(proj_query.shape[1])
    )
    keys_n = unit_norm(jax.nn.silu(short_conv(proj_key, kernel_key, seg_ids)))
    values = jax.nn.silu(short_conv(proj_value, kernel_value, seg_ids))
    decays = -jnp.exp(a_here) * jax.nn.softplus(proj_alpha + dt_here)
    beta_rate = jax.nn.sigmoid(proj_beta)
    return queries, keys_n, values, decays, beta_rate


def head_output(recurrent, proj_gate, o_gain, live_mask):
    return rms_norm(recurrent, o_gain, o_floor) * jax.nn.silu(proj_gate) * live_mask[:, None]


def local_mixer(
    proj_query,
    proj_key,
    proj_value,
    proj_gate,
    proj_alpha,
    proj_beta,
    kernel_query,
    kernel_key,
    kernel_value,
    a_here,
    dt_here,
    o_gain,
    seg_ids=None,
    live_mask=None,
):
    row_count = proj_query.shape[0]
    heads_here = proj_alpha.shape[1]

    def by_head(array):
        return jnp.moveaxis(array.reshape(row_count, heads_here, -1), 1, 0)

    def kernel_heads(kernel):
        return jnp.moveaxis(kernel.reshape(kernel.shape[0], heads_here, -1), 1, 0)

    queries, keys_n, values, decays, beta_rate = jax.vmap(
        head_inputs, in_axes=(0,) * 10 + (None,)
    )(
        by_head(proj_query),
        by_head(proj_key),
        by_head(proj_value),
        proj_alpha.T,
        proj_beta.T,
        kernel_heads(kernel_query),
        kernel_heads(kernel_key),
        kernel_heads(kernel_value),
        a_here,
        dt_here,
        seg_ids,
    )
    recurrent = delta_rule(queries, keys_n, values, decays, beta_rate, seg_ids)
    mixed_heads = jax.vmap(head_output, in_axes=(0, 0, None, None))(
        recurrent, by_head(proj_gate), o_gain, live_mask
    )
    return jnp.moveaxis(mixed_heads, 0, 1).reshape(row_count, -1)


MESH_ID = pl.DeviceIdType.MESH


def _ring_position(h, major, minor):
    a = h // minor
    b = h % minor
    return b * major + a + (b % 2) * (major - 1 - 2 * a)


def _ring_member(q, major, minor):
    count = major * minor
    q = (q + count) % count
    b = q // major
    r = q % major
    return (r + (b % 2) * (major - 1 - 2 * r)) * minor + b


def _ring_sides(major, minor):
    p = _ring_position(lax.axis_index("head"), major, minor)
    return p, _ring_member(p + 1, major, minor), _ring_member(p - 1, major, minor)


def _greet(nxt, prv, row):
    barrier = pltpu.get_barrier_semaphore()
    pl.semaphore_signal(barrier, 1, device_id=(prv, row), device_id_type=MESH_ID)
    pl.semaphore_signal(barrier, 1, device_id=(nxt, row), device_id_type=MESH_ID)
    pl.semaphore_wait(barrier, 2)


def _ring_gather_kernel(major, minor, x_ref, out_ref, send_sem, recv_sem):
    count = major * minor
    blk = x_ref.shape[0]
    half = blk // 2
    row = lax.axis_index("row")
    p, nxt, prv = _ring_sides(major, minor)
    out_ref[pl.ds(pl.multiple_of(lax.axis_index("head") * blk, blk), blk), :] = x_ref[...]
    _greet(nxt, prv, row)

    def piece(pos, off):
        return out_ref.at[pl.ds(pl.multiple_of(_ring_member(pos, major, minor) * blk + off, half), half)]

    def outgoing(d, s):
        pos = p - s if d == 0 else p + s
        target = nxt if d == 0 else prv
        ref = piece(pos, d * half)
        return pltpu.make_async_remote_copy(
            ref, ref, send_sem.at[d, s], recv_sem.at[d, s], device_id=(target, row),
            device_id_type=MESH_ID,
        )

    def incoming(d, s):
        pos = p - 1 - s if d == 0 else p + 1 + s
        source = prv if d == 0 else nxt
        ref = piece(pos, d * half)
        return pltpu.make_async_remote_copy(
            ref, ref, send_sem.at[d, s], recv_sem.at[d, s], device_id=(source, row),
            device_id_type=MESH_ID,
        )

    for s in range(count - 1):
        for d in (0, 1):
            if s > 0:
                incoming(d, s - 1).wait_recv()
            outgoing(d, s).start()
    for d in (0, 1):
        incoming(d, count - 2).wait_recv()
    for s in range(count - 1):
        for d in (0, 1):
            outgoing(d, s).wait_send()


def _ring_scatter_kernel(major, minor, y_ref, out_ref, buf, send_sem, recv_sem):
    count = major * minor
    blk = out_ref.shape[0]
    half = blk // 2
    row = lax.axis_index("row")
    p, nxt, prv = _ring_sides(major, minor)
    _greet(nxt, prv, row)

    def piece(pos, off):
        return y_ref.at[pl.ds(pl.multiple_of(_ring_member(pos, major, minor) * blk + off, half), half)]

    def outgoing(d, s):
        pos = p - s - 1 if d == 0 else p + s + 1
        target = nxt if d == 0 else prv
        source = piece(pos, d * half) if s == 0 else buf.at[d, s - 1]
        return pltpu.make_async_remote_copy(
            source, buf.at[d, s], send_sem.at[d, s], recv_sem.at[d, s],
            device_id=(target, row), device_id_type=MESH_ID,
        )

    def incoming(d, s):
        source = prv if d == 0 else nxt
        return pltpu.make_async_remote_copy(
            buf.at[d, s], buf.at[d, s], send_sem.at[d, s], recv_sem.at[d, s],
            device_id=(source, row), device_id_type=MESH_ID,
        )

    for s in range(count - 1):
        for d in (0, 1):
            if s > 0:
                incoming(d, s - 1).wait_recv()
                pos = p - s - 1 if d == 0 else p + s + 1
                buf[d, s - 1] = (
                    buf[d, s - 1].astype(jnp.float32)
                    + piece(pos, d * half)[...].astype(jnp.float32)
                ).astype(buf.dtype)
            outgoing(d, s).start()
    for d in (0, 1):
        incoming(d, count - 2).wait_recv()
        out_ref[pl.ds(d * half, half), :] = piece(p, d * half)[...].astype(
            jnp.float32
        ) + buf[d, count - 2].astype(jnp.float32)
    for s in range(count - 1):
        for d in (0, 1):
            outgoing(d, s).wait_send()


def ring_gather(x, ring, collective):
    major, minor = ring
    count = major * minor
    blk, width = x.shape
    return pl.pallas_call(
        partial(_ring_gather_kernel, major, minor),
        out_shape=jax.ShapeDtypeStruct((count * blk, width), x.dtype),
        in_specs=[pl.BlockSpec(memory_space=pltpu.VMEM)],
        out_specs=pl.BlockSpec(memory_space=pltpu.VMEM),
        scratch_shapes=[
            pltpu.SemaphoreType.DMA((2, count - 1)),
            pltpu.SemaphoreType.DMA((2, count - 1)),
        ],
        compiler_params=pltpu.CompilerParams(collective_id=collective, has_side_effects=True),
        name="ring_gather_head",
    )(x)


def ring_scatter(y, ring, collective):
    major, minor = ring
    count = major * minor
    rows, width = y.shape
    blk = rows // count
    return pl.pallas_call(
        partial(_ring_scatter_kernel, major, minor),
        out_shape=jax.ShapeDtypeStruct((blk, width), jnp.float32),
        in_specs=[pl.BlockSpec(memory_space=pltpu.VMEM)],
        out_specs=pl.BlockSpec(memory_space=pltpu.VMEM),
        scratch_shapes=[
            pltpu.VMEM((2, count - 1, blk // 2, width), y.dtype),
            pltpu.SemaphoreType.DMA((2, count - 1)),
            pltpu.SemaphoreType.DMA((2, count - 1)),
        ],
        compiler_params=pltpu.CompilerParams(collective_id=collective, has_side_effects=True),
        name="ring_scatter_head",
    )(y)


def head_ring(mesh):
    count = mesh.shape["head"]
    try:
        spots = [tuple(device.coords) for device in mesh.devices[:, 0]]
    except (AttributeError, TypeError):
        return (count, 1)
    moving = [axis for axis in range(len(spots[0])) if spots[0][axis] != spots[1][axis]]
    if len(moving) != 1:
        return (count, 1)
    minor = len({spot[moving[0]] for spot in spots})
    if count % minor or minor % 2:
        return (count, 1)
    return (count // minor, minor)


def contract_rows(left, right):
    return lax.dot_general(
        left, right, (((0,), (0,)), ((), ())), preferred_element_type=jnp.float32
    )


def contract_cols(left, right):
    return lax.dot_general(
        left, right, (((1,), (1,)), ((), ())), preferred_element_type=jnp.float32
    )


def on_device(
    ring,
    tokens,
    w_query,
    w_key,
    w_value,
    w_outgate,
    w_alpha,
    w_beta,
    conv_query,
    conv_key,
    conv_value,
    a_log,
    dt_bias,
    o_gain,
    w_out,
    gain_in,
    gain_ffn,
    w_gate,
    w_up,
    w_down,
    segments,
    valid_len,
    cotangent,
):
    residual = tokens[0].astype(jnp.float32)
    heads_here = w_alpha.shape[1]
    head_first = lax.axis_index("head") * heads_here
    norm_one, pull_one = jax.vjp(rms_norm, residual, gain_in)
    normed_one = norm_one.astype(jnp.bfloat16)
    row_count = lax.psum(1, "row")
    w_local = jnp.concatenate(
        [w_query, w_key, w_value, w_outgate, w_alpha, w_beta], axis=1
    ).astype(jnp.bfloat16)
    edges = [0]
    for member in (w_query, w_key, w_value, w_outgate, w_alpha, w_beta):
        edges.append(edges[-1] + member.shape[1])
    w_inward = lax.all_gather(w_local, "row", axis=0, tiled=True)
    conv_local = jnp.concatenate([conv_query, conv_key, conv_value], axis=1).astype(jnp.bfloat16)
    conv_edges = [0, conv_query.shape[1], conv_query.shape[1] + conv_key.shape[1], conv_local.shape[1]]
    conv_all = lax.all_gather(conv_local, "row", axis=1, tiled=True).reshape(
        conv_local.shape[0], row_count, conv_local.shape[1]
    )
    conv_parts = [
        conv_all[:, :, conv_edges[i] : conv_edges[i + 1]].reshape(conv_local.shape[0], -1)
        for i in range(3)
    ]
    out_matrix = lax.all_gather(w_out.astype(jnp.bfloat16), "row", axis=1, tiled=True)
    ff_width = w_gate.shape[1]
    ffn_local = jnp.concatenate([w_gate, w_up], axis=1).astype(jnp.bfloat16)
    down_local = w_down.T.astype(jnp.bfloat16)
    grad_out = cotangent[0]
    grad_out_rows = lax.all_gather(grad_out, "row", axis=0, tiled=True)
    all_rows = ring_gather(normed_one, ring, 0)
    all_rows, out_matrix, ffn_local = lax.optimization_barrier((all_rows, out_matrix, ffn_local))
    ffn_all = lax.all_gather(ffn_local, "head", axis=0, tiled=True)
    projected = jnp.dot(all_rows, w_inward, preferred_element_type=jnp.float32)
    proj_parts = [projected[:, edges[spot] : edges[spot + 1]] for spot in range(6)]
    seg_ids = segments[0]
    live_mask = (jnp.arange(seg_ids.shape[0]) < valid_len[0]).astype(jnp.float32)
    a_here = lax.dynamic_slice_in_dim(a_log, head_first, heads_here)
    dt_here = lax.dynamic_slice_in_dim(dt_bias, head_first, heads_here)
    mixer_fn = partial(local_mixer, seg_ids=seg_ids, live_mask=live_mask)
    mixed, pull_core = jax.vjp(
        mixer_fn,
        proj_parts[0],
        proj_parts[1],
        proj_parts[2],
        proj_parts[3],
        proj_parts[4],
        proj_parts[5],
        conv_parts[0].astype(jnp.float32),
        conv_parts[1].astype(jnp.float32),
        conv_parts[2].astype(jnp.float32),
        a_here,
        dt_here,
        o_gain,
    )
    mixed, ffn_all, grad_out_rows, down_local = lax.optimization_barrier(
        (mixed, ffn_all, grad_out_rows, down_local)
    )
    w_down_t = ring_gather(down_local, ring, 4)
    w_gate_all = ffn_all[:, :ff_width]
    w_up_all = ffn_all[:, ff_width : 2 * ff_width]
    mixed_half = mixed.astype(jnp.bfloat16)
    mixer_output = ring_scatter(
        jnp.dot(mixed_half, out_matrix, preferred_element_type=jnp.float32).astype(jnp.bfloat16),
        ring,
        1,
    )
    middle = residual + mixer_output
    norm_two, pull_two = jax.vjp(rms_norm, middle, gain_ffn)
    normed_two = norm_two.astype(jnp.bfloat16)
    ffn_inputs = lax.all_gather(normed_two, "row", axis=0, tiled=True)
    gate_pre = jnp.dot(ffn_inputs, w_gate_all, preferred_element_type=jnp.float32)
    up_pre = jnp.dot(ffn_inputs, w_up_all, preferred_element_type=jnp.float32)
    hidden_val, pull_act = jax.vjp(swiglu, gate_pre, up_pre)
    hidden_half = hidden_val.astype(jnp.bfloat16)
    ffn_partial = contract_cols(hidden_half, w_down_t).astype(jnp.bfloat16)
    grad_hidden = jnp.dot(grad_out_rows, w_down_t, preferred_element_type=jnp.float32)
    grad_down_t = contract_rows(grad_out_rows, hidden_half)
    grad_gate_f, grad_up_f = pull_act(grad_hidden)
    grad_gate = grad_gate_f.astype(jnp.bfloat16)
    grad_upper = grad_up_f.astype(jnp.bfloat16)
    grad_wgate = contract_rows(ffn_inputs, grad_gate)
    grad_wup = contract_rows(ffn_inputs, grad_upper)
    grad_norm_two = lax.psum_scatter(
        (contract_cols(grad_gate, w_gate_all) + contract_cols(grad_upper, w_up_all)).astype(
            jnp.bfloat16
        ),
        "row",
        scatter_dimension=0,
        tiled=True,
    ).astype(jnp.float32)
    grad_mid_part, grad_gain_ffn = pull_two(grad_norm_two)
    grad_middle = grad_out.astype(jnp.float32) + grad_mid_part
    ffn_grad_cat = jnp.concatenate([grad_wgate, grad_wup, grad_down_t], axis=1).astype(
        jnp.bfloat16
    )
    grad_mid_half = grad_middle.astype(jnp.bfloat16)
    grad_mid_rows = ring_gather(grad_mid_half, ring, 2)
    ffn_output = lax.psum_scatter(ffn_partial, "row", scatter_dimension=0, tiled=True)
    grad_mid_rows, ffn_grad_cat = lax.optimization_barrier((grad_mid_rows, ffn_grad_cat))
    ffn_grad_all = lax.psum_scatter(ffn_grad_cat, "head", scatter_dimension=0, tiled=True)
    grad_mixed = contract_cols(grad_mid_rows, out_matrix)
    grad_wout = contract_rows(mixed_half, grad_mid_rows).astype(jnp.bfloat16)
    wout_grad = lax.psum_scatter(grad_wout, "row", scatter_dimension=1, tiled=True)
    core_grads = pull_core(grad_mixed)
    core_grads, ffn_output, ffn_grad_all = lax.optimization_barrier(
        (core_grads, ffn_output, ffn_grad_all)
    )
    final_out = (middle + ffn_output.astype(jnp.float32)).astype(jnp.bfloat16)
    ffn_grad_all = ffn_grad_all.astype(jnp.float32)
    ffn_grads = (
        ffn_grad_all[:, :ff_width],
        ffn_grad_all[:, ff_width : 2 * ff_width],
        ffn_grad_all[:, 2 * ff_width :].T,
    )
    grad_proj = jnp.concatenate(
        [core_grads[0], core_grads[1], core_grads[2], core_grads[3], core_grads[4], core_grads[5]],
        axis=1,
    ).astype(jnp.bfloat16)
    grad_inward = contract_rows(all_rows, grad_proj).astype(jnp.bfloat16)
    grad_norm_one = ring_scatter(contract_cols(grad_proj, w_inward).astype(jnp.bfloat16), ring, 3)
    grad_norm_one, wout_grad = lax.optimization_barrier((grad_norm_one, wout_grad))
    grad_in_part, grad_gain_in = pull_one(grad_norm_one)
    grad_input = grad_middle + grad_in_part
    inward_all = lax.psum_scatter(
        grad_inward, "row", scatter_dimension=0, tiled=True
    ).astype(jnp.float32)
    conv_grad_local = jnp.concatenate(
        [
            core_grads[6 + i].reshape(conv_local.shape[0], row_count, -1)
            for i in range(3)
        ],
        axis=2,
    ).reshape(conv_local.shape[0], -1)
    conv_grad = lax.psum_scatter(
        conv_grad_local.astype(jnp.bfloat16), "row", scatter_dimension=1, tiled=True
    ).astype(jnp.float32)
    mixer_grads = tuple(inward_all[:, edges[spot] : edges[spot + 1]] for spot in range(6)) + tuple(
        conv_grad[:, conv_edges[i] : conv_edges[i + 1]] for i in range(3)
    ) + (wout_grad.astype(jnp.float32),)
    head_total = a_log.shape[0]
    grad_a_full = lax.dynamic_update_slice_in_dim(
        jnp.zeros((head_total,), jnp.float32), core_grads[9], head_first, 0
    )
    grad_dt_full = lax.dynamic_update_slice_in_dim(
        jnp.zeros((head_total,), jnp.float32), core_grads[10], head_first, 0
    )
    small_sums = lax.psum(
        (grad_gain_in, grad_gain_ffn, core_grads[11], grad_a_full, grad_dt_full), ("head", "row")
    )
    return (
        final_out[None],
        grad_input[None],
        mixer_grads[0],
        mixer_grads[1],
        mixer_grads[2],
        mixer_grads[3],
        mixer_grads[4],
        mixer_grads[5],
        mixer_grads[6],
        mixer_grads[7],
        mixer_grads[8],
        small_sums[3],
        small_sums[4],
        small_sums[2],
        mixer_grads[9],
        small_sums[0],
        small_sums[1],
        ffn_grads[0],
        ffn_grads[1],
        ffn_grads[2],
    )


def solution(mesh):
    return jax.shard_map(
        partial(on_device, head_ring(mesh)),
        mesh=mesh,
        in_specs=(
            P("row", "head", None),
            P("row", "head"),
            P("row", "head"),
            P("row", "head"),
            P("row", "head"),
            P("row", "head"),
            P("row", "head"),
            P(None, ("head", "row")),
            P(None, ("head", "row")),
            P(None, ("head", "row")),
            P(),
            P(),
            P(),
            P("head", "row"),
            P(),
            P(),
            P("head", "row"),
            P("head", "row"),
            P("row", "head"),
            P("row", None),
            P("row"),
            P("row", "head", None),
        ),
        out_specs=(
            P("row", "head", None),
            P("row", "head", None),
            P("row", "head"),
            P("row", "head"),
            P("row", "head"),
            P("row", "head"),
            P("row", "head"),
            P("row", "head"),
            P(None, ("head", "row")),
            P(None, ("head", "row")),
            P(None, ("head", "row")),
            P(),
            P(),
            P(),
            P("head", "row"),
            P(),
            P(),
            P("head", "row"),
            P("head", "row"),
            P("row", "head"),
        ),
        check_vma=False,
    )
```

```python
from functools import partial
import math

import jax
import jax.numpy as jnp
from jax import lax
from jax.sharding import PartitionSpec as P
from jax.experimental import pallas as pl
from jax.experimental.pallas import tpu as pltpu

BLOCK = 64


precise = lax.Precision.HIGHEST
epsilon = 1e-06
o_floor = 0.001


def rms_norm(vector, gain_vec, floor_add=epsilon):
    return (
        vector * lax.rsqrt(jnp.mean(vector * vector, axis=-1, keepdims=True) + floor_add) * gain_vec
    )


def unit_norm(vector):
    return vector * lax.rsqrt(jnp.sum(vector * vector, axis=-1, keepdims=True) + epsilon)


def swiglu(gate_pre, up_pre):
    return jax.nn.silu(gate_pre) * up_pre


def short_conv(signal, kernel, seg_ids):
    tap_count = kernel.shape[0]
    length = signal.shape[0]
    summed = signal * kernel[tap_count - 1]
    for offset in range(1, tap_count):
        shifted = jnp.concatenate(
            [jnp.zeros((offset, signal.shape[1]), signal.dtype), signal[: length - offset]], axis=0
        )
        seg_shift = jnp.concatenate(
            [jnp.full((offset,), -1, jnp.int32), seg_ids[: length - offset]]
        )
        keep_mask = (seg_shift == seg_ids).astype(signal.dtype)
        summed = summed + shifted * kernel[tap_count - 1 - offset] * keep_mask[:, None]
    return summed


def _recur_fwd_kernel(nb, u0_ref, w_ref, kt_ref, c_ref, s_out, u_out, s_scr):
    @pl.when(pl.program_id(1) == 0)
    def _():
        s_scr[...] = jnp.zeros_like(s_scr)

    def step(j, carry):
        state = s_scr[...]
        s_out[0, j] = state
        update = u0_ref[0, j] - lax.dot_general(
            w_ref[0, j], state, (((1,), (1,)), ((), ())),
            precision=precise, preferred_element_type=jnp.float32,
        )
        u_out[0, j] = update
        s_scr[...] = c_ref[0, j] * state + lax.dot_general(
            update, kt_ref[0, j], (((0,), (0,)), ((), ())),
            precision=precise, preferred_element_type=jnp.float32,
        )
        return carry

    lax.fori_loop(0, nb, step, 0)


def _recur_bwd_kernel(
    nb, s_ref, u_ref, w_ref, kt_ref, c_ref, ds_ref, du_ref,
    du0_out, dw_out, dkt_out, dc_out, g_scr,
):
    @pl.when(pl.program_id(1) == 0)
    def _():
        g_scr[...] = jnp.zeros_like(g_scr)

    def step(i, carry):
        j = nb - 1 - i
        grad_state = g_scr[...]
        state = s_ref[0, j]
        grad_update = du_ref[0, j] + lax.dot_general(
            kt_ref[0, j], grad_state, (((1,), (1,)), ((), ())),
            precision=precise, preferred_element_type=jnp.float32,
        )
        dkt_out[0, j] = jnp.dot(
            u_ref[0, j], grad_state, precision=precise, preferred_element_type=jnp.float32
        )
        dc_out[0, j] = jnp.sum(grad_state * state, axis=0, keepdims=True)
        du0_out[0, j] = grad_update
        dw_out[0, j] = -jnp.dot(
            grad_update, state, precision=precise, preferred_element_type=jnp.float32
        )
        g_scr[...] = (
            c_ref[0, j] * grad_state
            - lax.dot_general(
                grad_update, w_ref[0, j], (((0,), (0,)), ((), ())),
                precision=precise, preferred_element_type=jnp.float32,
            )
            + ds_ref[0, j]
        )
        return carry

    lax.fori_loop(0, nb, step, 0)


def _chunk_spec(nb, tail, reverse, count):
    if reverse:
        return pl.BlockSpec((1, nb) + tail, lambda h, b: (h, count - 1 - b, 0, 0))
    return pl.BlockSpec((1, nb) + tail, lambda h, b: (h, b, 0, 0))


def _recur_forward(u0, w, kt, c):
    heads, count, chunk, dv = u0.shape
    dk = w.shape[-1]
    nb = min(8, count)
    blocks = count // nb
    flops = 4 * heads * count * chunk * dk * dv * 6
    moved = 4 * heads * count * (2 * chunk * dv + 2 * chunk * dk + dv * dk)
    return pl.pallas_call(
        partial(_recur_fwd_kernel, nb),
        grid=(heads, blocks),
        in_specs=[
            _chunk_spec(nb, (chunk, dv), False, blocks),
            _chunk_spec(nb, (chunk, dk), False, blocks),
            _chunk_spec(nb, (chunk, dk), False, blocks),
            _chunk_spec(nb, (1, dk), False, blocks),
        ],
        out_specs=[
            _chunk_spec(nb, (dv, dk), False, blocks),
            _chunk_spec(nb, (chunk, dv), False, blocks),
        ],
        out_shape=[
            jax.ShapeDtypeStruct((heads, count, dv, dk), jnp.float32),
            jax.ShapeDtypeStruct((heads, count, chunk, dv), jnp.float32),
        ],
        scratch_shapes=[pltpu.VMEM((dv, dk), jnp.float32)],
        compiler_params=pltpu.CompilerParams(dimension_semantics=("arbitrary", "arbitrary")),
        cost_estimate=pl.CostEstimate(flops=flops, transcendentals=0, bytes_accessed=moved),
        name="delta_state_forward",
    )(u0, w, kt, c)


def _recur_backward(states, updates, w, kt, c, d_states, d_updates):
    heads, count, chunk, dv = updates.shape
    dk = w.shape[-1]
    nb = min(8, count)
    blocks = count // nb
    flops = 8 * heads * count * chunk * dk * dv * 6
    moved = 4 * heads * count * (4 * chunk * dv + 4 * chunk * dk + 2 * dv * dk)
    return pl.pallas_call(
        partial(_recur_bwd_kernel, nb),
        grid=(heads, blocks),
        in_specs=[
            _chunk_spec(nb, (dv, dk), True, blocks),
            _chunk_spec(nb, (chunk, dv), True, blocks),
            _chunk_spec(nb, (chunk, dk), True, blocks),
            _chunk_spec(nb, (chunk, dk), True, blocks),
            _chunk_spec(nb, (1, dk), True, blocks),
            _chunk_spec(nb, (dv, dk), True, blocks),
            _chunk_spec(nb, (chunk, dv), True, blocks),
        ],
        out_specs=[
            _chunk_spec(nb, (chunk, dv), True, blocks),
            _chunk_spec(nb, (chunk, dk), True, blocks),
            _chunk_spec(nb, (chunk, dk), True, blocks),
            _chunk_spec(nb, (1, dk), True, blocks),
        ],
        out_shape=[
            jax.ShapeDtypeStruct((heads, count, chunk, dv), jnp.float32),
            jax.ShapeDtypeStruct((heads, count, chunk, dk), jnp.float32),
            jax.ShapeDtypeStruct((heads, count, chunk, dk), jnp.float32),
            jax.ShapeDtypeStruct((heads, count, 1, dk), jnp.float32),
        ],
        scratch_shapes=[pltpu.VMEM((dv, dk), jnp.float32)],
        compiler_params=pltpu.CompilerParams(dimension_semantics=("arbitrary", "arbitrary")),
        cost_estimate=pl.CostEstimate(flops=flops, transcendentals=0, bytes_accessed=moved),
        name="delta_state_backward",
    )(states, updates, w, kt, c, d_states, d_updates)


@jax.custom_vjp
def state_recurrence(u0, w, kt, c):
    return _recur_forward(u0, w, kt, c)


def _recurrence_fwd(u0, w, kt, c):
    states, updates = _recur_forward(u0, w, kt, c)
    return (states, updates), (states, updates, w, kt, c)


def _recurrence_bwd(saved, grads):
    states, updates, w, kt, c = saved
    d_states, d_updates = grads
    du0, dw, dkt, dc_lanes = _recur_backward(states, updates, w, kt, c, d_states, d_updates)
    return du0, dw, dkt, dc_lanes


state_recurrence.defvjp(_recurrence_fwd, _recurrence_bwd)


def _unit_lower_inverse_small(system):
    size = system.shape[-1]
    strict = system - jnp.eye(size, dtype=system.dtype)
    power = -strict
    inverse = jnp.eye(size, dtype=system.dtype) + power
    done = 2
    while done < size:
        power = jnp.matmul(power, power, precision=precise)
        inverse = inverse + jnp.matmul(power, inverse, precision=precise)
        done *= 2
    return inverse


def _unit_lower_inverse_forward(system):
    size = system.shape[-1]
    base = min(8, size)
    lead = system.shape[:-2]
    count = size // base
    blocks = system.reshape(lead + (count, base, count, base))
    diag = jnp.stack([blocks[..., i, :, i, :] for i in range(count)], axis=-3)
    inverse = _unit_lower_inverse_small(diag)
    width = base
    while width < size:
        pairs = inverse.shape[-3] // 2
        upper = inverse[..., 0::2, :, :]
        lower = inverse[..., 1::2, :, :]
        below = jnp.stack(
            [
                system[..., (2 * i + 1) * width : (2 * i + 2) * width, 2 * i * width : (2 * i + 1) * width]
                for i in range(pairs)
            ],
            axis=-3,
        )
        corner = -jnp.matmul(
            lower, jnp.matmul(below, upper, precision=precise), precision=precise
        )
        zeros = jnp.zeros_like(upper)
        top = jnp.concatenate([upper, zeros], axis=-1)
        bottom = jnp.concatenate([corner, lower], axis=-1)
        inverse = jnp.concatenate([top, bottom], axis=-2)
        width *= 2
    return inverse[..., 0, :, :]


@jax.custom_vjp
def unit_lower_inverse(system):
    return _unit_lower_inverse_forward(system)


def _inverse_fwd(system):
    inverse = _unit_lower_inverse_forward(system)
    return inverse, inverse


def _inverse_bwd(inverse, grad):
    size = inverse.shape[-1]
    flipped = jnp.swapaxes(inverse, -1, -2)
    full = -jnp.matmul(jnp.matmul(flipped, grad, precision=precise), flipped, precision=precise)
    places = jnp.arange(size)
    return (full * (places[:, None] > places[None, :]).astype(full.dtype),)


unit_lower_inverse.defvjp(_inverse_fwd, _inverse_bwd)


def chunk_prepare(queries, keys_n, values, decays, beta_rate, seg_ids):
    length, dk = keys_n.shape
    count = length // BLOCK
    q = queries.reshape(count, BLOCK, dk)
    k = keys_n.reshape(count, BLOCK, dk)
    v = values.reshape(count, BLOCK, values.shape[1])
    beta = beta_rate.reshape(count, BLOCK)
    seg = seg_ids.reshape(count, BLOCK)
    cumulative = jnp.cumsum(decays.reshape(count, BLOCK), axis=1)
    places = jnp.arange(BLOCK)
    lower_tri = places[:, None] >= places[None, :]
    inside = jnp.logical_and(seg[:, :, None] == seg[:, None, :], lower_tri)
    log_gap = jnp.where(inside, cumulative[:, :, None] - cumulative[:, None, :], 0.0)
    within = jnp.exp(log_gap) * inside.astype(jnp.float32)
    strict = within * (places[:, None] > places[None, :]).astype(jnp.float32)
    last_seg = jnp.concatenate([jnp.full((1,), -1, seg.dtype), seg[:-1, BLOCK - 1]])
    carried = jnp.exp(cumulative) * (seg == last_seg[:, None]).astype(jnp.float32)
    key_gram = jnp.einsum("nid,njd->nij", k, k, precision=precise)
    system = jnp.eye(BLOCK, dtype=jnp.float32) + beta[:, :, None] * strict * key_gram
    right_side = jnp.concatenate([beta[:, :, None] * v, (beta * carried)[:, :, None] * k], axis=2)
    solved = jnp.matmul(unit_lower_inverse(system), right_side, precision=precise)
    dv = v.shape[2]
    kt = within[:, BLOCK - 1, :, None] * k
    scores = jnp.einsum("nid,njd->nij", q, k, precision=precise) * within
    return solved[:, :, :dv], solved[:, :, dv:], kt, carried[:, BLOCK - 1], carried, scores


def chunk_finish(queries, carried, scores, states, updates):
    count = states.shape[0]
    q = queries.reshape(count, BLOCK, queries.shape[1])
    output = carried[:, :, None] * jnp.einsum(
        "nid,nvd->niv", q, states, precision=precise
    ) + jnp.einsum("nij,njv->niv", scores, updates, precision=precise)
    return output.reshape(count * BLOCK, states.shape[1])


def delta_rule(queries, keys_n, values, decays, beta_rate, seg_ids):
    u0, w, kt, tail, carried, scores = jax.vmap(chunk_prepare, in_axes=(0, 0, 0, 0, 0, None))(
        queries, keys_n, values, decays, beta_rate, seg_ids
    )
    c = jnp.broadcast_to(tail[:, :, None, None], tail.shape + (1, w.shape[-1]))
    states, updates = state_recurrence(u0, w, kt, c)
    return jax.vmap(chunk_finish)(queries, carried, scores, states, updates)


def head_inputs(proj_query, proj_key, proj_value, proj_alpha, proj_beta,
                kernel_query, kernel_key, kernel_value, a_here, dt_here, seg_ids):
    queries = unit_norm(jax.nn.silu(short_conv(proj_query, kernel_query, seg_ids))) * (
        1.0 / math.sqrt(proj_query.shape[1])
    )
    keys_n = unit_norm(jax.nn.silu(short_conv(proj_key, kernel_key, seg_ids)))
    values = jax.nn.silu(short_conv(proj_value, kernel_value, seg_ids))
    decays = -jnp.exp(a_here) * jax.nn.softplus(proj_alpha + dt_here)
    beta_rate = jax.nn.sigmoid(proj_beta)
    return queries, keys_n, values, decays, beta_rate


def head_output(recurrent, proj_gate, o_gain, live_mask):
    return rms_norm(recurrent, o_gain, o_floor) * jax.nn.silu(proj_gate) * live_mask[:, None]


def local_mixer(
    proj_query,
    proj_key,
    proj_value,
    proj_gate,
    proj_alpha,
    proj_beta,
    kernel_query,
    kernel_key,
    kernel_value,
    a_here,
    dt_here,
    o_gain,
    seg_ids=None,
    live_mask=None,
):
    row_count = proj_query.shape[0]
    heads_here = proj_alpha.shape[1]

    def by_head(array):
        return jnp.moveaxis(array.reshape(row_count, heads_here, -1), 1, 0)

    def kernel_heads(kernel):
        return jnp.moveaxis(kernel.reshape(kernel.shape[0], heads_here, -1), 1, 0)

    queries, keys_n, values, decays, beta_rate = jax.vmap(
        head_inputs, in_axes=(0,) * 10 + (None,)
    )(
        by_head(proj_query),
        by_head(proj_key),
        by_head(proj_value),
        proj_alpha.T,
        proj_beta.T,
        kernel_heads(kernel_query),
        kernel_heads(kernel_key),
        kernel_heads(kernel_value),
        a_here,
        dt_here,
        seg_ids,
    )
    recurrent = delta_rule(queries, keys_n, values, decays, beta_rate, seg_ids)
    mixed_heads = jax.vmap(head_output, in_axes=(0, 0, None, None))(
        recurrent, by_head(proj_gate), o_gain, live_mask
    )
    return jnp.moveaxis(mixed_heads, 0, 1).reshape(row_count, -1)


MESH_ID = pl.DeviceIdType.MESH


def _ring_position(h, major, minor):
    a = h // minor
    b = h % minor
    return b * major + a + (b % 2) * (major - 1 - 2 * a)


def _ring_member(q, major, minor):
    count = major * minor
    q = (q + count) % count
    b = q // major
    r = q % major
    return (r + (b % 2) * (major - 1 - 2 * r)) * minor + b


def _ring_sides(major, minor):
    p = _ring_position(lax.axis_index("head"), major, minor)
    return p, _ring_member(p + 1, major, minor), _ring_member(p - 1, major, minor)


def _greet(nxt, prv, row):
    barrier = pltpu.get_barrier_semaphore()
    pl.semaphore_signal(barrier, 1, device_id=(prv, row), device_id_type=MESH_ID)
    pl.semaphore_signal(barrier, 1, device_id=(nxt, row), device_id_type=MESH_ID)
    pl.semaphore_wait(barrier, 2)


def _ring_gather_kernel(major, minor, x_ref, out_ref, send_sem, recv_sem):
    count = major * minor
    blk = x_ref.shape[0]
    half = blk // 2
    row = lax.axis_index("row")
    p, nxt, prv = _ring_sides(major, minor)
    out_ref[pl.ds(pl.multiple_of(lax.axis_index("head") * blk, blk), blk), :] = x_ref[...]
    _greet(nxt, prv, row)

    def piece(pos, off):
        return out_ref.at[pl.ds(pl.multiple_of(_ring_member(pos, major, minor) * blk + off, half), half)]

    def outgoing(d, s):
        pos = p - s if d == 0 else p + s
        target = nxt if d == 0 else prv
        ref = piece(pos, d * half)
        return pltpu.make_async_remote_copy(
            ref, ref, send_sem.at[d, s], recv_sem.at[d, s], device_id=(target, row),
            device_id_type=MESH_ID,
        )

    def incoming(d, s):
        pos = p - 1 - s if d == 0 else p + 1 + s
        source = prv if d == 0 else nxt
        ref = piece(pos, d * half)
        return pltpu.make_async_remote_copy(
            ref, ref, send_sem.at[d, s], recv_sem.at[d, s], device_id=(source, row),
            device_id_type=MESH_ID,
        )

    for s in range(count - 1):
        for d in (0, 1):
            if s > 0:
                incoming(d, s - 1).wait_recv()
            outgoing(d, s).start()
    for d in (0, 1):
        incoming(d, count - 2).wait_recv()
    for s in range(count - 1):
        for d in (0, 1):
            outgoing(d, s).wait_send()


def _ring_scatter_kernel(major, minor, y_ref, out_ref, buf, send_sem, recv_sem):
    count = major * minor
    blk = out_ref.shape[0]
    half = blk // 2
    row = lax.axis_index("row")
    p, nxt, prv = _ring_sides(major, minor)
    _greet(nxt, prv, row)

    def piece(pos, off):
        return y_ref.at[pl.ds(pl.multiple_of(_ring_member(pos, major, minor) * blk + off, half), half)]

    def outgoing(d, s):
        pos = p - s - 1 if d == 0 else p + s + 1
        target = nxt if d == 0 else prv
        source = piece(pos, d * half) if s == 0 else buf.at[d, s - 1]
        return pltpu.make_async_remote_copy(
            source, buf.at[d, s], send_sem.at[d, s], recv_sem.at[d, s],
            device_id=(target, row), device_id_type=MESH_ID,
        )

    def incoming(d, s):
        source = prv if d == 0 else nxt
        return pltpu.make_async_remote_copy(
            buf.at[d, s], buf.at[d, s], send_sem.at[d, s], recv_sem.at[d, s],
            device_id=(source, row), device_id_type=MESH_ID,
        )

    for s in range(count - 1):
        for d in (0, 1):
            if s > 0:
                incoming(d, s - 1).wait_recv()
                pos = p - s - 1 if d == 0 else p + s + 1
                buf[d, s - 1] = (
                    buf[d, s - 1].astype(jnp.float32)
                    + piece(pos, d * half)[...].astype(jnp.float32)
                ).astype(buf.dtype)
            outgoing(d, s).start()
    for d in (0, 1):
        incoming(d, count - 2).wait_recv()
        out_ref[pl.ds(d * half, half), :] = piece(p, d * half)[...].astype(
            jnp.float32
        ) + buf[d, count - 2].astype(jnp.float32)
    for s in range(count - 1):
        for d in (0, 1):
            outgoing(d, s).wait_send()


def ring_gather(x, ring, collective):
    major, minor = ring
    count = major * minor
    blk, width = x.shape
    return pl.pallas_call(
        partial(_ring_gather_kernel, major, minor),
        out_shape=jax.ShapeDtypeStruct((count * blk, width), x.dtype),
        in_specs=[pl.BlockSpec(memory_space=pltpu.VMEM)],
        out_specs=pl.BlockSpec(memory_space=pltpu.VMEM),
        scratch_shapes=[
            pltpu.SemaphoreType.DMA((2, count - 1)),
            pltpu.SemaphoreType.DMA((2, count - 1)),
        ],
        compiler_params=pltpu.CompilerParams(collective_id=collective, has_side_effects=True),
        name="ring_gather_head",
    )(x)


def ring_scatter(y, ring, collective):
    major, minor = ring
    count = major * minor
    rows, width = y.shape
    blk = rows // count
    return pl.pallas_call(
        partial(_ring_scatter_kernel, major, minor),
        out_shape=jax.ShapeDtypeStruct((blk, width), jnp.float32),
        in_specs=[pl.BlockSpec(memory_space=pltpu.VMEM)],
        out_specs=pl.BlockSpec(memory_space=pltpu.VMEM),
        scratch_shapes=[
            pltpu.VMEM((2, count - 1, blk // 2, width), y.dtype),
            pltpu.SemaphoreType.DMA((2, count - 1)),
            pltpu.SemaphoreType.DMA((2, count - 1)),
        ],
        compiler_params=pltpu.CompilerParams(collective_id=collective, has_side_effects=True),
        name="ring_scatter_head",
    )(y)


def head_ring(mesh):
    count = mesh.shape["head"]
    try:
        spots = [tuple(device.coords) for device in mesh.devices[:, 0]]
    except (AttributeError, TypeError):
        return (count, 1)
    moving = [axis for axis in range(len(spots[0])) if spots[0][axis] != spots[1][axis]]
    if len(moving) != 1:
        return (count, 1)
    minor = len({spot[moving[0]] for spot in spots})
    if count % minor or minor % 2:
        return (count, 1)
    return (count // minor, minor)


def contract_rows(left, right):
    return lax.dot_general(
        left, right, (((0,), (0,)), ((), ())), preferred_element_type=jnp.float32
    )


def contract_cols(left, right):
    return lax.dot_general(
        left, right, (((1,), (1,)), ((), ())), preferred_element_type=jnp.float32
    )


def on_device(
    ring,
    tokens,
    w_query,
    w_key,
    w_value,
    w_outgate,
    w_alpha,
    w_beta,
    conv_query,
    conv_key,
    conv_value,
    a_log,
    dt_bias,
    o_gain,
    w_out,
    gain_in,
    gain_ffn,
    w_gate,
    w_up,
    w_down,
    segments,
    valid_len,
    cotangent,
):
    residual = tokens[0].astype(jnp.float32)
    heads_here = w_alpha.shape[1]
    head_first = lax.axis_index("head") * heads_here
    norm_one, pull_one = jax.vjp(rms_norm, residual, gain_in)
    normed_one = norm_one.astype(jnp.bfloat16)
    row_count = lax.psum(1, "row")
    w_local = jnp.concatenate(
        [w_query, w_key, w_value, w_outgate, w_alpha, w_beta], axis=1
    ).astype(jnp.bfloat16)
    edges = [0]
    for member in (w_query, w_key, w_value, w_outgate, w_alpha, w_beta):
        edges.append(edges[-1] + member.shape[1])
    w_inward = lax.all_gather(w_local, "row", axis=0, tiled=True)
    conv_local = jnp.concatenate([conv_query, conv_key, conv_value], axis=1).astype(jnp.bfloat16)
    conv_edges = [0, conv_query.shape[1], conv_query.shape[1] + conv_key.shape[1], conv_local.shape[1]]
    conv_all = lax.all_gather(conv_local, "row", axis=1, tiled=True).reshape(
        conv_local.shape[0], row_count, conv_local.shape[1]
    )
    conv_parts = [
        conv_all[:, :, conv_edges[i] : conv_edges[i + 1]].reshape(conv_local.shape[0], -1)
        for i in range(3)
    ]
    out_matrix = lax.all_gather(w_out.astype(jnp.bfloat16), "row", axis=1, tiled=True)
    ff_width = w_gate.shape[1]
    ffn_local = jnp.concatenate([w_gate, w_up], axis=1).astype(jnp.bfloat16)
    down_local = w_down.T.astype(jnp.bfloat16)
    grad_out = cotangent[0]
    grad_out_rows = lax.all_gather(grad_out, "row", axis=0, tiled=True)
    all_rows = ring_gather(normed_one, ring, 0)
    all_rows, out_matrix, ffn_local = lax.optimization_barrier((all_rows, out_matrix, ffn_local))
    ffn_all = lax.all_gather(ffn_local, "head", axis=0, tiled=True)
    projected = jnp.dot(all_rows, w_inward, preferred_element_type=jnp.float32)
    proj_parts = [projected[:, edges[spot] : edges[spot + 1]] for spot in range(6)]
    seg_ids = segments[0]
    live_mask = (jnp.arange(seg_ids.shape[0]) < valid_len[0]).astype(jnp.float32)
    a_here = lax.dynamic_slice_in_dim(a_log, head_first, heads_here)
    dt_here = lax.dynamic_slice_in_dim(dt_bias, head_first, heads_here)
    mixer_fn = partial(local_mixer, seg_ids=seg_ids, live_mask=live_mask)
    mixed, pull_core = jax.vjp(
        mixer_fn,
        proj_parts[0],
        proj_parts[1],
        proj_parts[2],
        proj_parts[3],
        proj_parts[4],
        proj_parts[5],
        conv_parts[0].astype(jnp.float32),
        conv_parts[1].astype(jnp.float32),
        conv_parts[2].astype(jnp.float32),
        a_here,
        dt_here,
        o_gain,
    )
    mixed, ffn_all, grad_out_rows, down_local = lax.optimization_barrier(
        (mixed, ffn_all, grad_out_rows, down_local)
    )
    w_down_t = ring_gather(down_local, ring, 4)
    w_gate_all = ffn_all[:, :ff_width]
    w_up_all = ffn_all[:, ff_width : 2 * ff_width]
    mixed_half = mixed.astype(jnp.bfloat16)
    mixer_output = ring_scatter(
        jnp.dot(mixed_half, out_matrix, preferred_element_type=jnp.float32).astype(jnp.bfloat16),
        ring,
        1,
    )
    middle = residual + mixer_output
    norm_two, pull_two = jax.vjp(rms_norm, middle, gain_ffn)
    normed_two = norm_two.astype(jnp.bfloat16)
    ffn_inputs = lax.all_gather(normed_two, "row", axis=0, tiled=True)
    gate_pre = jnp.dot(ffn_inputs, w_gate_all, preferred_element_type=jnp.float32)
    up_pre = jnp.dot(ffn_inputs, w_up_all, preferred_element_type=jnp.float32)
    hidden_val, pull_act = jax.vjp(swiglu, gate_pre, up_pre)
    hidden_half = hidden_val.astype(jnp.bfloat16)
    ffn_partial = contract_cols(hidden_half, w_down_t).astype(jnp.bfloat16)
    grad_hidden = jnp.dot(grad_out_rows, w_down_t, preferred_element_type=jnp.float32)
    grad_down_t = contract_rows(grad_out_rows, hidden_half)
    grad_gate_f, grad_up_f = pull_act(grad_hidden)
    grad_gate = grad_gate_f.astype(jnp.bfloat16)
    grad_upper = grad_up_f.astype(jnp.bfloat16)
    grad_wgate = contract_rows(ffn_inputs, grad_gate)
    grad_wup = contract_rows(ffn_inputs, grad_upper)
    grad_norm_two = lax.psum_scatter(
        (contract_cols(grad_gate, w_gate_all) + contract_cols(grad_upper, w_up_all)).astype(
            jnp.bfloat16
        ),
        "row",
        scatter_dimension=0,
        tiled=True,
    ).astype(jnp.float32)
    grad_mid_part, grad_gain_ffn = pull_two(grad_norm_two)
    grad_middle = grad_out.astype(jnp.float32) + grad_mid_part
    ffn_grad_cat = jnp.concatenate([grad_wgate, grad_wup, grad_down_t], axis=1).astype(
        jnp.bfloat16
    )
    grad_mid_half = grad_middle.astype(jnp.bfloat16)
    grad_mid_rows = ring_gather(grad_mid_half, ring, 2)
    ffn_output = lax.psum_scatter(ffn_partial, "row", scatter_dimension=0, tiled=True)
    grad_mid_rows, ffn_grad_cat = lax.optimization_barrier((grad_mid_rows, ffn_grad_cat))
    ffn_grad_all = lax.psum_scatter(ffn_grad_cat, "head", scatter_dimension=0, tiled=True)
    grad_mixed = contract_cols(grad_mid_rows, out_matrix)
    grad_wout = contract_rows(mixed_half, grad_mid_rows).astype(jnp.bfloat16)
    wout_grad = lax.psum_scatter(grad_wout, "row", scatter_dimension=1, tiled=True)
    core_grads = pull_core(grad_mixed)
    core_grads, ffn_output = lax.optimization_barrier((core_grads, ffn_output))
    final_out = (middle + ffn_output.astype(jnp.float32)).astype(jnp.bfloat16)
    grad_proj = jnp.concatenate(
        [core_grads[0], core_grads[1], core_grads[2], core_grads[3], core_grads[4], core_grads[5]],
        axis=1,
    ).astype(jnp.bfloat16)
    grad_inward = contract_rows(all_rows, grad_proj).astype(jnp.bfloat16)
    grad_inward, ffn_grad_all = lax.optimization_barrier((grad_inward, ffn_grad_all))
    ffn_grad_all = ffn_grad_all.astype(jnp.float32)
    ffn_grads = (
        ffn_grad_all[:, :ff_width],
        ffn_grad_all[:, ff_width : 2 * ff_width],
        ffn_grad_all[:, 2 * ff_width :].T,
    )
    grad_norm_one = ring_scatter(contract_cols(grad_proj, w_inward).astype(jnp.bfloat16), ring, 3)
    grad_norm_one, wout_grad = lax.optimization_barrier((grad_norm_one, wout_grad))
    grad_in_part, grad_gain_in = pull_one(grad_norm_one)
    grad_input = grad_middle + grad_in_part
    inward_all = lax.psum_scatter(
        grad_inward, "row", scatter_dimension=0, tiled=True
    ).astype(jnp.float32)
    conv_grad_local = jnp.concatenate(
        [
            core_grads[6 + i].reshape(conv_local.shape[0], row_count, -1)
            for i in range(3)
        ],
        axis=2,
    ).reshape(conv_local.shape[0], -1)
    conv_grad = lax.psum_scatter(
        conv_grad_local.astype(jnp.bfloat16), "row", scatter_dimension=1, tiled=True
    ).astype(jnp.float32)
    mixer_grads = tuple(inward_all[:, edges[spot] : edges[spot + 1]] for spot in range(6)) + tuple(
        conv_grad[:, conv_edges[i] : conv_edges[i + 1]] for i in range(3)
    ) + (wout_grad.astype(jnp.float32),)
    head_total = a_log.shape[0]
    grad_a_full = lax.dynamic_update_slice_in_dim(
        jnp.zeros((head_total,), jnp.float32), core_grads[9], head_first, 0
    )
    grad_dt_full = lax.dynamic_update_slice_in_dim(
        jnp.zeros((head_total,), jnp.float32), core_grads[10], head_first, 0
    )
    small_sums = lax.psum(
        (grad_gain_in, grad_gain_ffn, core_grads[11], grad_a_full, grad_dt_full), ("head", "row")
    )
    return (
        final_out[None],
        grad_input[None],
        mixer_grads[0],
        mixer_grads[1],
        mixer_grads[2],
        mixer_grads[3],
        mixer_grads[4],
        mixer_grads[5],
        mixer_grads[6],
        mixer_grads[7],
        mixer_grads[8],
        small_sums[3],
        small_sums[4],
        small_sums[2],
        mixer_grads[9],
        small_sums[0],
        small_sums[1],
        ffn_grads[0],
        ffn_grads[1],
        ffn_grads[2],
    )


def solution(mesh):
    return jax.shard_map(
        partial(on_device, head_ring(mesh)),
        mesh=mesh,
        in_specs=(
            P("row", "head", None),
            P("row", "head"),
            P("row", "head"),
            P("row", "head"),
            P("row", "head"),
            P("row", "head"),
            P("row", "head"),
            P(None, ("head", "row")),
            P(None, ("head", "row")),
            P(None, ("head", "row")),
            P(),
            P(),
            P(),
            P("head", "row"),
            P(),
            P(),
            P("head", "row"),
            P("head", "row"),
            P("row", "head"),
            P("row", None),
            P("row"),
            P("row", "head", None),
        ),
        out_specs=(
            P("row", "head", None),
            P("row", "head", None),
            P("row", "head"),
            P("row", "head"),
            P("row", "head"),
            P("row", "head"),
            P("row", "head"),
            P("row", "head"),
            P(None, ("head", "row")),
            P(None, ("head", "row")),
            P(None, ("head", "row")),
            P(),
            P(),
            P(),
            P("head", "row"),
            P(),
            P(),
            P("head", "row"),
            P("head", "row"),
            P("row", "head"),
        ),
        check_vma=False,
    )
```

```python
from functools import partial
import math

import jax
import jax.numpy as jnp
from jax import lax
from jax.sharding import PartitionSpec as P
from jax.experimental import pallas as pl
from jax.experimental.pallas import tpu as pltpu

BLOCK = 64


precise = lax.Precision.HIGHEST
epsilon = 1e-06
o_floor = 0.001


def rms_norm(vector, gain_vec, floor_add=epsilon):
    return (
        vector * lax.rsqrt(jnp.mean(vector * vector, axis=-1, keepdims=True) + floor_add) * gain_vec
    )


def unit_norm(vector):
    return vector * lax.rsqrt(jnp.sum(vector * vector, axis=-1, keepdims=True) + epsilon)


def swiglu(gate_pre, up_pre):
    return jax.nn.silu(gate_pre) * up_pre


def short_conv(signal, kernel, seg_ids):
    tap_count = kernel.shape[0]
    length = signal.shape[0]
    summed = signal * kernel[tap_count - 1]
    for offset in range(1, tap_count):
        shifted = jnp.concatenate(
            [jnp.zeros((offset, signal.shape[1]), signal.dtype), signal[: length - offset]], axis=0
        )
        seg_shift = jnp.concatenate(
            [jnp.full((offset,), -1, jnp.int32), seg_ids[: length - offset]]
        )
        keep_mask = (seg_shift == seg_ids).astype(signal.dtype)
        summed = summed + shifted * kernel[tap_count - 1 - offset] * keep_mask[:, None]
    return summed


def _recur_fwd_kernel(nb, u0_ref, w_ref, kt_ref, c_ref, s_out, u_out, s_scr):
    @pl.when(pl.program_id(1) == 0)
    def _():
        s_scr[...] = jnp.zeros_like(s_scr)

    def step(j, carry):
        state = s_scr[...]
        s_out[0, j] = state
        update = u0_ref[0, j] - lax.dot_general(
            w_ref[0, j], state, (((1,), (1,)), ((), ())),
            precision=precise, preferred_element_type=jnp.float32,
        )
        u_out[0, j] = update
        s_scr[...] = c_ref[0, j] * state + lax.dot_general(
            update, kt_ref[0, j], (((0,), (0,)), ((), ())),
            precision=precise, preferred_element_type=jnp.float32,
        )
        return carry

    lax.fori_loop(0, nb, step, 0)


def _recur_bwd_kernel(
    nb, s_ref, u_ref, w_ref, kt_ref, c_ref, ds_ref, du_ref,
    du0_out, dw_out, dkt_out, dc_out, g_scr,
):
    @pl.when(pl.program_id(1) == 0)
    def _():
        g_scr[...] = jnp.zeros_like(g_scr)

    def step(i, carry):
        j = nb - 1 - i
        grad_state = g_scr[...]
        state = s_ref[0, j]
        grad_update = du_ref[0, j] + lax.dot_general(
            kt_ref[0, j], grad_state, (((1,), (1,)), ((), ())),
            precision=precise, preferred_element_type=jnp.float32,
        )
        dkt_out[0, j] = jnp.dot(
            u_ref[0, j], grad_state, precision=precise, preferred_element_type=jnp.float32
        )
        dc_out[0, j] = jnp.sum(grad_state * state, axis=0, keepdims=True)
        du0_out[0, j] = grad_update
        dw_out[0, j] = -jnp.dot(
            grad_update, state, precision=precise, preferred_element_type=jnp.float32
        )
        g_scr[...] = (
            c_ref[0, j] * grad_state
            - lax.dot_general(
                grad_update, w_ref[0, j], (((0,), (0,)), ((), ())),
                precision=precise, preferred_element_type=jnp.float32,
            )
            + ds_ref[0, j]
        )
        return carry

    lax.fori_loop(0, nb, step, 0)


def _chunk_spec(nb, tail, reverse, count):
    if reverse:
        return pl.BlockSpec((1, nb) + tail, lambda h, b: (h, count - 1 - b, 0, 0))
    return pl.BlockSpec((1, nb) + tail, lambda h, b: (h, b, 0, 0))


def _recur_forward(u0, w, kt, c):
    heads, count, chunk, dv = u0.shape
    dk = w.shape[-1]
    nb = min(8, count)
    blocks = count // nb
    flops = 4 * heads * count * chunk * dk * dv * 6
    moved = 4 * heads * count * (2 * chunk * dv + 2 * chunk * dk + dv * dk)
    return pl.pallas_call(
        partial(_recur_fwd_kernel, nb),
        grid=(heads, blocks),
        in_specs=[
            _chunk_spec(nb, (chunk, dv), False, blocks),
            _chunk_spec(nb, (chunk, dk), False, blocks),
            _chunk_spec(nb, (chunk, dk), False, blocks),
            _chunk_spec(nb, (1, dk), False, blocks),
        ],
        out_specs=[
            _chunk_spec(nb, (dv, dk), False, blocks),
            _chunk_spec(nb, (chunk, dv), False, blocks),
        ],
        out_shape=[
            jax.ShapeDtypeStruct((heads, count, dv, dk), jnp.float32),
            jax.ShapeDtypeStruct((heads, count, chunk, dv), jnp.float32),
        ],
        scratch_shapes=[pltpu.VMEM((dv, dk), jnp.float32)],
        compiler_params=pltpu.CompilerParams(dimension_semantics=("arbitrary", "arbitrary")),
        cost_estimate=pl.CostEstimate(flops=flops, transcendentals=0, bytes_accessed=moved),
        name="delta_state_forward",
    )(u0, w, kt, c)


def _recur_backward(states, updates, w, kt, c, d_states, d_updates):
    heads, count, chunk, dv = updates.shape
    dk = w.shape[-1]
    nb = min(8, count)
    blocks = count // nb
    flops = 8 * heads * count * chunk * dk * dv * 6
    moved = 4 * heads * count * (4 * chunk * dv + 4 * chunk * dk + 2 * dv * dk)
    return pl.pallas_call(
        partial(_recur_bwd_kernel, nb),
        grid=(heads, blocks),
        in_specs=[
            _chunk_spec(nb, (dv, dk), True, blocks),
            _chunk_spec(nb, (chunk, dv), True, blocks),
            _chunk_spec(nb, (chunk, dk), True, blocks),
            _chunk_spec(nb, (chunk, dk), True, blocks),
            _chunk_spec(nb, (1, dk), True, blocks),
            _chunk_spec(nb, (dv, dk), True, blocks),
            _chunk_spec(nb, (chunk, dv), True, blocks),
        ],
        out_specs=[
            _chunk_spec(nb, (chunk, dv), True, blocks),
            _chunk_spec(nb, (chunk, dk), True, blocks),
            _chunk_spec(nb, (chunk, dk), True, blocks),
            _chunk_spec(nb, (1, dk), True, blocks),
        ],
        out_shape=[
            jax.ShapeDtypeStruct((heads, count, chunk, dv), jnp.float32),
            jax.ShapeDtypeStruct((heads, count, chunk, dk), jnp.float32),
            jax.ShapeDtypeStruct((heads, count, chunk, dk), jnp.float32),
            jax.ShapeDtypeStruct((heads, count, 1, dk), jnp.float32),
        ],
        scratch_shapes=[pltpu.VMEM((dv, dk), jnp.float32)],
        compiler_params=pltpu.CompilerParams(dimension_semantics=("arbitrary", "arbitrary")),
        cost_estimate=pl.CostEstimate(flops=flops, transcendentals=0, bytes_accessed=moved),
        name="delta_state_backward",
    )(states, updates, w, kt, c, d_states, d_updates)


@jax.custom_vjp
def state_recurrence(u0, w, kt, c):
    return _recur_forward(u0, w, kt, c)


def _recurrence_fwd(u0, w, kt, c):
    states, updates = _recur_forward(u0, w, kt, c)
    return (states, updates), (states, updates, w, kt, c)


def _recurrence_bwd(saved, grads):
    states, updates, w, kt, c = saved
    d_states, d_updates = grads
    du0, dw, dkt, dc_lanes = _recur_backward(states, updates, w, kt, c, d_states, d_updates)
    return du0, dw, dkt, dc_lanes


state_recurrence.defvjp(_recurrence_fwd, _recurrence_bwd)


def _unit_lower_inverse_small(system):
    size = system.shape[-1]
    strict = system - jnp.eye(size, dtype=system.dtype)
    power = -strict
    inverse = jnp.eye(size, dtype=system.dtype) + power
    done = 2
    while done < size:
        power = jnp.matmul(power, power, precision=precise)
        inverse = inverse + jnp.matmul(power, inverse, precision=precise)
        done *= 2
    return inverse


def _unit_lower_inverse_forward(system):
    size = system.shape[-1]
    base = min(8, size)
    lead = system.shape[:-2]
    count = size // base
    blocks = system.reshape(lead + (count, base, count, base))
    diag = jnp.stack([blocks[..., i, :, i, :] for i in range(count)], axis=-3)
    inverse = _unit_lower_inverse_small(diag)
    width = base
    while width < size:
        pairs = inverse.shape[-3] // 2
        upper = inverse[..., 0::2, :, :]
        lower = inverse[..., 1::2, :, :]
        below = jnp.stack(
            [
                system[..., (2 * i + 1) * width : (2 * i + 2) * width, 2 * i * width : (2 * i + 1) * width]
                for i in range(pairs)
            ],
            axis=-3,
        )
        corner = -jnp.matmul(
            lower, jnp.matmul(below, upper, precision=precise), precision=precise
        )
        zeros = jnp.zeros_like(upper)
        top = jnp.concatenate([upper, zeros], axis=-1)
        bottom = jnp.concatenate([corner, lower], axis=-1)
        inverse = jnp.concatenate([top, bottom], axis=-2)
        width *= 2
    return inverse[..., 0, :, :]


@jax.custom_vjp
def unit_lower_inverse(system):
    return _unit_lower_inverse_forward(system)


def _inverse_fwd(system):
    inverse = _unit_lower_inverse_forward(system)
    return inverse, inverse


def _inverse_bwd(inverse, grad):
    size = inverse.shape[-1]
    flipped = jnp.swapaxes(inverse, -1, -2)
    full = -jnp.matmul(jnp.matmul(flipped, grad, precision=precise), flipped, precision=precise)
    places = jnp.arange(size)
    return (full * (places[:, None] > places[None, :]).astype(full.dtype),)


unit_lower_inverse.defvjp(_inverse_fwd, _inverse_bwd)


def chunk_prepare(queries, keys_n, values, decays, beta_rate, seg_ids):
    length, dk = keys_n.shape
    count = length // BLOCK
    q = queries.reshape(count, BLOCK, dk)
    k = keys_n.reshape(count, BLOCK, dk)
    v = values.reshape(count, BLOCK, values.shape[1])
    beta = beta_rate.reshape(count, BLOCK)
    seg = seg_ids.reshape(count, BLOCK)
    cumulative = jnp.cumsum(decays.reshape(count, BLOCK), axis=1)
    places = jnp.arange(BLOCK)
    lower_tri = places[:, None] >= places[None, :]
    inside = jnp.logical_and(seg[:, :, None] == seg[:, None, :], lower_tri)
    log_gap = jnp.where(inside, cumulative[:, :, None] - cumulative[:, None, :], 0.0)
    within = jnp.exp(log_gap) * inside.astype(jnp.float32)
    strict = within * (places[:, None] > places[None, :]).astype(jnp.float32)
    last_seg = jnp.concatenate([jnp.full((1,), -1, seg.dtype), seg[:-1, BLOCK - 1]])
    carried = jnp.exp(cumulative) * (seg == last_seg[:, None]).astype(jnp.float32)
    key_gram = jnp.einsum("nid,njd->nij", k, k, precision=precise)
    system = jnp.eye(BLOCK, dtype=jnp.float32) + beta[:, :, None] * strict * key_gram
    right_side = jnp.concatenate([beta[:, :, None] * v, (beta * carried)[:, :, None] * k], axis=2)
    solved = jnp.matmul(unit_lower_inverse(system), right_side, precision=precise)
    dv = v.shape[2]
    kt = within[:, BLOCK - 1, :, None] * k
    scores = jnp.einsum("nid,njd->nij", q, k, precision=precise) * within
    return solved[:, :, :dv], solved[:, :, dv:], kt, carried[:, BLOCK - 1], carried, scores


def chunk_finish(queries, carried, scores, states, updates):
    count = states.shape[0]
    q = queries.reshape(count, BLOCK, queries.shape[1])
    output = carried[:, :, None] * jnp.einsum(
        "nid,nvd->niv", q, states, precision=precise
    ) + jnp.einsum("nij,njv->niv", scores, updates, precision=precise)
    return output.reshape(count * BLOCK, states.shape[1])


def delta_rule(queries, keys_n, values, decays, beta_rate, seg_ids):
    u0, w, kt, tail, carried, scores = jax.vmap(chunk_prepare, in_axes=(0, 0, 0, 0, 0, None))(
        queries, keys_n, values, decays, beta_rate, seg_ids
    )
    c = jnp.broadcast_to(tail[:, :, None, None], tail.shape + (1, w.shape[-1]))
    states, updates = state_recurrence(u0, w, kt, c)
    return jax.vmap(chunk_finish)(queries, carried, scores, states, updates)


def head_inputs(proj_query, proj_key, proj_value, proj_alpha, proj_beta,
                kernel_query, kernel_key, kernel_value, a_here, dt_here, seg_ids):
    queries = unit_norm(jax.nn.silu(short_conv(proj_query, kernel_query, seg_ids))) * (
        1.0 / math.sqrt(proj_query.shape[1])
    )
    keys_n = unit_norm(jax.nn.silu(short_conv(proj_key, kernel_key, seg_ids)))
    values = jax.nn.silu(short_conv(proj_value, kernel_value, seg_ids))
    decays = -jnp.exp(a_here) * jax.nn.softplus(proj_alpha + dt_here)
    beta_rate = jax.nn.sigmoid(proj_beta)
    return queries, keys_n, values, decays, beta_rate


def head_output(recurrent, proj_gate, o_gain, live_mask):
    return rms_norm(recurrent, o_gain, o_floor) * jax.nn.silu(proj_gate) * live_mask[:, None]


def local_mixer(
    proj_query,
    proj_key,
    proj_value,
    proj_gate,
    proj_alpha,
    proj_beta,
    kernel_query,
    kernel_key,
    kernel_value,
    a_here,
    dt_here,
    o_gain,
    seg_ids=None,
    live_mask=None,
):
    row_count = proj_query.shape[0]
    heads_here = proj_alpha.shape[1]

    def by_head(array):
        return jnp.moveaxis(array.reshape(row_count, heads_here, -1), 1, 0)

    def kernel_heads(kernel):
        return jnp.moveaxis(kernel.reshape(kernel.shape[0], heads_here, -1), 1, 0)

    queries, keys_n, values, decays, beta_rate = jax.vmap(
        head_inputs, in_axes=(0,) * 10 + (None,)
    )(
        by_head(proj_query),
        by_head(proj_key),
        by_head(proj_value),
        proj_alpha.T,
        proj_beta.T,
        kernel_heads(kernel_query),
        kernel_heads(kernel_key),
        kernel_heads(kernel_value),
        a_here,
        dt_here,
        seg_ids,
    )
    recurrent = delta_rule(queries, keys_n, values, decays, beta_rate, seg_ids)
    mixed_heads = jax.vmap(head_output, in_axes=(0, 0, None, None))(
        recurrent, by_head(proj_gate), o_gain, live_mask
    )
    return jnp.moveaxis(mixed_heads, 0, 1).reshape(row_count, -1)


MESH_ID = pl.DeviceIdType.MESH


def _ring_position(h, major, minor):
    a = h // minor
    b = h % minor
    return b * major + a + (b % 2) * (major - 1 - 2 * a)


def _ring_member(q, major, minor):
    count = major * minor
    q = (q + count) % count
    b = q // major
    r = q % major
    return (r + (b % 2) * (major - 1 - 2 * r)) * minor + b


def _ring_sides(major, minor):
    p = _ring_position(lax.axis_index("head"), major, minor)
    return p, _ring_member(p + 1, major, minor), _ring_member(p - 1, major, minor)


def _greet(nxt, prv, row):
    barrier = pltpu.get_barrier_semaphore()
    pl.semaphore_signal(barrier, 1, device_id=(prv, row), device_id_type=MESH_ID)
    pl.semaphore_signal(barrier, 1, device_id=(nxt, row), device_id_type=MESH_ID)
    pl.semaphore_wait(barrier, 2)


def _ring_gather_kernel(major, minor, x_ref, out_ref, send_sem, recv_sem):
    count = major * minor
    blk = x_ref.shape[0]
    half = blk // 2
    row = lax.axis_index("row")
    p, nxt, prv = _ring_sides(major, minor)
    out_ref[pl.ds(pl.multiple_of(lax.axis_index("head") * blk, blk), blk), :] = x_ref[...]
    _greet(nxt, prv, row)

    def piece(pos, off):
        return out_ref.at[pl.ds(pl.multiple_of(_ring_member(pos, major, minor) * blk + off, half), half)]

    def outgoing(d, s):
        pos = p - s if d == 0 else p + s
        target = nxt if d == 0 else prv
        ref = piece(pos, d * half)
        return pltpu.make_async_remote_copy(
            ref, ref, send_sem.at[d, s], recv_sem.at[d, s], device_id=(target, row),
            device_id_type=MESH_ID,
        )

    def incoming(d, s):
        pos = p - 1 - s if d == 0 else p + 1 + s
        source = prv if d == 0 else nxt
        ref = piece(pos, d * half)
        return pltpu.make_async_remote_copy(
            ref, ref, send_sem.at[d, s], recv_sem.at[d, s], device_id=(source, row),
            device_id_type=MESH_ID,
        )

    for s in range(count - 1):
        for d in (0, 1):
            if s > 0:
                incoming(d, s - 1).wait_recv()
            outgoing(d, s).start()
    for d in (0, 1):
        incoming(d, count - 2).wait_recv()
    for s in range(count - 1):
        for d in (0, 1):
            outgoing(d, s).wait_send()


def _ring_scatter_kernel(major, minor, y_ref, out_ref, buf, send_sem, recv_sem):
    count = major * minor
    blk = out_ref.shape[0]
    half = blk // 2
    row = lax.axis_index("row")
    p, nxt, prv = _ring_sides(major, minor)
    _greet(nxt, prv, row)

    def piece(pos, off):
        return y_ref.at[pl.ds(pl.multiple_of(_ring_member(pos, major, minor) * blk + off, half), half)]

    def outgoing(d, s):
        pos = p - s - 1 if d == 0 else p + s + 1
        target = nxt if d == 0 else prv
        source = piece(pos, d * half) if s == 0 else buf.at[d, s - 1]
        return pltpu.make_async_remote_copy(
            source, buf.at[d, s], send_sem.at[d, s], recv_sem.at[d, s],
            device_id=(target, row), device_id_type=MESH_ID,
        )

    def incoming(d, s):
        source = prv if d == 0 else nxt
        return pltpu.make_async_remote_copy(
            buf.at[d, s], buf.at[d, s], send_sem.at[d, s], recv_sem.at[d, s],
            device_id=(source, row), device_id_type=MESH_ID,
        )

    for s in range(count - 1):
        for d in (0, 1):
            if s > 0:
                incoming(d, s - 1).wait_recv()
                pos = p - s - 1 if d == 0 else p + s + 1
                buf[d, s - 1] = (
                    buf[d, s - 1].astype(jnp.float32)
                    + piece(pos, d * half)[...].astype(jnp.float32)
                ).astype(buf.dtype)
            outgoing(d, s).start()
    for d in (0, 1):
        incoming(d, count - 2).wait_recv()
        out_ref[pl.ds(d * half, half), :] = piece(p, d * half)[...].astype(
            jnp.float32
        ) + buf[d, count - 2].astype(jnp.float32)
    for s in range(count - 1):
        for d in (0, 1):
            outgoing(d, s).wait_send()


def ring_gather(x, ring, collective):
    major, minor = ring
    count = major * minor
    blk, width = x.shape
    return pl.pallas_call(
        partial(_ring_gather_kernel, major, minor),
        out_shape=jax.ShapeDtypeStruct((count * blk, width), x.dtype),
        in_specs=[pl.BlockSpec(memory_space=pltpu.VMEM)],
        out_specs=pl.BlockSpec(memory_space=pltpu.VMEM),
        scratch_shapes=[
            pltpu.SemaphoreType.DMA((2, count - 1)),
            pltpu.SemaphoreType.DMA((2, count - 1)),
        ],
        compiler_params=pltpu.CompilerParams(collective_id=collective, has_side_effects=True),
        name="ring_gather_head",
    )(x)


def ring_scatter(y, ring, collective):
    major, minor = ring
    count = major * minor
    rows, width = y.shape
    blk = rows // count
    return pl.pallas_call(
        partial(_ring_scatter_kernel, major, minor),
        out_shape=jax.ShapeDtypeStruct((blk, width), jnp.float32),
        in_specs=[pl.BlockSpec(memory_space=pltpu.VMEM)],
        out_specs=pl.BlockSpec(memory_space=pltpu.VMEM),
        scratch_shapes=[
            pltpu.VMEM((2, count - 1, blk // 2, width), y.dtype),
            pltpu.SemaphoreType.DMA((2, count - 1)),
            pltpu.SemaphoreType.DMA((2, count - 1)),
        ],
        compiler_params=pltpu.CompilerParams(collective_id=collective, has_side_effects=True),
        name="ring_scatter_head",
    )(y)


def head_ring(mesh):
    count = mesh.shape["head"]
    try:
        spots = [tuple(device.coords) for device in mesh.devices[:, 0]]
    except (AttributeError, TypeError):
        return (count, 1)
    moving = [axis for axis in range(len(spots[0])) if spots[0][axis] != spots[1][axis]]
    if len(moving) != 1:
        return (count, 1)
    minor = len({spot[moving[0]] for spot in spots})
    if count % minor or minor % 2:
        return (count, 1)
    return (count // minor, minor)


def contract_rows(left, right):
    return lax.dot_general(
        left, right, (((0,), (0,)), ((), ())), preferred_element_type=jnp.float32
    )


def contract_cols(left, right):
    return lax.dot_general(
        left, right, (((1,), (1,)), ((), ())), preferred_element_type=jnp.float32
    )


def on_device(
    ring,
    tokens,
    w_query,
    w_key,
    w_value,
    w_outgate,
    w_alpha,
    w_beta,
    conv_query,
    conv_key,
    conv_value,
    a_log,
    dt_bias,
    o_gain,
    w_out,
    gain_in,
    gain_ffn,
    w_gate,
    w_up,
    w_down,
    segments,
    valid_len,
    cotangent,
):
    residual = tokens[0].astype(jnp.float32)
    heads_here = w_alpha.shape[1]
    head_first = lax.axis_index("head") * heads_here
    norm_one, pull_one = jax.vjp(rms_norm, residual, gain_in)
    normed_one = norm_one.astype(jnp.bfloat16)
    row_count = lax.psum(1, "row")
    w_local = jnp.concatenate(
        [w_query, w_key, w_value, w_outgate, w_alpha, w_beta], axis=1
    ).astype(jnp.bfloat16)
    edges = [0]
    for member in (w_query, w_key, w_value, w_outgate, w_alpha, w_beta):
        edges.append(edges[-1] + member.shape[1])
    w_inward = lax.all_gather(w_local, "row", axis=0, tiled=True)
    conv_local = jnp.concatenate([conv_query, conv_key, conv_value], axis=1).astype(jnp.bfloat16)
    conv_edges = [0, conv_query.shape[1], conv_query.shape[1] + conv_key.shape[1], conv_local.shape[1]]
    conv_all = lax.all_gather(conv_local, "row", axis=1, tiled=True).reshape(
        conv_local.shape[0], row_count, conv_local.shape[1]
    )
    conv_parts = [
        conv_all[:, :, conv_edges[i] : conv_edges[i + 1]].reshape(conv_local.shape[0], -1)
        for i in range(3)
    ]
    out_matrix = lax.all_gather(w_out.astype(jnp.bfloat16), "row", axis=1, tiled=True)
    ff_width = w_gate.shape[1]
    ffn_local = jnp.concatenate([w_gate, w_up], axis=1).astype(jnp.bfloat16)
    down_local = w_down.T.astype(jnp.bfloat16)
    grad_out = cotangent[0]
    grad_out_rows = lax.all_gather(grad_out, "row", axis=0, tiled=True)
    all_rows = ring_gather(normed_one, ring, 0)
    all_rows, out_matrix, ffn_local, down_local = lax.optimization_barrier(
        (all_rows, out_matrix, ffn_local, down_local)
    )
    ffn_all = lax.all_gather(ffn_local, "head", axis=0, tiled=True)
    down_all = lax.all_gather(down_local, "head", axis=0, tiled=True)
    projected = jnp.dot(all_rows, w_inward, preferred_element_type=jnp.float32)
    proj_parts = [projected[:, edges[spot] : edges[spot + 1]] for spot in range(6)]
    seg_ids = segments[0]
    live_mask = (jnp.arange(seg_ids.shape[0]) < valid_len[0]).astype(jnp.float32)
    a_here = lax.dynamic_slice_in_dim(a_log, head_first, heads_here)
    dt_here = lax.dynamic_slice_in_dim(dt_bias, head_first, heads_here)
    mixer_fn = partial(local_mixer, seg_ids=seg_ids, live_mask=live_mask)
    mixed, pull_core = jax.vjp(
        mixer_fn,
        proj_parts[0],
        proj_parts[1],
        proj_parts[2],
        proj_parts[3],
        proj_parts[4],
        proj_parts[5],
        conv_parts[0].astype(jnp.float32),
        conv_parts[1].astype(jnp.float32),
        conv_parts[2].astype(jnp.float32),
        a_here,
        dt_here,
        o_gain,
    )
    mixed, ffn_all, grad_out_rows, w_down_t = lax.optimization_barrier(
        (mixed, ffn_all, grad_out_rows, down_all)
    )
    w_gate_all = ffn_all[:, :ff_width]
    w_up_all = ffn_all[:, ff_width : 2 * ff_width]
    mixed_half = mixed.astype(jnp.bfloat16)
    mixer_output = ring_scatter(
        jnp.dot(mixed_half, out_matrix, preferred_element_type=jnp.float32).astype(jnp.bfloat16),
        ring,
        1,
    )
    middle = residual + mixer_output
    norm_two, pull_two = jax.vjp(rms_norm, middle, gain_ffn)
    normed_two = norm_two.astype(jnp.bfloat16)
    ffn_inputs = lax.all_gather(normed_two, "row", axis=0, tiled=True)
    gate_pre = jnp.dot(ffn_inputs, w_gate_all, preferred_element_type=jnp.float32)
    up_pre = jnp.dot(ffn_inputs, w_up_all, preferred_element_type=jnp.float32)
    hidden_val, pull_act = jax.vjp(swiglu, gate_pre, up_pre)
    hidden_half = hidden_val.astype(jnp.bfloat16)
    ffn_partial = contract_cols(hidden_half, w_down_t).astype(jnp.bfloat16)
    grad_hidden = jnp.dot(grad_out_rows, w_down_t, preferred_element_type=jnp.float32)
    grad_down_t = contract_rows(grad_out_rows, hidden_half)
    grad_gate_f, grad_up_f = pull_act(grad_hidden)
    grad_gate = grad_gate_f.astype(jnp.bfloat16)
    grad_upper = grad_up_f.astype(jnp.bfloat16)
    grad_wgate = contract_rows(ffn_inputs, grad_gate)
    grad_wup = contract_rows(ffn_inputs, grad_upper)
    grad_norm_two = lax.psum_scatter(
        (contract_cols(grad_gate, w_gate_all) + contract_cols(grad_upper, w_up_all)).astype(
            jnp.bfloat16
        ),
        "row",
        scatter_dimension=0,
        tiled=True,
    ).astype(jnp.float32)
    grad_mid_part, grad_gain_ffn = pull_two(grad_norm_two)
    grad_middle = grad_out.astype(jnp.float32) + grad_mid_part
    ffn_grad_cat = jnp.concatenate([grad_wgate, grad_wup, grad_down_t], axis=1).astype(
        jnp.bfloat16
    )
    grad_mid_half = grad_middle.astype(jnp.bfloat16)
    grad_mid_rows = ring_gather(grad_mid_half, ring, 2)
    ffn_output = lax.psum_scatter(ffn_partial, "row", scatter_dimension=0, tiled=True)
    grad_mid_rows, ffn_grad_cat = lax.optimization_barrier((grad_mid_rows, ffn_grad_cat))
    ffn_grad_all = lax.psum_scatter(ffn_grad_cat, "head", scatter_dimension=0, tiled=True)
    grad_mixed = contract_cols(grad_mid_rows, out_matrix)
    grad_wout = contract_rows(mixed_half, grad_mid_rows).astype(jnp.bfloat16)
    wout_grad = lax.psum_scatter(grad_wout, "row", scatter_dimension=1, tiled=True)
    core_grads = pull_core(grad_mixed)
    core_grads, ffn_output = lax.optimization_barrier((core_grads, ffn_output))
    final_out = (middle + ffn_output.astype(jnp.float32)).astype(jnp.bfloat16)
    grad_proj = jnp.concatenate(
        [core_grads[0], core_grads[1], core_grads[2], core_grads[3], core_grads[4], core_grads[5]],
        axis=1,
    ).astype(jnp.bfloat16)
    grad_inward = contract_rows(all_rows, grad_proj).astype(jnp.bfloat16)
    grad_inward, ffn_grad_all = lax.optimization_barrier((grad_inward, ffn_grad_all))
    ffn_grad_all = ffn_grad_all.astype(jnp.float32)
    ffn_grads = (
        ffn_grad_all[:, :ff_width],
        ffn_grad_all[:, ff_width : 2 * ff_width],
        ffn_grad_all[:, 2 * ff_width :].T,
    )
    grad_norm_one = ring_scatter(contract_cols(grad_proj, w_inward).astype(jnp.bfloat16), ring, 3)
    grad_norm_one, wout_grad = lax.optimization_barrier((grad_norm_one, wout_grad))
    grad_in_part, grad_gain_in = pull_one(grad_norm_one)
    grad_input = grad_middle + grad_in_part
    inward_all = lax.psum_scatter(
        grad_inward, "row", scatter_dimension=0, tiled=True
    ).astype(jnp.float32)
    conv_grad_local = jnp.concatenate(
        [
            core_grads[6 + i].reshape(conv_local.shape[0], row_count, -1)
            for i in range(3)
        ],
        axis=2,
    ).reshape(conv_local.shape[0], -1)
    conv_grad = lax.psum_scatter(
        conv_grad_local.astype(jnp.bfloat16), "row", scatter_dimension=1, tiled=True
    ).astype(jnp.float32)
    mixer_grads = tuple(inward_all[:, edges[spot] : edges[spot + 1]] for spot in range(6)) + tuple(
        conv_grad[:, conv_edges[i] : conv_edges[i + 1]] for i in range(3)
    ) + (wout_grad.astype(jnp.float32),)
    head_total = a_log.shape[0]
    grad_a_full = lax.dynamic_update_slice_in_dim(
        jnp.zeros((head_total,), jnp.float32), core_grads[9], head_first, 0
    )
    grad_dt_full = lax.dynamic_update_slice_in_dim(
        jnp.zeros((head_total,), jnp.float32), core_grads[10], head_first, 0
    )
    small_sums = lax.psum(
        (grad_gain_in, grad_gain_ffn, core_grads[11], grad_a_full, grad_dt_full), ("head", "row")
    )
    return (
        final_out[None],
        grad_input[None],
        mixer_grads[0],
        mixer_grads[1],
        mixer_grads[2],
        mixer_grads[3],
        mixer_grads[4],
        mixer_grads[5],
        mixer_grads[6],
        mixer_grads[7],
        mixer_grads[8],
        small_sums[3],
        small_sums[4],
        small_sums[2],
        mixer_grads[9],
        small_sums[0],
        small_sums[1],
        ffn_grads[0],
        ffn_grads[1],
        ffn_grads[2],
    )


def solution(mesh):
    return jax.shard_map(
        partial(on_device, head_ring(mesh)),
        mesh=mesh,
        in_specs=(
            P("row", "head", None),
            P("row", "head"),
            P("row", "head"),
            P("row", "head"),
            P("row", "head"),
            P("row", "head"),
            P("row", "head"),
            P(None, ("head", "row")),
            P(None, ("head", "row")),
            P(None, ("head", "row")),
            P(),
            P(),
            P(),
            P("head", "row"),
            P(),
            P(),
            P("head", "row"),
            P("head", "row"),
            P("row", "head"),
            P("row", None),
            P("row"),
            P("row", "head", None),
        ),
        out_specs=(
            P("row", "head", None),
            P("row", "head", None),
            P("row", "head"),
            P("row", "head"),
            P("row", "head"),
            P("row", "head"),
            P("row", "head"),
            P("row", "head"),
            P(None, ("head", "row")),
            P(None, ("head", "row")),
            P(None, ("head", "row")),
            P(),
            P(),
            P(),
            P("head", "row"),
            P(),
            P(),
            P("head", "row"),
            P("head", "row"),
            P("row", "head"),
        ),
        check_vma=False,
    )
```

```python
from functools import partial
import math

import jax
import jax.numpy as jnp
from jax import lax
from jax.sharding import PartitionSpec as P
from jax.experimental import pallas as pl
from jax.experimental.pallas import tpu as pltpu

BLOCK = 64


precise = lax.Precision.HIGHEST
epsilon = 1e-06
o_floor = 0.001


def rms_norm(vector, gain_vec, floor_add=epsilon):
    return (
        vector * lax.rsqrt(jnp.mean(vector * vector, axis=-1, keepdims=True) + floor_add) * gain_vec
    )


def unit_norm(vector):
    return vector * lax.rsqrt(jnp.sum(vector * vector, axis=-1, keepdims=True) + epsilon)


def swiglu(gate_pre, up_pre):
    return jax.nn.silu(gate_pre) * up_pre


def short_conv(signal, kernel, seg_ids):
    tap_count = kernel.shape[0]
    length = signal.shape[0]
    summed = signal * kernel[tap_count - 1]
    for offset in range(1, tap_count):
        shifted = jnp.concatenate(
            [jnp.zeros((offset, signal.shape[1]), signal.dtype), signal[: length - offset]], axis=0
        )
        seg_shift = jnp.concatenate(
            [jnp.full((offset,), -1, jnp.int32), seg_ids[: length - offset]]
        )
        keep_mask = (seg_shift == seg_ids).astype(signal.dtype)
        summed = summed + shifted * kernel[tap_count - 1 - offset] * keep_mask[:, None]
    return summed


def _recur_fwd_kernel(nb, u0_ref, w_ref, kt_ref, c_ref, s_out, u_out, s_scr):
    @pl.when(pl.program_id(1) == 0)
    def _():
        s_scr[...] = jnp.zeros_like(s_scr)

    def step(j, carry):
        state = s_scr[...]
        s_out[0, j] = state
        update = u0_ref[0, j] - lax.dot_general(
            w_ref[0, j], state, (((1,), (1,)), ((), ())),
            precision=precise, preferred_element_type=jnp.float32,
        )
        u_out[0, j] = update
        s_scr[...] = c_ref[0, j] * state + lax.dot_general(
            update, kt_ref[0, j], (((0,), (0,)), ((), ())),
            precision=precise, preferred_element_type=jnp.float32,
        )
        return carry

    lax.fori_loop(0, nb, step, 0)


def _recur_bwd_kernel(
    nb, s_ref, u_ref, w_ref, kt_ref, c_ref, ds_ref, du_ref,
    du0_out, dw_out, dkt_out, dc_out, g_scr,
):
    @pl.when(pl.program_id(1) == 0)
    def _():
        g_scr[...] = jnp.zeros_like(g_scr)

    def step(i, carry):
        j = nb - 1 - i
        grad_state = g_scr[...]
        state = s_ref[0, j]
        grad_update = du_ref[0, j] + lax.dot_general(
            kt_ref[0, j], grad_state, (((1,), (1,)), ((), ())),
            precision=precise, preferred_element_type=jnp.float32,
        )
        dkt_out[0, j] = jnp.dot(
            u_ref[0, j], grad_state, precision=precise, preferred_element_type=jnp.float32
        )
        dc_out[0, j] = jnp.sum(grad_state * state, axis=0, keepdims=True)
        du0_out[0, j] = grad_update
        dw_out[0, j] = -jnp.dot(
            grad_update, state, precision=precise, preferred_element_type=jnp.float32
        )
        g_scr[...] = (
            c_ref[0, j] * grad_state
            - lax.dot_general(
                grad_update, w_ref[0, j], (((0,), (0,)), ((), ())),
                precision=precise, preferred_element_type=jnp.float32,
            )
            + ds_ref[0, j]
        )
        return carry

    lax.fori_loop(0, nb, step, 0)


def _chunk_spec(nb, tail, reverse, count):
    if reverse:
        return pl.BlockSpec((1, nb) + tail, lambda h, b: (h, count - 1 - b, 0, 0))
    return pl.BlockSpec((1, nb) + tail, lambda h, b: (h, b, 0, 0))


def _recur_forward(u0, w, kt, c):
    heads, count, chunk, dv = u0.shape
    dk = w.shape[-1]
    nb = min(8, count)
    blocks = count // nb
    flops = 4 * heads * count * chunk * dk * dv * 6
    moved = 4 * heads * count * (2 * chunk * dv + 2 * chunk * dk + dv * dk)
    return pl.pallas_call(
        partial(_recur_fwd_kernel, nb),
        grid=(heads, blocks),
        in_specs=[
            _chunk_spec(nb, (chunk, dv), False, blocks),
            _chunk_spec(nb, (chunk, dk), False, blocks),
            _chunk_spec(nb, (chunk, dk), False, blocks),
            _chunk_spec(nb, (1, dk), False, blocks),
        ],
        out_specs=[
            _chunk_spec(nb, (dv, dk), False, blocks),
            _chunk_spec(nb, (chunk, dv), False, blocks),
        ],
        out_shape=[
            jax.ShapeDtypeStruct((heads, count, dv, dk), jnp.float32),
            jax.ShapeDtypeStruct((heads, count, chunk, dv), jnp.float32),
        ],
        scratch_shapes=[pltpu.VMEM((dv, dk), jnp.float32)],
        compiler_params=pltpu.CompilerParams(dimension_semantics=("arbitrary", "arbitrary")),
        cost_estimate=pl.CostEstimate(flops=flops, transcendentals=0, bytes_accessed=moved),
        name="delta_state_forward",
    )(u0, w, kt, c)


def _recur_backward(states, updates, w, kt, c, d_states, d_updates):
    heads, count, chunk, dv = updates.shape
    dk = w.shape[-1]
    nb = min(8, count)
    blocks = count // nb
    flops = 8 * heads * count * chunk * dk * dv * 6
    moved = 4 * heads * count * (4 * chunk * dv + 4 * chunk * dk + 2 * dv * dk)
    return pl.pallas_call(
        partial(_recur_bwd_kernel, nb),
        grid=(heads, blocks),
        in_specs=[
            _chunk_spec(nb, (dv, dk), True, blocks),
            _chunk_spec(nb, (chunk, dv), True, blocks),
            _chunk_spec(nb, (chunk, dk), True, blocks),
            _chunk_spec(nb, (chunk, dk), True, blocks),
            _chunk_spec(nb, (1, dk), True, blocks),
            _chunk_spec(nb, (dv, dk), True, blocks),
            _chunk_spec(nb, (chunk, dv), True, blocks),
        ],
        out_specs=[
            _chunk_spec(nb, (chunk, dv), True, blocks),
            _chunk_spec(nb, (chunk, dk), True, blocks),
            _chunk_spec(nb, (chunk, dk), True, blocks),
            _chunk_spec(nb, (1, dk), True, blocks),
        ],
        out_shape=[
            jax.ShapeDtypeStruct((heads, count, chunk, dv), jnp.float32),
            jax.ShapeDtypeStruct((heads, count, chunk, dk), jnp.float32),
            jax.ShapeDtypeStruct((heads, count, chunk, dk), jnp.float32),
            jax.ShapeDtypeStruct((heads, count, 1, dk), jnp.float32),
        ],
        scratch_shapes=[pltpu.VMEM((dv, dk), jnp.float32)],
        compiler_params=pltpu.CompilerParams(dimension_semantics=("arbitrary", "arbitrary")),
        cost_estimate=pl.CostEstimate(flops=flops, transcendentals=0, bytes_accessed=moved),
        name="delta_state_backward",
    )(states, updates, w, kt, c, d_states, d_updates)


@jax.custom_vjp
def state_recurrence(u0, w, kt, c):
    return _recur_forward(u0, w, kt, c)


def _recurrence_fwd(u0, w, kt, c):
    states, updates = _recur_forward(u0, w, kt, c)
    return (states, updates), (states, updates, w, kt, c)


def _recurrence_bwd(saved, grads):
    states, updates, w, kt, c = saved
    d_states, d_updates = grads
    du0, dw, dkt, dc_lanes = _recur_backward(states, updates, w, kt, c, d_states, d_updates)
    return du0, dw, dkt, dc_lanes


state_recurrence.defvjp(_recurrence_fwd, _recurrence_bwd)


def _unit_lower_inverse_small(system):
    size = system.shape[-1]
    strict = system - jnp.eye(size, dtype=system.dtype)
    power = -strict
    inverse = jnp.eye(size, dtype=system.dtype) + power
    done = 2
    while done < size:
        power = jnp.matmul(power, power, precision=precise)
        inverse = inverse + jnp.matmul(power, inverse, precision=precise)
        done *= 2
    return inverse


def _unit_lower_inverse_forward(system):
    size = system.shape[-1]
    base = min(8, size)
    lead = system.shape[:-2]
    count = size // base
    blocks = system.reshape(lead + (count, base, count, base))
    diag = jnp.stack([blocks[..., i, :, i, :] for i in range(count)], axis=-3)
    inverse = _unit_lower_inverse_small(diag)
    width = base
    while width < size:
        pairs = inverse.shape[-3] // 2
        upper = inverse[..., 0::2, :, :]
        lower = inverse[..., 1::2, :, :]
        below = jnp.stack(
            [
                system[..., (2 * i + 1) * width : (2 * i + 2) * width, 2 * i * width : (2 * i + 1) * width]
                for i in range(pairs)
            ],
            axis=-3,
        )
        corner = -jnp.matmul(
            lower, jnp.matmul(below, upper, precision=precise), precision=precise
        )
        zeros = jnp.zeros_like(upper)
        top = jnp.concatenate([upper, zeros], axis=-1)
        bottom = jnp.concatenate([corner, lower], axis=-1)
        inverse = jnp.concatenate([top, bottom], axis=-2)
        width *= 2
    return inverse[..., 0, :, :]


@jax.custom_vjp
def unit_lower_inverse(system):
    return _unit_lower_inverse_forward(system)


def _inverse_fwd(system):
    inverse = _unit_lower_inverse_forward(system)
    return inverse, inverse


def _inverse_bwd(inverse, grad):
    size = inverse.shape[-1]
    flipped = jnp.swapaxes(inverse, -1, -2)
    full = -jnp.matmul(jnp.matmul(flipped, grad, precision=precise), flipped, precision=precise)
    places = jnp.arange(size)
    return (full * (places[:, None] > places[None, :]).astype(full.dtype),)


unit_lower_inverse.defvjp(_inverse_fwd, _inverse_bwd)


def chunk_prepare(queries, keys_n, values, decays, beta_rate, seg_ids):
    length, dk = keys_n.shape
    count = length // BLOCK
    q = queries.reshape(count, BLOCK, dk)
    k = keys_n.reshape(count, BLOCK, dk)
    v = values.reshape(count, BLOCK, values.shape[1])
    beta = beta_rate.reshape(count, BLOCK)
    seg = seg_ids.reshape(count, BLOCK)
    cumulative = jnp.cumsum(decays.reshape(count, BLOCK), axis=1)
    places = jnp.arange(BLOCK)
    lower_tri = places[:, None] >= places[None, :]
    inside = jnp.logical_and(seg[:, :, None] == seg[:, None, :], lower_tri)
    log_gap = jnp.where(inside, cumulative[:, :, None] - cumulative[:, None, :], 0.0)
    within = jnp.exp(log_gap) * inside.astype(jnp.float32)
    strict = within * (places[:, None] > places[None, :]).astype(jnp.float32)
    last_seg = jnp.concatenate([jnp.full((1,), -1, seg.dtype), seg[:-1, BLOCK - 1]])
    carried = jnp.exp(cumulative) * (seg == last_seg[:, None]).astype(jnp.float32)
    key_gram = jnp.einsum("nid,njd->nij", k, k, precision=precise)
    system = jnp.eye(BLOCK, dtype=jnp.float32) + beta[:, :, None] * strict * key_gram
    right_side = jnp.concatenate([beta[:, :, None] * v, (beta * carried)[:, :, None] * k], axis=2)
    solved = jnp.matmul(unit_lower_inverse(system), right_side, precision=precise)
    dv = v.shape[2]
    kt = within[:, BLOCK - 1, :, None] * k
    scores = jnp.einsum("nid,njd->nij", q, k, precision=precise) * within
    return solved[:, :, :dv], solved[:, :, dv:], kt, carried[:, BLOCK - 1], carried, scores


def chunk_finish(queries, carried, scores, states, updates):
    count = states.shape[0]
    q = queries.reshape(count, BLOCK, queries.shape[1])
    output = carried[:, :, None] * jnp.einsum(
        "nid,nvd->niv", q, states, precision=precise
    ) + jnp.einsum("nij,njv->niv", scores, updates, precision=precise)
    return output.reshape(count * BLOCK, states.shape[1])


def delta_rule(queries, keys_n, values, decays, beta_rate, seg_ids):
    u0, w, kt, tail, carried, scores = jax.vmap(chunk_prepare, in_axes=(0, 0, 0, 0, 0, None))(
        queries, keys_n, values, decays, beta_rate, seg_ids
    )
    c = jnp.broadcast_to(tail[:, :, None, None], tail.shape + (1, w.shape[-1]))
    states, updates = state_recurrence(u0, w, kt, c)
    return jax.vmap(chunk_finish)(queries, carried, scores, states, updates)


def head_inputs(proj_query, proj_key, proj_value, proj_alpha, proj_beta,
                kernel_query, kernel_key, kernel_value, a_here, dt_here, seg_ids):
    queries = unit_norm(jax.nn.silu(short_conv(proj_query, kernel_query, seg_ids))) * (
        1.0 / math.sqrt(proj_query.shape[1])
    )
    keys_n = unit_norm(jax.nn.silu(short_conv(proj_key, kernel_key, seg_ids)))
    values = jax.nn.silu(short_conv(proj_value, kernel_value, seg_ids))
    decays = -jnp.exp(a_here) * jax.nn.softplus(proj_alpha + dt_here)
    beta_rate = jax.nn.sigmoid(proj_beta)
    return queries, keys_n, values, decays, beta_rate


def head_output(recurrent, proj_gate, o_gain, live_mask):
    return rms_norm(recurrent, o_gain, o_floor) * jax.nn.silu(proj_gate) * live_mask[:, None]


def local_mixer(
    proj_query,
    proj_key,
    proj_value,
    proj_gate,
    proj_alpha,
    proj_beta,
    kernel_query,
    kernel_key,
    kernel_value,
    a_here,
    dt_here,
    o_gain,
    seg_ids=None,
    live_mask=None,
):
    row_count = proj_query.shape[0]
    heads_here = proj_alpha.shape[1]

    def by_head(array):
        return jnp.moveaxis(array.reshape(row_count, heads_here, -1), 1, 0)

    def kernel_heads(kernel):
        return jnp.moveaxis(kernel.reshape(kernel.shape[0], heads_here, -1), 1, 0)

    queries, keys_n, values, decays, beta_rate = jax.vmap(
        head_inputs, in_axes=(0,) * 10 + (None,)
    )(
        by_head(proj_query),
        by_head(proj_key),
        by_head(proj_value),
        proj_alpha.T,
        proj_beta.T,
        kernel_heads(kernel_query),
        kernel_heads(kernel_key),
        kernel_heads(kernel_value),
        a_here,
        dt_here,
        seg_ids,
    )
    recurrent = delta_rule(queries, keys_n, values, decays, beta_rate, seg_ids)
    mixed_heads = jax.vmap(head_output, in_axes=(0, 0, None, None))(
        recurrent, by_head(proj_gate), o_gain, live_mask
    )
    return jnp.moveaxis(mixed_heads, 0, 1).reshape(row_count, -1)


MESH_ID = pl.DeviceIdType.MESH


def _ring_position(h, major, minor):
    a = h // minor
    b = h % minor
    return b * major + a + (b % 2) * (major - 1 - 2 * a)


def _ring_member(q, major, minor):
    count = major * minor
    q = (q + count) % count
    b = q // major
    r = q % major
    return (r + (b % 2) * (major - 1 - 2 * r)) * minor + b


def _ring_sides(major, minor):
    p = _ring_position(lax.axis_index("head"), major, minor)
    return p, _ring_member(p + 1, major, minor), _ring_member(p - 1, major, minor)


def _greet(nxt, prv, row):
    barrier = pltpu.get_barrier_semaphore()
    pl.semaphore_signal(barrier, 1, device_id=(prv, row), device_id_type=MESH_ID)
    pl.semaphore_signal(barrier, 1, device_id=(nxt, row), device_id_type=MESH_ID)
    pl.semaphore_wait(barrier, 2)


def _ring_gather_kernel(major, minor, x_ref, out_ref, send_sem, recv_sem):
    count = major * minor
    blk = x_ref.shape[0]
    half = blk // 2
    row = lax.axis_index("row")
    p, nxt, prv = _ring_sides(major, minor)
    out_ref[pl.ds(pl.multiple_of(lax.axis_index("head") * blk, blk), blk), :] = x_ref[...]
    _greet(nxt, prv, row)

    def piece(pos, off):
        return out_ref.at[pl.ds(pl.multiple_of(_ring_member(pos, major, minor) * blk + off, half), half)]

    def outgoing(d, s):
        pos = p - s if d == 0 else p + s
        target = nxt if d == 0 else prv
        ref = piece(pos, d * half)
        return pltpu.make_async_remote_copy(
            ref, ref, send_sem.at[d, s], recv_sem.at[d, s], device_id=(target, row),
            device_id_type=MESH_ID,
        )

    def incoming(d, s):
        pos = p - 1 - s if d == 0 else p + 1 + s
        source = prv if d == 0 else nxt
        ref = piece(pos, d * half)
        return pltpu.make_async_remote_copy(
            ref, ref, send_sem.at[d, s], recv_sem.at[d, s], device_id=(source, row),
            device_id_type=MESH_ID,
        )

    for s in range(count - 1):
        for d in (0, 1):
            if s > 0:
                incoming(d, s - 1).wait_recv()
            outgoing(d, s).start()
    for d in (0, 1):
        incoming(d, count - 2).wait_recv()
    for s in range(count - 1):
        for d in (0, 1):
            outgoing(d, s).wait_send()


def _ring_scatter_kernel(major, minor, y_ref, out_ref, buf, send_sem, recv_sem):
    count = major * minor
    blk = out_ref.shape[0]
    half = blk // 2
    row = lax.axis_index("row")
    p, nxt, prv = _ring_sides(major, minor)
    _greet(nxt, prv, row)

    def piece(pos, off):
        return y_ref.at[pl.ds(pl.multiple_of(_ring_member(pos, major, minor) * blk + off, half), half)]

    def outgoing(d, s):
        pos = p - s - 1 if d == 0 else p + s + 1
        target = nxt if d == 0 else prv
        source = piece(pos, d * half) if s == 0 else buf.at[d, s - 1]
        return pltpu.make_async_remote_copy(
            source, buf.at[d, s], send_sem.at[d, s], recv_sem.at[d, s],
            device_id=(target, row), device_id_type=MESH_ID,
        )

    def incoming(d, s):
        source = prv if d == 0 else nxt
        return pltpu.make_async_remote_copy(
            buf.at[d, s], buf.at[d, s], send_sem.at[d, s], recv_sem.at[d, s],
            device_id=(source, row), device_id_type=MESH_ID,
        )

    for s in range(count - 1):
        for d in (0, 1):
            if s > 0:
                incoming(d, s - 1).wait_recv()
                pos = p - s - 1 if d == 0 else p + s + 1
                buf[d, s - 1] = (
                    buf[d, s - 1].astype(jnp.float32)
                    + piece(pos, d * half)[...].astype(jnp.float32)
                ).astype(buf.dtype)
            outgoing(d, s).start()
    for d in (0, 1):
        incoming(d, count - 2).wait_recv()
        out_ref[pl.ds(d * half, half), :] = piece(p, d * half)[...].astype(
            jnp.float32
        ) + buf[d, count - 2].astype(jnp.float32)
    for s in range(count - 1):
        for d in (0, 1):
            outgoing(d, s).wait_send()


def ring_gather(x, ring, collective):
    major, minor = ring
    count = major * minor
    blk, width = x.shape
    return pl.pallas_call(
        partial(_ring_gather_kernel, major, minor),
        out_shape=jax.ShapeDtypeStruct((count * blk, width), x.dtype),
        in_specs=[pl.BlockSpec(memory_space=pltpu.VMEM)],
        out_specs=pl.BlockSpec(memory_space=pltpu.VMEM),
        scratch_shapes=[
            pltpu.SemaphoreType.DMA((2, count - 1)),
            pltpu.SemaphoreType.DMA((2, count - 1)),
        ],
        compiler_params=pltpu.CompilerParams(collective_id=collective, has_side_effects=True),
        name="ring_gather_head",
    )(x)


def ring_scatter(y, ring, collective):
    major, minor = ring
    count = major * minor
    rows, width = y.shape
    blk = rows // count
    return pl.pallas_call(
        partial(_ring_scatter_kernel, major, minor),
        out_shape=jax.ShapeDtypeStruct((blk, width), jnp.float32),
        in_specs=[pl.BlockSpec(memory_space=pltpu.VMEM)],
        out_specs=pl.BlockSpec(memory_space=pltpu.VMEM),
        scratch_shapes=[
            pltpu.VMEM((2, count - 1, blk // 2, width), y.dtype),
            pltpu.SemaphoreType.DMA((2, count - 1)),
            pltpu.SemaphoreType.DMA((2, count - 1)),
        ],
        compiler_params=pltpu.CompilerParams(collective_id=collective, has_side_effects=True),
        name="ring_scatter_head",
    )(y)


def head_ring(mesh):
    count = mesh.shape["head"]
    try:
        spots = [tuple(device.coords) for device in mesh.devices[:, 0]]
    except (AttributeError, TypeError):
        return (count, 1)
    moving = [axis for axis in range(len(spots[0])) if spots[0][axis] != spots[1][axis]]
    if len(moving) != 1:
        return (count, 1)
    minor = len({spot[moving[0]] for spot in spots})
    if count % minor or minor % 2:
        return (count, 1)
    return (count // minor, minor)


def contract_rows(left, right):
    return lax.dot_general(
        left, right, (((0,), (0,)), ((), ())), preferred_element_type=jnp.float32
    )


def contract_cols(left, right):
    return lax.dot_general(
        left, right, (((1,), (1,)), ((), ())), preferred_element_type=jnp.float32
    )


def on_device(
    ring,
    tokens,
    w_query,
    w_key,
    w_value,
    w_outgate,
    w_alpha,
    w_beta,
    conv_query,
    conv_key,
    conv_value,
    a_log,
    dt_bias,
    o_gain,
    w_out,
    gain_in,
    gain_ffn,
    w_gate,
    w_up,
    w_down,
    segments,
    valid_len,
    cotangent,
):
    residual = tokens[0].astype(jnp.float32)
    heads_here = w_alpha.shape[1]
    head_first = lax.axis_index("head") * heads_here
    norm_one, pull_one = jax.vjp(rms_norm, residual, gain_in)
    normed_one = norm_one.astype(jnp.bfloat16)
    row_count = lax.psum(1, "row")
    w_local = jnp.concatenate(
        [w_query, w_key, w_value, w_outgate, w_alpha, w_beta], axis=1
    ).astype(jnp.bfloat16)
    edges = [0]
    for member in (w_query, w_key, w_value, w_outgate, w_alpha, w_beta):
        edges.append(edges[-1] + member.shape[1])
    w_inward = lax.all_gather(w_local, "row", axis=0, tiled=True)
    conv_local = jnp.concatenate([conv_query, conv_key, conv_value], axis=1).astype(jnp.bfloat16)
    conv_edges = [0, conv_query.shape[1], conv_query.shape[1] + conv_key.shape[1], conv_local.shape[1]]
    conv_all = lax.all_gather(conv_local, "row", axis=1, tiled=True).reshape(
        conv_local.shape[0], row_count, conv_local.shape[1]
    )
    conv_parts = [
        conv_all[:, :, conv_edges[i] : conv_edges[i + 1]].reshape(conv_local.shape[0], -1)
        for i in range(3)
    ]
    out_matrix = lax.all_gather(w_out.astype(jnp.bfloat16), "row", axis=1, tiled=True)
    ff_width = w_gate.shape[1]
    ffn_local = jnp.concatenate([w_gate, w_up], axis=1).astype(jnp.bfloat16)
    down_local = w_down.T.astype(jnp.bfloat16)
    grad_out = cotangent[0]
    grad_out_rows = lax.all_gather(grad_out, "row", axis=0, tiled=True)
    all_rows = ring_gather(normed_one, ring, 0)
    all_rows, out_matrix, ffn_local, down_local = lax.optimization_barrier(
        (all_rows, out_matrix, ffn_local, down_local)
    )
    ffn_all = lax.all_gather(ffn_local, "head", axis=0, tiled=True)
    down_all = lax.all_gather(down_local, "head", axis=0, tiled=True)
    projected = jnp.dot(all_rows, w_inward, preferred_element_type=jnp.float32)
    proj_parts = [projected[:, edges[spot] : edges[spot + 1]] for spot in range(6)]
    seg_ids = segments[0]
    live_mask = (jnp.arange(seg_ids.shape[0]) < valid_len[0]).astype(jnp.float32)
    a_here = lax.dynamic_slice_in_dim(a_log, head_first, heads_here)
    dt_here = lax.dynamic_slice_in_dim(dt_bias, head_first, heads_here)
    mixer_fn = partial(local_mixer, seg_ids=seg_ids, live_mask=live_mask)
    mixed, pull_core = jax.vjp(
        mixer_fn,
        proj_parts[0],
        proj_parts[1],
        proj_parts[2],
        proj_parts[3],
        proj_parts[4],
        proj_parts[5],
        conv_parts[0].astype(jnp.float32),
        conv_parts[1].astype(jnp.float32),
        conv_parts[2].astype(jnp.float32),
        a_here,
        dt_here,
        o_gain,
    )
    mixed, ffn_all, grad_out_rows = lax.optimization_barrier((mixed, ffn_all, grad_out_rows))
    w_down_t = down_all
    w_gate_all = ffn_all[:, :ff_width]
    w_up_all = ffn_all[:, ff_width : 2 * ff_width]
    mixed_half = mixed.astype(jnp.bfloat16)
    mixer_output = ring_scatter(
        jnp.dot(mixed_half, out_matrix, preferred_element_type=jnp.float32).astype(jnp.bfloat16),
        ring,
        1,
    )
    middle = residual + mixer_output
    norm_two, pull_two = jax.vjp(rms_norm, middle, gain_ffn)
    normed_two = norm_two.astype(jnp.bfloat16)
    ffn_inputs = lax.all_gather(normed_two, "row", axis=0, tiled=True)
    gate_pre = jnp.dot(ffn_inputs, w_gate_all, preferred_element_type=jnp.float32)
    up_pre = jnp.dot(ffn_inputs, w_up_all, preferred_element_type=jnp.float32)
    hidden_val, pull_act = jax.vjp(swiglu, gate_pre, up_pre)
    hidden_half = hidden_val.astype(jnp.bfloat16)
    ffn_partial = contract_cols(hidden_half, w_down_t).astype(jnp.bfloat16)
    grad_hidden = jnp.dot(grad_out_rows, w_down_t, preferred_element_type=jnp.float32)
    grad_down_t = contract_rows(grad_out_rows, hidden_half)
    grad_gate_f, grad_up_f = pull_act(grad_hidden)
    grad_gate = grad_gate_f.astype(jnp.bfloat16)
    grad_upper = grad_up_f.astype(jnp.bfloat16)
    grad_wgate = contract_rows(ffn_inputs, grad_gate)
    grad_wup = contract_rows(ffn_inputs, grad_upper)
    grad_norm_two = lax.psum_scatter(
        (contract_cols(grad_gate, w_gate_all) + contract_cols(grad_upper, w_up_all)).astype(
            jnp.bfloat16
        ),
        "row",
        scatter_dimension=0,
        tiled=True,
    ).astype(jnp.float32)
    grad_mid_part, grad_gain_ffn = pull_two(grad_norm_two)
    grad_middle = grad_out.astype(jnp.float32) + grad_mid_part
    ffn_grad_cat = jnp.concatenate([grad_wgate, grad_wup, grad_down_t], axis=1).astype(
        jnp.bfloat16
    )
    grad_mid_half = grad_middle.astype(jnp.bfloat16)
    grad_mid_rows = ring_gather(grad_mid_half, ring, 2)
    ffn_output = lax.psum_scatter(ffn_partial, "row", scatter_dimension=0, tiled=True)
    grad_mid_rows, ffn_grad_cat = lax.optimization_barrier((grad_mid_rows, ffn_grad_cat))
    ffn_grad_all = lax.psum_scatter(ffn_grad_cat, "head", scatter_dimension=0, tiled=True)
    grad_mixed = contract_cols(grad_mid_rows, out_matrix)
    grad_wout = contract_rows(mixed_half, grad_mid_rows).astype(jnp.bfloat16)
    wout_grad = lax.psum_scatter(grad_wout, "row", scatter_dimension=1, tiled=True)
    core_grads = pull_core(grad_mixed)
    core_grads, ffn_output = lax.optimization_barrier((core_grads, ffn_output))
    final_out = (middle + ffn_output.astype(jnp.float32)).astype(jnp.bfloat16)
    grad_proj = jnp.concatenate(
        [core_grads[0], core_grads[1], core_grads[2], core_grads[3], core_grads[4], core_grads[5]],
        axis=1,
    ).astype(jnp.bfloat16)
    grad_inward = contract_rows(all_rows, grad_proj).astype(jnp.bfloat16)
    grad_inward, ffn_grad_all = lax.optimization_barrier((grad_inward, ffn_grad_all))
    ffn_grad_all = ffn_grad_all.astype(jnp.float32)
    ffn_grads = (
        ffn_grad_all[:, :ff_width],
        ffn_grad_all[:, ff_width : 2 * ff_width],
        ffn_grad_all[:, 2 * ff_width :].T,
    )
    grad_norm_one = ring_scatter(contract_cols(grad_proj, w_inward).astype(jnp.bfloat16), ring, 3)
    grad_norm_one, wout_grad = lax.optimization_barrier((grad_norm_one, wout_grad))
    grad_in_part, grad_gain_in = pull_one(grad_norm_one)
    grad_input = grad_middle + grad_in_part
    inward_all = lax.psum_scatter(
        grad_inward, "row", scatter_dimension=0, tiled=True
    ).astype(jnp.float32)
    conv_grad_local = jnp.concatenate(
        [
            core_grads[6 + i].reshape(conv_local.shape[0], row_count, -1)
            for i in range(3)
        ],
        axis=2,
    ).reshape(conv_local.shape[0], -1)
    conv_grad = lax.psum_scatter(
        conv_grad_local.astype(jnp.bfloat16), "row", scatter_dimension=1, tiled=True
    ).astype(jnp.float32)
    mixer_grads = tuple(inward_all[:, edges[spot] : edges[spot + 1]] for spot in range(6)) + tuple(
        conv_grad[:, conv_edges[i] : conv_edges[i + 1]] for i in range(3)
    ) + (wout_grad.astype(jnp.float32),)
    head_total = a_log.shape[0]
    grad_a_full = lax.dynamic_update_slice_in_dim(
        jnp.zeros((head_total,), jnp.float32), core_grads[9], head_first, 0
    )
    grad_dt_full = lax.dynamic_update_slice_in_dim(
        jnp.zeros((head_total,), jnp.float32), core_grads[10], head_first, 0
    )
    small_sums = lax.psum(
        (grad_gain_in, grad_gain_ffn, core_grads[11], grad_a_full, grad_dt_full), ("head", "row")
    )
    return (
        final_out[None],
        grad_input[None],
        mixer_grads[0],
        mixer_grads[1],
        mixer_grads[2],
        mixer_grads[3],
        mixer_grads[4],
        mixer_grads[5],
        mixer_grads[6],
        mixer_grads[7],
        mixer_grads[8],
        small_sums[3],
        small_sums[4],
        small_sums[2],
        mixer_grads[9],
        small_sums[0],
        small_sums[1],
        ffn_grads[0],
        ffn_grads[1],
        ffn_grads[2],
    )


def solution(mesh):
    return jax.shard_map(
        partial(on_device, head_ring(mesh)),
        mesh=mesh,
        in_specs=(
            P("row", "head", None),
            P("row", "head"),
            P("row", "head"),
            P("row", "head"),
            P("row", "head"),
            P("row", "head"),
            P("row", "head"),
            P(None, ("head", "row")),
            P(None, ("head", "row")),
            P(None, ("head", "row")),
            P(),
            P(),
            P(),
            P("head", "row"),
            P(),
            P(),
            P("head", "row"),
            P("head", "row"),
            P("row", "head"),
            P("row", None),
            P("row"),
            P("row", "head", None),
        ),
        out_specs=(
            P("row", "head", None),
            P("row", "head", None),
            P("row", "head"),
            P("row", "head"),
            P("row", "head"),
            P("row", "head"),
            P("row", "head"),
            P("row", "head"),
            P(None, ("head", "row")),
            P(None, ("head", "row")),
            P(None, ("head", "row")),
            P(),
            P(),
            P(),
            P("head", "row"),
            P(),
            P(),
            P("head", "row"),
            P("head", "row"),
            P("row", "head"),
        ),
        check_vma=False,
    )
```

```python
from functools import partial
import math

import jax
import jax.numpy as jnp
from jax import lax
from jax.sharding import PartitionSpec as P
from jax.experimental import pallas as pl
from jax.experimental.pallas import tpu as pltpu

BLOCK = 64


precise = lax.Precision.HIGHEST
epsilon = 1e-06
o_floor = 0.001


def rms_norm(vector, gain_vec, floor_add=epsilon):
    return (
        vector * lax.rsqrt(jnp.mean(vector * vector, axis=-1, keepdims=True) + floor_add) * gain_vec
    )


def unit_norm(vector):
    return vector * lax.rsqrt(jnp.sum(vector * vector, axis=-1, keepdims=True) + epsilon)


def swiglu(gate_pre, up_pre):
    return jax.nn.silu(gate_pre) * up_pre


def short_conv(signal, kernel, seg_ids):
    tap_count = kernel.shape[0]
    length = signal.shape[0]
    summed = signal * kernel[tap_count - 1]
    for offset in range(1, tap_count):
        shifted = jnp.concatenate(
            [jnp.zeros((offset, signal.shape[1]), signal.dtype), signal[: length - offset]], axis=0
        )
        seg_shift = jnp.concatenate(
            [jnp.full((offset,), -1, jnp.int32), seg_ids[: length - offset]]
        )
        keep_mask = (seg_shift == seg_ids).astype(signal.dtype)
        summed = summed + shifted * kernel[tap_count - 1 - offset] * keep_mask[:, None]
    return summed


def _recur_fwd_kernel(nb, u0_ref, w_ref, kt_ref, c_ref, s_out, u_out, s_scr):
    @pl.when(pl.program_id(1) == 0)
    def _():
        s_scr[...] = jnp.zeros_like(s_scr)

    def step(j, carry):
        state = s_scr[...]
        s_out[0, j] = state
        update = u0_ref[0, j] - lax.dot_general(
            w_ref[0, j], state, (((1,), (1,)), ((), ())),
            precision=precise, preferred_element_type=jnp.float32,
        )
        u_out[0, j] = update
        s_scr[...] = c_ref[0, j] * state + lax.dot_general(
            update, kt_ref[0, j], (((0,), (0,)), ((), ())),
            precision=precise, preferred_element_type=jnp.float32,
        )
        return carry

    lax.fori_loop(0, nb, step, 0)


def _recur_bwd_kernel(
    nb, s_ref, u_ref, w_ref, kt_ref, c_ref, ds_ref, du_ref,
    du0_out, dw_out, dkt_out, dc_out, g_scr,
):
    @pl.when(pl.program_id(1) == 0)
    def _():
        g_scr[...] = jnp.zeros_like(g_scr)

    def step(i, carry):
        j = nb - 1 - i
        grad_state = g_scr[...]
        state = s_ref[0, j]
        grad_update = du_ref[0, j] + lax.dot_general(
            kt_ref[0, j], grad_state, (((1,), (1,)), ((), ())),
            precision=precise, preferred_element_type=jnp.float32,
        )
        dkt_out[0, j] = jnp.dot(
            u_ref[0, j], grad_state, precision=precise, preferred_element_type=jnp.float32
        )
        dc_out[0, j] = jnp.sum(grad_state * state, axis=0, keepdims=True)
        du0_out[0, j] = grad_update
        dw_out[0, j] = -jnp.dot(
            grad_update, state, precision=precise, preferred_element_type=jnp.float32
        )
        g_scr[...] = (
            c_ref[0, j] * grad_state
            - lax.dot_general(
                grad_update, w_ref[0, j], (((0,), (0,)), ((), ())),
                precision=precise, preferred_element_type=jnp.float32,
            )
            + ds_ref[0, j]
        )
        return carry

    lax.fori_loop(0, nb, step, 0)


def _chunk_spec(nb, tail, reverse, count):
    if reverse:
        return pl.BlockSpec((1, nb) + tail, lambda h, b: (h, count - 1 - b, 0, 0))
    return pl.BlockSpec((1, nb) + tail, lambda h, b: (h, b, 0, 0))


def _recur_forward(u0, w, kt, c):
    heads, count, chunk, dv = u0.shape
    dk = w.shape[-1]
    nb = min(8, count)
    blocks = count // nb
    flops = 4 * heads * count * chunk * dk * dv * 6
    moved = 4 * heads * count * (2 * chunk * dv + 2 * chunk * dk + dv * dk)
    return pl.pallas_call(
        partial(_recur_fwd_kernel, nb),
        grid=(heads, blocks),
        in_specs=[
            _chunk_spec(nb, (chunk, dv), False, blocks),
            _chunk_spec(nb, (chunk, dk), False, blocks),
            _chunk_spec(nb, (chunk, dk), False, blocks),
            _chunk_spec(nb, (1, dk), False, blocks),
        ],
        out_specs=[
            _chunk_spec(nb, (dv, dk), False, blocks),
            _chunk_spec(nb, (chunk, dv), False, blocks),
        ],
        out_shape=[
            jax.ShapeDtypeStruct((heads, count, dv, dk), jnp.float32),
            jax.ShapeDtypeStruct((heads, count, chunk, dv), jnp.float32),
        ],
        scratch_shapes=[pltpu.VMEM((dv, dk), jnp.float32)],
        compiler_params=pltpu.CompilerParams(dimension_semantics=("arbitrary", "arbitrary")),
        cost_estimate=pl.CostEstimate(flops=flops, transcendentals=0, bytes_accessed=moved),
        name="delta_state_forward",
    )(u0, w, kt, c)


def _recur_backward(states, updates, w, kt, c, d_states, d_updates):
    heads, count, chunk, dv = updates.shape
    dk = w.shape[-1]
    nb = min(8, count)
    blocks = count // nb
    flops = 8 * heads * count * chunk * dk * dv * 6
    moved = 4 * heads * count * (4 * chunk * dv + 4 * chunk * dk + 2 * dv * dk)
    return pl.pallas_call(
        partial(_recur_bwd_kernel, nb),
        grid=(heads, blocks),
        in_specs=[
            _chunk_spec(nb, (dv, dk), True, blocks),
            _chunk_spec(nb, (chunk, dv), True, blocks),
            _chunk_spec(nb, (chunk, dk), True, blocks),
            _chunk_spec(nb, (chunk, dk), True, blocks),
            _chunk_spec(nb, (1, dk), True, blocks),
            _chunk_spec(nb, (dv, dk), True, blocks),
            _chunk_spec(nb, (chunk, dv), True, blocks),
        ],
        out_specs=[
            _chunk_spec(nb, (chunk, dv), True, blocks),
            _chunk_spec(nb, (chunk, dk), True, blocks),
            _chunk_spec(nb, (chunk, dk), True, blocks),
            _chunk_spec(nb, (1, dk), True, blocks),
        ],
        out_shape=[
            jax.ShapeDtypeStruct((heads, count, chunk, dv), jnp.float32),
            jax.ShapeDtypeStruct((heads, count, chunk, dk), jnp.float32),
            jax.ShapeDtypeStruct((heads, count, chunk, dk), jnp.float32),
            jax.ShapeDtypeStruct((heads, count, 1, dk), jnp.float32),
        ],
        scratch_shapes=[pltpu.VMEM((dv, dk), jnp.float32)],
        compiler_params=pltpu.CompilerParams(dimension_semantics=("arbitrary", "arbitrary")),
        cost_estimate=pl.CostEstimate(flops=flops, transcendentals=0, bytes_accessed=moved),
        name="delta_state_backward",
    )(states, updates, w, kt, c, d_states, d_updates)


@jax.custom_vjp
def state_recurrence(u0, w, kt, c):
    return _recur_forward(u0, w, kt, c)


def _recurrence_fwd(u0, w, kt, c):
    states, updates = _recur_forward(u0, w, kt, c)
    return (states, updates), (states, updates, w, kt, c)


def _recurrence_bwd(saved, grads):
    states, updates, w, kt, c = saved
    d_states, d_updates = grads
    du0, dw, dkt, dc_lanes = _recur_backward(states, updates, w, kt, c, d_states, d_updates)
    return du0, dw, dkt, dc_lanes


state_recurrence.defvjp(_recurrence_fwd, _recurrence_bwd)


def _unit_lower_inverse_small(system):
    size = system.shape[-1]
    strict = system - jnp.eye(size, dtype=system.dtype)
    power = -strict
    inverse = jnp.eye(size, dtype=system.dtype) + power
    done = 2
    while done < size:
        power = jnp.matmul(power, power, precision=precise)
        inverse = inverse + jnp.matmul(power, inverse, precision=precise)
        done *= 2
    return inverse


def _unit_lower_inverse_forward(system):
    size = system.shape[-1]
    base = min(8, size)
    lead = system.shape[:-2]
    count = size // base
    blocks = system.reshape(lead + (count, base, count, base))
    diag = jnp.stack([blocks[..., i, :, i, :] for i in range(count)], axis=-3)
    inverse = _unit_lower_inverse_small(diag)
    width = base
    while width < size:
        pairs = inverse.shape[-3] // 2
        upper = inverse[..., 0::2, :, :]
        lower = inverse[..., 1::2, :, :]
        below = jnp.stack(
            [
                system[..., (2 * i + 1) * width : (2 * i + 2) * width, 2 * i * width : (2 * i + 1) * width]
                for i in range(pairs)
            ],
            axis=-3,
        )
        corner = -jnp.matmul(
            lower, jnp.matmul(below, upper, precision=precise), precision=precise
        )
        zeros = jnp.zeros_like(upper)
        top = jnp.concatenate([upper, zeros], axis=-1)
        bottom = jnp.concatenate([corner, lower], axis=-1)
        inverse = jnp.concatenate([top, bottom], axis=-2)
        width *= 2
    return inverse[..., 0, :, :]


@jax.custom_vjp
def unit_lower_inverse(system):
    return _unit_lower_inverse_forward(system)


def _inverse_fwd(system):
    inverse = _unit_lower_inverse_forward(system)
    return inverse, inverse


def _inverse_bwd(inverse, grad):
    size = inverse.shape[-1]
    flipped = jnp.swapaxes(inverse, -1, -2)
    full = -jnp.matmul(jnp.matmul(flipped, grad, precision=precise), flipped, precision=precise)
    places = jnp.arange(size)
    return (full * (places[:, None] > places[None, :]).astype(full.dtype),)


unit_lower_inverse.defvjp(_inverse_fwd, _inverse_bwd)


def chunk_prepare(queries, keys_n, values, decays, beta_rate, seg_ids):
    length, dk = keys_n.shape
    count = length // BLOCK
    q = queries.reshape(count, BLOCK, dk)
    k = keys_n.reshape(count, BLOCK, dk)
    v = values.reshape(count, BLOCK, values.shape[1])
    beta = beta_rate.reshape(count, BLOCK)
    seg = seg_ids.reshape(count, BLOCK)
    cumulative = jnp.cumsum(decays.reshape(count, BLOCK), axis=1)
    places = jnp.arange(BLOCK)
    lower_tri = places[:, None] >= places[None, :]
    inside = jnp.logical_and(seg[:, :, None] == seg[:, None, :], lower_tri)
    log_gap = jnp.where(inside, cumulative[:, :, None] - cumulative[:, None, :], 0.0)
    within = jnp.exp(log_gap) * inside.astype(jnp.float32)
    strict = within * (places[:, None] > places[None, :]).astype(jnp.float32)
    last_seg = jnp.concatenate([jnp.full((1,), -1, seg.dtype), seg[:-1, BLOCK - 1]])
    carried = jnp.exp(cumulative) * (seg == last_seg[:, None]).astype(jnp.float32)
    key_gram = jnp.einsum("nid,njd->nij", k, k, precision=precise)
    system = jnp.eye(BLOCK, dtype=jnp.float32) + beta[:, :, None] * strict * key_gram
    right_side = jnp.concatenate([beta[:, :, None] * v, (beta * carried)[:, :, None] * k], axis=2)
    solved = jnp.matmul(unit_lower_inverse(system), right_side, precision=precise)
    dv = v.shape[2]
    kt = within[:, BLOCK - 1, :, None] * k
    scores = jnp.einsum("nid,njd->nij", q, k, precision=precise) * within
    return solved[:, :, :dv], solved[:, :, dv:], kt, carried[:, BLOCK - 1], carried, scores


def chunk_finish(queries, carried, scores, states, updates):
    count = states.shape[0]
    q = queries.reshape(count, BLOCK, queries.shape[1])
    output = carried[:, :, None] * jnp.einsum(
        "nid,nvd->niv", q, states, precision=precise
    ) + jnp.einsum("nij,njv->niv", scores, updates, precision=precise)
    return output.reshape(count * BLOCK, states.shape[1])


def delta_rule(queries, keys_n, values, decays, beta_rate, seg_ids):
    u0, w, kt, tail, carried, scores = jax.vmap(chunk_prepare, in_axes=(0, 0, 0, 0, 0, None))(
        queries, keys_n, values, decays, beta_rate, seg_ids
    )
    c = jnp.broadcast_to(tail[:, :, None, None], tail.shape + (1, w.shape[-1]))
    states, updates = state_recurrence(u0, w, kt, c)
    return jax.vmap(chunk_finish)(queries, carried, scores, states, updates)


def head_inputs(proj_query, proj_key, proj_value, proj_alpha, proj_beta,
                kernel_query, kernel_key, kernel_value, a_here, dt_here, seg_ids):
    queries = unit_norm(jax.nn.silu(short_conv(proj_query, kernel_query, seg_ids))) * (
        1.0 / math.sqrt(proj_query.shape[1])
    )
    keys_n = unit_norm(jax.nn.silu(short_conv(proj_key, kernel_key, seg_ids)))
    values = jax.nn.silu(short_conv(proj_value, kernel_value, seg_ids))
    decays = -jnp.exp(a_here) * jax.nn.softplus(proj_alpha + dt_here)
    beta_rate = jax.nn.sigmoid(proj_beta)
    return queries, keys_n, values, decays, beta_rate


def head_output(recurrent, proj_gate, o_gain, live_mask):
    return rms_norm(recurrent, o_gain, o_floor) * jax.nn.silu(proj_gate) * live_mask[:, None]


def local_mixer(
    proj_query,
    proj_key,
    proj_value,
    proj_gate,
    proj_alpha,
    proj_beta,
    kernel_query,
    kernel_key,
    kernel_value,
    a_here,
    dt_here,
    o_gain,
    seg_ids=None,
    live_mask=None,
):
    row_count = proj_query.shape[0]
    heads_here = proj_alpha.shape[1]

    def by_head(array):
        return jnp.moveaxis(array.reshape(row_count, heads_here, -1), 1, 0)

    def kernel_heads(kernel):
        return jnp.moveaxis(kernel.reshape(kernel.shape[0], heads_here, -1), 1, 0)

    queries, keys_n, values, decays, beta_rate = jax.vmap(
        head_inputs, in_axes=(0,) * 10 + (None,)
    )(
        by_head(proj_query),
        by_head(proj_key),
        by_head(proj_value),
        proj_alpha.T,
        proj_beta.T,
        kernel_heads(kernel_query),
        kernel_heads(kernel_key),
        kernel_heads(kernel_value),
        a_here,
        dt_here,
        seg_ids,
    )
    recurrent = delta_rule(queries, keys_n, values, decays, beta_rate, seg_ids)
    mixed_heads = jax.vmap(head_output, in_axes=(0, 0, None, None))(
        recurrent, by_head(proj_gate), o_gain, live_mask
    )
    return jnp.moveaxis(mixed_heads, 0, 1).reshape(row_count, -1)


MESH_ID = pl.DeviceIdType.MESH


def _ring_position(h, major, minor):
    a = h // minor
    b = h % minor
    return b * major + a + (b % 2) * (major - 1 - 2 * a)


def _ring_member(q, major, minor):
    count = major * minor
    q = (q + count) % count
    b = q // major
    r = q % major
    return (r + (b % 2) * (major - 1 - 2 * r)) * minor + b


def _ring_sides(major, minor):
    p = _ring_position(lax.axis_index("head"), major, minor)
    return p, _ring_member(p + 1, major, minor), _ring_member(p - 1, major, minor)


def _greet(nxt, prv, row):
    barrier = pltpu.get_barrier_semaphore()
    pl.semaphore_signal(barrier, 1, device_id=(prv, row), device_id_type=MESH_ID)
    pl.semaphore_signal(barrier, 1, device_id=(nxt, row), device_id_type=MESH_ID)
    pl.semaphore_wait(barrier, 2)


def _ring_gather_kernel(major, minor, x_ref, out_ref, send_sem, recv_sem):
    count = major * minor
    blk = x_ref.shape[0]
    half = blk // 2
    row = lax.axis_index("row")
    p, nxt, prv = _ring_sides(major, minor)
    out_ref[pl.ds(pl.multiple_of(lax.axis_index("head") * blk, blk), blk), :] = x_ref[...]
    _greet(nxt, prv, row)

    def piece(pos, off):
        return out_ref.at[pl.ds(pl.multiple_of(_ring_member(pos, major, minor) * blk + off, half), half)]

    def outgoing(d, s):
        pos = p - s if d == 0 else p + s
        target = nxt if d == 0 else prv
        ref = piece(pos, d * half)
        return pltpu.make_async_remote_copy(
            ref, ref, send_sem.at[d, s], recv_sem.at[d, s], device_id=(target, row),
            device_id_type=MESH_ID,
        )

    def incoming(d, s):
        pos = p - 1 - s if d == 0 else p + 1 + s
        source = prv if d == 0 else nxt
        ref = piece(pos, d * half)
        return pltpu.make_async_remote_copy(
            ref, ref, send_sem.at[d, s], recv_sem.at[d, s], device_id=(source, row),
            device_id_type=MESH_ID,
        )

    for s in range(count - 1):
        for d in (0, 1):
            if s > 0:
                incoming(d, s - 1).wait_recv()
            outgoing(d, s).start()
    for d in (0, 1):
        incoming(d, count - 2).wait_recv()
    for s in range(count - 1):
        for d in (0, 1):
            outgoing(d, s).wait_send()


def _ring_scatter_kernel(major, minor, y_ref, out_ref, buf, send_sem, recv_sem):
    count = major * minor
    blk = out_ref.shape[0]
    half = blk // 2
    row = lax.axis_index("row")
    p, nxt, prv = _ring_sides(major, minor)
    _greet(nxt, prv, row)

    def piece(pos, off):
        return y_ref.at[pl.ds(pl.multiple_of(_ring_member(pos, major, minor) * blk + off, half), half)]

    def outgoing(d, s):
        pos = p - s - 1 if d == 0 else p + s + 1
        target = nxt if d == 0 else prv
        source = piece(pos, d * half) if s == 0 else buf.at[d, s - 1]
        return pltpu.make_async_remote_copy(
            source, buf.at[d, s], send_sem.at[d, s], recv_sem.at[d, s],
            device_id=(target, row), device_id_type=MESH_ID,
        )

    def incoming(d, s):
        source = prv if d == 0 else nxt
        return pltpu.make_async_remote_copy(
            buf.at[d, s], buf.at[d, s], send_sem.at[d, s], recv_sem.at[d, s],
            device_id=(source, row), device_id_type=MESH_ID,
        )

    for s in range(count - 1):
        for d in (0, 1):
            if s > 0:
                incoming(d, s - 1).wait_recv()
                pos = p - s - 1 if d == 0 else p + s + 1
                buf[d, s - 1] = (
                    buf[d, s - 1].astype(jnp.float32)
                    + piece(pos, d * half)[...].astype(jnp.float32)
                ).astype(buf.dtype)
            outgoing(d, s).start()
    for d in (0, 1):
        incoming(d, count - 2).wait_recv()
        out_ref[pl.ds(d * half, half), :] = piece(p, d * half)[...].astype(
            jnp.float32
        ) + buf[d, count - 2].astype(jnp.float32)
    for s in range(count - 1):
        for d in (0, 1):
            outgoing(d, s).wait_send()


def ring_gather(x, ring, collective):
    major, minor = ring
    count = major * minor
    blk, width = x.shape
    return pl.pallas_call(
        partial(_ring_gather_kernel, major, minor),
        out_shape=jax.ShapeDtypeStruct((count * blk, width), x.dtype),
        in_specs=[pl.BlockSpec(memory_space=pltpu.VMEM)],
        out_specs=pl.BlockSpec(memory_space=pltpu.VMEM),
        scratch_shapes=[
            pltpu.SemaphoreType.DMA((2, count - 1)),
            pltpu.SemaphoreType.DMA((2, count - 1)),
        ],
        compiler_params=pltpu.CompilerParams(collective_id=collective, has_side_effects=True),
        name="ring_gather_head",
    )(x)


def ring_scatter(y, ring, collective):
    major, minor = ring
    count = major * minor
    rows, width = y.shape
    blk = rows // count
    return pl.pallas_call(
        partial(_ring_scatter_kernel, major, minor),
        out_shape=jax.ShapeDtypeStruct((blk, width), jnp.float32),
        in_specs=[pl.BlockSpec(memory_space=pltpu.VMEM)],
        out_specs=pl.BlockSpec(memory_space=pltpu.VMEM),
        scratch_shapes=[
            pltpu.VMEM((2, count - 1, blk // 2, width), y.dtype),
            pltpu.SemaphoreType.DMA((2, count - 1)),
            pltpu.SemaphoreType.DMA((2, count - 1)),
        ],
        compiler_params=pltpu.CompilerParams(collective_id=collective, has_side_effects=True),
        name="ring_scatter_head",
    )(y)


def head_ring(mesh):
    count = mesh.shape["head"]
    try:
        spots = [tuple(device.coords) for device in mesh.devices[:, 0]]
    except (AttributeError, TypeError):
        return (count, 1)
    moving = [axis for axis in range(len(spots[0])) if spots[0][axis] != spots[1][axis]]
    if len(moving) != 1:
        return (count, 1)
    minor = len({spot[moving[0]] for spot in spots})
    if count % minor or minor % 2:
        return (count, 1)
    return (count // minor, minor)


def contract_rows(left, right):
    return lax.dot_general(
        left, right, (((0,), (0,)), ((), ())), preferred_element_type=jnp.float32
    )


def contract_cols(left, right):
    return lax.dot_general(
        left, right, (((1,), (1,)), ((), ())), preferred_element_type=jnp.float32
    )


def on_device(
    ring,
    tokens,
    w_query,
    w_key,
    w_value,
    w_outgate,
    w_alpha,
    w_beta,
    conv_query,
    conv_key,
    conv_value,
    a_log,
    dt_bias,
    o_gain,
    w_out,
    gain_in,
    gain_ffn,
    w_gate,
    w_up,
    w_down,
    segments,
    valid_len,
    cotangent,
):
    residual = tokens[0].astype(jnp.float32)
    heads_here = w_alpha.shape[1]
    head_first = lax.axis_index("head") * heads_here
    norm_one, pull_one = jax.vjp(rms_norm, residual, gain_in)
    normed_one = norm_one.astype(jnp.bfloat16)
    row_count = lax.psum(1, "row")
    w_local = jnp.concatenate(
        [w_query, w_key, w_value, w_outgate, w_alpha, w_beta], axis=1
    ).astype(jnp.bfloat16)
    edges = [0]
    for member in (w_query, w_key, w_value, w_outgate, w_alpha, w_beta):
        edges.append(edges[-1] + member.shape[1])
    w_inward = lax.all_gather(w_local, "row", axis=0, tiled=True)
    conv_local = jnp.concatenate([conv_query, conv_key, conv_value], axis=1).astype(jnp.bfloat16)
    conv_edges = [0, conv_query.shape[1], conv_query.shape[1] + conv_key.shape[1], conv_local.shape[1]]
    conv_all = lax.all_gather(conv_local, "row", axis=1, tiled=True).reshape(
        conv_local.shape[0], row_count, conv_local.shape[1]
    )
    conv_parts = [
        conv_all[:, :, conv_edges[i] : conv_edges[i + 1]].reshape(conv_local.shape[0], -1)
        for i in range(3)
    ]
    out_matrix = lax.all_gather(w_out.astype(jnp.bfloat16), "row", axis=1, tiled=True)
    ff_width = w_gate.shape[1]
    ffn_local = jnp.concatenate([w_gate, w_up], axis=1).astype(jnp.bfloat16)
    down_local = w_down.T.astype(jnp.bfloat16)
    grad_out = cotangent[0]
    grad_out_rows = lax.all_gather(grad_out, "row", axis=0, tiled=True)
    all_rows = ring_gather(normed_one, ring, 0)
    all_rows, out_matrix, ffn_local, down_local = lax.optimization_barrier(
        (all_rows, out_matrix, ffn_local, down_local)
    )
    ffn_all = lax.all_gather(ffn_local, "head", axis=0, tiled=True)
    down_all = lax.all_gather(down_local, "head", axis=0, tiled=True)
    projected = jnp.dot(all_rows, w_inward, preferred_element_type=jnp.float32)
    proj_parts = [projected[:, edges[spot] : edges[spot + 1]] for spot in range(6)]
    seg_ids = segments[0]
    live_mask = (jnp.arange(seg_ids.shape[0]) < valid_len[0]).astype(jnp.float32)
    a_here = lax.dynamic_slice_in_dim(a_log, head_first, heads_here)
    dt_here = lax.dynamic_slice_in_dim(dt_bias, head_first, heads_here)
    mixer_fn = partial(local_mixer, seg_ids=seg_ids, live_mask=live_mask)
    mixed, pull_core = jax.vjp(
        mixer_fn,
        proj_parts[0],
        proj_parts[1],
        proj_parts[2],
        proj_parts[3],
        proj_parts[4],
        proj_parts[5],
        conv_parts[0].astype(jnp.float32),
        conv_parts[1].astype(jnp.float32),
        conv_parts[2].astype(jnp.float32),
        a_here,
        dt_here,
        o_gain,
    )
    mixed, ffn_all, grad_out_rows = lax.optimization_barrier((mixed, ffn_all, grad_out_rows))
    w_down_t = down_all
    w_gate_all = ffn_all[:, :ff_width]
    w_up_all = ffn_all[:, ff_width : 2 * ff_width]
    mixed_half = mixed.astype(jnp.bfloat16)
    mixer_output = ring_scatter(
        jnp.dot(mixed_half, out_matrix, preferred_element_type=jnp.float32).astype(jnp.bfloat16),
        ring,
        1,
    )
    middle = residual + mixer_output
    norm_two, pull_two = jax.vjp(rms_norm, middle, gain_ffn)
    normed_two = norm_two.astype(jnp.bfloat16)
    ffn_inputs = lax.all_gather(normed_two, "row", axis=0, tiled=True)
    gate_pre = jnp.dot(ffn_inputs, w_gate_all, preferred_element_type=jnp.float32)
    up_pre = jnp.dot(ffn_inputs, w_up_all, preferred_element_type=jnp.float32)
    hidden_val, pull_act = jax.vjp(swiglu, gate_pre, up_pre)
    hidden_half = hidden_val.astype(jnp.bfloat16)
    ffn_partial = contract_cols(hidden_half, w_down_t).astype(jnp.bfloat16)
    grad_hidden = jnp.dot(grad_out_rows, w_down_t, preferred_element_type=jnp.float32)
    grad_down_t = contract_rows(grad_out_rows, hidden_half)
    grad_gate_f, grad_up_f = pull_act(grad_hidden)
    grad_gate = grad_gate_f.astype(jnp.bfloat16)
    grad_upper = grad_up_f.astype(jnp.bfloat16)
    grad_wgate = contract_rows(ffn_inputs, grad_gate)
    grad_wup = contract_rows(ffn_inputs, grad_upper)
    grad_norm_two = lax.psum_scatter(
        (contract_cols(grad_gate, w_gate_all) + contract_cols(grad_upper, w_up_all)).astype(
            jnp.bfloat16
        ),
        "row",
        scatter_dimension=0,
        tiled=True,
    ).astype(jnp.float32)
    grad_mid_part, grad_gain_ffn = pull_two(grad_norm_two)
    grad_middle = grad_out.astype(jnp.float32) + grad_mid_part
    ffn_grad_cat = jnp.concatenate([grad_wgate, grad_wup, grad_down_t], axis=1).astype(
        jnp.bfloat16
    )
    grad_mid_half = grad_middle.astype(jnp.bfloat16)
    grad_mid_rows = ring_gather(grad_mid_half, ring, 2)
    ffn_output = lax.psum_scatter(ffn_partial, "row", scatter_dimension=0, tiled=True)
    grad_mid_rows, ffn_grad_cat = lax.optimization_barrier((grad_mid_rows, ffn_grad_cat))
    ffn_grad_all = lax.psum_scatter(ffn_grad_cat, "head", scatter_dimension=0, tiled=True)
    grad_mixed = contract_cols(grad_mid_rows, out_matrix)
    grad_wout = contract_rows(mixed_half, grad_mid_rows).astype(jnp.bfloat16)
    wout_grad = lax.psum_scatter(grad_wout, "row", scatter_dimension=1, tiled=True)
    core_grads = pull_core(grad_mixed)
    core_grads, ffn_output = lax.optimization_barrier((core_grads, ffn_output))
    final_out = (middle + ffn_output.astype(jnp.float32)).astype(jnp.bfloat16)
    wide = edges[4]
    grad_proj = jnp.concatenate(
        [core_grads[0], core_grads[1], core_grads[2], core_grads[3]], axis=1
    ).astype(jnp.bfloat16)
    grad_proj_ab = jnp.concatenate([core_grads[4], core_grads[5]], axis=1).astype(jnp.bfloat16)
    grad_inward = contract_rows(all_rows, grad_proj).astype(jnp.bfloat16)
    grad_inward_ab = contract_rows(all_rows, grad_proj_ab).astype(jnp.bfloat16)
    grad_inward, ffn_grad_all = lax.optimization_barrier((grad_inward, ffn_grad_all))
    ffn_grad_all = ffn_grad_all.astype(jnp.float32)
    ffn_grads = (
        ffn_grad_all[:, :ff_width],
        ffn_grad_all[:, ff_width : 2 * ff_width],
        ffn_grad_all[:, 2 * ff_width :].T,
    )
    grad_norm_one = ring_scatter(
        (
            contract_cols(grad_proj, w_inward[:, :wide])
            + contract_cols(grad_proj_ab, w_inward[:, wide:])
        ).astype(jnp.bfloat16),
        ring,
        3,
    )
    grad_norm_one, wout_grad = lax.optimization_barrier((grad_norm_one, wout_grad))
    grad_in_part, grad_gain_in = pull_one(grad_norm_one)
    grad_input = grad_middle + grad_in_part
    inward_all = lax.psum_scatter(
        grad_inward, "row", scatter_dimension=0, tiled=True
    ).astype(jnp.float32)
    inward_ab = lax.psum_scatter(
        grad_inward_ab, "row", scatter_dimension=0, tiled=True
    ).astype(jnp.float32)
    conv_grad_local = jnp.concatenate(
        [
            core_grads[6 + i].reshape(conv_local.shape[0], row_count, -1)
            for i in range(3)
        ],
        axis=2,
    ).reshape(conv_local.shape[0], -1)
    conv_grad = lax.psum_scatter(
        conv_grad_local.astype(jnp.bfloat16), "row", scatter_dimension=1, tiled=True
    ).astype(jnp.float32)
    mixer_grads = tuple(inward_all[:, edges[spot] : edges[spot + 1]] for spot in range(4)) + (
        inward_ab[:, : edges[5] - wide],
        inward_ab[:, edges[5] - wide :],
    ) + tuple(
        conv_grad[:, conv_edges[i] : conv_edges[i + 1]] for i in range(3)
    ) + (wout_grad.astype(jnp.float32),)
    head_total = a_log.shape[0]
    grad_a_full = lax.dynamic_update_slice_in_dim(
        jnp.zeros((head_total,), jnp.float32), core_grads[9], head_first, 0
    )
    grad_dt_full = lax.dynamic_update_slice_in_dim(
        jnp.zeros((head_total,), jnp.float32), core_grads[10], head_first, 0
    )
    small_sums = lax.psum(
        (grad_gain_in, grad_gain_ffn, core_grads[11], grad_a_full, grad_dt_full), ("head", "row")
    )
    return (
        final_out[None],
        grad_input[None],
        mixer_grads[0],
        mixer_grads[1],
        mixer_grads[2],
        mixer_grads[3],
        mixer_grads[4],
        mixer_grads[5],
        mixer_grads[6],
        mixer_grads[7],
        mixer_grads[8],
        small_sums[3],
        small_sums[4],
        small_sums[2],
        mixer_grads[9],
        small_sums[0],
        small_sums[1],
        ffn_grads[0],
        ffn_grads[1],
        ffn_grads[2],
    )


def solution(mesh):
    return jax.shard_map(
        partial(on_device, head_ring(mesh)),
        mesh=mesh,
        in_specs=(
            P("row", "head", None),
            P("row", "head"),
            P("row", "head"),
            P("row", "head"),
            P("row", "head"),
            P("row", "head"),
            P("row", "head"),
            P(None, ("head", "row")),
            P(None, ("head", "row")),
            P(None, ("head", "row")),
            P(),
            P(),
            P(),
            P("head", "row"),
            P(),
            P(),
            P("head", "row"),
            P("head", "row"),
            P("row", "head"),
            P("row", None),
            P("row"),
            P("row", "head", None),
        ),
        out_specs=(
            P("row", "head", None),
            P("row", "head", None),
            P("row", "head"),
            P("row", "head"),
            P("row", "head"),
            P("row", "head"),
            P("row", "head"),
            P("row", "head"),
            P(None, ("head", "row")),
            P(None, ("head", "row")),
            P(None, ("head", "row")),
            P(),
            P(),
            P(),
            P("head", "row"),
            P(),
            P(),
            P("head", "row"),
            P("head", "row"),
            P("row", "head"),
        ),
        check_vma=False,
    )
```

```python
from functools import partial
import math

import jax
import jax.numpy as jnp
from jax import lax
from jax.sharding import PartitionSpec as P
from jax.experimental import pallas as pl
from jax.experimental.pallas import tpu as pltpu

BLOCK = 64


precise = lax.Precision.HIGHEST
epsilon = 1e-06
o_floor = 0.001


def rms_norm(vector, gain_vec, floor_add=epsilon):
    return (
        vector * lax.rsqrt(jnp.mean(vector * vector, axis=-1, keepdims=True) + floor_add) * gain_vec
    )


def unit_norm(vector):
    return vector * lax.rsqrt(jnp.sum(vector * vector, axis=-1, keepdims=True) + epsilon)


def swiglu(gate_pre, up_pre):
    return jax.nn.silu(gate_pre) * up_pre


def short_conv(signal, kernel, seg_ids):
    tap_count = kernel.shape[0]
    length = signal.shape[0]
    summed = signal * kernel[tap_count - 1]
    for offset in range(1, tap_count):
        shifted = jnp.concatenate(
            [jnp.zeros((offset, signal.shape[1]), signal.dtype), signal[: length - offset]], axis=0
        )
        seg_shift = jnp.concatenate(
            [jnp.full((offset,), -1, jnp.int32), seg_ids[: length - offset]]
        )
        keep_mask = (seg_shift == seg_ids).astype(signal.dtype)
        summed = summed + shifted * kernel[tap_count - 1 - offset] * keep_mask[:, None]
    return summed


def _recur_fwd_kernel(nb, u0_ref, w_ref, kt_ref, c_ref, s_out, u_out, s_scr):
    @pl.when(pl.program_id(1) == 0)
    def _():
        s_scr[...] = jnp.zeros_like(s_scr)

    def step(j, carry):
        state = s_scr[...]
        s_out[0, j] = state
        update = u0_ref[0, j] - lax.dot_general(
            w_ref[0, j], state, (((1,), (1,)), ((), ())),
            precision=precise, preferred_element_type=jnp.float32,
        )
        u_out[0, j] = update
        s_scr[...] = c_ref[0, j] * state + lax.dot_general(
            update, kt_ref[0, j], (((0,), (0,)), ((), ())),
            precision=precise, preferred_element_type=jnp.float32,
        )
        return carry

    lax.fori_loop(0, nb, step, 0)


def _recur_bwd_kernel(
    nb, s_ref, u_ref, w_ref, kt_ref, c_ref, ds_ref, du_ref,
    du0_out, dw_out, dkt_out, dc_out, g_scr,
):
    @pl.when(pl.program_id(1) == 0)
    def _():
        g_scr[...] = jnp.zeros_like(g_scr)

    def step(i, carry):
        j = nb - 1 - i
        grad_state = g_scr[...]
        state = s_ref[0, j]
        grad_update = du_ref[0, j] + lax.dot_general(
            kt_ref[0, j], grad_state, (((1,), (1,)), ((), ())),
            precision=precise, preferred_element_type=jnp.float32,
        )
        dkt_out[0, j] = jnp.dot(
            u_ref[0, j], grad_state, precision=precise, preferred_element_type=jnp.float32
        )
        dc_out[0, j] = jnp.sum(grad_state * state, axis=0, keepdims=True)
        du0_out[0, j] = grad_update
        dw_out[0, j] = -jnp.dot(
            grad_update, state, precision=precise, preferred_element_type=jnp.float32
        )
        g_scr[...] = (
            c_ref[0, j] * grad_state
            - lax.dot_general(
                grad_update, w_ref[0, j], (((0,), (0,)), ((), ())),
                precision=precise, preferred_element_type=jnp.float32,
            )
            + ds_ref[0, j]
        )
        return carry

    lax.fori_loop(0, nb, step, 0)


def _chunk_spec(nb, tail, reverse, count):
    if reverse:
        return pl.BlockSpec((1, nb) + tail, lambda h, b: (h, count - 1 - b, 0, 0))
    return pl.BlockSpec((1, nb) + tail, lambda h, b: (h, b, 0, 0))


def _recur_forward(u0, w, kt, c):
    heads, count, chunk, dv = u0.shape
    dk = w.shape[-1]
    nb = min(8, count)
    blocks = count // nb
    flops = 4 * heads * count * chunk * dk * dv * 6
    moved = 4 * heads * count * (2 * chunk * dv + 2 * chunk * dk + dv * dk)
    return pl.pallas_call(
        partial(_recur_fwd_kernel, nb),
        grid=(heads, blocks),
        in_specs=[
            _chunk_spec(nb, (chunk, dv), False, blocks),
            _chunk_spec(nb, (chunk, dk), False, blocks),
            _chunk_spec(nb, (chunk, dk), False, blocks),
            _chunk_spec(nb, (1, dk), False, blocks),
        ],
        out_specs=[
            _chunk_spec(nb, (dv, dk), False, blocks),
            _chunk_spec(nb, (chunk, dv), False, blocks),
        ],
        out_shape=[
            jax.ShapeDtypeStruct((heads, count, dv, dk), jnp.float32),
            jax.ShapeDtypeStruct((heads, count, chunk, dv), jnp.float32),
        ],
        scratch_shapes=[pltpu.VMEM((dv, dk), jnp.float32)],
        compiler_params=pltpu.CompilerParams(dimension_semantics=("arbitrary", "arbitrary")),
        cost_estimate=pl.CostEstimate(flops=flops, transcendentals=0, bytes_accessed=moved),
        name="delta_state_forward",
    )(u0, w, kt, c)


def _recur_backward(states, updates, w, kt, c, d_states, d_updates):
    heads, count, chunk, dv = updates.shape
    dk = w.shape[-1]
    nb = min(8, count)
    blocks = count // nb
    flops = 8 * heads * count * chunk * dk * dv * 6
    moved = 4 * heads * count * (4 * chunk * dv + 4 * chunk * dk + 2 * dv * dk)
    return pl.pallas_call(
        partial(_recur_bwd_kernel, nb),
        grid=(heads, blocks),
        in_specs=[
            _chunk_spec(nb, (dv, dk), True, blocks),
            _chunk_spec(nb, (chunk, dv), True, blocks),
            _chunk_spec(nb, (chunk, dk), True, blocks),
            _chunk_spec(nb, (chunk, dk), True, blocks),
            _chunk_spec(nb, (1, dk), True, blocks),
            _chunk_spec(nb, (dv, dk), True, blocks),
            _chunk_spec(nb, (chunk, dv), True, blocks),
        ],
        out_specs=[
            _chunk_spec(nb, (chunk, dv), True, blocks),
            _chunk_spec(nb, (chunk, dk), True, blocks),
            _chunk_spec(nb, (chunk, dk), True, blocks),
            _chunk_spec(nb, (1, dk), True, blocks),
        ],
        out_shape=[
            jax.ShapeDtypeStruct((heads, count, chunk, dv), jnp.float32),
            jax.ShapeDtypeStruct((heads, count, chunk, dk), jnp.float32),
            jax.ShapeDtypeStruct((heads, count, chunk, dk), jnp.float32),
            jax.ShapeDtypeStruct((heads, count, 1, dk), jnp.float32),
        ],
        scratch_shapes=[pltpu.VMEM((dv, dk), jnp.float32)],
        compiler_params=pltpu.CompilerParams(dimension_semantics=("arbitrary", "arbitrary")),
        cost_estimate=pl.CostEstimate(flops=flops, transcendentals=0, bytes_accessed=moved),
        name="delta_state_backward",
    )(states, updates, w, kt, c, d_states, d_updates)


@jax.custom_vjp
def state_recurrence(u0, w, kt, c):
    return _recur_forward(u0, w, kt, c)


def _recurrence_fwd(u0, w, kt, c):
    states, updates = _recur_forward(u0, w, kt, c)
    return (states, updates), (states, updates, w, kt, c)


def _recurrence_bwd(saved, grads):
    states, updates, w, kt, c = saved
    d_states, d_updates = grads
    du0, dw, dkt, dc_lanes = _recur_backward(states, updates, w, kt, c, d_states, d_updates)
    return du0, dw, dkt, dc_lanes


state_recurrence.defvjp(_recurrence_fwd, _recurrence_bwd)


def _unit_lower_inverse_small(system):
    size = system.shape[-1]
    strict = system - jnp.eye(size, dtype=system.dtype)
    power = -strict
    inverse = jnp.eye(size, dtype=system.dtype) + power
    done = 2
    while done < size:
        power = jnp.matmul(power, power, precision=precise)
        inverse = inverse + jnp.matmul(power, inverse, precision=precise)
        done *= 2
    return inverse


def _unit_lower_inverse_forward(system):
    size = system.shape[-1]
    base = min(8, size)
    lead = system.shape[:-2]
    count = size // base
    blocks = system.reshape(lead + (count, base, count, base))
    diag = jnp.stack([blocks[..., i, :, i, :] for i in range(count)], axis=-3)
    inverse = _unit_lower_inverse_small(diag)
    width = base
    while width < size:
        pairs = inverse.shape[-3] // 2
        upper = inverse[..., 0::2, :, :]
        lower = inverse[..., 1::2, :, :]
        below = jnp.stack(
            [
                system[..., (2 * i + 1) * width : (2 * i + 2) * width, 2 * i * width : (2 * i + 1) * width]
                for i in range(pairs)
            ],
            axis=-3,
        )
        corner = -jnp.matmul(
            lower, jnp.matmul(below, upper, precision=precise), precision=precise
        )
        zeros = jnp.zeros_like(upper)
        top = jnp.concatenate([upper, zeros], axis=-1)
        bottom = jnp.concatenate([corner, lower], axis=-1)
        inverse = jnp.concatenate([top, bottom], axis=-2)
        width *= 2
    return inverse[..., 0, :, :]


@jax.custom_vjp
def unit_lower_inverse(system):
    return _unit_lower_inverse_forward(system)


def _inverse_fwd(system):
    inverse = _unit_lower_inverse_forward(system)
    return inverse, inverse


def _inverse_bwd(inverse, grad):
    size = inverse.shape[-1]
    flipped = jnp.swapaxes(inverse, -1, -2)
    full = -jnp.matmul(jnp.matmul(flipped, grad, precision=precise), flipped, precision=precise)
    places = jnp.arange(size)
    return (full * (places[:, None] > places[None, :]).astype(full.dtype),)


unit_lower_inverse.defvjp(_inverse_fwd, _inverse_bwd)


def chunk_prepare(queries, keys_n, values, decays, beta_rate, seg_ids):
    length, dk = keys_n.shape
    count = length // BLOCK
    q = queries.reshape(count, BLOCK, dk)
    k = keys_n.reshape(count, BLOCK, dk)
    v = values.reshape(count, BLOCK, values.shape[1])
    beta = beta_rate.reshape(count, BLOCK)
    seg = seg_ids.reshape(count, BLOCK)
    cumulative = jnp.cumsum(decays.reshape(count, BLOCK), axis=1)
    places = jnp.arange(BLOCK)
    lower_tri = places[:, None] >= places[None, :]
    inside = jnp.logical_and(seg[:, :, None] == seg[:, None, :], lower_tri)
    log_gap = jnp.where(inside, cumulative[:, :, None] - cumulative[:, None, :], 0.0)
    within = jnp.exp(log_gap) * inside.astype(jnp.float32)
    strict = within * (places[:, None] > places[None, :]).astype(jnp.float32)
    last_seg = jnp.concatenate([jnp.full((1,), -1, seg.dtype), seg[:-1, BLOCK - 1]])
    carried = jnp.exp(cumulative) * (seg == last_seg[:, None]).astype(jnp.float32)
    key_gram = jnp.einsum("nid,njd->nij", k, k, precision=precise)
    system = jnp.eye(BLOCK, dtype=jnp.float32) + beta[:, :, None] * strict * key_gram
    right_side = jnp.concatenate([beta[:, :, None] * v, (beta * carried)[:, :, None] * k], axis=2)
    solved = jnp.matmul(unit_lower_inverse(system), right_side, precision=precise)
    dv = v.shape[2]
    kt = within[:, BLOCK - 1, :, None] * k
    scores = jnp.einsum("nid,njd->nij", q, k, precision=precise) * within
    return solved[:, :, :dv], solved[:, :, dv:], kt, carried[:, BLOCK - 1], carried, scores


def chunk_finish(queries, carried, scores, states, updates):
    count = states.shape[0]
    q = queries.reshape(count, BLOCK, queries.shape[1])
    output = carried[:, :, None] * jnp.einsum(
        "nid,nvd->niv", q, states, precision=precise
    ) + jnp.einsum("nij,njv->niv", scores, updates, precision=precise)
    return output.reshape(count * BLOCK, states.shape[1])


def delta_rule(queries, keys_n, values, decays, beta_rate, seg_ids):
    u0, w, kt, tail, carried, scores = jax.vmap(chunk_prepare, in_axes=(0, 0, 0, 0, 0, None))(
        queries, keys_n, values, decays, beta_rate, seg_ids
    )
    c = jnp.broadcast_to(tail[:, :, None, None], tail.shape + (1, w.shape[-1]))
    states, updates = state_recurrence(u0, w, kt, c)
    return jax.vmap(chunk_finish)(queries, carried, scores, states, updates)


def head_inputs(proj_query, proj_key, proj_value, proj_alpha, proj_beta,
                kernel_query, kernel_key, kernel_value, a_here, dt_here, seg_ids):
    queries = unit_norm(jax.nn.silu(short_conv(proj_query, kernel_query, seg_ids))) * (
        1.0 / math.sqrt(proj_query.shape[1])
    )
    keys_n = unit_norm(jax.nn.silu(short_conv(proj_key, kernel_key, seg_ids)))
    values = jax.nn.silu(short_conv(proj_value, kernel_value, seg_ids))
    decays = -jnp.exp(a_here) * jax.nn.softplus(proj_alpha + dt_here)
    beta_rate = jax.nn.sigmoid(proj_beta)
    return queries, keys_n, values, decays, beta_rate


def head_output(recurrent, proj_gate, o_gain, live_mask):
    return rms_norm(recurrent, o_gain, o_floor) * jax.nn.silu(proj_gate) * live_mask[:, None]


def local_mixer(
    proj_query,
    proj_key,
    proj_value,
    proj_gate,
    proj_alpha,
    proj_beta,
    kernel_query,
    kernel_key,
    kernel_value,
    a_here,
    dt_here,
    o_gain,
    seg_ids=None,
    live_mask=None,
):
    row_count = proj_query.shape[0]
    heads_here = proj_alpha.shape[1]

    def by_head(array):
        return jnp.moveaxis(array.reshape(row_count, heads_here, -1), 1, 0)

    def kernel_heads(kernel):
        return jnp.moveaxis(kernel.reshape(kernel.shape[0], heads_here, -1), 1, 0)

    queries, keys_n, values, decays, beta_rate = jax.vmap(
        head_inputs, in_axes=(0,) * 10 + (None,)
    )(
        by_head(proj_query),
        by_head(proj_key),
        by_head(proj_value),
        proj_alpha.T,
        proj_beta.T,
        kernel_heads(kernel_query),
        kernel_heads(kernel_key),
        kernel_heads(kernel_value),
        a_here,
        dt_here,
        seg_ids,
    )
    recurrent = delta_rule(queries, keys_n, values, decays, beta_rate, seg_ids)
    mixed_heads = jax.vmap(head_output, in_axes=(0, 0, None, None))(
        recurrent, by_head(proj_gate), o_gain, live_mask
    )
    return jnp.moveaxis(mixed_heads, 0, 1).reshape(row_count, -1)


MESH_ID = pl.DeviceIdType.MESH


def _ring_position(h, major, minor):
    a = h // minor
    b = h % minor
    return b * major + a + (b % 2) * (major - 1 - 2 * a)


def _ring_member(q, major, minor):
    count = major * minor
    q = (q + count) % count
    b = q // major
    r = q % major
    return (r + (b % 2) * (major - 1 - 2 * r)) * minor + b


def _ring_sides(major, minor):
    p = _ring_position(lax.axis_index("head"), major, minor)
    return p, _ring_member(p + 1, major, minor), _ring_member(p - 1, major, minor)


def _greet(nxt, prv, row):
    barrier = pltpu.get_barrier_semaphore()
    pl.semaphore_signal(barrier, 1, device_id=(prv, row), device_id_type=MESH_ID)
    pl.semaphore_signal(barrier, 1, device_id=(nxt, row), device_id_type=MESH_ID)
    pl.semaphore_wait(barrier, 2)


def _ring_gather_kernel(major, minor, x_ref, out_ref, send_sem, recv_sem):
    count = major * minor
    blk = x_ref.shape[0]
    half = blk // 2
    row = lax.axis_index("row")
    p, nxt, prv = _ring_sides(major, minor)
    out_ref[pl.ds(pl.multiple_of(lax.axis_index("head") * blk, blk), blk), :] = x_ref[...]
    _greet(nxt, prv, row)

    def piece(pos, off):
        return out_ref.at[pl.ds(pl.multiple_of(_ring_member(pos, major, minor) * blk + off, half), half)]

    def outgoing(d, s):
        pos = p - s if d == 0 else p + s
        target = nxt if d == 0 else prv
        ref = piece(pos, d * half)
        return pltpu.make_async_remote_copy(
            ref, ref, send_sem.at[d, s], recv_sem.at[d, s], device_id=(target, row),
            device_id_type=MESH_ID,
        )

    def incoming(d, s):
        pos = p - 1 - s if d == 0 else p + 1 + s
        source = prv if d == 0 else nxt
        ref = piece(pos, d * half)
        return pltpu.make_async_remote_copy(
            ref, ref, send_sem.at[d, s], recv_sem.at[d, s], device_id=(source, row),
            device_id_type=MESH_ID,
        )

    for s in range(count - 1):
        for d in (0, 1):
            if s > 0:
                incoming(d, s - 1).wait_recv()
            outgoing(d, s).start()
    for d in (0, 1):
        incoming(d, count - 2).wait_recv()
    for s in range(count - 1):
        for d in (0, 1):
            outgoing(d, s).wait_send()


def _ring_scatter_kernel(major, minor, y_ref, out_ref, buf, send_sem, recv_sem):
    count = major * minor
    blk = out_ref.shape[0]
    half = blk // 2
    row = lax.axis_index("row")
    p, nxt, prv = _ring_sides(major, minor)
    _greet(nxt, prv, row)

    def piece(pos, off):
        return y_ref.at[pl.ds(pl.multiple_of(_ring_member(pos, major, minor) * blk + off, half), half)]

    def outgoing(d, s):
        pos = p - s - 1 if d == 0 else p + s + 1
        target = nxt if d == 0 else prv
        source = piece(pos, d * half) if s == 0 else buf.at[d, s - 1]
        return pltpu.make_async_remote_copy(
            source, buf.at[d, s], send_sem.at[d, s], recv_sem.at[d, s],
            device_id=(target, row), device_id_type=MESH_ID,
        )

    def incoming(d, s):
        source = prv if d == 0 else nxt
        return pltpu.make_async_remote_copy(
            buf.at[d, s], buf.at[d, s], send_sem.at[d, s], recv_sem.at[d, s],
            device_id=(source, row), device_id_type=MESH_ID,
        )

    for s in range(count - 1):
        for d in (0, 1):
            if s > 0:
                incoming(d, s - 1).wait_recv()
                pos = p - s - 1 if d == 0 else p + s + 1
                buf[d, s - 1] = (
                    buf[d, s - 1].astype(jnp.float32)
                    + piece(pos, d * half)[...].astype(jnp.float32)
                ).astype(buf.dtype)
            outgoing(d, s).start()
    for d in (0, 1):
        incoming(d, count - 2).wait_recv()
        out_ref[pl.ds(d * half, half), :] = piece(p, d * half)[...].astype(
            jnp.float32
        ) + buf[d, count - 2].astype(jnp.float32)
    for s in range(count - 1):
        for d in (0, 1):
            outgoing(d, s).wait_send()


def ring_gather(x, ring, collective):
    major, minor = ring
    count = major * minor
    blk, width = x.shape
    return pl.pallas_call(
        partial(_ring_gather_kernel, major, minor),
        out_shape=jax.ShapeDtypeStruct((count * blk, width), x.dtype),
        in_specs=[pl.BlockSpec(memory_space=pltpu.VMEM)],
        out_specs=pl.BlockSpec(memory_space=pltpu.VMEM),
        scratch_shapes=[
            pltpu.SemaphoreType.DMA((2, count - 1)),
            pltpu.SemaphoreType.DMA((2, count - 1)),
        ],
        compiler_params=pltpu.CompilerParams(collective_id=collective, has_side_effects=True),
        name="ring_gather_head",
    )(x)


def ring_scatter(y, ring, collective):
    major, minor = ring
    count = major * minor
    rows, width = y.shape
    blk = rows // count
    return pl.pallas_call(
        partial(_ring_scatter_kernel, major, minor),
        out_shape=jax.ShapeDtypeStruct((blk, width), jnp.float32),
        in_specs=[pl.BlockSpec(memory_space=pltpu.VMEM)],
        out_specs=pl.BlockSpec(memory_space=pltpu.VMEM),
        scratch_shapes=[
            pltpu.VMEM((2, count - 1, blk // 2, width), y.dtype),
            pltpu.SemaphoreType.DMA((2, count - 1)),
            pltpu.SemaphoreType.DMA((2, count - 1)),
        ],
        compiler_params=pltpu.CompilerParams(collective_id=collective, has_side_effects=True),
        name="ring_scatter_head",
    )(y)


def head_ring(mesh):
    count = mesh.shape["head"]
    try:
        spots = [tuple(device.coords) for device in mesh.devices[:, 0]]
    except (AttributeError, TypeError):
        return (count, 1)
    moving = [axis for axis in range(len(spots[0])) if spots[0][axis] != spots[1][axis]]
    if len(moving) != 1:
        return (count, 1)
    minor = len({spot[moving[0]] for spot in spots})
    if count % minor or minor % 2:
        return (count, 1)
    return (count // minor, minor)


def contract_rows(left, right):
    return lax.dot_general(
        left, right, (((0,), (0,)), ((), ())), preferred_element_type=jnp.float32
    )


def contract_cols(left, right):
    return lax.dot_general(
        left, right, (((1,), (1,)), ((), ())), preferred_element_type=jnp.float32
    )


def on_device(
    ring,
    tokens,
    w_query,
    w_key,
    w_value,
    w_outgate,
    w_alpha,
    w_beta,
    conv_query,
    conv_key,
    conv_value,
    a_log,
    dt_bias,
    o_gain,
    w_out,
    gain_in,
    gain_ffn,
    w_gate,
    w_up,
    w_down,
    segments,
    valid_len,
    cotangent,
):
    residual = tokens[0].astype(jnp.float32)
    heads_here = w_alpha.shape[1]
    head_first = lax.axis_index("head") * heads_here
    norm_one, pull_one = jax.vjp(rms_norm, residual, gain_in)
    normed_one = norm_one.astype(jnp.bfloat16)
    row_count = lax.psum(1, "row")
    w_local = jnp.concatenate(
        [w_query, w_key, w_value, w_outgate, w_alpha, w_beta], axis=1
    ).astype(jnp.bfloat16)
    edges = [0]
    for member in (w_query, w_key, w_value, w_outgate, w_alpha, w_beta):
        edges.append(edges[-1] + member.shape[1])
    w_inward = lax.all_gather(w_local, "row", axis=0, tiled=True)
    conv_local = jnp.concatenate([conv_query, conv_key, conv_value], axis=1).astype(jnp.bfloat16)
    conv_edges = [0, conv_query.shape[1], conv_query.shape[1] + conv_key.shape[1], conv_local.shape[1]]
    conv_all = lax.all_gather(conv_local, "row", axis=1, tiled=True).reshape(
        conv_local.shape[0], row_count, conv_local.shape[1]
    )
    conv_parts = [
        conv_all[:, :, conv_edges[i] : conv_edges[i + 1]].reshape(conv_local.shape[0], -1)
        for i in range(3)
    ]
    out_matrix = lax.all_gather(w_out.astype(jnp.bfloat16), "row", axis=1, tiled=True)
    ff_width = w_gate.shape[1]
    ffn_local = jnp.concatenate([w_gate, w_up], axis=1).astype(jnp.bfloat16)
    down_local = w_down.T.astype(jnp.bfloat16)
    grad_out = cotangent[0]
    grad_out_rows = lax.all_gather(grad_out, "row", axis=0, tiled=True)
    all_rows = ring_gather(normed_one, ring, 0)
    all_rows, out_matrix, ffn_local, down_local = lax.optimization_barrier(
        (all_rows, out_matrix, ffn_local, down_local)
    )
    ffn_all = lax.all_gather(ffn_local, "head", axis=0, tiled=True)
    down_all = lax.all_gather(down_local, "head", axis=0, tiled=True)
    projected = jnp.dot(all_rows, w_inward, preferred_element_type=jnp.float32)
    proj_parts = [projected[:, edges[spot] : edges[spot + 1]] for spot in range(6)]
    seg_ids = segments[0]
    live_mask = (jnp.arange(seg_ids.shape[0]) < valid_len[0]).astype(jnp.float32)
    a_here = lax.dynamic_slice_in_dim(a_log, head_first, heads_here)
    dt_here = lax.dynamic_slice_in_dim(dt_bias, head_first, heads_here)
    mixer_fn = partial(local_mixer, seg_ids=seg_ids, live_mask=live_mask)
    mixed, pull_core = jax.vjp(
        mixer_fn,
        proj_parts[0],
        proj_parts[1],
        proj_parts[2],
        proj_parts[3],
        proj_parts[4],
        proj_parts[5],
        conv_parts[0].astype(jnp.float32),
        conv_parts[1].astype(jnp.float32),
        conv_parts[2].astype(jnp.float32),
        a_here,
        dt_here,
        o_gain,
    )
    mixed, ffn_all, grad_out_rows = lax.optimization_barrier((mixed, ffn_all, grad_out_rows))
    w_down_t = down_all
    w_gate_all = ffn_all[:, :ff_width]
    w_up_all = ffn_all[:, ff_width : 2 * ff_width]
    mixed_half = mixed.astype(jnp.bfloat16)
    mixer_output = ring_scatter(
        jnp.dot(mixed_half, out_matrix, preferred_element_type=jnp.float32).astype(jnp.bfloat16),
        ring,
        1,
    )
    middle = residual + mixer_output
    norm_two, pull_two = jax.vjp(rms_norm, middle, gain_ffn)
    normed_two = norm_two.astype(jnp.bfloat16)
    ffn_inputs = lax.all_gather(normed_two, "row", axis=0, tiled=True)
    gate_pre = jnp.dot(ffn_inputs, w_gate_all, preferred_element_type=jnp.float32)
    up_pre = jnp.dot(ffn_inputs, w_up_all, preferred_element_type=jnp.float32)
    hidden_val, pull_act = jax.vjp(swiglu, gate_pre, up_pre)
    hidden_half = hidden_val.astype(jnp.bfloat16)
    ffn_partial = contract_cols(hidden_half, w_down_t).astype(jnp.bfloat16)
    grad_hidden = jnp.dot(grad_out_rows, w_down_t, preferred_element_type=jnp.float32)
    grad_down_t = contract_rows(grad_out_rows, hidden_half)
    grad_gate_f, grad_up_f = pull_act(grad_hidden)
    grad_gate = grad_gate_f.astype(jnp.bfloat16)
    grad_upper = grad_up_f.astype(jnp.bfloat16)
    grad_wgate = contract_rows(ffn_inputs, grad_gate)
    grad_wup = contract_rows(ffn_inputs, grad_upper)
    grad_norm_two = lax.psum_scatter(
        (contract_cols(grad_gate, w_gate_all) + contract_cols(grad_upper, w_up_all)).astype(
            jnp.bfloat16
        ),
        "row",
        scatter_dimension=0,
        tiled=True,
    ).astype(jnp.float32)
    grad_mid_part, grad_gain_ffn = pull_two(grad_norm_two)
    grad_middle = grad_out.astype(jnp.float32) + grad_mid_part
    ffn_grad_cat = jnp.concatenate([grad_wgate, grad_wup, grad_down_t], axis=1).astype(
        jnp.bfloat16
    )
    grad_mid_half = grad_middle.astype(jnp.bfloat16)
    grad_mid_rows = ring_gather(grad_mid_half, ring, 2)
    ffn_output = lax.psum_scatter(ffn_partial, "row", scatter_dimension=0, tiled=True)
    grad_mid_rows, ffn_grad_cat = lax.optimization_barrier((grad_mid_rows, ffn_grad_cat))
    ffn_grad_all = lax.psum_scatter(ffn_grad_cat, "head", scatter_dimension=0, tiled=True)
    grad_mixed = contract_cols(grad_mid_rows, out_matrix)
    grad_wout = contract_rows(mixed_half, grad_mid_rows).astype(jnp.bfloat16)
    wout_grad = lax.psum_scatter(grad_wout, "row", scatter_dimension=1, tiled=True)
    core_grads = pull_core(grad_mixed)
    core_grads, ffn_output = lax.optimization_barrier((core_grads, ffn_output))
    final_out = (middle + ffn_output.astype(jnp.float32)).astype(jnp.bfloat16)
    wide = edges[4]
    grad_proj = jnp.concatenate(
        [core_grads[0], core_grads[1], core_grads[2], core_grads[3]], axis=1
    ).astype(jnp.bfloat16)
    grad_proj_ab = jnp.concatenate([core_grads[4], core_grads[5]], axis=1).astype(jnp.bfloat16)
    grad_inward = contract_rows(all_rows, grad_proj).astype(jnp.bfloat16)
    grad_inward_ab = contract_rows(all_rows, grad_proj_ab).astype(jnp.bfloat16)
    norm_one_partial = (
        contract_cols(grad_proj, w_inward[:, :wide])
        + contract_cols(grad_proj_ab, w_inward[:, wide:])
    ).astype(jnp.bfloat16)
    grad_inward, norm_one_partial = lax.optimization_barrier((grad_inward, norm_one_partial))
    grad_inward, ffn_grad_all = lax.optimization_barrier((grad_inward, ffn_grad_all))
    ffn_grad_all = ffn_grad_all.astype(jnp.float32)
    ffn_grads = (
        ffn_grad_all[:, :ff_width],
        ffn_grad_all[:, ff_width : 2 * ff_width],
        ffn_grad_all[:, 2 * ff_width :].T,
    )
    grad_norm_one = ring_scatter(norm_one_partial, ring, 3)
    grad_norm_one, wout_grad = lax.optimization_barrier((grad_norm_one, wout_grad))
    grad_in_part, grad_gain_in = pull_one(grad_norm_one)
    grad_input = grad_middle + grad_in_part
    inward_all = lax.psum_scatter(
        grad_inward, "row", scatter_dimension=0, tiled=True
    ).astype(jnp.float32)
    inward_ab = lax.psum_scatter(
        grad_inward_ab, "row", scatter_dimension=0, tiled=True
    ).astype(jnp.float32)
    conv_grad_local = jnp.concatenate(
        [
            core_grads[6 + i].reshape(conv_local.shape[0], row_count, -1)
            for i in range(3)
        ],
        axis=2,
    ).reshape(conv_local.shape[0], -1)
    conv_grad = lax.psum_scatter(
        conv_grad_local.astype(jnp.bfloat16), "row", scatter_dimension=1, tiled=True
    ).astype(jnp.float32)
    mixer_grads = tuple(inward_all[:, edges[spot] : edges[spot + 1]] for spot in range(4)) + (
        inward_ab[:, : edges[5] - wide],
        inward_ab[:, edges[5] - wide :],
    ) + tuple(
        conv_grad[:, conv_edges[i] : conv_edges[i + 1]] for i in range(3)
    ) + (wout_grad.astype(jnp.float32),)
    head_total = a_log.shape[0]
    grad_a_full = lax.dynamic_update_slice_in_dim(
        jnp.zeros((head_total,), jnp.float32), core_grads[9], head_first, 0
    )
    grad_dt_full = lax.dynamic_update_slice_in_dim(
        jnp.zeros((head_total,), jnp.float32), core_grads[10], head_first, 0
    )
    small_sums = lax.psum(
        (grad_gain_in, grad_gain_ffn, core_grads[11], grad_a_full, grad_dt_full), ("head", "row")
    )
    return (
        final_out[None],
        grad_input[None],
        mixer_grads[0],
        mixer_grads[1],
        mixer_grads[2],
        mixer_grads[3],
        mixer_grads[4],
        mixer_grads[5],
        mixer_grads[6],
        mixer_grads[7],
        mixer_grads[8],
        small_sums[3],
        small_sums[4],
        small_sums[2],
        mixer_grads[9],
        small_sums[0],
        small_sums[1],
        ffn_grads[0],
        ffn_grads[1],
        ffn_grads[2],
    )


def solution(mesh):
    return jax.shard_map(
        partial(on_device, head_ring(mesh)),
        mesh=mesh,
        in_specs=(
            P("row", "head", None),
            P("row", "head"),
            P("row", "head"),
            P("row", "head"),
            P("row", "head"),
            P("row", "head"),
            P("row", "head"),
            P(None, ("head", "row")),
            P(None, ("head", "row")),
            P(None, ("head", "row")),
            P(),
            P(),
            P(),
            P("head", "row"),
            P(),
            P(),
            P("head", "row"),
            P("head", "row"),
            P("row", "head"),
            P("row", None),
            P("row"),
            P("row", "head", None),
        ),
        out_specs=(
            P("row", "head", None),
            P("row", "head", None),
            P("row", "head"),
            P("row", "head"),
            P("row", "head"),
            P("row", "head"),
            P("row", "head"),
            P("row", "head"),
            P(None, ("head", "row")),
            P(None, ("head", "row")),
            P(None, ("head", "row")),
            P(),
            P(),
            P(),
            P("head", "row"),
            P(),
            P(),
            P("head", "row"),
            P("head", "row"),
            P("row", "head"),
        ),
        check_vma=False,
    )
```

```python
from functools import partial
import math

import jax
import jax.numpy as jnp
from jax import lax
from jax.sharding import PartitionSpec as P
from jax.experimental import pallas as pl
from jax.experimental.pallas import tpu as pltpu

BLOCK = 64


precise = lax.Precision.HIGHEST
epsilon = 1e-06
o_floor = 0.001


def rms_norm(vector, gain_vec, floor_add=epsilon):
    return (
        vector * lax.rsqrt(jnp.mean(vector * vector, axis=-1, keepdims=True) + floor_add) * gain_vec
    )


def unit_norm(vector):
    return vector * lax.rsqrt(jnp.sum(vector * vector, axis=-1, keepdims=True) + epsilon)


def swiglu(gate_pre, up_pre):
    return jax.nn.silu(gate_pre) * up_pre


def short_conv(signal, kernel, seg_ids):
    tap_count = kernel.shape[0]
    length = signal.shape[0]
    summed = signal * kernel[tap_count - 1]
    for offset in range(1, tap_count):
        shifted = jnp.concatenate(
            [jnp.zeros((offset, signal.shape[1]), signal.dtype), signal[: length - offset]], axis=0
        )
        seg_shift = jnp.concatenate(
            [jnp.full((offset,), -1, jnp.int32), seg_ids[: length - offset]]
        )
        keep_mask = (seg_shift == seg_ids).astype(signal.dtype)
        summed = summed + shifted * kernel[tap_count - 1 - offset] * keep_mask[:, None]
    return summed


def _recur_fwd_kernel(nb, u0_ref, w_ref, kt_ref, c_ref, s_out, u_out, s_scr):
    @pl.when(pl.program_id(1) == 0)
    def _():
        s_scr[...] = jnp.zeros_like(s_scr)

    def step(j, carry):
        state = s_scr[...]
        s_out[0, j] = state
        update = u0_ref[0, j] - lax.dot_general(
            w_ref[0, j], state, (((1,), (1,)), ((), ())),
            precision=precise, preferred_element_type=jnp.float32,
        )
        u_out[0, j] = update
        s_scr[...] = c_ref[0, j] * state + lax.dot_general(
            update, kt_ref[0, j], (((0,), (0,)), ((), ())),
            precision=precise, preferred_element_type=jnp.float32,
        )
        return carry

    lax.fori_loop(0, nb, step, 0)


def _recur_bwd_kernel(
    nb, s_ref, u_ref, w_ref, kt_ref, c_ref, ds_ref, du_ref,
    du0_out, dw_out, dkt_out, dc_out, g_scr,
):
    @pl.when(pl.program_id(1) == 0)
    def _():
        g_scr[...] = jnp.zeros_like(g_scr)

    def step(i, carry):
        j = nb - 1 - i
        grad_state = g_scr[...]
        state = s_ref[0, j]
        grad_update = du_ref[0, j] + lax.dot_general(
            kt_ref[0, j], grad_state, (((1,), (1,)), ((), ())),
            precision=precise, preferred_element_type=jnp.float32,
        )
        dkt_out[0, j] = jnp.dot(
            u_ref[0, j], grad_state, precision=precise, preferred_element_type=jnp.float32
        )
        dc_out[0, j] = jnp.sum(grad_state * state, axis=0, keepdims=True)
        du0_out[0, j] = grad_update
        dw_out[0, j] = -jnp.dot(
            grad_update, state, precision=precise, preferred_element_type=jnp.float32
        )
        g_scr[...] = (
            c_ref[0, j] * grad_state
            - lax.dot_general(
                grad_update, w_ref[0, j], (((0,), (0,)), ((), ())),
                precision=precise, preferred_element_type=jnp.float32,
            )
            + ds_ref[0, j]
        )
        return carry

    lax.fori_loop(0, nb, step, 0)


def _chunk_spec(nb, tail, reverse, count):
    if reverse:
        return pl.BlockSpec((1, nb) + tail, lambda h, b: (h, count - 1 - b, 0, 0))
    return pl.BlockSpec((1, nb) + tail, lambda h, b: (h, b, 0, 0))


def _recur_forward(u0, w, kt, c):
    heads, count, chunk, dv = u0.shape
    dk = w.shape[-1]
    nb = min(8, count)
    blocks = count // nb
    flops = 4 * heads * count * chunk * dk * dv * 6
    moved = 4 * heads * count * (2 * chunk * dv + 2 * chunk * dk + dv * dk)
    return pl.pallas_call(
        partial(_recur_fwd_kernel, nb),
        grid=(heads, blocks),
        in_specs=[
            _chunk_spec(nb, (chunk, dv), False, blocks),
            _chunk_spec(nb, (chunk, dk), False, blocks),
            _chunk_spec(nb, (chunk, dk), False, blocks),
            _chunk_spec(nb, (1, dk), False, blocks),
        ],
        out_specs=[
            _chunk_spec(nb, (dv, dk), False, blocks),
            _chunk_spec(nb, (chunk, dv), False, blocks),
        ],
        out_shape=[
            jax.ShapeDtypeStruct((heads, count, dv, dk), jnp.float32),
            jax.ShapeDtypeStruct((heads, count, chunk, dv), jnp.float32),
        ],
        scratch_shapes=[pltpu.VMEM((dv, dk), jnp.float32)],
        compiler_params=pltpu.CompilerParams(dimension_semantics=("arbitrary", "arbitrary")),
        cost_estimate=pl.CostEstimate(flops=flops, transcendentals=0, bytes_accessed=moved),
        name="delta_state_forward",
    )(u0, w, kt, c)


def _recur_backward(states, updates, w, kt, c, d_states, d_updates):
    heads, count, chunk, dv = updates.shape
    dk = w.shape[-1]
    nb = min(8, count)
    blocks = count // nb
    flops = 8 * heads * count * chunk * dk * dv * 6
    moved = 4 * heads * count * (4 * chunk * dv + 4 * chunk * dk + 2 * dv * dk)
    return pl.pallas_call(
        partial(_recur_bwd_kernel, nb),
        grid=(heads, blocks),
        in_specs=[
            _chunk_spec(nb, (dv, dk), True, blocks),
            _chunk_spec(nb, (chunk, dv), True, blocks),
            _chunk_spec(nb, (chunk, dk), True, blocks),
            _chunk_spec(nb, (chunk, dk), True, blocks),
            _chunk_spec(nb, (1, dk), True, blocks),
            _chunk_spec(nb, (dv, dk), True, blocks),
            _chunk_spec(nb, (chunk, dv), True, blocks),
        ],
        out_specs=[
            _chunk_spec(nb, (chunk, dv), True, blocks),
            _chunk_spec(nb, (chunk, dk), True, blocks),
            _chunk_spec(nb, (chunk, dk), True, blocks),
            _chunk_spec(nb, (1, dk), True, blocks),
        ],
        out_shape=[
            jax.ShapeDtypeStruct((heads, count, chunk, dv), jnp.float32),
            jax.ShapeDtypeStruct((heads, count, chunk, dk), jnp.float32),
            jax.ShapeDtypeStruct((heads, count, chunk, dk), jnp.float32),
            jax.ShapeDtypeStruct((heads, count, 1, dk), jnp.float32),
        ],
        scratch_shapes=[pltpu.VMEM((dv, dk), jnp.float32)],
        compiler_params=pltpu.CompilerParams(dimension_semantics=("arbitrary", "arbitrary")),
        cost_estimate=pl.CostEstimate(flops=flops, transcendentals=0, bytes_accessed=moved),
        name="delta_state_backward",
    )(states, updates, w, kt, c, d_states, d_updates)


@jax.custom_vjp
def state_recurrence(u0, w, kt, c):
    return _recur_forward(u0, w, kt, c)


def _recurrence_fwd(u0, w, kt, c):
    states, updates = _recur_forward(u0, w, kt, c)
    return (states, updates), (states, updates, w, kt, c)


def _recurrence_bwd(saved, grads):
    states, updates, w, kt, c = saved
    d_states, d_updates = grads
    du0, dw, dkt, dc_lanes = _recur_backward(states, updates, w, kt, c, d_states, d_updates)
    return du0, dw, dkt, dc_lanes


state_recurrence.defvjp(_recurrence_fwd, _recurrence_bwd)


def _unit_lower_inverse_small(system):
    size = system.shape[-1]
    strict = system - jnp.eye(size, dtype=system.dtype)
    power = -strict
    inverse = jnp.eye(size, dtype=system.dtype) + power
    done = 2
    while done < size:
        power = jnp.matmul(power, power, precision=precise)
        inverse = inverse + jnp.matmul(power, inverse, precision=precise)
        done *= 2
    return inverse


def _unit_lower_inverse_forward(system):
    size = system.shape[-1]
    base = min(8, size)
    lead = system.shape[:-2]
    count = size // base
    blocks = system.reshape(lead + (count, base, count, base))
    diag = jnp.stack([blocks[..., i, :, i, :] for i in range(count)], axis=-3)
    inverse = _unit_lower_inverse_small(diag)
    width = base
    while width < size:
        pairs = inverse.shape[-3] // 2
        upper = inverse[..., 0::2, :, :]
        lower = inverse[..., 1::2, :, :]
        below = jnp.stack(
            [
                system[..., (2 * i + 1) * width : (2 * i + 2) * width, 2 * i * width : (2 * i + 1) * width]
                for i in range(pairs)
            ],
            axis=-3,
        )
        corner = -jnp.matmul(
            lower, jnp.matmul(below, upper, precision=precise), precision=precise
        )
        zeros = jnp.zeros_like(upper)
        top = jnp.concatenate([upper, zeros], axis=-1)
        bottom = jnp.concatenate([corner, lower], axis=-1)
        inverse = jnp.concatenate([top, bottom], axis=-2)
        width *= 2
    return inverse[..., 0, :, :]


@jax.custom_vjp
def unit_lower_inverse(system):
    return _unit_lower_inverse_forward(system)


def _inverse_fwd(system):
    inverse = _unit_lower_inverse_forward(system)
    return inverse, inverse


def _inverse_bwd(inverse, grad):
    size = inverse.shape[-1]
    flipped = jnp.swapaxes(inverse, -1, -2)
    full = -jnp.matmul(jnp.matmul(flipped, grad, precision=precise), flipped, precision=precise)
    places = jnp.arange(size)
    return (full * (places[:, None] > places[None, :]).astype(full.dtype),)


unit_lower_inverse.defvjp(_inverse_fwd, _inverse_bwd)


def chunk_prepare(queries, keys_n, values, decays, beta_rate, seg_ids):
    length, dk = keys_n.shape
    count = length // BLOCK
    q = queries.reshape(count, BLOCK, dk)
    k = keys_n.reshape(count, BLOCK, dk)
    v = values.reshape(count, BLOCK, values.shape[1])
    beta = beta_rate.reshape(count, BLOCK)
    seg = seg_ids.reshape(count, BLOCK)
    cumulative = jnp.cumsum(decays.reshape(count, BLOCK), axis=1)
    places = jnp.arange(BLOCK)
    lower_tri = places[:, None] >= places[None, :]
    inside = jnp.logical_and(seg[:, :, None] == seg[:, None, :], lower_tri)
    log_gap = jnp.where(inside, cumulative[:, :, None] - cumulative[:, None, :], 0.0)
    within = jnp.exp(log_gap) * inside.astype(jnp.float32)
    strict = within * (places[:, None] > places[None, :]).astype(jnp.float32)
    last_seg = jnp.concatenate([jnp.full((1,), -1, seg.dtype), seg[:-1, BLOCK - 1]])
    carried = jnp.exp(cumulative) * (seg == last_seg[:, None]).astype(jnp.float32)
    key_gram = jnp.einsum("nid,njd->nij", k, k, precision=precise)
    system = jnp.eye(BLOCK, dtype=jnp.float32) + beta[:, :, None] * strict * key_gram
    right_side = jnp.concatenate([beta[:, :, None] * v, (beta * carried)[:, :, None] * k], axis=2)
    solved = jnp.matmul(unit_lower_inverse(system), right_side, precision=precise)
    dv = v.shape[2]
    kt = within[:, BLOCK - 1, :, None] * k
    scores = jnp.einsum("nid,njd->nij", q, k, precision=precise) * within
    return solved[:, :, :dv], solved[:, :, dv:], kt, carried[:, BLOCK - 1], carried, scores


def chunk_finish(queries, carried, scores, states, updates):
    count = states.shape[0]
    q = queries.reshape(count, BLOCK, queries.shape[1])
    output = carried[:, :, None] * jnp.einsum(
        "nid,nvd->niv", q, states, precision=precise
    ) + jnp.einsum("nij,njv->niv", scores, updates, precision=precise)
    return output.reshape(count * BLOCK, states.shape[1])


def delta_rule(queries, keys_n, values, decays, beta_rate, seg_ids):
    u0, w, kt, tail, carried, scores = jax.vmap(chunk_prepare, in_axes=(0, 0, 0, 0, 0, None))(
        queries, keys_n, values, decays, beta_rate, seg_ids
    )
    c = jnp.broadcast_to(tail[:, :, None, None], tail.shape + (1, w.shape[-1]))
    states, updates = state_recurrence(u0, w, kt, c)
    return jax.vmap(chunk_finish)(queries, carried, scores, states, updates)


def head_inputs(proj_query, proj_key, proj_value, proj_alpha, proj_beta,
                kernel_query, kernel_key, kernel_value, a_here, dt_here, seg_ids):
    queries = unit_norm(jax.nn.silu(short_conv(proj_query, kernel_query, seg_ids))) * (
        1.0 / math.sqrt(proj_query.shape[1])
    )
    keys_n = unit_norm(jax.nn.silu(short_conv(proj_key, kernel_key, seg_ids)))
    values = jax.nn.silu(short_conv(proj_value, kernel_value, seg_ids))
    decays = -jnp.exp(a_here) * jax.nn.softplus(proj_alpha + dt_here)
    beta_rate = jax.nn.sigmoid(proj_beta)
    return queries, keys_n, values, decays, beta_rate


def head_output(recurrent, proj_gate, o_gain, live_mask):
    return rms_norm(recurrent, o_gain, o_floor) * jax.nn.silu(proj_gate) * live_mask[:, None]


def local_mixer(
    proj_query,
    proj_key,
    proj_value,
    proj_gate,
    proj_alpha,
    proj_beta,
    kernel_query,
    kernel_key,
    kernel_value,
    a_here,
    dt_here,
    o_gain,
    seg_ids=None,
    live_mask=None,
):
    row_count = proj_query.shape[0]
    heads_here = proj_alpha.shape[1]

    def by_head(array):
        return jnp.moveaxis(array.reshape(row_count, heads_here, -1), 1, 0)

    def kernel_heads(kernel):
        return jnp.moveaxis(kernel.reshape(kernel.shape[0], heads_here, -1), 1, 0)

    queries, keys_n, values, decays, beta_rate = jax.vmap(
        head_inputs, in_axes=(0,) * 10 + (None,)
    )(
        by_head(proj_query),
        by_head(proj_key),
        by_head(proj_value),
        proj_alpha.T,
        proj_beta.T,
        kernel_heads(kernel_query),
        kernel_heads(kernel_key),
        kernel_heads(kernel_value),
        a_here,
        dt_here,
        seg_ids,
    )
    recurrent = delta_rule(queries, keys_n, values, decays, beta_rate, seg_ids)
    mixed_heads = jax.vmap(head_output, in_axes=(0, 0, None, None))(
        recurrent, by_head(proj_gate), o_gain, live_mask
    )
    return jnp.moveaxis(mixed_heads, 0, 1).reshape(row_count, -1)


MESH_ID = pl.DeviceIdType.MESH


def _ring_position(h, major, minor):
    a = h // minor
    b = h % minor
    return b * major + a + (b % 2) * (major - 1 - 2 * a)


def _ring_member(q, major, minor):
    count = major * minor
    q = (q + count) % count
    b = q // major
    r = q % major
    return (r + (b % 2) * (major - 1 - 2 * r)) * minor + b


def _ring_sides(major, minor):
    p = _ring_position(lax.axis_index("head"), major, minor)
    return p, _ring_member(p + 1, major, minor), _ring_member(p - 1, major, minor)


def _greet(nxt, prv, row):
    barrier = pltpu.get_barrier_semaphore()
    pl.semaphore_signal(barrier, 1, device_id=(prv, row), device_id_type=MESH_ID)
    pl.semaphore_signal(barrier, 1, device_id=(nxt, row), device_id_type=MESH_ID)
    pl.semaphore_wait(barrier, 2)


def _ring_gather_kernel(major, minor, x_ref, out_ref, send_sem, recv_sem):
    count = major * minor
    blk = x_ref.shape[0]
    half = blk // 2
    row = lax.axis_index("row")
    p, nxt, prv = _ring_sides(major, minor)
    out_ref[pl.ds(pl.multiple_of(lax.axis_index("head") * blk, blk), blk), :] = x_ref[...]
    _greet(nxt, prv, row)

    def piece(pos, off):
        return out_ref.at[pl.ds(pl.multiple_of(_ring_member(pos, major, minor) * blk + off, half), half)]

    def outgoing(d, s):
        pos = p - s if d == 0 else p + s
        target = nxt if d == 0 else prv
        ref = piece(pos, d * half)
        return pltpu.make_async_remote_copy(
            ref, ref, send_sem.at[d, s], recv_sem.at[d, s], device_id=(target, row),
            device_id_type=MESH_ID,
        )

    def incoming(d, s):
        pos = p - 1 - s if d == 0 else p + 1 + s
        source = prv if d == 0 else nxt
        ref = piece(pos, d * half)
        return pltpu.make_async_remote_copy(
            ref, ref, send_sem.at[d, s], recv_sem.at[d, s], device_id=(source, row),
            device_id_type=MESH_ID,
        )

    for s in range(count - 1):
        for d in (0, 1):
            if s > 0:
                incoming(d, s - 1).wait_recv()
            outgoing(d, s).start()
    for d in (0, 1):
        incoming(d, count - 2).wait_recv()
    for s in range(count - 1):
        for d in (0, 1):
            outgoing(d, s).wait_send()


def _ring_scatter_kernel(major, minor, y_ref, out_ref, buf, send_sem, recv_sem):
    count = major * minor
    blk = out_ref.shape[0]
    half = blk // 2
    row = lax.axis_index("row")
    p, nxt, prv = _ring_sides(major, minor)
    _greet(nxt, prv, row)

    def piece(pos, off):
        return y_ref.at[pl.ds(pl.multiple_of(_ring_member(pos, major, minor) * blk + off, half), half)]

    def outgoing(d, s):
        pos = p - s - 1 if d == 0 else p + s + 1
        target = nxt if d == 0 else prv
        source = piece(pos, d * half) if s == 0 else buf.at[d, s - 1]
        return pltpu.make_async_remote_copy(
            source, buf.at[d, s], send_sem.at[d, s], recv_sem.at[d, s],
            device_id=(target, row), device_id_type=MESH_ID,
        )

    def incoming(d, s):
        source = prv if d == 0 else nxt
        return pltpu.make_async_remote_copy(
            buf.at[d, s], buf.at[d, s], send_sem.at[d, s], recv_sem.at[d, s],
            device_id=(source, row), device_id_type=MESH_ID,
        )

    for s in range(count - 1):
        for d in (0, 1):
            if s > 0:
                incoming(d, s - 1).wait_recv()
                pos = p - s - 1 if d == 0 else p + s + 1
                buf[d, s - 1] = (
                    buf[d, s - 1].astype(jnp.float32)
                    + piece(pos, d * half)[...].astype(jnp.float32)
                ).astype(buf.dtype)
            outgoing(d, s).start()
    for d in (0, 1):
        incoming(d, count - 2).wait_recv()
        out_ref[pl.ds(d * half, half), :] = piece(p, d * half)[...].astype(
            jnp.float32
        ) + buf[d, count - 2].astype(jnp.float32)
    for s in range(count - 1):
        for d in (0, 1):
            outgoing(d, s).wait_send()


def ring_gather(x, ring, collective):
    major, minor = ring
    count = major * minor
    blk, width = x.shape
    return pl.pallas_call(
        partial(_ring_gather_kernel, major, minor),
        out_shape=jax.ShapeDtypeStruct((count * blk, width), x.dtype),
        in_specs=[pl.BlockSpec(memory_space=pltpu.VMEM)],
        out_specs=pl.BlockSpec(memory_space=pltpu.VMEM),
        scratch_shapes=[
            pltpu.SemaphoreType.DMA((2, count - 1)),
            pltpu.SemaphoreType.DMA((2, count - 1)),
        ],
        compiler_params=pltpu.CompilerParams(collective_id=collective, has_side_effects=True),
        name="ring_gather_head",
    )(x)


def ring_scatter(y, ring, collective):
    major, minor = ring
    count = major * minor
    rows, width = y.shape
    blk = rows // count
    return pl.pallas_call(
        partial(_ring_scatter_kernel, major, minor),
        out_shape=jax.ShapeDtypeStruct((blk, width), jnp.float32),
        in_specs=[pl.BlockSpec(memory_space=pltpu.VMEM)],
        out_specs=pl.BlockSpec(memory_space=pltpu.VMEM),
        scratch_shapes=[
            pltpu.VMEM((2, count - 1, blk // 2, width), y.dtype),
            pltpu.SemaphoreType.DMA((2, count - 1)),
            pltpu.SemaphoreType.DMA((2, count - 1)),
        ],
        compiler_params=pltpu.CompilerParams(collective_id=collective, has_side_effects=True),
        name="ring_scatter_head",
    )(y)


def head_ring(mesh):
    count = mesh.shape["head"]
    try:
        spots = [tuple(device.coords) for device in mesh.devices[:, 0]]
    except (AttributeError, TypeError):
        return (count, 1)
    moving = [axis for axis in range(len(spots[0])) if spots[0][axis] != spots[1][axis]]
    if len(moving) != 1:
        return (count, 1)
    minor = len({spot[moving[0]] for spot in spots})
    if count % minor or minor % 2:
        return (count, 1)
    return (count // minor, minor)


def contract_rows(left, right):
    return lax.dot_general(
        left, right, (((0,), (0,)), ((), ())), preferred_element_type=jnp.float32
    )


def contract_cols(left, right):
    return lax.dot_general(
        left, right, (((1,), (1,)), ((), ())), preferred_element_type=jnp.float32
    )


def on_device(
    ring,
    tokens,
    w_query,
    w_key,
    w_value,
    w_outgate,
    w_alpha,
    w_beta,
    conv_query,
    conv_key,
    conv_value,
    a_log,
    dt_bias,
    o_gain,
    w_out,
    gain_in,
    gain_ffn,
    w_gate,
    w_up,
    w_down,
    segments,
    valid_len,
    cotangent,
):
    residual = tokens[0].astype(jnp.float32)
    heads_here = w_alpha.shape[1]
    head_first = lax.axis_index("head") * heads_here
    norm_one, pull_one = jax.vjp(rms_norm, residual, gain_in)
    normed_one = norm_one.astype(jnp.bfloat16)
    row_count = lax.psum(1, "row")
    w_local = jnp.concatenate(
        [w_query, w_key, w_value, w_outgate, w_alpha, w_beta], axis=1
    ).astype(jnp.bfloat16)
    edges = [0]
    for member in (w_query, w_key, w_value, w_outgate, w_alpha, w_beta):
        edges.append(edges[-1] + member.shape[1])
    w_inward = lax.all_gather(w_local, "row", axis=0, tiled=True)
    conv_local = jnp.concatenate([conv_query, conv_key, conv_value], axis=1).astype(jnp.bfloat16)
    conv_edges = [0, conv_query.shape[1], conv_query.shape[1] + conv_key.shape[1], conv_local.shape[1]]
    conv_all = lax.all_gather(conv_local, "row", axis=1, tiled=True).reshape(
        conv_local.shape[0], row_count, conv_local.shape[1]
    )
    conv_parts = [
        conv_all[:, :, conv_edges[i] : conv_edges[i + 1]].reshape(conv_local.shape[0], -1)
        for i in range(3)
    ]
    out_matrix = lax.all_gather(w_out.astype(jnp.bfloat16), "row", axis=1, tiled=True)
    ff_width = w_gate.shape[1]
    ffn_local = jnp.concatenate([w_gate, w_up], axis=1).astype(jnp.bfloat16)
    down_local = w_down.T.astype(jnp.bfloat16)
    grad_out = cotangent[0]
    grad_out_rows = lax.all_gather(grad_out, "row", axis=0, tiled=True)
    all_rows = ring_gather(normed_one, ring, 0)
    all_rows, out_matrix, ffn_local, down_local = lax.optimization_barrier(
        (all_rows, out_matrix, ffn_local, down_local)
    )
    ffn_all = lax.all_gather(ffn_local, "head", axis=0, tiled=True)
    down_all = lax.all_gather(down_local, "head", axis=0, tiled=True)
    projected = jnp.dot(all_rows, w_inward, preferred_element_type=jnp.float32)
    proj_parts = [projected[:, edges[spot] : edges[spot + 1]] for spot in range(6)]
    seg_ids = segments[0]
    live_mask = (jnp.arange(seg_ids.shape[0]) < valid_len[0]).astype(jnp.float32)
    a_here = lax.dynamic_slice_in_dim(a_log, head_first, heads_here)
    dt_here = lax.dynamic_slice_in_dim(dt_bias, head_first, heads_here)
    mixer_fn = partial(local_mixer, seg_ids=seg_ids, live_mask=live_mask)
    mixed, pull_core = jax.vjp(
        mixer_fn,
        proj_parts[0],
        proj_parts[1],
        proj_parts[2],
        proj_parts[3],
        proj_parts[4],
        proj_parts[5],
        conv_parts[0].astype(jnp.float32),
        conv_parts[1].astype(jnp.float32),
        conv_parts[2].astype(jnp.float32),
        a_here,
        dt_here,
        o_gain,
    )
    mixed, ffn_all, grad_out_rows = lax.optimization_barrier((mixed, ffn_all, grad_out_rows))
    w_down_t = down_all
    w_gate_all = ffn_all[:, :ff_width]
    w_up_all = ffn_all[:, ff_width : 2 * ff_width]
    mixed_half = mixed.astype(jnp.bfloat16)
    mixer_output = ring_scatter(
        jnp.dot(mixed_half, out_matrix, preferred_element_type=jnp.float32).astype(jnp.bfloat16),
        ring,
        1,
    )
    middle = residual + mixer_output
    norm_two, pull_two = jax.vjp(rms_norm, middle, gain_ffn)
    normed_two = norm_two.astype(jnp.bfloat16)
    ffn_inputs = lax.all_gather(normed_two, "row", axis=0, tiled=True)
    gate_pre = jnp.dot(ffn_inputs, w_gate_all, preferred_element_type=jnp.float32)
    up_pre = jnp.dot(ffn_inputs, w_up_all, preferred_element_type=jnp.float32)
    hidden_val, pull_act = jax.vjp(swiglu, gate_pre, up_pre)
    hidden_half = hidden_val.astype(jnp.bfloat16)
    ffn_partial = contract_cols(hidden_half, w_down_t).astype(jnp.bfloat16)
    grad_hidden = jnp.dot(grad_out_rows, w_down_t, preferred_element_type=jnp.float32)
    grad_down_t = contract_rows(grad_out_rows, hidden_half)
    grad_gate_f, grad_up_f = pull_act(grad_hidden)
    grad_gate = grad_gate_f.astype(jnp.bfloat16)
    grad_upper = grad_up_f.astype(jnp.bfloat16)
    grad_wgate = contract_rows(ffn_inputs, grad_gate)
    grad_wup = contract_rows(ffn_inputs, grad_upper)
    grad_norm_two = lax.psum_scatter(
        (contract_cols(grad_gate, w_gate_all) + contract_cols(grad_upper, w_up_all)).astype(
            jnp.bfloat16
        ),
        "row",
        scatter_dimension=0,
        tiled=True,
    ).astype(jnp.float32)
    grad_mid_part, grad_gain_ffn = pull_two(grad_norm_two)
    grad_middle = grad_out.astype(jnp.float32) + grad_mid_part
    ffn_grad_cat = jnp.concatenate([grad_wgate, grad_wup, grad_down_t], axis=1).astype(
        jnp.bfloat16
    )
    grad_mid_half = grad_middle.astype(jnp.bfloat16)
    grad_mid_rows = ring_gather(grad_mid_half, ring, 2)
    ffn_output = lax.psum_scatter(ffn_partial, "row", scatter_dimension=0, tiled=True)
    grad_mid_rows, ffn_grad_cat = lax.optimization_barrier((grad_mid_rows, ffn_grad_cat))
    ffn_grad_all = lax.psum_scatter(ffn_grad_cat, "head", scatter_dimension=0, tiled=True)
    grad_mixed = contract_cols(grad_mid_rows, out_matrix)
    grad_wout = contract_rows(mixed_half, grad_mid_rows).astype(jnp.bfloat16)
    wout_grad = lax.psum_scatter(grad_wout, "row", scatter_dimension=1, tiled=True)
    core_grads = pull_core(grad_mixed)
    core_grads, ffn_output = lax.optimization_barrier((core_grads, ffn_output))
    final_out = (middle + ffn_output.astype(jnp.float32)).astype(jnp.bfloat16)
    wide = edges[4]
    grad_proj = jnp.concatenate(
        [core_grads[0], core_grads[1], core_grads[2], core_grads[3]], axis=1
    ).astype(jnp.bfloat16)
    grad_proj_ab = jnp.concatenate([core_grads[4], core_grads[5]], axis=1).astype(jnp.bfloat16)
    grad_inward = contract_rows(all_rows, grad_proj).astype(jnp.bfloat16)
    grad_inward_ab = contract_rows(all_rows, grad_proj_ab).astype(jnp.bfloat16)
    norm_one_partial = (
        contract_cols(grad_proj, w_inward[:, :wide])
        + contract_cols(grad_proj_ab, w_inward[:, wide:])
    ).astype(jnp.bfloat16)
    grad_inward, norm_one_partial = lax.optimization_barrier((grad_inward, norm_one_partial))
    grad_inward, ffn_grad_all = lax.optimization_barrier((grad_inward, ffn_grad_all))
    ffn_grad_all = ffn_grad_all.astype(jnp.float32)
    ffn_grads = (
        ffn_grad_all[:, :ff_width],
        ffn_grad_all[:, ff_width : 2 * ff_width],
        ffn_grad_all[:, 2 * ff_width :].T,
    )
    grad_norm_one = ring_scatter(norm_one_partial, ring, 3)
    grad_norm_one, wout_grad = lax.optimization_barrier((grad_norm_one, wout_grad))
    grad_in_part, grad_gain_in = pull_one(grad_norm_one)
    grad_input = grad_middle + grad_in_part
    inward_all = lax.psum_scatter(
        grad_inward, "row", scatter_dimension=0, tiled=True
    ).astype(jnp.float32)
    inward_ab = lax.psum_scatter(
        grad_inward_ab, "row", scatter_dimension=0, tiled=True
    ).astype(jnp.float32)
    conv_grad_local = jnp.concatenate(
        [
            core_grads[6 + i].reshape(conv_local.shape[0], row_count, -1)
            for i in range(3)
        ],
        axis=2,
    ).reshape(conv_local.shape[0], -1)
    conv_grad = lax.psum_scatter(
        conv_grad_local.astype(jnp.bfloat16), "row", scatter_dimension=1, tiled=True
    ).astype(jnp.float32)
    mixer_grads = tuple(inward_all[:, edges[spot] : edges[spot + 1]] for spot in range(4)) + (
        inward_ab[:, : edges[5] - wide],
        inward_ab[:, edges[5] - wide :],
    ) + tuple(
        conv_grad[:, conv_edges[i] : conv_edges[i + 1]] for i in range(3)
    ) + (wout_grad.astype(jnp.float32),)
    head_total = a_log.shape[0]
    grad_a_full = lax.dynamic_update_slice_in_dim(
        jnp.zeros((head_total,), jnp.float32), core_grads[9], head_first, 0
    )
    grad_dt_full = lax.dynamic_update_slice_in_dim(
        jnp.zeros((head_total,), jnp.float32), core_grads[10], head_first, 0
    )
    small_parts = (grad_gain_in, grad_gain_ffn, core_grads[11], grad_a_full, grad_dt_full)
    small_edges = [0]
    for part in small_parts:
        small_edges.append(small_edges[-1] + part.shape[0])
    small_width = 384
    small_rows = -(-small_edges[-1] // (16 * small_width)) * 16
    small_local = jnp.pad(
        jnp.concatenate(small_parts), (0, small_rows * small_width - small_edges[-1])
    ).reshape(small_rows, small_width)
    small_heads = ring_gather(small_local, ring, 5).reshape(-1, small_rows, small_width)
    small_all = lax.psum(jnp.sum(small_heads, axis=0), "row").reshape(-1)
    small_sums = [small_all[small_edges[i] : small_edges[i + 1]] for i in range(5)]
    return (
        final_out[None],
        grad_input[None],
        mixer_grads[0],
        mixer_grads[1],
        mixer_grads[2],
        mixer_grads[3],
        mixer_grads[4],
        mixer_grads[5],
        mixer_grads[6],
        mixer_grads[7],
        mixer_grads[8],
        small_sums[3],
        small_sums[4],
        small_sums[2],
        mixer_grads[9],
        small_sums[0],
        small_sums[1],
        ffn_grads[0],
        ffn_grads[1],
        ffn_grads[2],
    )


def solution(mesh):
    return jax.shard_map(
        partial(on_device, head_ring(mesh)),
        mesh=mesh,
        in_specs=(
            P("row", "head", None),
            P("row", "head"),
            P("row", "head"),
            P("row", "head"),
            P("row", "head"),
            P("row", "head"),
            P("row", "head"),
            P(None, ("head", "row")),
            P(None, ("head", "row")),
            P(None, ("head", "row")),
            P(),
            P(),
            P(),
            P("head", "row"),
            P(),
            P(),
            P("head", "row"),
            P("head", "row"),
            P("row", "head"),
            P("row", None),
            P("row"),
            P("row", "head", None),
        ),
        out_specs=(
            P("row", "head", None),
            P("row", "head", None),
            P("row", "head"),
            P("row", "head"),
            P("row", "head"),
            P("row", "head"),
            P("row", "head"),
            P("row", "head"),
            P(None, ("head", "row")),
            P(None, ("head", "row")),
            P(None, ("head", "row")),
            P(),
            P(),
            P(),
            P("head", "row"),
            P(),
            P(),
            P("head", "row"),
            P("head", "row"),
            P("row", "head"),
        ),
        check_vma=False,
    )
```
